32 devices in a mesh: items: 8 (over z, y), rows: 4 (over x, core).
Axes of the slice: x: 2, y: 2, z: 4, core: 2. Of those that a mesh axis runs over, the one named last changes fastest.
Arguments:
- images: bfloat16 [128, 3, 256, 256], P('items', None, 'rows'), may hold values from -6 to 6
- item_segment: int32 [128], P('items'), may hold values from 0 to 3, as said below
- conv_weight: bfloat16 [32, 3, 3, 3], replicated, may hold values from -1.25 to 1.25
- conv_bias: bfloat16 [32], replicated, may hold values from -1.5 to 1.5
- patch_weight: bfloat16 [8192, 768], replicated, may hold values from -0.125 to 0.125
- patch_bias: bfloat16 [768], replicated, may hold values from -1.5 to 1.5
- norm1_gain: bfloat16 [768], replicated, may hold values from 0.3984375 to 1.59375
- norm1_bias: bfloat16 [768], replicated, may hold values from -1.5 to 1.5
- query_weight: bfloat16 [768, 768], replicated, may hold values from -0.21875 to 0.21875
- query_bias: bfloat16 [768], replicated, may hold values from -1.5 to 1.5
- key_weight: bfloat16 [768, 768], replicated, may hold values from -0.21875 to 0.21875
- value_weight: bfloat16 [768, 768], replicated, may hold values from -0.21875 to 0.21875
- value_bias: bfloat16 [768], replicated, may hold values from -1.5 to 1.5
- output_weight: bfloat16 [768, 768], replicated, may hold values from -1.75 to 1.75
- output_bias: bfloat16 [768], replicated, may hold values from -1.5 to 1.5
- norm2_gain: bfloat16 [768], replicated, may hold values from 0.3984375 to 1.59375
- norm2_bias: bfloat16 [768], replicated, may hold values from -1.5 to 1.5
- hidden_weight: bfloat16 [768, 3072], replicated, may hold values from -0.21875 to 0.21875
- hidden_bias: bfloat16 [3072], replicated, may hold values from -1.5 to 1.5
- result_weight: bfloat16 [3072, 768], replicated, may hold values from -0.15625 to 0.15625
- result_bias: bfloat16 [768], replicated, may hold values from -1.5 to 1.5
- cotangent: bfloat16 [32768, 768], P(('items', 'rows')), may hold values from -6 to 6
Outputs:
- block_out: bfloat16 [32768, 768], P(('items', 'rows'))
- image_grad: float32 [128, 3, 256, 256], P('items', None, 'rows')
- conv_weight_grad: float32 [32, 3, 3, 3], replicated
- conv_bias_grad: float32 [32], replicated
- patch_weight_grad: float32 [8192, 768], P('items', 'rows')
- patch_bias_grad: float32 [768], replicated
- norm1_gain_grad: float32 [768], replicated
- norm1_bias_grad: float32 [768], replicated
- query_weight_grad: float32 [768, 768], P('items', 'rows')
- query_bias_grad: float32 [768], replicated
- key_weight_grad: float32 [768, 768], P('items', 'rows')
- value_weight_grad: float32 [768, 768], P('items', 'rows')
- value_bias_grad: float32 [768], replicated
- output_weight_grad: float32 [768, 768], P('items', 'rows')
- output_bias_grad: float32 [768], replicated
- norm2_gain_grad: float32 [768], replicated
- norm2_bias_grad: float32 [768], replicated
- hidden_weight_grad: float32 [768, 3072], P('items', 'rows')
- hidden_bias_grad: float32 [3072], replicated
- result_weight_grad: float32 [3072, 768], P('items', 'rows')
- result_bias_grad: float32 [768], replicated
The draws below stay inside these ranges and needn't reach their ends.
Inputs may be any that keep to these rules, and one draw needn't show every extreme that they name: `item_segment`: within each sequence of 4 consecutive items the ids start at 0 and rise by 0 or 1 from one item to the next.
All inputs are finite; a program needn't handle non-finite values.
Results may differ from the reference program's by a relative error of at most 0.02.
Values may be sent and summed in bfloat16 or wider, within the bound.
A program may use at most 640 MiB of HBM per device.

```python
import jax
import jax.numpy as jnp
from jax import lax

D = 768
HEADS = 12
HD = 64
FF = 3072
IMG = 256
PATCH = 16
CH = 32
CIN = 3
SEQ_ITEMS = 4
ITEMS = 128
NP = 16
NPATCH = 256
TOK = 1024
TOKENS = 32768
PF = 8192


def draw_item_segment(key, part):
    count = ITEMS // SEQ_ITEMS
    flags = jax.random.randint(key, (count, SEQ_ITEMS), 0, 2)
    column = jnp.arange(SEQ_ITEMS, dtype=jnp.int32)[None, :]
    rowidx = jnp.arange(count, dtype=jnp.int32)[:, None]
    flags = jnp.where(rowidx == 0, 1, flags)
    flags = jnp.where(column == 0, 0, flags)
    return jnp.cumsum(flags, axis=1).reshape(-1).astype(jnp.int32)


def block_scale(own_key, shape, pieces, smallest, top_value):
    def one(axis_at, shards_of):
        steps = jax.random.uniform(jax.random.fold_in(jax.random.fold_in(own_key, 6), axis_at), (shards_of,), jnp.float32, smallest / len(pieces), top_value / len(pieces))
        return jnp.repeat(jnp.exp(steps), shape[axis_at] // shards_of).reshape((-1,) + (1,) * (len(shape) - axis_at - 1))

    gain = one(*pieces[0])
    for cut in pieces[1:]:
        gain = gain * one(*cut)
    return gain


def noise(own_key, dims, scale, most, split=(), held_as=jnp.bfloat16):
    loudness = block_scale(own_key, dims, split, -0.22, 0.18) if split else 1.0
    entries = jax.random.normal(own_key, dims, jnp.float32) * scale * loudness
    return jnp.minimum(jnp.maximum(entries, -most), most).astype(held_as)


def setup_inputs(seed: int = 0) -> dict:
    key_of = jax.random.split(jax.random.key(seed), 23)
    return {
        "images": noise(key_of[0], (ITEMS, CIN, IMG, IMG), 1.0, 6.0, ((0, 8), (2, 4))),
        "item_segment": draw_item_segment(jax.random.fold_in(key_of[22], 71), 0),
        "conv_weight": noise(key_of[2], (CH, CIN, 3, 3), (CIN * 9) ** -0.5, 1.25),
        "conv_bias": noise(key_of[3], (CH,), 0.3, 1.5),
        "patch_weight": noise(key_of[4], (PF, D), (PF // 4) ** -0.5, 0.125),
        "patch_bias": noise(key_of[5], (D,), 0.3, 1.5),
        "norm1_gain": jnp.clip(1.0 + 0.12 * jax.random.normal(key_of[6], (D,), jnp.float32), 0.3984375, 1.59375).astype(jnp.bfloat16),
        "norm1_bias": noise(key_of[7], (D,), 0.3, 1.5),
        "query_weight": noise(key_of[8], (D, D), D ** -0.5, 0.21875),
        "query_bias": noise(key_of[9], (D,), 0.3, 1.5),
        "key_weight": noise(key_of[10], (D, D), D ** -0.5, 0.21875),
        "value_weight": noise(key_of[11], (D, D), D ** -0.5, 0.21875),
        "value_bias": noise(key_of[12], (D,), 0.3, 1.5),
        "output_weight": noise(key_of[13], (D, D), (max(D // 64, 1)) ** -0.5, 1.75),
        "output_bias": noise(key_of[14], (D,), 0.3, 1.5),
        "norm2_gain": jnp.clip(1.0 + 0.12 * jax.random.normal(key_of[15], (D,), jnp.float32), 0.3984375, 1.59375).astype(jnp.bfloat16),
        "norm2_bias": noise(key_of[16], (D,), 0.3, 1.5),
        "hidden_weight": noise(key_of[17], (D, FF), D ** -0.5, 0.21875),
        "hidden_bias": noise(key_of[18], (FF,), 0.3, 1.5),
        "result_weight": noise(key_of[19], (FF, D), (FF // 2) ** -0.5, 0.15625),
        "result_bias": noise(key_of[20], (D,), 0.3, 1.5),
        "cotangent": noise(key_of[21], (TOKENS, D), 1.0, 6.0, ((0, 32),)),
    }


@jax.custom_vjp
def low(v):
    return lax.optimization_barrier(v.astype(jnp.bfloat16)).astype(jnp.float32)

@jax.custom_vjp
def low_back(v):
    return v

def low_keep(v):
    return (low(v), None)

def low_pass(kept, grad):
    return (grad,)

def back_keep(v):
    return (v, None)

def back_low(kept, grad):
    return (low(grad),)
low.defvjp(low_keep, low_pass)
low_back.defvjp(back_keep, back_low)
highest = lax.Precision.HIGHEST

def product(left, right):
    return jnp.dot(left, right, precision=highest)

def layer_norm(values, scaling, shifting):
    centred = values - lax.optimization_barrier(jnp.mean(values, axis=-1, keepdims=True))
    spread = lax.optimization_barrier(jnp.mean(centred * centred, axis=-1, keepdims=True))
    return centred * lax.rsqrt(spread + 1e-06) * scaling + shifting

def token_mask(segments):
    order = jnp.arange(SEQ_ITEMS, dtype=jnp.int32)
    same = segments[:, None] == segments[None, :]
    first = lax.optimization_barrier(jnp.min(jnp.where(same, order[None, :], SEQ_ITEMS), axis=1))
    group = order - first
    allowed = same & (group[None, :] <= group[:, None])
    return jnp.repeat(jnp.repeat(allowed, NPATCH, axis=0), NPATCH, axis=1)

def block_forward(params, pixels, allowed):
    conv_w, conv_b, patch_w, patch_b, norm1_g, norm1_b, query_w, query_b, key_w, value_w, value_b, output_w, output_b, norm2_g, norm2_b, hidden_w, hidden_b, result_w, result_b = params
    conv = lax.conv_general_dilated(pixels, conv_w, (1, 1), ((1, 1), (1, 1)), dimension_numbers=('NCHW', 'OIHW', 'NCHW'), precision=highest)
    pre_act = low_back(conv + conv_b[None, :, None, None])
    activated = low(jax.nn.gelu(pre_act))
    tiles = activated.reshape(SEQ_ITEMS, CH, NP, PATCH, NP, PATCH).transpose(0, 2, 4, 1, 3, 5)
    patches = tiles.reshape(TOK, PF)
    tokens = low_back(low(product(patches, patch_w) + patch_b))
    normed1 = low(layer_norm(tokens, norm1_g, norm1_b))
    queries = low_back(low(product(normed1, query_w) + query_b)).reshape(TOK, HEADS, HD)
    keys = low_back(low(product(normed1, key_w))).reshape(TOK, HEADS, HD)
    values = low_back(low(product(normed1, value_w) + value_b)).reshape(TOK, HEADS, HD)
    scores = low_back(jnp.einsum('qhd,khd->hqk', queries, keys, precision=highest)) * HD ** (-0.5)
    scores = jnp.where(allowed[None], scores, -1e+30)
    row_max = lax.optimization_barrier(jnp.max(scores, axis=-1, keepdims=True))
    raised = jnp.exp(scores - row_max)
    probs = raised / lax.optimization_barrier(jnp.sum(raised, axis=-1, keepdims=True))
    probs_low = low(probs)
    attended = jnp.einsum('hqk,khd->qhd', probs_low, values, precision=highest).reshape(TOK, D)
    attended = low_back(low(attended))
    branch = low_back(product(attended, output_w) + output_b)
    middle = tokens + branch
    normed2 = low(layer_norm(middle, norm2_g, norm2_b))
    hidden_pre = low_back(product(normed2, hidden_w) + hidden_b)
    hidden_act = low(jax.nn.gelu(hidden_pre))
    mixed = low_back(product(hidden_act, result_w) + result_b)
    return middle + mixed

def reference(images, item_segment, conv_weight, conv_bias, patch_weight, patch_bias, norm1_gain, norm1_bias, query_weight, query_bias, key_weight, value_weight, value_bias, output_weight, output_bias, norm2_gain, norm2_bias, hidden_weight, hidden_bias, result_weight, result_bias, cotangent):
    params = tuple((v.astype(jnp.float32) for v in (conv_weight, conv_bias, patch_weight, patch_bias, norm1_gain, norm1_bias, query_weight, query_bias, key_weight, value_weight, value_bias, output_weight, output_bias, norm2_gain, norm2_bias, hidden_weight, hidden_bias, result_weight, result_bias)))
    pixels = images.astype(jnp.float32).reshape(-1, SEQ_ITEMS, CIN, IMG, IMG)
    segments = item_segment.reshape(-1, SEQ_ITEMS)
    upstream = cotangent.astype(jnp.float32).reshape(-1, TOK, D)
    zero_grads = jax.tree.map(jnp.zeros_like, params)

    def one_sequence(totals, inputs):
        seq_pixels, seq_segments, seq_upstream = inputs
        allowed = token_mask(seq_segments)

        def forward(weights, picture):
            return block_forward(weights, picture, allowed)
        result, pullback = jax.vjp(forward, params, seq_pixels)
        weight_grads, pixel_grad = pullback(seq_upstream)
        totals = jax.tree.map(jnp.add, totals, weight_grads)
        return (totals, (result.astype(jnp.bfloat16), pixel_grad))
    totals, outputs = lax.scan(one_sequence, zero_grads, (pixels, segments, upstream))
    results, pixel_grads = outputs
    return (results.reshape(-1, D), pixel_grads.reshape(images.shape), totals[0], totals[1], totals[2], totals[3], totals[4], totals[5], totals[6], totals[7], totals[8], totals[9], totals[10], totals[11], totals[12], totals[13], totals[14], totals[15], totals[16], totals[17], totals[18])
```

```python
import functools

import jax
import jax.numpy as jnp
from jax import lax
from jax.experimental import pallas as pl
from jax.experimental.pallas import tpu as pltpu
from jax.sharding import PartitionSpec as P

BF = jnp.bfloat16
F32 = jnp.float32
D = 768
HEADS = 12
HD = 64
FF = 3072
IMG = 256
PATCH = 16
CH = 32
CIN = 3
SEQ_ITEMS = 4
NPATCH = 256
TOK = 1024
NP = IMG // PATCH
PF = CH * PATCH * PATCH
HALF = 64
WIN = PATCH + 2
ONE_LANE = CIN * WIN
SLABS = (PATCH + 2) // 2
STEPS = PATCH // 2
FEAT = PF // STEPS
GELU_A = 0.7978845608028654
GELU_B = GELU_A * 0.044715
VMEM_CAP = 60 * 1024 * 1024


def mm(left, right):
    return jnp.dot(left, right, preferred_element_type=F32)


def mm_t(left, right):
    return lax.dot_general(left, right, (((1,), (1,)), ((), ())), preferred_element_type=F32)


def params(**extra):
    return pltpu.CompilerParams(vmem_limit_bytes=VMEM_CAP, **extra)


def whole(shape):
    zeros = (0,) * len(shape)
    return pl.BlockSpec(shape, lambda *_: zeros, pipeline_mode=pl.Buffered(1))


def gelu_pair(v):
    square = v * v
    gate = 0.5 + 0.5 * jnp.tanh(v * (GELU_A + GELU_B * square))
    act = v * gate
    slope = gate + act * (1.0 - gate) * (2.0 * GELU_A + (6.0 * GELU_B) * square)
    return act, slope


def patchify_kernel(img_ref, top_ref, bot_ref, x_ref, xt_ref, sel_ref, pix, rows):
    items, _, height, width = img_ref.shape
    nrow = height // PATCH
    group = items * nrow
    for ch in range(CIN):
        for item in range(items):
            full = img_ref[item, ch].astype(F32)
            for k in range(width // 128):
                pix[ch, k, item * height : (item + 1) * height, :] = full[:, k * 128 : (k + 1) * 128]
    patch_row = lax.broadcasted_iota(jnp.int32, (group, width), 0) % nrow
    for ch in range(CIN):
        cols = slice(ch * width, (ch + 1) * width)
        for r in range(PATCH):
            v = jnp.concatenate([pix[ch, k, pl.ds(r, group, stride=PATCH), :] for k in range(width // 128)], axis=1)
            rows[(r + 1) * group : (r + 2) * group, cols] = v.astype(BF)
            if r == PATCH - 1:
                up = jnp.where(patch_row == 0, top_ref[ch], pltpu.roll(v, 1, 0))
                rows[0:group, cols] = up.astype(BF)
            if r == 0:
                down = jnp.where(patch_row == nrow - 1, bot_ref[ch], pltpu.roll(v, group - 1, 0))
                rows[(PATCH + 1) * group : (PATCH + 2) * group, cols] = down.astype(BF)
    lane = lax.broadcasted_iota(jnp.int32, (1, NP * HALF), 1)
    col, spot = lane // HALF, lane % HALF
    for ch in range(CIN):
        inside = (spot >= WIN * ch) & (spot < WIN * (ch + 1))
        want = jnp.where(inside, PATCH * col + spot - WIN * ch - 1, -5)
        here = lax.broadcasted_iota(jnp.int32, (width, NP * HALF), 0)
        sel_ref[ch * width : (ch + 1) * width, :] = jnp.where(here == want, 1.0, 0.0).astype(BF)
    lane = lax.broadcasted_iota(jnp.int32, (group, 2 * HALF), 1)
    low = lane < HALF
    ones = (lane % HALF) == ONE_LANE
    for quarter in range(NP * HALF // 256):
        res = mm(rows[...], sel_ref[:, quarter * 256 : (quarter + 1) * 256])
        for j in range(SLABS):
            first = res[2 * j * group : (2 * j + 1) * group]
            second = res[(2 * j + 1) * group : (2 * j + 2) * group]
            for pair in range(2):
                a = first[:, pair * 128 : (pair + 1) * 128]
                b = second[:, pair * 128 : (pair + 1) * 128]
                even = jnp.where(ones, 1.0, jnp.where(low, a, pltpu.roll(b, HALF, 1)))
                odd = jnp.where(ones, 1.0, jnp.where(low, pltpu.roll(a, HALF, 1), b))
                at = (quarter * 4 + pair * 2) * group
                x_ref[j, at : at + group, :] = even.astype(BF)
                x_ref[j, at + group : at + 2 * group, :] = odd.astype(BF)
    for j in range(SLABS):
        xt_ref[j] = x_ref[j].T


def patchify(images, top, bot):
    items, _, height, width = images.shape
    tokens = items * (height // PATCH) * NP
    return pl.pallas_call(
        patchify_kernel,
        name="patchify",
        out_shape=(
            jax.ShapeDtypeStruct((SLABS, tokens, 128), BF),
            jax.ShapeDtypeStruct((SLABS, 128, tokens), BF),
            jax.ShapeDtypeStruct((CIN * width, NP * HALF), BF),
        ),
        scratch_shapes=[
            pltpu.VMEM((CIN, width // 128, items * height, 128), F32),
            pltpu.VMEM((WIN * tokens // NP, CIN * width), BF),
        ],
        compiler_params=params(),
    )(images, top, bot)


def stem_kernel(x_ref, t_ref, w_ref, pb_ref, tok_ref, act_ref, slope_ref, acc, nat):
    p = pl.program_id(0)
    tokens = acc.shape[0]
    group = tokens // NP

    @pl.when(p == 0)
    def _():
        acc[...] = jnp.broadcast_to(pb_ref[...], acc.shape)

    weight = w_ref[...].reshape(FEAT, D)
    for s in range(tokens // 256):
        rs = slice(s * 256, (s + 1) * 256)
        xs = jnp.concatenate([x_ref[p, rs, :], x_ref[p + 1, rs, :]], axis=1)
        for n in range(FEAT // 256):
            cs = slice(n * 256, (n + 1) * 256)
            pre = mm(xs, t_ref[:, cs])
            act, slope = gelu_pair(pre)
            act_ref[0, rs, cs] = act.astype(BF)
            slope_ref[0, rs, cs] = slope.astype(BF)
        acc[rs, :] += mm(act_ref[0, rs, :], weight)

    @pl.when(p == STEPS - 1)
    def _():
        for c in range(NP):
            for k in range(D // 128):
                nat[k, pl.ds(c, group, stride=NP), :] = acc[c * group : (c + 1) * group, k * 128 : (k + 1) * 128]
        for k in range(D // 128):
            tok_ref[:, k * 128 : (k + 1) * 128] = nat[k].astype(BF)


def stem_forward(x, taps, weight, bias):
    tokens = x.shape[1]
    return pl.pallas_call(
        stem_kernel,
        name="stem_forward",
        grid=(STEPS,),
        in_specs=[
            whole(x.shape),
            whole(taps.shape),
            pl.BlockSpec((CH, 1, 2 * PATCH, D), lambda p: (0, p, 0, 0)),
            whole((1, D)),
        ],
        out_specs=(
            whole((tokens, D)),
            pl.BlockSpec((1, tokens, FEAT), lambda p: (p, 0, 0)),
            pl.BlockSpec((1, tokens, FEAT), lambda p: (p, 0, 0)),
        ),
        out_shape=(
            jax.ShapeDtypeStruct((tokens, D), BF),
            jax.ShapeDtypeStruct((STEPS, tokens, FEAT), BF),
            jax.ShapeDtypeStruct((STEPS, tokens, FEAT), BF),
        ),
        scratch_shapes=[pltpu.VMEM((tokens, D), F32), pltpu.VMEM((D // 128, tokens, 128), F32)],
        compiler_params=params(),
    )(x, taps, weight, bias)


def norm_stats(v):
    centred = v - jnp.mean(v, axis=-1, keepdims=True)
    inv = lax.rsqrt(jnp.mean(centred * centred, axis=-1, keepdims=True) + 1e-06)
    return centred * inv, inv


def three_terms(v):
    hi = v.astype(BF)
    rest = v - hi.astype(F32)
    mid = rest.astype(BF)
    lo = (rest - mid.astype(F32)).astype(BF)
    return hi, mid, lo


def minus_terms(v, lane, base):
    hi, mid, lo = three_terms(-v)
    out = jnp.where(lane == 4, hi.astype(F32), base)
    out = jnp.where(lane == 5, mid.astype(F32), out)
    return jnp.where(lane == 6, lo.astype(F32), out).astype(BF)


def attend_kernel(tok_ref, g_ref, b_ref, qx_ref, kx_ref, wq_ref, wk_ref, wv_ref, qb_ref, vb_ref,
                  q_ref, k_ref, v_ref, o_ref, lx_ref, n1, kaug, vaug):
    @pl.when(pl.program_id(0) == 0)
    def _():
        for s in range(TOK // 128):
            rs = slice(s * 128, (s + 1) * 128)
            hat, _ = norm_stats(tok_ref[rs, :].astype(F32))
            n1[rs, :] = (hat * g_ref[...] + b_ref[...]).astype(BF)

    q_ref[...] = ((mm(n1[...], wq_ref[...]) + qb_ref[...]).astype(BF) * 0.125).astype(BF)
    k_ref[...] = mm(n1[...], wk_ref[...]).astype(BF)
    v_ref[...] = (mm(n1[...], wv_ref[...]) + vb_ref[...]).astype(BF)
    lane = lax.broadcasted_iota(jnp.int32, (NPATCH, 128), 1)
    low = lane < HD
    for i in range(SEQ_ITEMS):
        rs = slice(i * NPATCH, (i + 1) * NPATCH)
        kaug[rs, 128:256] = jnp.broadcast_to(kx_ref[i : i + 1, :], (NPATCH, 128)).astype(BF)
        vaug[rs, 128:256] = jnp.ones((NPATCH, 128), BF)
    for pair in range(2):
        cs = slice(pair * 128, (pair + 1) * 128)
        kaug[:, 0:128] = k_ref[:, cs]
        vaug[:, 0:128] = v_ref[:, cs]
        for i in range(SEQ_ITEMS):
            rs = slice(i * NPATCH, (i + 1) * NPATCH)
            span = slice(0, (i + 1) * NPATCH)
            qp = q_ref[rs, cs]
            qx = jnp.broadcast_to(qx_ref[i : i + 1, :], (NPATCH, 128))
            halves = []
            for h in range(2):
                mine = low if h == 0 else ~low
                qaug = jnp.concatenate([jnp.where(mine, qp, jnp.zeros_like(qp)), qx.astype(BF)], axis=1)
                scores = mm_t(qaug, kaug[span, :])
                top = jnp.max(scores, axis=1, keepdims=True)
                raised = jnp.exp(scores - top).astype(BF)
                out = mm(raised, vaug[span, :])
                total = out[:, 128:256]
                halves.append(out[:, 0:128] / total)
                lx_ref[pair * 2 + h, rs, :] = minus_terms(top + jnp.log(total), lane, qx)
            o_ref[rs, cs] = jnp.where(low, halves[0], halves[1]).astype(BF)


def attend(tokens, gain, shift, qx, kx, wq, wk, wv, qb, vb):
    col = pl.BlockSpec((D, 256), lambda g: (0, g))
    row = pl.BlockSpec((1, 256), lambda g: (0, g))
    out = pl.BlockSpec((TOK, 256), lambda g: (0, g))
    return pl.pallas_call(
        attend_kernel,
        name="attend",
        grid=(D // 256,),
        in_specs=[whole((TOK, D)), whole((1, D)), whole((1, D)), whole(qx.shape), whole(kx.shape),
                  col, col, col, row, row],
        out_specs=(out, out, out, out, pl.BlockSpec((4, TOK, 128), lambda g: (g, 0, 0))),
        out_shape=(jax.ShapeDtypeStruct((TOK, D), BF),) * 4 + (jax.ShapeDtypeStruct((HEADS, TOK, 128), BF),),
        scratch_shapes=[pltpu.VMEM((TOK, D), BF), pltpu.VMEM((TOK, 256), BF), pltpu.VMEM((TOK, 256), BF)],
        compiler_params=params(),
    )(tokens, gain, shift, qx, kx, wq, wk, wv, qb, vb)


def norm_back(e, hat, inv, gain):
    f = e * gain
    return inv * (f - jnp.mean(f, axis=-1, keepdims=True) - hat * jnp.mean(f * hat, axis=-1, keepdims=True))


def col_sum(v):
    return jnp.sum(v, axis=0, keepdims=True)


def store_square(ref, n, grad):
    items, rows, _, height, width = ref.shape
    for r in range(rows):
        ref[:, r, n] = grad[:, r * width : (r + 1) * width].reshape(items, height, width)


def mixer_kernel(tok_ref, att_ref, cot_ref, wo_ref, vec_ref, wh_ref, hb_ref, wr_ref,
                 out_ref, mid_ref, ag_ref, wog_ref, whg_ref, wrg_ref, sums_ref, hbg_ref,
                 middle, n2, n2t, cott, acc, back, act, hg):
    step = pl.program_id(0)
    last = pl.num_programs(0) - 1
    chunk = wh_ref.shape[1]
    blocks = [slice(s * 256, (s + 1) * 256) for s in range(TOK // 256)]

    @pl.when(step == 0)
    def _():
        for rs in blocks:
            row = tok_ref[rs, :].astype(F32) + mm(att_ref[rs, :], wo_ref[...]) + vec_ref[0:1, :]
            middle[rs, :] = row
            acc[rs, :] = row + vec_ref[3:4, :]
            back[rs, :] = jnp.zeros((256, D), F32)
            hat, _ = norm_stats(row)
            low = (hat * vec_ref[1:2, :] + vec_ref[2:3, :]).astype(BF)
            n2[rs, :] = low
            n2t[:, rs] = low.T
            cott[:, rs] = cot_ref[rs, :].T

    hsum = jnp.zeros((1, chunk), F32)
    for rs in blocks:
        for n in range(chunk // 128 // 3):
            cs = slice(n * 384, (n + 1) * 384)
            pre = mm(n2[rs, :], wh_ref[:, cs]) + hb_ref[:, cs]
            up = mm_t(cot_ref[rs, :], wr_ref[cs, :])
            a, slope = gelu_pair(pre)
            act[rs, cs] = a.astype(BF)
            hg[rs, cs] = (slope * up).astype(BF)
        acc[rs, :] += mm(act[rs, :], wr_ref[...])
        back[rs, :] += mm_t(hg[rs, :], wh_ref[...])
        hsum = hsum + col_sum(hg[rs, :].astype(F32))
    hbg_ref[...] = hsum
    grad = mm(n2t[...], hg[...]).astype(BF)
    whg_ref[...] = grad.reshape(whg_ref.shape)
    grad = mm(cott[...], act[...]).astype(BF)
    rows, width = wrg_ref.shape[1], wrg_ref.shape[3]
    for c in range(wrg_ref.shape[0]):
        wrg_ref[c] = grad[:, c * width : (c + 1) * width].reshape(rows, D // rows, width)

    @pl.when(step == last)
    def _():
        gsum = jnp.zeros((1, D), F32)
        bsum = jnp.zeros((1, D), F32)
        osum = jnp.zeros((1, D), F32)
        rsum = jnp.zeros((1, D), F32)
        for rs in blocks:
            out_ref[rs, :] = acc[rs, :].astype(BF)
            hat, inv = norm_stats(middle[rs, :])
            e = back[rs, :]
            gsum = gsum + col_sum(e * hat)
            bsum = bsum + col_sum(e)
            cot = cot_ref[rs, :].astype(F32)
            rsum = rsum + col_sum(cot)
            mid = cot + norm_back(e, hat, inv, vec_ref[1:2, :])
            mid_ref[rs, :] = mid
            low = mid.astype(BF)
            osum = osum + col_sum(low.astype(F32))
            n2[rs, :] = low
            n2t[:, rs] = att_ref[rs, :].T
            ag_ref[rs, :] = mm_t(low, wo_ref[...]).astype(BF)
        store_square(wog_ref, 0, mm(n2t[...], n2[...]).astype(BF))
        sums_ref[0:1, :] = gsum
        sums_ref[1:2, :] = bsum
        sums_ref[2:3, :] = osum
        sums_ref[3:4, :] = rsum


def mixer(tokens, attended, cotangent, wo, vecs, wh, hb, wr, items, rows):
    chunk = FF // rows
    per = items // rows
    return pl.pallas_call(
        mixer_kernel,
        name="mixer",
        grid=(rows,),
        in_specs=[
            whole((TOK, D)), whole((TOK, D)), whole((TOK, D)), whole((D, D)), whole(vecs.shape),
            pl.BlockSpec((D, chunk), lambda r: (0, r)),
            pl.BlockSpec((1, chunk), lambda r: (0, r)),
            pl.BlockSpec((chunk, D), lambda r: (r, 0)),
        ],
        out_specs=(
            whole((TOK, D)), whole((TOK, D)), whole((TOK, D)), whole((items, rows, 1, D // items, D // rows)),
            pl.BlockSpec((items, 1, D // items, chunk), lambda r: (0, r, 0, 0)),
            pl.BlockSpec((per, rows, D // rows, FF // items), lambda r: (r, 0, 0, 0)),
            whole((8, D)),
            pl.BlockSpec((1, chunk), lambda r: (0, r)),
        ),
        out_shape=(
            jax.ShapeDtypeStruct((TOK, D), BF),
            jax.ShapeDtypeStruct((TOK, D), F32),
            jax.ShapeDtypeStruct((TOK, D), BF),
            jax.ShapeDtypeStruct((items, rows, 1, D // items, D // rows), BF),
            jax.ShapeDtypeStruct((items, rows, D // items, chunk), BF),
            jax.ShapeDtypeStruct((items, rows, D // rows, FF // items), BF),
            jax.ShapeDtypeStruct((8, D), F32),
            jax.ShapeDtypeStruct((1, FF), F32),
        ),
        scratch_shapes=[
            pltpu.VMEM((TOK, D), F32), pltpu.VMEM((TOK, D), BF), pltpu.VMEM((D, TOK), BF),
            pltpu.VMEM((D, TOK), BF), pltpu.VMEM((TOK, D), F32), pltpu.VMEM((TOK, D), F32),
            pltpu.VMEM((TOK, chunk), BF), pltpu.VMEM((TOK, chunk), BF),
        ],
        compiler_params=params(),
    )(tokens, attended, cotangent, wo, vecs, wh, hb, wr)


def attend_back_kernel(tok_ref, g_ref, b_ref, kx_ref, mid_ref, q_ref, k_ref, v_ref, o_ref, ag_ref, lx_ref,
                       wq_ref, wk_ref, wv_ref,
                       tg_ref, sq_ref, sums_ref, qvs_ref,
                       n1t, back, kaug, vaug, qaug, oaug, dqt, dq, dk, dv, square):
    step = pl.program_id(0)
    blocks = [slice(s * 256, (s + 1) * 256) for s in range(TOK // 256)]

    @pl.when(step == 0)
    def _():
        for rs in blocks:
            hat, _ = norm_stats(tok_ref[rs, :].astype(F32))
            n1t[:, rs] = (hat * g_ref[...] + b_ref[...]).astype(BF).T
            back[rs, :] = jnp.zeros((256, D), F32)

    lane = lax.broadcasted_iota(jnp.int32, (NPATCH, 128), 1)
    low = lane < HD
    ones = jnp.where((lane >= 4) & (lane < 7), 1.0, 0.0).astype(BF)
    for i, rs in enumerate(blocks):
        kaug[rs, 128:256] = jnp.broadcast_to(kx_ref[i : i + 1, :], (NPATCH, 128)).astype(BF)
        vaug[rs, 128:256] = ones
    pick_row = lax.broadcasted_iota(jnp.int32, (256, 256), 0) % 128 // HD
    pick_col = lax.broadcasted_iota(jnp.int32, (256, 256), 1) // 128
    pick = jnp.where(pick_row == pick_col, 1.0, 0.0).astype(BF)
    for pair in range(2):
        cs = slice(pair * 128, (pair + 1) * 128)
        kaug[:, 0:128] = k_ref[:, cs]
        vaug[:, 0:128] = v_ref[:, cs]
        kt = k_ref[:, cs].T
        for rs in blocks:
            qp = q_ref[rs, cs]
            gp = ag_ref[rs, cs]
            prod = gp.astype(F32) * o_ref[rs, cs].astype(F32)
            hi = prod.astype(BF)
            both = jnp.concatenate([hi, (prod - hi.astype(F32)).astype(BF)], axis=1)
            dots = mm(both, pick)
            for h in range(2):
                mine = low if h == 0 else ~low
                qaug[h, rs, 0:128] = jnp.where(mine, qp, jnp.zeros_like(qp))
                qaug[h, rs, 128:256] = lx_ref[pair * 2 + h, rs, :]
                oaug[h, rs, 0:128] = jnp.where(mine, gp, jnp.zeros_like(gp))
                oaug[h, rs, 128:256] = minus_terms(dots[:, h * 128 : (h + 1) * 128], lane, jnp.zeros((NPATCH, 128), F32))
        for j, rs in enumerate(blocks):
            span = slice(j * NPATCH, TOK)
            parts_k, parts_v = [], []
            for h in range(2):
                probs = jnp.exp(mm_t(kaug[rs, :], qaug[h, span, :]))
                rise = mm_t(vaug[rs, :], oaug[h, span, :])
                grad = (probs * rise).astype(BF)
                probs_low = probs.astype(BF)
                parts_v.append(mm(probs_low, ag_ref[span, cs]))
                parts_k.append(mm(grad, q_ref[span, cs]))
                hs = slice(h * HD, (h + 1) * HD)
                part = mm(kt[hs, rs], grad)
                if j == 0:
                    dqt[hs, :] = part
                else:
                    dqt[hs, span] += part
            dk[rs, cs] = jnp.where(low, parts_k[0], parts_k[1]).astype(BF)
            dv[rs, cs] = jnp.where(low, parts_v[0], parts_v[1]).astype(BF)
        dq[:, cs] = (dqt[...].T * 0.125).astype(BF)
    qvs_ref[0:1, :] = col_sum(dq[...].astype(F32))
    qvs_ref[1:2, :] = col_sum(dv[...].astype(F32))
    for n, part in enumerate((dq, dk, dv)):
        square[n, step] = mm(n1t[...], part[...]).astype(BF)
    for rs in blocks:
        back[rs, :] += (
            mm_t(dq[rs, :], wq_ref[...]) + mm_t(dk[rs, :], wk_ref[...]) + mm_t(dv[rs, :], wv_ref[...])
        )

    @pl.when(step == pl.num_programs(0) - 1)
    def _():
        gsum = jnp.zeros((1, D), F32)
        bsum = jnp.zeros((1, D), F32)
        for rs in blocks:
            hat, inv = norm_stats(tok_ref[rs, :].astype(F32))
            e = back[rs, :]
            gsum = gsum + col_sum(e * hat)
            bsum = bsum + col_sum(e)
            tg_ref[rs, :] = (mid_ref[rs, :] + norm_back(e, hat, inv, g_ref[...])).astype(BF)
        sums_ref[0:1, :] = gsum
        sums_ref[1:2, :] = bsum
        for n in range(3):
            store_square(sq_ref, n, jnp.concatenate([square[n, g] for g in range(D // 256)], axis=1))


def attend_back(tokens, gain, shift, kx, mid, q, k, v, o, ag, lx, wq, wk, wv, items, rows):
    squares = (items, rows, 3, D // items, D // rows)
    col = pl.BlockSpec((D, 256), lambda g: (0, g))
    part = pl.BlockSpec((TOK, 256), lambda g: (0, g))
    return pl.pallas_call(
        attend_back_kernel,
        name="attend_back",
        grid=(D // 256,),
        in_specs=[whole((TOK, D)), whole((1, D)), whole((1, D)), whole(kx.shape), whole((TOK, D)),
                  part, part, part, part, part, pl.BlockSpec((4, TOK, 128), lambda g: (g, 0, 0)),
                  col, col, col],
        out_specs=(whole((TOK, D)), whole(squares), whole((8, D)), pl.BlockSpec((8, 256), lambda g: (0, g))),
        out_shape=(
            jax.ShapeDtypeStruct((TOK, D), BF),
            jax.ShapeDtypeStruct(squares, BF),
            jax.ShapeDtypeStruct((8, D), F32),
            jax.ShapeDtypeStruct((8, D), F32),
        ),
        scratch_shapes=[
            pltpu.VMEM((D, TOK), BF), pltpu.VMEM((TOK, D), F32),
            pltpu.VMEM((TOK, 256), BF), pltpu.VMEM((TOK, 256), BF),
            pltpu.VMEM((2, TOK, 256), BF), pltpu.VMEM((2, TOK, 256), BF),
            pltpu.VMEM((128, TOK), F32),
            pltpu.VMEM((TOK, 256), BF), pltpu.VMEM((TOK, 256), BF), pltpu.VMEM((TOK, 256), BF),
            pltpu.VMEM((3, D // 256, D, 256), BF),
        ],
        compiler_params=params(),
    )(tokens, gain, shift, kx, mid, q, k, v, o, ag, lx, wq, wk, wv)


def patch_grad_kernel(tg_ref, act_ref, tgc_ref, wg_ref, sums_ref, nat, tgt):
    tokens = nat.shape[1]
    group = tokens // NP

    @pl.when(pl.program_id(0) == 0)
    def _():
        for k in range(D // 128):
            nat[k] = tg_ref[:, k * 128 : (k + 1) * 128].astype(F32)
        total = jnp.zeros((1, D), F32)
        for c in range(NP):
            part = jnp.concatenate([nat[k, pl.ds(c, group, stride=NP), :] for k in range(D // 128)], axis=1)
            total = total + col_sum(part)
            tgc_ref[c * group : (c + 1) * group, :] = part.astype(BF)
        sums_ref[0:1, :] = total
        for s in range(tokens // 256):
            rs = slice(s * 256, (s + 1) * 256)
            tgt[:, rs] = tgc_ref[rs, :].T

    items, rows = wg_ref.shape[0], wg_ref.shape[1]
    width = FEAT // items
    for n in range(FEAT // 256):
        grad = mm(tgt[...], act_ref[0, :, n * 256 : (n + 1) * 256]).astype(BF)
        for c in range(256 // width):
            piece = grad[:, c * width : (c + 1) * width]
            wg_ref[n * (256 // width) + c, :, 0, :, :] = piece.reshape(rows, D // rows, width)


def patch_grad(tg, act, items, rows):
    tokens = tg.shape[0]
    return pl.pallas_call(
        patch_grad_kernel,
        name="patch_grad",
        grid=(STEPS,),
        in_specs=[whole((tokens, D)), pl.BlockSpec((1, tokens, FEAT), lambda p: (p, 0, 0))],
        out_specs=(
            whole((tokens, D)),
            pl.BlockSpec((items, rows, 1, D // rows, FEAT // items), lambda p: (0, 0, p, 0, 0)),
            whole((8, D)),
        ),
        out_shape=(
            jax.ShapeDtypeStruct((tokens, D), BF),
            jax.ShapeDtypeStruct((items, rows, STEPS, D // rows, FEAT // items), BF),
            jax.ShapeDtypeStruct((8, D), F32),
        ),
        scratch_shapes=[pltpu.VMEM((D // 128, tokens, 128), F32), pltpu.VMEM((D, tokens), BF)],
        compiler_params=params(),
    )(tg, act)


def stem_back_kernel(tg_ref, w_ref, slope_ref, xt_ref, t_ref, dx_ref, taps_ref, dxa, pg, cw_ref):
    p = pl.program_id(0)
    tokens = tg_ref.shape[0]
    weight = w_ref[...].reshape(FEAT, D)

    @pl.when(p == 0)
    def _():
        cw_ref[...] = jnp.zeros_like(cw_ref)
        dxa[0] = jnp.zeros((tokens, 128), F32)

    for s in range(tokens // 256):
        rs = slice(s * 256, (s + 1) * 256)
        for n in range(FEAT // 256):
            cs = slice(n * 256, (n + 1) * 256)
            da = mm_t(tg_ref[rs, :], weight[cs, :])
            pg[rs, cs] = (slope_ref[0, rs, cs].astype(F32) * da).astype(BF)
        back = mm_t(pg[rs, :], t_ref[...])
        dxa[p, rs, :] += back[:, 0:128]
        dxa[p + 1, rs, :] = back[:, 128:256]
    xt = jnp.concatenate([xt_ref[p], xt_ref[p + 1]], axis=0)
    cw_ref[...] += mm(xt, pg[...])

    @pl.when(p == STEPS - 1)
    def _():
        for j in range(SLABS):
            dx_ref[j] = dxa[j].astype(BF)
        taps_ref[...] = tap_grad_rows(cw_ref[...])


def stem_back(tg, weight, slope, xt, taps):
    tokens = tg.shape[0]
    return pl.pallas_call(
        stem_back_kernel,
        name="stem_back",
        grid=(STEPS,),
        in_specs=[
            whole((tokens, D)),
            pl.BlockSpec((CH, 1, 2 * PATCH, D), lambda p: (0, p, 0, 0)),
            pl.BlockSpec((1, tokens, FEAT), lambda p: (p, 0, 0)),
            whole(xt.shape),
            whole(taps.shape),
        ],
        out_specs=(whole((SLABS, tokens, 128)), whole((32, 128))),
        out_shape=(
            jax.ShapeDtypeStruct((SLABS, tokens, 128), BF),
            jax.ShapeDtypeStruct((32, 128), F32),
        ),
        scratch_shapes=[
            pltpu.VMEM((SLABS, tokens, 128), F32), pltpu.VMEM((tokens, FEAT), BF), pltpu.VMEM((256, FEAT), F32),
        ],
        compiler_params=params(),
    )(tg, weight, slope, xt, taps)


def image_grad_kernel(dx_ref, sel_ref, ig_ref, edge_ref, rows, flat):
    items, _, height, width = ig_ref.shape
    nrow = height // PATCH
    group = items * nrow
    low = lax.broadcasted_iota(jnp.int32, (group, 2 * HALF), 1) < HALF
    for j in range(SLABS):
        for pair in range(NP // 2):
            at = 2 * pair * group
            a = dx_ref[j, at : at + group, :].astype(F32)
            b = dx_ref[j, at + group : at + 2 * group, :].astype(F32)
            cs = slice(pair * 128, (pair + 1) * 128)
            rows[2 * j * group : (2 * j + 1) * group, cs] = jnp.where(low, a, pltpu.roll(b, HALF, 1)).astype(BF)
            rows[(2 * j + 1) * group : (2 * j + 2) * group, cs] = jnp.where(low, pltpu.roll(a, HALF, 1), b).astype(BF)
    patch_row = lax.broadcasted_iota(jnp.int32, (group, width), 0) % nrow
    for ch in range(CIN):
        cs = slice(ch * width, (ch + 1) * width)
        res = mm_t(rows[...], sel_ref[cs, :])
        head = res[0:group]
        tail = res[(PATCH + 1) * group : (PATCH + 2) * group]
        edge_ref[0, ch] = head
        edge_ref[1, ch] = tail
        for r in range(PATCH):
            v = res[(r + 1) * group : (r + 2) * group]
            if r == 0:
                v = v + jnp.where(patch_row == 0, 0.0, pltpu.roll(tail, 1, 0))
            if r == PATCH - 1:
                v = v + jnp.where(patch_row == nrow - 1, 0.0, pltpu.roll(head, group - 1, 0))
            flat[0, pl.ds(r, group, stride=PATCH), :] = v[:, 0:128]
            flat[1, pl.ds(r, group, stride=PATCH), :] = v[:, 128:256]
        for item in range(items):
            at = slice(item * height, (item + 1) * height)
            ig_ref[item, ch, :, 0:128] = flat[0, at, :]
            ig_ref[item, ch, :, 128:256] = flat[1, at, :]


def image_grad_call(dx, sel, items, height):
    group = items * height // PATCH
    return pl.pallas_call(
        image_grad_kernel,
        name="image_grad",
        out_shape=(
            jax.ShapeDtypeStruct((items, CIN, height, IMG), F32),
            jax.ShapeDtypeStruct((2, CIN, group, IMG), F32),
        ),
        scratch_shapes=[
            pltpu.VMEM((WIN * group, NP * HALF), BF),
            pltpu.VMEM((2, group * PATCH, 128), F32),
        ],
        compiler_params=params(),
    )(dx, sel)


def feature_parts(rows):
    feat = lax.broadcasted_iota(jnp.int32, (rows, FEAT), 1)
    return feat // (2 * PATCH), feat // PATCH % 2, feat % PATCH


def tap_rows(wide, ch, r, b, half):
    parts = []
    for r2 in range(2):
        a = r - r2
        parts.append(wide[9 * ch + 3 * a + b : 9 * ch + 3 * a + b + 1, :] if 0 <= a < 3 else jnp.zeros((1, FEAT), F32))
    return jnp.where(half == 0, parts[0], parts[1])


def tap_matrix_kernel(cw_ref, t_ref):
    chan, _, _ = feature_parts(32)
    expand = jnp.where(chan == lax.broadcasted_iota(jnp.int32, (32, FEAT), 0), 1.0, 0.0).astype(BF)
    wide = mm(cw_ref[...], expand)
    _, half, spot = feature_parts(1)
    line = lax.broadcasted_iota(jnp.int32, (HALF, FEAT), 0)
    for r in range(4):
        block = jnp.zeros((HALF, FEAT), F32)
        if r == 0:
            block = jnp.where(line == ONE_LANE, wide[27:28, :], block)
        for ch in range(CIN):
            for b in range(3):
                block = jnp.where(line == WIN * ch + b + spot, tap_rows(wide, ch, r, b, half), block)
        t_ref[r * HALF : (r + 1) * HALF, :] = block.astype(BF)


def tap_matrix(conv_weight, conv_bias):
    flat = jnp.concatenate([conv_weight.reshape(CH, 27), conv_bias[:, None], jnp.zeros((CH, 4), BF)], axis=1)
    return pl.pallas_call(
        tap_matrix_kernel,
        name="tap_matrix",
        out_shape=jax.ShapeDtypeStruct((4 * HALF, FEAT), BF),
        compiler_params=params(),
    )(flat.T)


def tap_grad_rows(full):
    chan, half, spot = feature_parts(1)
    line = lax.broadcasted_iota(jnp.int32, (HALF, FEAT), 0)
    sums = [[None] * 3 for _ in range(9)]
    for r in range(4):
        block = full[r * HALF : (r + 1) * HALF]
        for ch in range(CIN):
            for b in range(3):
                line_sum = jnp.sum(jnp.where(line == WIN * ch + b + spot, block, 0.0), axis=0, keepdims=True)
                for a in range(3):
                    if 0 <= r - a < 2:
                        part = jnp.where(half == r - a, line_sum, 0.0)
                        old = sums[3 * ch + b][a]
                        sums[3 * ch + b][a] = part if old is None else old + part
    lines = [sums[3 * ch + b][a] for ch in range(CIN) for a in range(3) for b in range(3)]
    lines.append(full[ONE_LANE : ONE_LANE + 1])
    lines.append(jnp.zeros((4, FEAT), F32))
    table = jnp.concatenate(lines, axis=0)
    chan, _, _ = feature_parts(128)
    expand = jnp.where(chan == lax.broadcasted_iota(jnp.int32, (128, FEAT), 0), 1.0, 0.0).astype(BF)
    hi, mid, lo = three_terms(table)
    return mm_t(hi, expand) + (mm_t(mid, expand) + mm_t(lo, expand))


def scatter_sum(chunks):
    shape = chunks.shape
    return lax.psum_scatter(
        chunks.reshape((shape[0] * shape[1],) + shape[2:]), ("items", "rows"), scatter_dimension=0, tiled=True
    )[0]


def unfold_kernel(in_ref, out_ref):
    width = in_ref.shape[2]
    for p in range(STEPS):
        turned = in_ref[p].astype(F32).T
        for c in range(width // (2 * PATCH)):
            at = c * PATCH * PATCH + p * 2 * PATCH
            out_ref[at : at + 2 * PATCH, :] = turned[c * 2 * PATCH : (c + 1) * 2 * PATCH, :]


def unfold(chunk):
    _, cols, width = chunk.shape
    return pl.pallas_call(
        unfold_kernel,
        name="unfold",
        out_shape=jax.ShapeDtypeStruct((STEPS * width, cols), F32),
        compiler_params=params(),
    )(chunk)


def on_device(
    images, item_segment, conv_weight, conv_bias, patch_weight, patch_bias, norm1_gain, norm1_bias,
    query_weight, query_bias, key_weight, value_weight, value_bias, output_weight, output_bias,
    norm2_gain, norm2_bias, hidden_weight, hidden_bias, result_weight, result_bias, cotangent,
):
    items, rows = lax.axis_size("items"), lax.axis_size("rows")
    count, _, height, _ = images.shape
    nrow = height // PATCH
    group = count * nrow

    def vec(v):
        return v.astype(F32).reshape(1, -1)

    down = [(i, i + 1) for i in range(rows - 1)]
    up = [(i + 1, i) for i in range(rows - 1)]
    top = lax.ppermute(images[:, :, height - 1], "rows", down)
    bot = lax.ppermute(images[:, :, 0], "rows", up)

    def spread(edge):
        edge = edge.transpose(1, 0, 2)[:, :, None, :].astype(F32)
        return jnp.broadcast_to(edge, (CIN, count, nrow, IMG)).reshape(CIN, group, IMG)

    segments = lax.dynamic_slice_in_dim(item_segment, lax.axis_index("rows") * SEQ_ITEMS, SEQ_ITEMS)
    lanes = jnp.arange(128)[None, :]
    same = lanes == segments[:, None]
    qx = jnp.where(same, 1.0, 0.0).astype(F32)
    kx = jnp.where((lanes < 4) & ~same, -1e30, 0.0) + jnp.where((lanes >= 4) & (lanes < 7), 1.0, 0.0)
    kx = kx.astype(F32)

    taps = tap_matrix(conv_weight, conv_bias)
    weight4 = patch_weight.reshape(CH, STEPS, 2 * PATCH, D)
    x, xt, sel = patchify(images, spread(top), spread(bot))
    embedded, act, slope = stem_forward(x, taps, weight4, vec(patch_bias))
    tokens = lax.all_to_all(
        embedded.reshape(count, nrow, NP, D), "rows", split_axis=0, concat_axis=1, tiled=True
    ).reshape(TOK, D)
    gain1, shift1 = vec(norm1_gain), vec(norm1_bias)
    q, k, v, attended, lx = attend(
        tokens, gain1, shift1, qx, kx, query_weight, key_weight, value_weight, vec(query_bias), vec(value_bias)
    )
    vecs = jnp.concatenate([vec(output_bias), vec(norm2_gain), vec(norm2_bias), vec(result_bias)], axis=0)
    block_out, middle_grad, attended_grad, wo_grad, wh_grad, wr_grad, sums2, hb_grad = mixer(
        tokens, attended, cotangent, output_weight, vecs, hidden_weight, vec(hidden_bias), result_weight, items, rows
    )
    wh_grad = scatter_sum(wh_grad)
    wr_grad = scatter_sum(wr_grad)
    wo_grad = scatter_sum(wo_grad)
    token_grad, squares, sums1, qvs = attend_back(
        tokens, gain1, shift1, kx, middle_grad, q, k, v, attended, attended_grad, lx,
        query_weight, key_weight, value_weight, items, rows,
    )
    squares = scatter_sum(squares)
    embed_grad = lax.all_to_all(
        token_grad.reshape(SEQ_ITEMS, NP, NP, D), "rows", split_axis=1, concat_axis=0, tiled=True
    ).reshape(-1, D)
    tgc, pw_grad, sums0 = patch_grad(embed_grad, act, items, rows)
    pw_grad = scatter_sum(pw_grad)
    dx, tap_grads = stem_back(tgc, weight4, slope, xt, taps)
    image_grad, edges = image_grad_call(dx, sel, count, height)
    edges = edges.reshape(2, CIN, count, nrow, IMG)
    from_below = lax.ppermute(edges[0, :, :, 0].astype(BF), "rows", up).astype(F32)
    from_above = lax.ppermute(edges[1, :, :, nrow - 1].astype(BF), "rows", down).astype(F32)
    image_grad = image_grad.at[:, :, height - 1].add(from_below.transpose(1, 0, 2))
    image_grad = image_grad.at[:, :, 0].add(from_above.transpose(1, 0, 2))
    small = lax.psum(
        (tap_grads[:, 0:CH], sums0[0:1], sums1[0:2], qvs[0:2], sums2[0:4], hb_grad), ("items", "rows")
    )
    return (
        block_out,
        image_grad,
        small[0][0:27].T.reshape(conv_weight.shape),
        small[0][27],
        unfold(pw_grad),
        small[1][0],
        small[2][0],
        small[2][1],
        squares[0].astype(F32),
        small[3][0],
        squares[1].astype(F32),
        squares[2].astype(F32),
        small[3][1],
        wo_grad[0].astype(F32),
        small[4][2],
        small[4][0],
        small[4][1],
        wh_grad.astype(F32),
        small[5][0],
        wr_grad.T.astype(F32),
        small[4][3],
    )


def solution(mesh):
    split = P("items", "rows")
    flat = P(("items", "rows"), None)
    image = P("items", None, "rows", None)
    return jax.shard_map(
        on_device,
        mesh=mesh,
        in_specs=(image, P("items")) + (P(),) * 19 + (flat,),
        out_specs=(
            flat, image, P(), P(), split, P(), P(), P(), split, P(), split, split,
            P(), split, P(), P(), P(), split, P(), split, P(),
        ),
        check_vma=False,
    )
```

```python
import functools

import jax
import jax.numpy as jnp
from jax import lax
from jax.experimental import pallas as pl
from jax.experimental.pallas import tpu as pltpu
from jax.sharding import PartitionSpec as P

BF = jnp.bfloat16
F32 = jnp.float32
D = 768
HEADS = 12
HD = 64
FF = 3072
IMG = 256
PATCH = 16
CH = 32
CIN = 3
SEQ_ITEMS = 4
NPATCH = 256
TOK = 1024
NP = IMG // PATCH
PF = CH * PATCH * PATCH
HALF = 64
WIN = PATCH + 2
ONE_LANE = CIN * WIN
SLABS = (PATCH + 2) // 2
STEPS = PATCH // 2
FEAT = PF // STEPS
GELU_A = 0.7978845608028654
GELU_B = GELU_A * 0.044715
VMEM_CAP = 60 * 1024 * 1024


def mm(left, right):
    return jnp.dot(left, right, preferred_element_type=F32)


def mm_t(left, right):
    return lax.dot_general(left, right, (((1,), (1,)), ((), ())), preferred_element_type=F32)


def params(**extra):
    return pltpu.CompilerParams(vmem_limit_bytes=VMEM_CAP, **extra)


def whole(shape):
    zeros = (0,) * len(shape)
    return pl.BlockSpec(shape, lambda *_: zeros, pipeline_mode=pl.Buffered(1))


def gelu_pair(v):
    square = v * v
    gate = 0.5 + 0.5 * jnp.tanh(v * (GELU_A + GELU_B * square))
    act = v * gate
    slope = gate + act * (1.0 - gate) * (2.0 * GELU_A + (6.0 * GELU_B) * square)
    return act, slope


MESH = pl.DeviceIdType.MESH


def grid_sizes(items, rows):
    nx = rows // 2
    ny = nx if items % nx == 0 else 1
    return (2, nx, ny, items // ny)


def place(sizes):
    item, row = lax.axis_index("items"), lax.axis_index("rows")
    return (row % 2, row // 2, item % sizes[2], item // sizes[2])


def peer(sizes, pos, axis, k):
    moved = list(pos)
    moved[axis] = lax.rem(pos[axis] + k, sizes[axis])
    return (moved[3] * sizes[2] + moved[2], moved[1] * 2 + moved[0]), moved[axis]


def greet(sizes, pos, sides):
    barrier = pltpu.get_barrier_semaphore()
    count = 0
    for axis, size in enumerate(sizes):
        for k in range(1, size):
            pl.semaphore_signal(barrier, inc=1, device_id=peer(sizes, pos, axis, k)[0], device_id_type=MESH)
            count += 1
    if sides:
        item, row = lax.axis_index("items"), lax.axis_index("rows")
        for there, step in ((row > 0, -1), (row < lax.axis_size("rows") - 1, 1)):
            @pl.when(there)
            def _(step=step):
                pl.semaphore_signal(barrier, inc=1, device_id=(item, row + step), device_id_type=MESH)
    if sides:
        count = count + (row > 0).astype(jnp.int32) + (row < lax.axis_size("rows") - 1).astype(jnp.int32)
    pl.semaphore_wait(barrier, count)


def add_up(first, rest):
    total = first.astype(F32)
    for term in rest:
        total = total + term.astype(F32)
    return total


class Piece:
    def __init__(self, sizes, pos, order, source, own, bufs, send, recv):
        self.sizes, self.pos = sizes, pos
        self.source, self.own, self.bufs = source, own, bufs
        self.send, self.recv = send, recv
        self.axes = (0,) + order

    def at(self, stage, where):
        left = sorted(self.axes[stage:])
        return (slice(None),) * left.index(self.axes[stage]) + (where,)

    def copies(self, stage):
        out = []
        for k in range(1, self.sizes[self.axes[stage]]):
            device, there = peer(self.sizes, self.pos, self.axes[stage], k)
            if stage == 0:
                src, dst = self.source.at[there], self.bufs[0]
            else:
                held = self.at(stage, there)
                src = self.bufs[0].at[held] if stage == 1 else self.bufs[stage - 1].at[(0,) + held]
                dst = self.bufs[stage].at[k - 1]
            out.append(
                pltpu.make_async_remote_copy(
                    src_ref=src, dst_ref=dst, send_sem=self.send.at[stage, k - 1], recv_sem=self.recv.at[stage, k - 1],
                    device_id=device, device_id_type=MESH,
                )
            )
        return out

    def start(self, stage):
        for copy in self.copies(stage):
            copy.start()

    def gather(self, stage):
        for copy in self.copies(stage):
            copy.wait_recv()
        bufs = self.bufs
        if stage == 0:
            bufs[0][...] = bufs[0][...] + self.own[...]
            return None
        held = self.at(stage, self.pos[self.axes[stage]])
        base = bufs[0][held] if stage == 1 else bufs[stage - 1][(0,) + held]
        terms = self.sizes[self.axes[stage]] - 1
        if stage < 3 and terms == 1:
            bufs[stage][0] = base + bufs[stage][0]
            return None
        total = add_up(base, [bufs[stage][k] for k in range(terms)])
        if stage == 3:
            return total
        bufs[stage][0] = total.astype(BF)

    def advance(self, stage):
        self.gather(stage - 1)
        self.start(stage)

    def drain(self, stages=(0, 1, 2, 3)):
        for stage in stages:
            for copy in self.copies(stage):
                copy.wait_send()


def piece_scratch(sizes, orders, shape):
    out = []
    for order in orders:
        out.append(pltpu.VMEM(sizes[1:] + shape, BF))
        for stage in range(3):
            left = tuple(sizes[axis] for axis in sorted(order[stage + 1 :]))
            out.append(pltpu.VMEM((sizes[order[stage]] - 1,) + left + shape, BF))
    sems = pltpu.SemaphoreType.DMA((len(orders), 4, max(sizes) - 1))
    return out + [sems, sems]


def own_scratch(sizes, count, shape):
    return [pltpu.VMEM((count,) + sizes[1:] + shape, BF), pltpu.SemaphoreType.DMA((count,))]


def make_pieces(sizes, pos, orders, sources, owns, refs):
    count = len(orders)
    return [
        Piece(sizes, pos, orders[n], sources[n], owns[n], refs[4 * n : 4 * n + 4], refs[4 * count].at[n], refs[4 * count + 1].at[n])
        for n in range(count)
    ]


class SmallSum:
    def __init__(self, sizes, pos, bufs, send, recv):
        self.sizes, self.pos, self.bufs, self.send, self.recv = sizes, pos, bufs, send, recv

    def copies(self, axis, receive):
        buf, here = self.bufs[axis], self.pos[axis]
        out = []
        for k in range(1, self.sizes[axis]):
            device, _ = peer(self.sizes, self.pos, axis, k)
            slot = lax.rem(here + self.sizes[axis] - k, self.sizes[axis]) if receive else here
            out.append(
                pltpu.make_async_remote_copy(
                    src_ref=buf.at[here], dst_ref=buf.at[slot], send_sem=self.send.at[axis, k - 1],
                    recv_sem=self.recv.at[axis, k - 1], device_id=device, device_id_type=MESH,
                )
            )
        return out

    def start(self, axis, value):
        self.bufs[axis][self.pos[axis]] = value
        for copy in self.copies(axis, False):
            copy.start()

    def gather(self, axis):
        for copy in self.copies(axis, True):
            copy.wait_recv()
        total = self.bufs[axis][0]
        for k in range(1, self.sizes[axis]):
            total = total + self.bufs[axis][k]
        return total

    def advance(self, axis):
        self.start(axis, self.gather(axis - 1))

    def drain(self):
        for axis in range(4):
            for copy in self.copies(axis, False):
                copy.wait_send()


def small_scratch(sizes, height):
    return [pltpu.VMEM((size, height, 128), F32) for size in sizes] + [
        pltpu.SemaphoreType.DMA((4, max(sizes) - 1)),
        pltpu.SemaphoreType.DMA((4, max(sizes) - 1)),
    ]


def folds(width):
    return width % 128 == HALF and width > 128


def narrow(width):
    return 128 // width if width < 128 and 128 % width == 0 else 1


def folded_shape(height, width):
    if folds(width) or narrow(width) > 1:
        return (height * width // 128, 128)
    return (height, width)


def fold_block(block):
    height, width = block.shape
    if narrow(width) > 1:
        part = height // narrow(width)
        return jnp.concatenate([block[k * part : (k + 1) * part] for k in range(narrow(width))], axis=1)
    if not folds(width):
        return block
    wide = width - HALF
    side = jnp.concatenate([block[: height // 2, wide:], block[height // 2 :, wide:]], axis=1)
    return jnp.concatenate([block[:, k * 128 : (k + 1) * 128] for k in range(wide // 128)] + [side], axis=0)


def unfold_block(block, height, width):
    if narrow(width) > 1:
        return jnp.concatenate([block[:, k * width : (k + 1) * width] for k in range(narrow(width))], axis=0)
    if not folds(width):
        return block
    parts = [block[k * height : (k + 1) * height] for k in range(width // 128)]
    side = block[width // 128 * height :]
    return jnp.concatenate(parts + [jnp.concatenate([side[:, :HALF], side[:, HALF:]], axis=0)], axis=1)


def run_events(step, table, slots):
    for (when, slot), todo in table.items():
        if slot in slots:
            @pl.when(step == when)
            def _(todo=todo):
                for call in todo:
                    call()


def patchify_kernel(img_ref, top_ref, bot_ref, x_ref, xt_ref, sel_ref, pix, rows):
    items, _, height, width = img_ref.shape
    nrow = height // PATCH
    group = items * nrow
    for ch in range(CIN):
        for item in range(items):
            full = img_ref[item, ch].astype(F32)
            for k in range(width // 128):
                pix[ch, k, item * height : (item + 1) * height, :] = full[:, k * 128 : (k + 1) * 128]
    patch_row = lax.broadcasted_iota(jnp.int32, (group, width), 0) % nrow
    for ch in range(CIN):
        cols = slice(ch * width, (ch + 1) * width)
        for r in range(PATCH):
            v = jnp.concatenate([pix[ch, k, pl.ds(r, group, stride=PATCH), :] for k in range(width // 128)], axis=1)
            rows[(r + 1) * group : (r + 2) * group, cols] = v.astype(BF)
            if r == PATCH - 1:
                up = jnp.where(patch_row == 0, top_ref[ch], pltpu.roll(v, 1, 0))
                rows[0:group, cols] = up.astype(BF)
            if r == 0:
                down = jnp.where(patch_row == nrow - 1, bot_ref[ch], pltpu.roll(v, group - 1, 0))
                rows[(PATCH + 1) * group : (PATCH + 2) * group, cols] = down.astype(BF)
    lane = lax.broadcasted_iota(jnp.int32, (1, NP * HALF), 1)
    col, spot = lane // HALF, lane % HALF
    for ch in range(CIN):
        inside = (spot >= WIN * ch) & (spot < WIN * (ch + 1))
        want = jnp.where(inside, PATCH * col + spot - WIN * ch - 1, -5)
        here = lax.broadcasted_iota(jnp.int32, (width, NP * HALF), 0)
        sel_ref[ch * width : (ch + 1) * width, :] = jnp.where(here == want, 1.0, 0.0).astype(BF)
    lane = lax.broadcasted_iota(jnp.int32, (group, 2 * HALF), 1)
    low = lane < HALF
    ones = (lane % HALF) == ONE_LANE
    for quarter in range(NP * HALF // 256):
        res = mm(rows[...], sel_ref[:, quarter * 256 : (quarter + 1) * 256])
        for j in range(SLABS):
            first = res[2 * j * group : (2 * j + 1) * group]
            second = res[(2 * j + 1) * group : (2 * j + 2) * group]
            for pair in range(2):
                a = first[:, pair * 128 : (pair + 1) * 128]
                b = second[:, pair * 128 : (pair + 1) * 128]
                even = jnp.where(ones, 1.0, jnp.where(low, a, pltpu.roll(b, HALF, 1)))
                odd = jnp.where(ones, 1.0, jnp.where(low, pltpu.roll(a, HALF, 1), b))
                at = (quarter * 4 + pair * 2) * group
                x_ref[j, at : at + group, :] = even.astype(BF)
                x_ref[j, at + group : at + 2 * group, :] = odd.astype(BF)
    for j in range(SLABS):
        xt_ref[j] = x_ref[j].T


def patchify(images, top, bot):
    items, _, height, width = images.shape
    tokens = items * (height // PATCH) * NP
    return pl.pallas_call(
        patchify_kernel,
        name="patchify",
        out_shape=(
            jax.ShapeDtypeStruct((SLABS, tokens, 128), BF),
            jax.ShapeDtypeStruct((SLABS, 128, tokens), BF),
            jax.ShapeDtypeStruct((CIN * width, NP * HALF), BF),
        ),
        scratch_shapes=[
            pltpu.VMEM((CIN, width // 128, items * height, 128), F32),
            pltpu.VMEM((WIN * tokens // NP, CIN * width), BF),
        ],
        compiler_params=params(),
    )(images, top, bot)


def stem_kernel(x_ref, t_ref, w_ref, pb_ref, tok_ref, saved_ref, acc, nat):
    p = pl.program_id(0)
    tokens = acc.shape[0]
    group = tokens // NP

    @pl.when(p == 0)
    def _():
        acc[...] = jnp.broadcast_to(pb_ref[...], acc.shape)

    weight = w_ref[...].reshape(FEAT, D)
    for s in range(tokens // 256):
        rs = slice(s * 256, (s + 1) * 256)
        xs = jnp.concatenate([x_ref[p, rs, :], x_ref[p + 1, rs, :]], axis=1)
        for n in range(FEAT // 256):
            cs = slice(n * 256, (n + 1) * 256)
            pre = mm(xs, t_ref[:, cs])
            act, slope = gelu_pair(pre)
            saved_ref[0, 0, rs, cs] = act.astype(BF)
            saved_ref[0, 1, rs, cs] = slope.astype(BF)
        acc[rs, :] += mm(saved_ref[0, 0, rs, :], weight)

    @pl.when(p == STEPS - 1)
    def _():
        for c in range(NP):
            for k in range(D // 128):
                nat[k, pl.ds(c, group, stride=NP), :] = acc[c * group : (c + 1) * group, k * 128 : (k + 1) * 128]
        for k in range(D // 128):
            tok_ref[:, k * 128 : (k + 1) * 128] = nat[k].astype(BF)


def stem_forward(x, taps, weight, bias):
    tokens = x.shape[1]
    return pl.pallas_call(
        stem_kernel,
        name="stem_forward",
        grid=(STEPS,),
        in_specs=[
            whole(x.shape),
            whole(taps.shape),
            pl.BlockSpec((CH, 1, 2 * PATCH, D), lambda p: (0, p, 0, 0)),
            whole((1, D)),
        ],
        out_specs=(
            whole((tokens, D)),
            pl.BlockSpec((1, 2, tokens, FEAT), lambda p: (p, 0, 0, 0)),
        ),
        out_shape=(
            jax.ShapeDtypeStruct((tokens, D), BF),
            jax.ShapeDtypeStruct((STEPS, 2, tokens, FEAT), BF),
        ),
        scratch_shapes=[pltpu.VMEM((tokens, D), F32), pltpu.VMEM((D // 128, tokens, 128), F32)],
        compiler_params=params(),
    )(x, taps, weight, bias)


def norm_stats(v):
    centred = v - jnp.mean(v, axis=-1, keepdims=True)
    inv = lax.rsqrt(jnp.mean(centred * centred, axis=-1, keepdims=True) + 1e-06)
    return centred * inv, inv


def three_terms(v):
    hi = v.astype(BF)
    rest = v - hi.astype(F32)
    mid = rest.astype(BF)
    lo = (rest - mid.astype(F32)).astype(BF)
    return hi, mid, lo


def minus_terms(v, lane, base):
    hi, mid, lo = three_terms(-v)
    out = jnp.where(lane == 4, hi.astype(F32), base)
    out = jnp.where(lane == 5, mid.astype(F32), out)
    return jnp.where(lane == 6, lo.astype(F32), out).astype(BF)


def attend_kernel(tok_ref, g_ref, b_ref, qx_ref, kx_ref, wq_ref, wk_ref, wv_ref, qb_ref, vb_ref,
                  q_ref, k_ref, v_ref, o_ref, lx_ref, n1, kaug, vaug):
    @pl.when(pl.program_id(0) == 0)
    def _():
        for s in range(TOK // 128):
            rs = slice(s * 128, (s + 1) * 128)
            hat, _ = norm_stats(tok_ref[rs, :].astype(F32))
            n1[rs, :] = (hat * g_ref[...] + b_ref[...]).astype(BF)

    q_ref[...] = ((mm(n1[...], wq_ref[...]) + qb_ref[...]).astype(BF) * 0.125).astype(BF)
    k_ref[...] = mm(n1[...], wk_ref[...]).astype(BF)
    v_ref[...] = (mm(n1[...], wv_ref[...]) + vb_ref[...]).astype(BF)
    lane = lax.broadcasted_iota(jnp.int32, (NPATCH, 128), 1)
    low = lane < HD
    for i in range(SEQ_ITEMS):
        rs = slice(i * NPATCH, (i + 1) * NPATCH)
        kaug[rs, 128:256] = jnp.broadcast_to(kx_ref[i : i + 1, :], (NPATCH, 128)).astype(BF)
        vaug[rs, 128:256] = jnp.ones((NPATCH, 128), BF)
    for pair in range(2):
        cs = slice(pair * 128, (pair + 1) * 128)
        kaug[:, 0:128] = k_ref[:, cs]
        vaug[:, 0:128] = v_ref[:, cs]
        for i in range(SEQ_ITEMS):
            rs = slice(i * NPATCH, (i + 1) * NPATCH)
            span = slice(0, (i + 1) * NPATCH)
            qp = q_ref[rs, cs]
            qx = jnp.broadcast_to(qx_ref[i : i + 1, :], (NPATCH, 128))
            halves = []
            for h in range(2):
                mine = low if h == 0 else ~low
                qaug = jnp.concatenate([jnp.where(mine, qp, jnp.zeros_like(qp)), qx.astype(BF)], axis=1)
                scores = mm_t(qaug, kaug[span, :])
                top = jnp.max(scores, axis=1, keepdims=True)
                raised = jnp.exp(scores - top).astype(BF)
                out = mm(raised, vaug[span, :])
                total = out[:, 128:256]
                halves.append(out[:, 0:128] / total)
                lx_ref[pair * 2 + h, rs, :] = minus_terms(top + jnp.log(total), lane, qx)
            o_ref[rs, cs] = jnp.where(low, halves[0], halves[1]).astype(BF)


def attend(tokens, gain, shift, qx, kx, wq, wk, wv, qb, vb):
    col = pl.BlockSpec((D, 256), lambda g: (0, g))
    row = pl.BlockSpec((1, 256), lambda g: (0, g))
    out = pl.BlockSpec((TOK, 256), lambda g: (0, g))
    return pl.pallas_call(
        attend_kernel,
        name="attend",
        grid=(D // 256,),
        in_specs=[whole((TOK, D)), whole((1, D)), whole((1, D)), whole(qx.shape), whole(kx.shape),
                  col, col, col, row, row],
        out_specs=(out, out, out, out, pl.BlockSpec((4, TOK, 128), lambda g: (g, 0, 0))),
        out_shape=(jax.ShapeDtypeStruct((TOK, D), BF),) * 4 + (jax.ShapeDtypeStruct((HEADS, TOK, 128), BF),),
        scratch_shapes=[pltpu.VMEM((TOK, D), BF), pltpu.VMEM((TOK, 256), BF), pltpu.VMEM((TOK, 256), BF)],
        compiler_params=params(),
    )(tokens, gain, shift, qx, kx, wq, wk, wv, qb, vb)


def norm_back(e, hat, inv, gain):
    f = e * gain
    return inv * (f - jnp.mean(f, axis=-1, keepdims=True) - hat * jnp.mean(f * hat, axis=-1, keepdims=True))


def col_sum(v):
    return jnp.sum(v, axis=0, keepdims=True)


def store_square(ref, n, grad):
    _, _, nx, ny, nz, _, _ = ref.shape
    height, width = D // (ny * nz), D // (2 * nx)
    for r in range(2 * nx):
        part = grad[:, r * width : (r + 1) * width]
        for i in range(ny * nz):
            ref[n, r % 2, r // 2, i % ny, i // ny] = fold_block(part[i * height : (i + 1) * height])


def mixer_kernel(tok_ref, att_ref, cot_ref, wo_ref, vec_ref, wh_ref, hb_ref, wr_ref,
                 out_ref, mid_ref, ag_ref, wog_ref, whg_ref, wrg_ref, sums_ref, hbg_ref,
                 middle, n2, n2t, cott, acc, back, act, hg):
    step = pl.program_id(0)
    last = pl.num_programs(0) - 1
    chunk = wh_ref.shape[1]
    blocks = [slice(s * 256, (s + 1) * 256) for s in range(TOK // 256)]

    @pl.when(step == 0)
    def _():
        for rs in blocks:
            row = tok_ref[rs, :].astype(F32) + mm(att_ref[rs, :], wo_ref[...]) + vec_ref[0:1, :]
            middle[rs, :] = row
            acc[rs, :] = row + vec_ref[3:4, :]
            back[rs, :] = jnp.zeros((256, D), F32)
            hat, _ = norm_stats(row)
            low = (hat * vec_ref[1:2, :] + vec_ref[2:3, :]).astype(BF)
            n2[rs, :] = low
            n2t[:, rs] = low.T
            cott[:, rs] = cot_ref[rs, :].T

    hsum = jnp.zeros((1, chunk), F32)
    for rs in blocks:
        for n in range(chunk // 128 // 3):
            cs = slice(n * 384, (n + 1) * 384)
            pre = mm(n2[rs, :], wh_ref[:, cs]) + hb_ref[:, cs]
            up = mm_t(cot_ref[rs, :], wr_ref[cs, :])
            a, slope = gelu_pair(pre)
            act[rs, cs] = a.astype(BF)
            hg[rs, cs] = (slope * up).astype(BF)
        acc[rs, :] += mm(act[rs, :], wr_ref[...])
        back[rs, :] += mm_t(hg[rs, :], wh_ref[...])
        hsum = hsum + col_sum(hg[rs, :].astype(F32))
    hbg_ref[...] = hsum
    _, _, nx, ny, nz, height, _ = whg_ref.shape
    for n in range(3):
        width = chunk // 3
        grad = mm(n2t[...], hg[:, n * width : (n + 1) * width]).astype(BF)
        for i in range(ny * nz):
            whg_ref[n, 0, 0, i % ny, i // ny] = grad[i * height : (i + 1) * height]
    _, _, nx, ny, _, _, _ = wrg_ref.shape
    height, width = D // (2 * nx), chunk // ny // 3
    for y in range(ny):
        grad = mm(cott[...], act[:, y * 3 * width : (y + 1) * 3 * width]).astype(BF)
        for n in range(3):
            for r in range(2 * nx):
                part = grad[r * height : (r + 1) * height, n * width : (n + 1) * width]
                wrg_ref[n, r % 2, r // 2, y, 0] = fold_block(part)

    @pl.when(step == last)
    def _():
        gsum = jnp.zeros((1, D), F32)
        bsum = jnp.zeros((1, D), F32)
        osum = jnp.zeros((1, D), F32)
        rsum = jnp.zeros((1, D), F32)
        for rs in blocks:
            out_ref[rs, :] = acc[rs, :].astype(BF)
            hat, inv = norm_stats(middle[rs, :])
            e = back[rs, :]
            gsum = gsum + col_sum(e * hat)
            bsum = bsum + col_sum(e)
            cot = cot_ref[rs, :].astype(F32)
            rsum = rsum + col_sum(cot)
            mid = cot + norm_back(e, hat, inv, vec_ref[1:2, :])
            mid_ref[rs, :] = mid
            low = mid.astype(BF)
            osum = osum + col_sum(low.astype(F32))
            n2[rs, :] = low
            n2t[:, rs] = att_ref[rs, :].T
            ag_ref[rs, :] = mm_t(low, wo_ref[...]).astype(BF)
        store_square(wog_ref, 0, mm(n2t[...], n2[...]).astype(BF))
        sums_ref[0:1, :] = gsum
        sums_ref[1:2, :] = bsum
        sums_ref[2:3, :] = osum
        sums_ref[3:4, :] = rsum


def mixer(tokens, attended, cotangent, wo, vecs, wh, hb, wr, sizes):
    nc, nx, ny, nz = sizes
    rows, items = nc * nx, ny * nz
    chunk = FF // rows
    square = (1,) + sizes + folded_shape(D // items, D // rows)
    return pl.pallas_call(
        mixer_kernel,
        name="mixer",
        grid=(rows,),
        in_specs=[
            whole((TOK, D)), whole((TOK, D)), whole((TOK, D)), whole((D, D)), whole(vecs.shape),
            pl.BlockSpec((D, chunk), lambda r: (0, r)),
            pl.BlockSpec((1, chunk), lambda r: (0, r)),
            pl.BlockSpec((chunk, D), lambda r: (r, 0)),
        ],
        out_specs=(
            whole((TOK, D)), whole((TOK, D)), whole((TOK, D)), whole(square),
            pl.BlockSpec((3, 1, 1, ny, nz, D // items, chunk // 3), lambda r: (0, r % 2, r // 2, 0, 0, 0, 0)),
            pl.BlockSpec((3, nc, nx, ny, 1) + folded_shape(D // rows, FF // items // 3), lambda r: (0, 0, 0, 0, r, 0, 0)),
            whole((8, D)),
            pl.BlockSpec((1, chunk), lambda r: (0, r)),
        ),
        out_shape=(
            jax.ShapeDtypeStruct((TOK, D), BF),
            jax.ShapeDtypeStruct((TOK, D), F32),
            jax.ShapeDtypeStruct((TOK, D), BF),
            jax.ShapeDtypeStruct(square, BF),
            jax.ShapeDtypeStruct((3,) + sizes + (D // items, chunk // 3), BF),
            jax.ShapeDtypeStruct((3,) + sizes + folded_shape(D // rows, FF // items // 3), BF),
            jax.ShapeDtypeStruct((8, D), F32),
            jax.ShapeDtypeStruct((1, FF), F32),
        ),
        scratch_shapes=[
            pltpu.VMEM((TOK, D), F32), pltpu.VMEM((TOK, D), BF), pltpu.VMEM((D, TOK), BF),
            pltpu.VMEM((D, TOK), BF), pltpu.VMEM((TOK, D), F32), pltpu.VMEM((TOK, D), F32),
            pltpu.VMEM((TOK, chunk), BF), pltpu.VMEM((TOK, chunk), BF),
        ],
        compiler_params=params(),
    )(tokens, attended, cotangent, wo, vecs, wh, hb, wr)


def attend_back_kernel(sizes, tok_ref, g_ref, b_ref, kx_ref, mid_ref, q_ref, k_ref, v_ref, o_ref, ag_ref, lx_ref,
                       wq_ref, wk_ref, wv_ref, whg_ref, wrg_ref, wog_ref,
                       tg_ref, sq_ref, sums_ref, qvs_ref, who_ref, wro_ref, woo_ref,
                       n1t, back, kaug, vaug, qaug, oaug, dqt, dq, dk, dv, square, *comm):
    step = pl.program_id(0)
    blocks = [slice(s * 256, (s + 1) * 256) for s in range(TOK // 256)]
    pos = place(sizes)
    groups = ((whg_ref, who_ref), (wrg_ref, wro_ref), (wog_ref, woo_ref))
    pieces, loads, base, at = [], [], 0, 0
    for source, _ in groups:
        count = source.shape[0]
        refs, keep = comm[at : at + 4 * count + 2], comm[at + 4 * count + 2 : at + 4 * count + 4]
        at += 4 * count + 4
        pieces += make_pieces(
            sizes, pos, BACK_ORDERS[base : base + count], [source.at[n] for n in range(count)],
            [keep[0].at[n] for n in range(count)], refs,
        )
        loads += [pltpu.make_async_copy(source.at[n, pos[0]], keep[0].at[n], keep[1].at[n]) for n in range(count)]
        base += count

    def event(index, stage):
        if stage == 0:
            pieces[index].start(0)
            loads[index].start()
        elif stage < 4:
            if stage == 1:
                loads[index].wait()
            pieces[index].advance(stage)
        else:
            total = pieces[index].gather(3)
            if index < 3:
                width = total.shape[1]
                who_ref[:, index * width : (index + 1) * width] = total
            elif index < 6:
                height, width = D // (2 * sizes[1]), FF // (sizes[2] * sizes[3]) // 3
                wro_ref[:, (index - 3) * width : (index - 2) * width] = unfold_block(total, height, width)
            else:
                woo_ref[...] = unfold_block(total, *woo_ref.shape)

    def finish():
        for part in pieces:
            part.drain()

    table = {(0, 0): [functools.partial(greet, sizes, pos, False)]}
    for when, index, stage in BACK_PLAN:
        if when < 2:
            key = (0, when)
        elif when < 26:
            key = ((when - 2) // 8, 2 + (when - 2) % 8)
        else:
            key = (2, 10)
        table.setdefault(key, []).append(functools.partial(event, index, stage))
    table.setdefault((2, 10), []).append(finish)
    run_events(step, table, (0,))

    @pl.when(step == 0)
    def _():
        for rs in blocks:
            hat, _ = norm_stats(tok_ref[rs, :].astype(F32))
            n1t[:, rs] = (hat * g_ref[...] + b_ref[...]).astype(BF).T
            back[rs, :] = jnp.zeros((256, D), F32)

    run_events(step, table, (1,))
    lane = lax.broadcasted_iota(jnp.int32, (NPATCH, 128), 1)
    low = lane < HD
    ones = jnp.where((lane >= 4) & (lane < 7), 1.0, 0.0).astype(BF)
    for i, rs in enumerate(blocks):
        kaug[rs, 128:256] = jnp.broadcast_to(kx_ref[i : i + 1, :], (NPATCH, 128)).astype(BF)
        vaug[rs, 128:256] = ones
    pick_row = lax.broadcasted_iota(jnp.int32, (256, 256), 0) % 128 // HD
    pick_col = lax.broadcasted_iota(jnp.int32, (256, 256), 1) // 128
    pick = jnp.where(pick_row == pick_col, 1.0, 0.0).astype(BF)
    for pair in range(2):
        cs = slice(pair * 128, (pair + 1) * 128)
        kaug[:, 0:128] = k_ref[:, cs]
        vaug[:, 0:128] = v_ref[:, cs]
        kt = k_ref[:, cs].T
        for rs in blocks:
            qp = q_ref[rs, cs]
            gp = ag_ref[rs, cs]
            prod = gp.astype(F32) * o_ref[rs, cs].astype(F32)
            hi = prod.astype(BF)
            both = jnp.concatenate([hi, (prod - hi.astype(F32)).astype(BF)], axis=1)
            dots = mm(both, pick)
            for h in range(2):
                mine = low if h == 0 else ~low
                qaug[h, rs, 0:128] = jnp.where(mine, qp, jnp.zeros_like(qp))
                qaug[h, rs, 128:256] = lx_ref[pair * 2 + h, rs, :]
                oaug[h, rs, 0:128] = jnp.where(mine, gp, jnp.zeros_like(gp))
                oaug[h, rs, 128:256] = minus_terms(dots[:, h * 128 : (h + 1) * 128], lane, jnp.zeros((NPATCH, 128), F32))
        for j, rs in enumerate(blocks):
            span = slice(j * NPATCH, TOK)
            parts_k, parts_v = [], []
            for h in range(2):
                probs = jnp.exp(mm_t(kaug[rs, :], qaug[h, span, :]))
                rise = mm_t(vaug[rs, :], oaug[h, span, :])
                grad = (probs * rise).astype(BF)
                probs_low = probs.astype(BF)
                parts_v.append(mm(probs_low, ag_ref[span, cs]))
                parts_k.append(mm(grad, q_ref[span, cs]))
                hs = slice(h * HD, (h + 1) * HD)
                part = mm(kt[hs, rs], grad)
                if j == 0:
                    dqt[hs, :] = part
                else:
                    dqt[hs, span] += part
            dk[rs, cs] = jnp.where(low, parts_k[0], parts_k[1]).astype(BF)
            dv[rs, cs] = jnp.where(low, parts_v[0], parts_v[1]).astype(BF)
            run_events(step, table, (2 + pair * 4 + j,))
        dq[:, cs] = (dqt[...].T * 0.125).astype(BF)
    qvs_ref[0:1, :] = col_sum(dq[...].astype(F32))
    qvs_ref[1:2, :] = col_sum(dv[...].astype(F32))
    for n, part in enumerate((dq, dk, dv)):
        square[n, step] = mm(n1t[...], part[...]).astype(BF)
    for rs in blocks:
        back[rs, :] += (
            mm_t(dq[rs, :], wq_ref[...]) + mm_t(dk[rs, :], wk_ref[...]) + mm_t(dv[rs, :], wv_ref[...])
        )

    @pl.when(step == pl.num_programs(0) - 1)
    def _():
        gsum = jnp.zeros((1, D), F32)
        bsum = jnp.zeros((1, D), F32)
        for rs in blocks:
            hat, inv = norm_stats(tok_ref[rs, :].astype(F32))
            e = back[rs, :]
            gsum = gsum + col_sum(e * hat)
            bsum = bsum + col_sum(e)
            tg_ref[rs, :] = (mid_ref[rs, :] + norm_back(e, hat, inv, g_ref[...])).astype(BF)
        sums_ref[0:1, :] = gsum
        sums_ref[1:2, :] = bsum
        for n in range(3):
            store_square(sq_ref, n, jnp.concatenate([square[n, g] for g in range(D // 256)], axis=1))

    run_events(step, table, (10,))


BACK_ORDERS = (
    (2, 1, 3), (3, 1, 2), (1, 2, 3), (2, 1, 3), (1, 3, 2), (2, 1, 3),
    (2, 1, 3),
)
BACK_PLAN = (
    (0, 1, 0), (0, 3, 0), (0, 4, 0), (0, 6, 0), (0, 5, 0), (0, 0, 0), (0, 2, 0), (2, 1, 1), (2, 3, 1),
    (3, 4, 1), (5, 0, 1), (6, 5, 1), (6, 6, 1), (7, 3, 2), (9, 2, 1), (10, 4, 2), (13, 0, 2), (14, 3, 3),
    (16, 5, 2), (17, 0, 3), (17, 2, 2), (19, 5, 3), (20, 1, 2), (20, 6, 2), (21, 2, 3), (21, 4, 3), (22, 1, 3),
    (23, 6, 3), (23, 1, 4), (23, 3, 4), (27, 4, 4), (28, 2, 4), (29, 5, 4), (29, 0, 4), (29, 6, 4),
)


def attend_back(tokens, gain, shift, kx, mid, q, k, v, o, ag, lx, wq, wk, wv, whg, wrg, wog, sizes):
    squares = (3,) + sizes + wog.shape[5:]
    col = pl.BlockSpec((D, 256), lambda g: (0, g))
    part = pl.BlockSpec((TOK, 256), lambda g: (0, g))
    far = pl.BlockSpec(memory_space=pl.ANY)
    items, rows = sizes[2] * sizes[3], 2 * sizes[1]
    outs = [(D // items, FF // rows), (D // rows, FF // items), (D // items, D // rows)]
    return pl.pallas_call(
        functools.partial(attend_back_kernel, sizes),
        name="attend_back",
        grid=(D // 256,),
        in_specs=[whole((TOK, D)), whole((1, D)), whole((1, D)), whole(kx.shape), whole((TOK, D)),
                  part, part, part, part, part, pl.BlockSpec((4, TOK, 128), lambda g: (g, 0, 0)),
                  col, col, col, far, far, far],
        out_specs=(whole((TOK, D)), whole(squares), whole((8, D)), pl.BlockSpec((8, 256), lambda g: (0, g)))
        + tuple(whole(shape) for shape in outs),
        out_shape=(
            jax.ShapeDtypeStruct((TOK, D), BF),
            jax.ShapeDtypeStruct(squares, BF),
            jax.ShapeDtypeStruct((8, D), F32),
            jax.ShapeDtypeStruct((8, D), F32),
        ) + tuple(jax.ShapeDtypeStruct(shape, F32) for shape in outs),
        scratch_shapes=[
            pltpu.VMEM((D, TOK), BF), pltpu.VMEM((TOK, D), F32),
            pltpu.VMEM((TOK, 256), BF), pltpu.VMEM((TOK, 256), BF),
            pltpu.VMEM((2, TOK, 256), BF), pltpu.VMEM((2, TOK, 256), BF),
            pltpu.VMEM((128, TOK), F32),
            pltpu.VMEM((TOK, 256), BF), pltpu.VMEM((TOK, 256), BF), pltpu.VMEM((TOK, 256), BF),
            pltpu.VMEM((3, D // 256, D, 256), BF),
        ]
        + piece_scratch(sizes, BACK_ORDERS[0:3], whg.shape[5:]) + own_scratch(sizes, 3, whg.shape[5:])
        + piece_scratch(sizes, BACK_ORDERS[3:6], wrg.shape[5:]) + own_scratch(sizes, 3, wrg.shape[5:])
        + piece_scratch(sizes, BACK_ORDERS[6:7], wog.shape[5:]) + own_scratch(sizes, 1, wog.shape[5:]),
        compiler_params=params(collective_id=1, has_side_effects=True),
    )(tokens, gain, shift, kx, mid, q, k, v, o, ag, lx, wq, wk, wv, whg, wrg, wog)


EARLY = 80
FINISH_STEPS = 2 * STEPS + CIN
LAST = FINISH_STEPS - 1
FINISH_ORDERS = (
    (1, 3, 2), (2, 3, 1), (1, 3, 2), (1, 2, 3), (2, 1, 3), (2, 1, 3),
    (1, 2, 3), (2, 1, 3), (1, 2, 3), (3, 1, 2), (2, 3, 1),
)
FINISH_PLAN = (
    (0, 8, 0), (0, 9, 0), (0, 10, 0), (1, 0, 0), (1, 11, 0), (1, 9, 1), (1, 8, 1), (1, 10, 1), (2, 1, 0),
    (2, 0, 1), (2, 11, 1), (3, 2, 0), (3, 1, 1), (4, 3, 0), (4, 2, 1), (4, 10, 2), (5, 4, 0), (5, 3, 1),
    (5, 8, 2), (6, 5, 0), (6, 4, 1), (7, 5, 1), (7, 6, 0), (7, 1, 2), (8, 7, 0), (8, 6, 1), (9, 7, 1),
    (9, 2, 2), (9, 0, 2), (11, 3, 2), (11, 4, 2), (12, 5, 2), (12, 8, 3), (12, 2, 3), (13, 10, 3), (14, 7, 2),
    (14, 4, 3), (14, 0, 3), (15, 6, 2), (15, 3, 3), (16, 12, 0), (16, 7, 3), (16, 1, 3), (16, 5, 3), (17, 9, 2),
    (17, 1, 4), (17, 6, 3), (19, 12, 1), (19, 9, 3), (19, 7, 4), (20, 11, 2), (20, 0, 4), (21, 12, 2), (21, 11, 3),
    (21, 3, 4), (22, 8, 4), (22, 9, 4), (23, 12, 3), (23, 2, 4), (23, 10, 4), (23, 5, 4), (23, 4, 4), (24, 6, 4),
    (24, 11, 4), (24, 12, 4),
)


def finish_kernel(sizes, tg_ref, saved_ref, w_ref, xt_ref, t_ref, sel_ref, sq_ref, early_ref,
                  pw_ref, sq0_ref, sq1_ref, sq2_ref, ig_ref, earlyo_ref, tapso_ref,
                  tgc, tgt, dxa, pg, cw, lines, flat, grads, edge, edge_send, edge_recv, *comm):
    t = pl.program_id(0)
    nc, nx, ny, nz = sizes
    items, rows = ny * nz, nc * nx
    tokens = tgc.shape[0]
    group = tokens // NP
    count, _, height, width = ig_ref.shape
    nrow = height // PATCH
    pos = place(sizes)
    item, row = lax.axis_index("items"), lax.axis_index("rows")
    final_row = lax.axis_size("rows") - 1
    at = 4 * STEPS + 2
    patch = make_pieces(
        sizes, pos, FINISH_ORDERS[0:STEPS], [grads.at[q % 2] for q in range(STEPS)],
        [grads.at[q % 2, pos[0]] for q in range(STEPS)], comm[0:at],
    )
    keep = comm[at + 14 : at + 16]
    square = make_pieces(
        sizes, pos, FINISH_ORDERS[STEPS : STEPS + 3], [sq_ref.at[n] for n in range(3)],
        [keep[0].at[n] for n in range(3)], comm[at : at + 14],
    )
    loads = [pltpu.make_async_copy(sq_ref.at[n, pos[0]], keep[0].at[n], keep[1].at[n]) for n in range(3)]
    at += 16
    early = SmallSum(sizes, pos, comm[at : at + 4], comm[at + 4], comm[at + 5])
    late = SmallSum(sizes, pos, comm[at + 6 : at + 10], comm[at + 10], comm[at + 11])

    def edge_copy(n):
        step = -1 if n == 0 else 1
        return pltpu.make_async_remote_copy(
            src_ref=edge.at[n], dst_ref=edge.at[2 + n], send_sem=edge_send.at[n], recv_sem=edge_recv.at[n],
            device_id=(item, row + step), device_id_type=MESH,
        )

    def put_lines(j):
        low = lax.broadcasted_iota(jnp.int32, (group, 2 * HALF), 1) < HALF
        for pair in range(NP // 2):
            at = 2 * pair * group
            a = dxa[j, at : at + group, :]
            b = dxa[j, at + group : at + 2 * group, :]
            cs = slice(pair * 128, (pair + 1) * 128)
            lines[2 * j * group : (2 * j + 1) * group, cs] = jnp.where(low, a, pltpu.roll(b, HALF, 1)).astype(BF)
            lines[(2 * j + 1) * group : (2 * j + 2) * group, cs] = jnp.where(low, pltpu.roll(a, HALF, 1), b).astype(BF)

    @pl.when(t == 0)
    def _():
        @pl.when(row == final_row)
        def _():
            edge[2] = jnp.zeros(edge.shape[1:], BF)

        @pl.when(row == 0)
        def _():
            edge[3] = jnp.zeros(edge.shape[1:], BF)

        greet(sizes, pos, True)
        for n in range(3):
            square[n].start(0)
            loads[n].start()
        for k in range(D // 128):
            dxa[k] = tg_ref[:, k * 128 : (k + 1) * 128].astype(F32)
        total = jnp.zeros((1, D), F32)
        for c in range(NP):
            part = jnp.concatenate([dxa[k, pl.ds(c, group, stride=NP), :] for k in range(D // 128)], axis=1)
            total = total + col_sum(part)
            tgc[c * group : (c + 1) * group, :] = part.astype(BF)
        for s in range(tokens // 256):
            rs = slice(s * 256, (s + 1) * 256)
            tgt[:, rs] = tgc[rs, :].T
        bias = [total[:, k * 128 : (k + 1) * 128] for k in range(D // 128)]
        early.start(0, jnp.concatenate([early_ref[...]] + bias + [jnp.zeros((2, 128), F32)], axis=0))

    @pl.when(t < STEPS)
    def _():
        for q in range(2, STEPS):
            @pl.when(t == q)
            def _(q=q):
                patch[q - 2].drain((0,))

        feats = FEAT // items
        slot = t % 2
        for n in range(FEAT // 256):
            grad = mm(tgt[...], saved_ref[0, 0, :, n * 256 : (n + 1) * 256]).astype(BF)
            for c in range(256 // feats):
                i = n * (256 // feats) + c
                for r in range(rows):
                    block = grad[r * (D // rows) : (r + 1) * (D // rows), c * feats : (c + 1) * feats]
                    grads[slot, r % 2, r // 2, i % ny, i // ny] = fold_block(block)

    @pl.when((t >= STEPS) & (t < 2 * STEPS))
    def _():
        p = t - STEPS
        weight = w_ref[...].reshape(FEAT, D)

        @pl.when(p == 0)
        def _():
            cw[...] = jnp.zeros_like(cw)
            dxa[0] = jnp.zeros((tokens, 128), F32)

        for s in range(tokens // 256):
            rs = slice(s * 256, (s + 1) * 256)
            for n in range(FEAT // 256):
                cs = slice(n * 256, (n + 1) * 256)
                da = mm_t(tgc[rs, :], weight[cs, :])
                pg[rs, cs] = (saved_ref[0, 0, rs, cs].astype(F32) * da).astype(BF)
            back = mm_t(pg[rs, :], t_ref[...])
            dxa[p, rs, :] += back[:, 0:128]
            dxa[p + 1, rs, :] = back[:, 128:256]
        xt = jnp.concatenate([xt_ref[p], xt_ref[p + 1]], axis=0)
        cw[...] += mm(xt, pg[...])

        @pl.when(p == 0)
        def _():
            put_lines(0)
            for ch in range(CIN):
                head = mm_t(lines[0:group], sel_ref[ch * width : (ch + 1) * width, :])
                edge[0, ch] = (pltpu.roll(head, nrow - 1, 0) if nrow > 1 else head).astype(BF)

            @pl.when(row > 0)
            def _():
                edge_copy(0).start()

        @pl.when(p == STEPS - 1)
        def _():
            put_lines(SLABS - 1)
            for ch in range(CIN):
                tail = mm_t(lines[(WIN - 1) * group : WIN * group], sel_ref[ch * width : (ch + 1) * width, :])
                edge[1, ch] = (pltpu.roll(tail, group - nrow + 1, 0) if nrow > 1 else tail).astype(BF)

            @pl.when(row < final_row)
            def _():
                edge_copy(1).start()

            late.start(0, tap_grad_rows(cw[...]))

    @pl.when(t >= 2 * STEPS)
    def _():
        ch = t - 2 * STEPS

        @pl.when(t == 2 * STEPS)
        def _():
            for j in range(1, SLABS - 1):
                put_lines(j)

            @pl.when(row < final_row)
            def _():
                edge_copy(0).wait_recv()

            @pl.when(row > 0)
            def _():
                edge_copy(1).wait_recv()

        patch_row = lax.broadcasted_iota(jnp.int32, (group, width), 0) % nrow
        res = mm_t(lines[...], sel_ref[pl.ds(pl.multiple_of(ch * width, width), width), :])
        head = res[0:group]
        tail = res[(PATCH + 1) * group : (PATCH + 2) * group]
        for r in range(PATCH):
            v = res[(r + 1) * group : (r + 2) * group]
            if r == 0:
                v = v + jnp.where(patch_row == 0, edge[3, ch].astype(F32), pltpu.roll(tail, 1, 0))
            if r == PATCH - 1:
                v = v + jnp.where(patch_row == nrow - 1, edge[2, ch].astype(F32), pltpu.roll(head, group - 1, 0))
            flat[0, pl.ds(r, group, stride=PATCH), :] = v[:, 0:128]
            flat[1, pl.ds(r, group, stride=PATCH), :] = v[:, 128:256]
        for n in range(count):
            at = slice(n * height, (n + 1) * height)
            ig_ref[n, 0, :, 0:128] = flat[0, at, :]
            ig_ref[n, 0, :, 128:256] = flat[1, at, :]

    def event(index, stage):
        if index < STEPS:
            if stage == 0:
                patch[index].start(0)
            elif stage < 4:
                patch[index].advance(stage)
            else:
                total = unfold_block(patch[index].gather(3), D // rows, FEAT // items)
                for c in range(CH // items):
                    at = c * PATCH * PATCH + index * 2 * PATCH
                    pw_ref[:, at : at + 2 * PATCH] = total[:, c * 2 * PATCH : (c + 1) * 2 * PATCH]
        elif index < STEPS + 3:
            n = index - STEPS
            if stage == 1:
                loads[n].wait()
            if stage < 4:
                square[n].advance(stage)
            else:
                out = (sq0_ref, sq1_ref, sq2_ref)[n]
                out[...] = unfold_block(square[n].gather(3), *out.shape)
        else:
            part, out = ((early, earlyo_ref), (late, tapso_ref))[index - STEPS - 3]
            if stage < 4:
                part.advance(stage)
            else:
                out[...] = part.gather(3)

    def close():
        for part in square:
            part.drain()
        for q, part in enumerate(patch):
            part.drain((1, 2, 3) if q < STEPS - 2 else (0, 1, 2, 3))
        early.drain()
        late.drain()

        @pl.when(row > 0)
        def _():
            edge_copy(0).wait_send()

        @pl.when(row < final_row)
        def _():
            edge_copy(1).wait_send()

    table = {}
    for when, index, stage in FINISH_PLAN:
        if stage > 0 or index < STEPS:
            table.setdefault((min(when - 1, LAST), 0), []).append(functools.partial(event, index, stage))
    table.setdefault((LAST, 0), []).append(close)
    run_events(t, table, (0,))


def finish(tg, saved, weight, xt, taps, sel, squares, early, count, height, sizes):
    nc, nx, ny, nz = sizes
    items, rows = ny * nz, nc * nx
    tokens = tg.shape[0]
    group = tokens // NP
    feats = FEAT // items
    square = squares.shape[5:]

    def clip(v, low, high):
        return jnp.minimum(jnp.maximum(v, low), high)

    return pl.pallas_call(
        functools.partial(finish_kernel, sizes),
        name="finish",
        grid=(FINISH_STEPS,),
        in_specs=[
            whole((tokens, D)),
            pl.BlockSpec(
                (1, 1, tokens, FEAT),
                lambda t: (jnp.where(t < 2 * STEPS, t % STEPS, STEPS - 1), jnp.where(t < STEPS, 0, 1), 0, 0),
            ),
            pl.BlockSpec((CH, 1, 2 * PATCH, D), lambda t: (0, clip(t - STEPS, 0, STEPS - 1), 0, 0)),
            whole(xt.shape),
            whole(taps.shape),
            whole(sel.shape),
            pl.BlockSpec(memory_space=pl.ANY),
            whole(early.shape),
        ],
        out_specs=(
            whole((D // rows, PF // items)),
            whole((D // items, D // rows)),
            whole((D // items, D // rows)),
            whole((D // items, D // rows)),
            pl.BlockSpec((count, 1, height, IMG), lambda t: (0, clip(t - 2 * STEPS, 0, CIN - 1), 0, 0)),
            whole((EARLY, 128)),
            whole((32, 128)),
        ),
        out_shape=(
            jax.ShapeDtypeStruct((D // rows, PF // items), F32),
            jax.ShapeDtypeStruct((D // items, D // rows), F32),
            jax.ShapeDtypeStruct((D // items, D // rows), F32),
            jax.ShapeDtypeStruct((D // items, D // rows), F32),
            jax.ShapeDtypeStruct((count, CIN, height, IMG), F32),
            jax.ShapeDtypeStruct((EARLY, 128), F32),
            jax.ShapeDtypeStruct((32, 128), F32),
        ),
        scratch_shapes=[
            pltpu.VMEM((tokens, D), BF),
            pltpu.VMEM((D, tokens), BF),
            pltpu.VMEM((SLABS, tokens, 128), F32),
            pltpu.VMEM((tokens, FEAT), BF),
            pltpu.VMEM((4 * HALF, FEAT), F32),
            pltpu.VMEM((WIN * group, NP * HALF), BF),
            pltpu.VMEM((2, group * PATCH, 128), F32),
            pltpu.VMEM((2,) + sizes + folded_shape(D // rows, feats), BF),
            pltpu.VMEM((4, CIN, group, IMG), BF),
            pltpu.SemaphoreType.DMA((2,)),
            pltpu.SemaphoreType.DMA((2,)),
        ]
        + piece_scratch(sizes, FINISH_ORDERS[0:STEPS], folded_shape(D // rows, feats))
        + piece_scratch(sizes, FINISH_ORDERS[STEPS : STEPS + 3], square) + own_scratch(sizes, 3, square)
        + small_scratch(sizes, EARLY)
        + small_scratch(sizes, 32),
        compiler_params=params(collective_id=2, has_side_effects=True),
    )(tg, saved, weight, xt, taps, sel, squares, early)


def feature_parts(rows):
    feat = lax.broadcasted_iota(jnp.int32, (rows, FEAT), 1)
    return feat // (2 * PATCH), feat // PATCH % 2, feat % PATCH


def tap_rows(wide, ch, r, b, half):
    parts = []
    for r2 in range(2):
        a = r - r2
        parts.append(wide[9 * ch + 3 * a + b : 9 * ch + 3 * a + b + 1, :] if 0 <= a < 3 else jnp.zeros((1, FEAT), F32))
    return jnp.where(half == 0, parts[0], parts[1])


def tap_matrix_kernel(cw_ref, t_ref):
    chan, _, _ = feature_parts(32)
    expand = jnp.where(chan == lax.broadcasted_iota(jnp.int32, (32, FEAT), 0), 1.0, 0.0).astype(BF)
    wide = mm(cw_ref[...], expand)
    _, half, spot = feature_parts(1)
    line = lax.broadcasted_iota(jnp.int32, (HALF, FEAT), 0)
    for r in range(4):
        block = jnp.zeros((HALF, FEAT), F32)
        if r == 0:
            block = jnp.where(line == ONE_LANE, wide[27:28, :], block)
        for ch in range(CIN):
            for b in range(3):
                block = jnp.where(line == WIN * ch + b + spot, tap_rows(wide, ch, r, b, half), block)
        t_ref[r * HALF : (r + 1) * HALF, :] = block.astype(BF)


def tap_matrix(conv_weight, conv_bias):
    flat = jnp.concatenate([conv_weight.reshape(CH, 27), conv_bias[:, None], jnp.zeros((CH, 4), BF)], axis=1)
    return pl.pallas_call(
        tap_matrix_kernel,
        name="tap_matrix",
        out_shape=jax.ShapeDtypeStruct((4 * HALF, FEAT), BF),
        compiler_params=params(),
    )(flat.T)


def tap_grad_rows(full):
    chan, half, spot = feature_parts(1)
    line = lax.broadcasted_iota(jnp.int32, (HALF, FEAT), 0)
    sums = [[None] * 3 for _ in range(9)]
    for r in range(4):
        block = full[r * HALF : (r + 1) * HALF]
        for ch in range(CIN):
            for b in range(3):
                line_sum = jnp.sum(jnp.where(line == WIN * ch + b + spot, block, 0.0), axis=0, keepdims=True)
                for a in range(3):
                    if 0 <= r - a < 2:
                        part = jnp.where(half == r - a, line_sum, 0.0)
                        old = sums[3 * ch + b][a]
                        sums[3 * ch + b][a] = part if old is None else old + part
    lines = [sums[3 * ch + b][a] for ch in range(CIN) for a in range(3) for b in range(3)]
    lines.append(full[ONE_LANE : ONE_LANE + 1])
    lines.append(jnp.zeros((4, FEAT), F32))
    table = jnp.concatenate(lines, axis=0)
    chan, _, _ = feature_parts(128)
    expand = jnp.where(chan == lax.broadcasted_iota(jnp.int32, (128, FEAT), 0), 1.0, 0.0).astype(BF)
    hi, mid, lo = three_terms(table)
    return mm_t(hi, expand) + (mm_t(mid, expand) + mm_t(lo, expand))


def on_device(
    images, item_segment, conv_weight, conv_bias, patch_weight, patch_bias, norm1_gain, norm1_bias,
    query_weight, query_bias, key_weight, value_weight, value_bias, output_weight, output_bias,
    norm2_gain, norm2_bias, hidden_weight, hidden_bias, result_weight, result_bias, cotangent,
):
    items, rows = lax.axis_size("items"), lax.axis_size("rows")
    sizes = grid_sizes(items, rows)
    count, _, height, _ = images.shape
    nrow = height // PATCH
    group = count * nrow

    def vec(v):
        return v.astype(F32).reshape(1, -1)

    down = [(i, i + 1) for i in range(rows - 1)]
    up = [(i + 1, i) for i in range(rows - 1)]
    top = lax.ppermute(images[:, :, height - 1], "rows", down)
    bot = lax.ppermute(images[:, :, 0], "rows", up)

    def spread(edge):
        edge = edge.transpose(1, 0, 2)[:, :, None, :].astype(F32)
        return jnp.broadcast_to(edge, (CIN, count, nrow, IMG)).reshape(CIN, group, IMG)

    segments = lax.dynamic_slice_in_dim(item_segment, lax.axis_index("rows") * SEQ_ITEMS, SEQ_ITEMS)
    lanes = jnp.arange(128)[None, :]
    same = lanes == segments[:, None]
    qx = jnp.where(same, 1.0, 0.0).astype(F32)
    kx = jnp.where((lanes < 4) & ~same, -1e30, 0.0) + jnp.where((lanes >= 4) & (lanes < 7), 1.0, 0.0)
    kx = kx.astype(F32)

    taps = tap_matrix(conv_weight, conv_bias)
    weight4 = patch_weight.reshape(CH, STEPS, 2 * PATCH, D)
    x, xt, sel = patchify(images, spread(top), spread(bot))
    embedded, saved = stem_forward(x, taps, weight4, vec(patch_bias))
    tokens = lax.all_to_all(
        embedded.reshape(count, nrow, NP, D), "rows", split_axis=0, concat_axis=1, tiled=True
    ).reshape(TOK, D)
    gain1, shift1 = vec(norm1_gain), vec(norm1_bias)
    q, k, v, attended, lx = attend(
        tokens, gain1, shift1, qx, kx, query_weight, key_weight, value_weight, vec(query_bias), vec(value_bias)
    )
    vecs = jnp.concatenate([vec(output_bias), vec(norm2_gain), vec(norm2_bias), vec(result_bias)], axis=0)
    block_out, middle_grad, attended_grad, wo_grad, wh_grad, wr_grad, sums2, hb_grad = mixer(
        tokens, attended, cotangent, output_weight, vecs, hidden_weight, vec(hidden_bias), result_weight, sizes
    )
    token_grad, squares, sums1, qvs, wh_grad, wr_grad, wo_grad = attend_back(
        tokens, gain1, shift1, kx, middle_grad, q, k, v, attended, attended_grad, lx,
        query_weight, key_weight, value_weight, wh_grad, wr_grad, wo_grad, sizes,
    )
    embed_grad = lax.all_to_all(
        token_grad.reshape(SEQ_ITEMS, NP, NP, D), "rows", split_axis=1, concat_axis=0, tiled=True
    ).reshape(-1, D)
    early = jnp.concatenate([v.reshape(-1, 128) for v in (sums2[0:4], hb_grad, sums1[0:2], qvs[0:2])], axis=0)
    pw_grad, wq_grad, wk_grad, wv_grad, image_grad, sums, tap_grads = finish(
        embed_grad, saved, weight4, xt, taps, sel, squares, early, count, height, sizes
    )
    wide = D // 128

    def row_of(at):
        return sums[at * wide : (at + 1) * wide].reshape(D)

    return (
        block_out,
        image_grad,
        tap_grads[0:27, 0:CH].T.reshape(conv_weight.shape),
        tap_grads[27, 0:CH],
        pw_grad.T,
        row_of(12),
        row_of(8),
        row_of(9),
        wq_grad,
        row_of(10),
        wk_grad,
        wv_grad,
        row_of(11),
        wo_grad,
        row_of(2),
        row_of(0),
        row_of(1),
        wh_grad,
        sums[4 * wide : 8 * wide].reshape(FF),
        wr_grad.T,
        row_of(3),
    )


def solution(mesh):
    split = P("items", "rows")
    flat = P(("items", "rows"), None)
    image = P("items", None, "rows", None)
    return jax.shard_map(
        on_device,
        mesh=mesh,
        in_specs=(image, P("items")) + (P(),) * 19 + (flat,),
        out_specs=(
            flat, image, P(), P(), split, P(), P(), P(), split, P(), split, split,
            P(), split, P(), P(), P(), split, P(), split, P(),
        ),
        check_vma=False,
    )
```

```python
import functools

import jax
import jax.numpy as jnp
from jax import lax
from jax.experimental import pallas as pl
from jax.experimental.pallas import tpu as pltpu
from jax.sharding import PartitionSpec as P

BF = jnp.bfloat16
F32 = jnp.float32
D = 768
HEADS = 12
HD = 64
FF = 3072
IMG = 256
PATCH = 16
CH = 32
CIN = 3
SEQ_ITEMS = 4
NPATCH = 256
TOK = 1024
NP = IMG // PATCH
PF = CH * PATCH * PATCH
HALF = 64
WIN = PATCH + 2
ONE_LANE = CIN * WIN
SLABS = (PATCH + 2) // 2
STEPS = PATCH // 2
FEAT = PF // STEPS
GELU_A = 0.7978845608028654
GELU_B = GELU_A * 0.044715
VMEM_CAP = 60 * 1024 * 1024


def mm(left, right):
    return jnp.dot(left, right, preferred_element_type=F32)


def mm_t(left, right):
    return lax.dot_general(left, right, (((1,), (1,)), ((), ())), preferred_element_type=F32)


def params(**extra):
    return pltpu.CompilerParams(vmem_limit_bytes=VMEM_CAP, **extra)


def whole(shape):
    zeros = (0,) * len(shape)
    return pl.BlockSpec(shape, lambda *_: zeros, pipeline_mode=pl.Buffered(1))


def gelu_pair(v):
    square = v * v
    gate = 0.5 + 0.5 * jnp.tanh(v * (GELU_A + GELU_B * square))
    act = v * gate
    slope = gate + act * (1.0 - gate) * (2.0 * GELU_A + (6.0 * GELU_B) * square)
    return act, slope


MESH = pl.DeviceIdType.MESH


def grid_sizes(items, rows):
    nx = rows // 2
    ny = nx if items % nx == 0 else 1
    return (2, nx, ny, items // ny)


def place(sizes):
    item, row = lax.axis_index("items"), lax.axis_index("rows")
    return (row % 2, row // 2, item % sizes[2], item // sizes[2])


def peer(sizes, pos, axis, k):
    moved = list(pos)
    moved[axis] = lax.rem(pos[axis] + k, sizes[axis])
    return (moved[3] * sizes[2] + moved[2], moved[1] * 2 + moved[0]), moved[axis]


def greet(sizes, pos, near, far):
    barrier = pltpu.get_barrier_semaphore()
    item, row, rows = lax.axis_index("items"), lax.axis_index("rows"), 2 * sizes[1]
    peers = [(item, lax.rem(row + k, rows)) for k in range(1, rows)] if near else []
    for axis in (2, 3) if far else ():
        peers += [peer(sizes, pos, axis, k)[0] for k in range(1, sizes[axis])]
    for device in peers:
        pl.semaphore_signal(barrier, inc=1, device_id=device, device_id_type=MESH)
    pl.semaphore_wait(barrier, len(peers))


def turn_of(sizes, pos, x):
    return lax.rem(x + 2 * sizes[1] - 1 - pos[1], sizes[1])


def add_up(first, rest):
    total = first.astype(F32)
    for term in rest:
        total = total + term.astype(F32)
    return total


class Piece:
    def __init__(self, sizes, pos, order, source, own, bufs, send, recv):
        self.sizes, self.pos = sizes, pos
        self.source, self.own, self.bufs = source, own, bufs
        self.send, self.recv = send, recv
        self.axes = (0,) + order

    def at(self, stage, where):
        left = sorted(self.axes[stage:])
        return (slice(None),) * left.index(self.axes[stage]) + (where,)

    def copies(self, stage):
        out = []
        for k in range(1, self.sizes[self.axes[stage]]):
            device, there = peer(self.sizes, self.pos, self.axes[stage], k)
            if stage == 0:
                src, dst = self.source.at[there], self.bufs[0]
            else:
                held = self.at(stage, there)
                src = self.bufs[0].at[held] if stage == 1 else self.bufs[stage - 1].at[(0,) + held]
                dst = self.bufs[stage].at[k - 1]
            out.append(
                pltpu.make_async_remote_copy(
                    src_ref=src, dst_ref=dst, send_sem=self.send.at[stage, k - 1], recv_sem=self.recv.at[stage, k - 1],
                    device_id=device, device_id_type=MESH,
                )
            )
        return out

    def start(self, stage):
        for copy in self.copies(stage):
            copy.start()

    def gather(self, stage):
        for copy in self.copies(stage):
            copy.wait_recv()
        bufs = self.bufs
        if stage == 0:
            bufs[0][...] = bufs[0][...] + self.own[...]
            return None
        held = self.at(stage, self.pos[self.axes[stage]])
        base = bufs[0][held] if stage == 1 else bufs[stage - 1][(0,) + held]
        terms = self.sizes[self.axes[stage]] - 1
        if stage < 3 and terms == 1:
            bufs[stage][0] = base + bufs[stage][0]
            return None
        total = add_up(base, [bufs[stage][k] for k in range(terms)])
        if stage == 3:
            return total
        bufs[stage][0] = total.astype(BF)

    def advance(self, stage):
        self.gather(stage - 1)
        self.start(stage)

    def drain(self, stages=(0, 1, 2, 3)):
        for stage in stages:
            for copy in self.copies(stage):
                copy.wait_send()


def piece_scratch(sizes, orders, shape):
    out = []
    for order in orders:
        out.append(pltpu.VMEM(sizes[1:] + shape, BF))
        for stage in range(3):
            left = tuple(sizes[axis] for axis in sorted(order[stage + 1 :]))
            out.append(pltpu.VMEM((sizes[order[stage]] - 1,) + left + shape, BF))
    sems = pltpu.SemaphoreType.DMA((len(orders), 4, max(sizes) - 1))
    return out + [sems, sems]


def own_scratch(sizes, count, shape):
    return [pltpu.VMEM((count,) + sizes[1:] + shape, BF), pltpu.SemaphoreType.DMA((count,))]


def make_pieces(sizes, pos, orders, sources, owns, refs):
    count = len(orders)
    return [
        Piece(sizes, pos, orders[n], sources[n], owns[n], refs[4 * n : 4 * n + 4], refs[4 * count].at[n], refs[4 * count + 1].at[n])
        for n in range(count)
    ]


class SmallSum:
    def __init__(self, sizes, pos, bufs, send, recv):
        self.sizes, self.pos, self.bufs, self.send, self.recv = sizes, pos, bufs, send, recv

    def copies(self, axis, receive):
        buf, here = self.bufs[axis], self.pos[axis]
        out = []
        for k in range(1, self.sizes[axis]):
            device, _ = peer(self.sizes, self.pos, axis, k)
            slot = lax.rem(here + self.sizes[axis] - k, self.sizes[axis]) if receive else here
            out.append(
                pltpu.make_async_remote_copy(
                    src_ref=buf.at[here], dst_ref=buf.at[slot], send_sem=self.send.at[axis, k - 1],
                    recv_sem=self.recv.at[axis, k - 1], device_id=device, device_id_type=MESH,
                )
            )
        return out

    def start(self, axis, value):
        self.bufs[axis][self.pos[axis]] = value
        for copy in self.copies(axis, False):
            copy.start()

    def gather(self, axis):
        for copy in self.copies(axis, True):
            copy.wait_recv()
        total = self.bufs[axis][0]
        for k in range(1, self.sizes[axis]):
            total = total + self.bufs[axis][k]
        return total

    def advance(self, axis):
        self.start(axis, self.gather(axis - 1))

    def drain(self):
        for axis in range(4):
            for copy in self.copies(axis, False):
                copy.wait_send()


def small_scratch(sizes, height):
    return [pltpu.VMEM((size, height, 128), F32) for size in sizes] + [
        pltpu.SemaphoreType.DMA((4, max(sizes) - 1)),
        pltpu.SemaphoreType.DMA((4, max(sizes) - 1)),
    ]


def folds(width):
    return width % 128 == HALF and width > 128


def narrow(width):
    return 128 // width if width < 128 and 128 % width == 0 else 1


def folded_shape(height, width):
    if folds(width) or narrow(width) > 1:
        return (height * width // 128, 128)
    return (height, width)


def fold_block(block):
    height, width = block.shape
    if narrow(width) > 1:
        part = height // narrow(width)
        return jnp.concatenate([block[k * part : (k + 1) * part] for k in range(narrow(width))], axis=1)
    return block


def unfold_block(block, height, width, odd=False):
    if narrow(width) > 1:
        return jnp.concatenate([block[:, k * width : (k + 1) * width] for k in range(narrow(width))], axis=0)
    if not folds(width):
        return block
    main, side = block[:height], block[height:]
    side = jnp.concatenate([side[:, :HALF], side[:, HALF:]], axis=0)
    return jnp.where(odd, jnp.concatenate([side, main], axis=1), jnp.concatenate([main, side], axis=1))


def run_events(step, table, slots):
    for (when, slot), todo in table.items():
        if slot in slots:
            @pl.when(step == when)
            def _(todo=todo):
                for call in todo:
                    call()


def make_windows(sizes, pos, img_ref, edge, edge_copies, x, xt_ref, sel_ref, pix, lines):
    items, _, height, width = img_ref.shape
    nrow = height // PATCH
    group = items * nrow
    row, final_row = lax.axis_index("rows"), lax.axis_size("rows") - 1
    for ch in range(CIN):
        for item in range(items):
            full = img_ref[item, ch].astype(F32)
            for k in range(width // 128):
                pix[ch, k, item * height : (item + 1) * height, :] = full[:, k * 128 : (k + 1) * 128]

    def line(ch, r):
        return jnp.concatenate([pix[ch, k, pl.ds(r, group, stride=PATCH), :] for k in range(width // 128)], axis=1)

    for ch in range(CIN):
        first, final = line(ch, 0), line(ch, PATCH - 1)
        edge[0, ch] = pltpu.roll(first, nrow - 1, 0).astype(BF)
        edge[1, ch] = pltpu.roll(final, group - nrow + 1, 0).astype(BF)

    @pl.when(row > 0)
    def _():
        edge_copies[0].start()

    @pl.when(row < final_row)
    def _():
        edge_copies[1].start()

    for ch in range(CIN):
        cols = slice(ch * width, (ch + 1) * width)
        for r in range(PATCH):
            lines[(r + 1) * group : (r + 2) * group, cols] = line(ch, r).astype(BF)
    lane = lax.broadcasted_iota(jnp.int32, (1, NP * HALF), 1)
    col, spot = lane // HALF, lane % HALF
    for ch in range(CIN):
        inside = (spot >= WIN * ch) & (spot < WIN * (ch + 1))
        want = jnp.where(inside, PATCH * col + spot - WIN * ch - 1, -5)
        here = lax.broadcasted_iota(jnp.int32, (width, NP * HALF), 0)
        sel_ref[ch * width : (ch + 1) * width, :] = jnp.where(here == want, 1.0, 0.0).astype(BF)

    @pl.when(row < final_row)
    def _():
        edge_copies[0].wait_recv()

    @pl.when(row > 0)
    def _():
        edge_copies[1].wait_recv()

    patch_row = lax.broadcasted_iota(jnp.int32, (group, width), 0) % nrow
    for ch in range(CIN):
        cols = slice(ch * width, (ch + 1) * width)
        up = jnp.where(patch_row == 0, edge[3, ch].astype(F32), pltpu.roll(line(ch, PATCH - 1), 1, 0))
        lines[0:group, cols] = up.astype(BF)
        down = jnp.where(patch_row == nrow - 1, edge[2, ch].astype(F32), pltpu.roll(line(ch, 0), group - 1, 0))
        lines[(PATCH + 1) * group : (PATCH + 2) * group, cols] = down.astype(BF)
    lane = lax.broadcasted_iota(jnp.int32, (group, 2 * HALF), 1)
    low = lane < HALF
    ones = (lane % HALF) == ONE_LANE
    nx = sizes[1]
    share, per = items * nrow * NP // nx, group // nx
    turns = [turn_of(sizes, pos, xg) * share for xg in range(nx)]

    def put(j, c, block):
        low_bits = block.astype(BF)
        for xg in range(nx):
            x[j, pl.ds(pl.multiple_of(turns[xg] + c * per, per), per), :] = low_bits[xg * per : (xg + 1) * per]

    for quarter in range(NP * HALF // 256):
        res = mm(lines[...], sel_ref[:, quarter * 256 : (quarter + 1) * 256])
        for j in range(SLABS):
            first = res[2 * j * group : (2 * j + 1) * group]
            second = res[(2 * j + 1) * group : (2 * j + 2) * group]
            for pair in range(2):
                a = first[:, pair * 128 : (pair + 1) * 128]
                b = second[:, pair * 128 : (pair + 1) * 128]
                put(j, quarter * 4 + pair * 2, jnp.where(ones, 1.0, jnp.where(low, a, pltpu.roll(b, HALF, 1))))
                put(j, quarter * 4 + pair * 2 + 1, jnp.where(ones, 1.0, jnp.where(low, pltpu.roll(a, HALF, 1), b)))
    for j in range(SLABS):
        xt_ref[j] = x[j].T


def stem_kernel(sizes, img_ref, cw_ref, w_ref, pb_ref, tok_ref, saved_ref, xt_ref, sel_ref, t_ref,
                x, pix, lines, edge, edge_send, edge_recv, acc, nat, parcel, got, send, recv):
    t = pl.program_id(0)
    p = t % STEPS
    nx = sizes[1]
    rows = 2 * nx
    pos = place(sizes)
    item, row, final_row = lax.axis_index("items"), lax.axis_index("rows"), lax.axis_size("rows") - 1
    share = acc.shape[0]
    per = share // NP

    def edge_copy(n):
        return pltpu.make_async_remote_copy(
            src_ref=edge.at[n], dst_ref=edge.at[2 + n], send_sem=edge_send.at[n], recv_sem=edge_recv.at[n],
            device_id=(item, row + (2 * n - 1)), device_id_type=MESH,
        )

    @pl.when(t == 0)
    def _():
        @pl.when(row == final_row)
        def _():
            edge[2] = jnp.zeros(edge.shape[1:], BF)

        @pl.when(row == 0)
        def _():
            edge[3] = jnp.zeros(edge.shape[1:], BF)

        greet(sizes, pos, True, False)
        tap_matrix(cw_ref, t_ref)
        make_windows(sizes, pos, img_ref, edge, [edge_copy(0), edge_copy(1)], x, xt_ref, sel_ref, pix, lines)

    @pl.when(p == 0)
    def _():
        acc[...] = jnp.broadcast_to(pb_ref[...], acc.shape)

    weight = w_ref[...].reshape(FEAT, D)
    for s in range(share // 256):
        rs = slice(s * 256, (s + 1) * 256)
        here = pl.ds(pl.multiple_of(t // STEPS * share + s * 256, 256), 256)
        xs = jnp.concatenate([x[p, here, :], x[p + 1, here, :]], axis=1)
        for n in range(FEAT // 256):
            cs = slice(n * 256, (n + 1) * 256)
            act, slope = gelu_pair(mm(xs, t_ref[:, cs]))
            saved_ref[0, 0, rs, cs] = act.astype(BF)
            saved_ref[0, 1, rs, cs] = slope.astype(BF)
        acc[rs, :] += mm(saved_ref[0, 0, rs, :], weight)

    @pl.when(p == STEPS - 1)
    def _():
        for c in range(NP):
            for k in range(D // 128):
                nat[k, pl.ds(c, per, stride=NP), :] = acc[c * per : (c + 1) * per, k * 128 : (k + 1) * 128]

    def parcel_copy(turn, core, slot):
        to = lax.rem(pos[1] + 1 + turn, nx) * 2 + core
        return pltpu.make_async_remote_copy(
            src_ref=parcel.at[turn, core], dst_ref=got.at[:, row], send_sem=send.at[turn, slot], recv_sem=recv.at[row],
            device_id=(item, to), device_id_type=MESH,
        )

    for turn in range(nx):
        @pl.when(t == turn * STEPS + STEPS - 1)
        def _(turn=turn):
            for k in range(D // 128):
                cut = nat[k].astype(BF).reshape(parcel.shape[1:4] + (128,))
                parcel[turn, :, :, :, k * 128 : (k + 1) * 128] = cut
            if turn < nx - 1:
                for core in range(2):
                    parcel_copy(turn, core, core).start()
            else:
                parcel_copy(turn, 1 - pos[0], 0).start()
                got[:, row] = parcel[turn, pos[0]]

    @pl.when(t == nx * STEPS - 1)
    def _():
        for k in range(1, rows):
            source = lax.rem(row + k, rows)
            pltpu.make_async_remote_copy(
                src_ref=parcel.at[0, 0], dst_ref=got.at[:, source], send_sem=send.at[0, 0], recv_sem=recv.at[source],
                device_id=(item, source), device_id_type=MESH,
            ).wait_recv()
        tok_ref[...] = got[...]
        for turn in range(nx - 1):
            for core in range(2):
                parcel_copy(turn, core, core).wait_send()
        parcel_copy(nx - 1, 1 - pos[0], 0).wait_send()

        @pl.when(row > 0)
        def _():
            edge_copy(0).wait_send()

        @pl.when(row < final_row)
        def _():
            edge_copy(1).wait_send()


def stem_forward(images, cw, weight, bias, sizes):
    count, _, height, width = images.shape
    nx = sizes[1]
    nrow = height // PATCH
    group = count * nrow
    tokens = group * NP
    share = tokens // nx
    arrived = (SEQ_ITEMS, 2 * nx, nrow * NP, D)
    return pl.pallas_call(
        functools.partial(stem_kernel, sizes),
        name="stem_forward",
        grid=(nx * STEPS,),
        in_specs=[
            whole(images.shape),
            whole(cw.shape),
            pl.BlockSpec((CH, 1, 2 * PATCH, D), lambda t: (0, t % STEPS, 0, 0)),
            whole((1, D)),
        ],
        out_specs=(
            whole(arrived),
            pl.BlockSpec((1, 2, share, FEAT), lambda t: (t % STEPS, 0, t // STEPS, 0)),
            whole((SLABS, 128, tokens)),
            whole((CIN * width, NP * HALF)),
            whole((4 * HALF, FEAT)),
        ),
        out_shape=(
            jax.ShapeDtypeStruct(arrived, BF),
            jax.ShapeDtypeStruct((STEPS, 2, tokens, FEAT), BF),
            jax.ShapeDtypeStruct((SLABS, 128, tokens), BF),
            jax.ShapeDtypeStruct((CIN * width, NP * HALF), BF),
            jax.ShapeDtypeStruct((4 * HALF, FEAT), BF),
        ),
        scratch_shapes=[
            pltpu.VMEM((SLABS, tokens, 128), BF),
            pltpu.VMEM((CIN, width // 128, count * height, 128), F32),
            pltpu.VMEM((WIN * group, CIN * width), BF),
            pltpu.VMEM((4, CIN, group, width), BF),
            pltpu.SemaphoreType.DMA((2,)),
            pltpu.SemaphoreType.DMA((2,)),
            pltpu.VMEM((share, D), F32),
            pltpu.VMEM((D // 128, share, 128), F32),
            pltpu.VMEM((nx, 2, SEQ_ITEMS, nrow * NP, D), BF),
            pltpu.VMEM(arrived, BF),
            pltpu.SemaphoreType.DMA((nx, 2)),
            pltpu.SemaphoreType.DMA((2 * nx,)),
        ],
        compiler_params=params(collective_id=0, has_side_effects=True),
    )(images, cw, weight, bias)


def norm_stats(v):
    centred = v - jnp.mean(v, axis=-1, keepdims=True)
    inv = lax.rsqrt(jnp.mean(centred * centred, axis=-1, keepdims=True) + 1e-06)
    return centred * inv, inv


def three_terms(v):
    hi = v.astype(BF)
    rest = v - hi.astype(F32)
    mid = rest.astype(BF)
    lo = (rest - mid.astype(F32)).astype(BF)
    return hi, mid, lo


def minus_terms(v, lane, base):
    hi, mid, lo = three_terms(-v)
    out = jnp.where(lane == 4, hi.astype(F32), base)
    out = jnp.where(lane == 5, mid.astype(F32), out)
    return jnp.where(lane == 6, lo.astype(F32), out).astype(BF)


def attend_kernel(tok_ref, g_ref, b_ref, qx_ref, kx_ref, wq_ref, wk_ref, wv_ref, qb_ref, vb_ref,
                  q_ref, k_ref, v_ref, o_ref, lx_ref, n1, kaug, vaug):
    @pl.when(pl.program_id(0) == 0)
    def _():
        for s in range(TOK // 128):
            rs = slice(s * 128, (s + 1) * 128)
            hat, _ = norm_stats(tok_ref[rs, :].astype(F32))
            n1[rs, :] = (hat * g_ref[...] + b_ref[...]).astype(BF)

    q_ref[...] = ((mm(n1[...], wq_ref[...]) + qb_ref[...]).astype(BF) * 0.125).astype(BF)
    k_ref[...] = mm(n1[...], wk_ref[...]).astype(BF)
    v_ref[...] = (mm(n1[...], wv_ref[...]) + vb_ref[...]).astype(BF)
    lane = lax.broadcasted_iota(jnp.int32, (NPATCH, 128), 1)
    low = lane < HD
    for i in range(SEQ_ITEMS):
        rs = slice(i * NPATCH, (i + 1) * NPATCH)
        kaug[rs, 128:256] = jnp.broadcast_to(kx_ref[i : i + 1, :], (NPATCH, 128)).astype(BF)
        vaug[rs, 128:256] = jnp.ones((NPATCH, 128), BF)
    for pair in range(2):
        cs = slice(pair * 128, (pair + 1) * 128)
        kaug[:, 0:128] = k_ref[:, cs]
        vaug[:, 0:128] = v_ref[:, cs]
        for i in range(SEQ_ITEMS):
            rs = slice(i * NPATCH, (i + 1) * NPATCH)
            span = slice(0, (i + 1) * NPATCH)
            qp = q_ref[rs, cs]
            qx = jnp.broadcast_to(qx_ref[i : i + 1, :], (NPATCH, 128))
            halves = []
            for h in range(2):
                mine = low if h == 0 else ~low
                qaug = jnp.concatenate([jnp.where(mine, qp, jnp.zeros_like(qp)), qx.astype(BF)], axis=1)
                scores = mm_t(qaug, kaug[span, :])
                top = jnp.max(scores, axis=1, keepdims=True)
                raised = jnp.exp(scores - top).astype(BF)
                out = mm(raised, vaug[span, :])
                total = out[:, 128:256]
                halves.append(out[:, 0:128] / total)
                lx_ref[pair * 2 + h, rs, :] = minus_terms(top + jnp.log(total), lane, qx)
            o_ref[rs, cs] = jnp.where(low, halves[0], halves[1]).astype(BF)


def attend(tokens, gain, shift, qx, kx, wq, wk, wv, qb, vb):
    col = pl.BlockSpec((D, 256), lambda g: (0, g))
    row = pl.BlockSpec((1, 256), lambda g: (0, g))
    out = pl.BlockSpec((TOK, 256), lambda g: (0, g))
    return pl.pallas_call(
        attend_kernel,
        name="attend",
        grid=(D // 256,),
        in_specs=[whole((TOK, D)), whole((1, D)), whole((1, D)), whole(qx.shape), whole(kx.shape),
                  col, col, col, row, row],
        out_specs=(out, out, out, out, pl.BlockSpec((4, TOK, 128), lambda g: (g, 0, 0))),
        out_shape=(jax.ShapeDtypeStruct((TOK, D), BF),) * 4 + (jax.ShapeDtypeStruct((HEADS, TOK, 128), BF),),
        scratch_shapes=[pltpu.VMEM((TOK, D), BF), pltpu.VMEM((TOK, 256), BF), pltpu.VMEM((TOK, 256), BF)],
        compiler_params=params(),
    )(tokens, gain, shift, qx, kx, wq, wk, wv, qb, vb)


def norm_back(e, hat, inv, gain):
    f = e * gain
    return inv * (f - jnp.mean(f, axis=-1, keepdims=True) - hat * jnp.mean(f * hat, axis=-1, keepdims=True))


def col_sum(v):
    return jnp.sum(v, axis=0, keepdims=True)


def store_square(ref, n, grad):
    _, _, nx, ny, nz, _, _ = ref.shape
    height, width = D // (ny * nz), D // (2 * nx)
    if not folds(width):
        for r in range(2 * nx):
            part = grad[:, r * width : (r + 1) * width]
            for i in range(ny * nz):
                ref[n, r % 2, r // 2, i % ny, i // ny] = part[i * height : (i + 1) * height]
        return
    half = height // 2
    low = lax.broadcasted_iota(jnp.int32, (half, 128), 1) < HALF
    for x in range(nx):
        base = 2 * x * width
        shared = grad[:, base + 128 : base + 256]
        turned = jnp.concatenate([shared[:, HALF:], shared[:, :HALF]], axis=1)
        for i in range(ny * nz):
            top, end = i * height, (i + 1) * height
            mid = top + half
            ref[n, 0, x, i % ny, i // ny, 0:height] = grad[top:end, base : base + 128]
            ref[n, 0, x, i % ny, i // ny, height:] = jnp.where(low, shared[top:mid], turned[mid:end])
            ref[n, 1, x, i % ny, i // ny, 0:height] = grad[top:end, base + 256 : base + 384]
            ref[n, 1, x, i % ny, i // ny, height:] = jnp.where(low, turned[top:mid], shared[mid:end])


def mixer_kernel(tok_ref, att_ref, cot_ref, wo_ref, vec_ref, wh_ref, hb_ref, wr_ref,
                 out_ref, mid_ref, ag_ref, wog_ref, whg_ref, wrg_ref, sums_ref, hbg_ref,
                 middle, n2, n2t, cott, acc, back, act, hg):
    step = pl.program_id(0)
    last = pl.num_programs(0) - 1
    chunk = wh_ref.shape[1]
    tile = 2 if chunk % 256 == 0 else 3
    blocks = [slice(s * 256, (s + 1) * 256) for s in range(TOK // 256)]

    @pl.when(step == 0)
    def _():
        for rs in blocks:
            row = tok_ref[rs, :].astype(F32) + mm(att_ref[rs, :], wo_ref[...]) + vec_ref[0:1, :]
            middle[rs, :] = row
            acc[rs, :] = row + vec_ref[3:4, :]
            back[rs, :] = jnp.zeros((256, D), F32)
            hat, _ = norm_stats(row)
            low = (hat * vec_ref[1:2, :] + vec_ref[2:3, :]).astype(BF)
            n2[rs, :] = low
            n2t[:, rs] = low.T
            cott[:, rs] = cot_ref[rs, :].T

    hsum = jnp.zeros((1, chunk), F32)
    for rs in blocks:
        for n in range(chunk // 128 // tile):
            cs = slice(n * 128 * tile, (n + 1) * 128 * tile)
            pre = mm(n2[rs, :], wh_ref[:, cs]) + hb_ref[:, cs]
            up = mm_t(cot_ref[rs, :], wr_ref[cs, :])
            a, slope = gelu_pair(pre)
            act[rs, cs] = a.astype(BF)
            hg[rs, cs] = (slope * up).astype(BF)
        acc[rs, :] += mm(act[rs, :], wr_ref[...])
        back[rs, :] += mm_t(hg[rs, :], wh_ref[...])
        hsum = hsum + col_sum(hg[rs, :].astype(F32))
    hbg_ref[...] = hsum
    _, _, nx, ny, nz, height, _ = whg_ref.shape
    for n in range(3):
        width = chunk // 3
        grad = mm(n2t[...], hg[:, n * width : (n + 1) * width]).astype(BF)
        for i in range(ny * nz):
            whg_ref[n, 0, 0, i % ny, i // ny] = grad[i * height : (i + 1) * height]
    _, _, nx, ny, _, _, _ = wrg_ref.shape
    height, width = D // (2 * nx), chunk // ny // 3
    for y in range(ny):
        grad = mm(cott[...], act[:, y * 3 * width : (y + 1) * 3 * width]).astype(BF)
        for n in range(3):
            for r in range(2 * nx):
                part = grad[r * height : (r + 1) * height, n * width : (n + 1) * width]
                wrg_ref[n, r % 2, r // 2, y, 0] = fold_block(part)

    @pl.when(step == last)
    def _():
        gsum = jnp.zeros((1, D), F32)
        bsum = jnp.zeros((1, D), F32)
        osum = jnp.zeros((1, D), F32)
        rsum = jnp.zeros((1, D), F32)
        for rs in blocks:
            out_ref[rs, :] = acc[rs, :].astype(BF)
            hat, inv = norm_stats(middle[rs, :])
            e = back[rs, :]
            gsum = gsum + col_sum(e * hat)
            bsum = bsum + col_sum(e)
            cot = cot_ref[rs, :].astype(F32)
            rsum = rsum + col_sum(cot)
            mid = cot + norm_back(e, hat, inv, vec_ref[1:2, :])
            mid_ref[rs, :] = mid
            low = mid.astype(BF)
            osum = osum + col_sum(low.astype(F32))
            n2[rs, :] = low
            n2t[:, rs] = att_ref[rs, :].T
            ag_ref[rs, :] = mm_t(low, wo_ref[...]).astype(BF)
        store_square(wog_ref, 0, mm(n2t[...], n2[...]).astype(BF))
        sums_ref[0:1, :] = gsum
        sums_ref[1:2, :] = bsum
        sums_ref[2:3, :] = osum
        sums_ref[3:4, :] = rsum


def mixer(tokens, attended, cotangent, wo, vecs, wh, hb, wr, sizes):
    nc, nx, ny, nz = sizes
    rows, items = nc * nx, ny * nz
    chunk = FF // rows
    square = (1,) + sizes + folded_shape(D // items, D // rows)
    return pl.pallas_call(
        mixer_kernel,
        name="mixer",
        grid=(rows,),
        in_specs=[
            whole((TOK, D)), whole((TOK, D)), whole((TOK, D)), whole((D, D)), whole(vecs.shape),
            pl.BlockSpec((D, chunk), lambda r: (0, r)),
            pl.BlockSpec((1, chunk), lambda r: (0, r)),
            pl.BlockSpec((chunk, D), lambda r: (r, 0)),
        ],
        out_specs=(
            whole((TOK, D)), whole((TOK, D)), whole((TOK, D)), whole(square),
            pl.BlockSpec((3, 1, 1, ny, nz, D // items, chunk // 3), lambda r: (0, r % 2, r // 2, 0, 0, 0, 0)),
            pl.BlockSpec((3, nc, nx, ny, 1) + folded_shape(D // rows, FF // items // 3), lambda r: (0, 0, 0, 0, r, 0, 0)),
            whole((8, D)),
            pl.BlockSpec((1, chunk), lambda r: (0, r)),
        ),
        out_shape=(
            jax.ShapeDtypeStruct((TOK, D), BF),
            jax.ShapeDtypeStruct((TOK, D), F32),
            jax.ShapeDtypeStruct((TOK, D), BF),
            jax.ShapeDtypeStruct(square, BF),
            jax.ShapeDtypeStruct((3,) + sizes + (D // items, chunk // 3), BF),
            jax.ShapeDtypeStruct((3,) + sizes + folded_shape(D // rows, FF // items // 3), BF),
            jax.ShapeDtypeStruct((8, D), F32),
            jax.ShapeDtypeStruct((1, FF), F32),
        ),
        scratch_shapes=[
            pltpu.VMEM((TOK, D), F32), pltpu.VMEM((TOK, D), BF), pltpu.VMEM((D, TOK), BF),
            pltpu.VMEM((D, TOK), BF), pltpu.VMEM((TOK, D), F32), pltpu.VMEM((TOK, D), F32),
            pltpu.VMEM((TOK, chunk), BF), pltpu.VMEM((TOK, chunk), BF),
        ],
        compiler_params=params(),
    )(tokens, attended, cotangent, wo, vecs, wh, hb, wr)


def attend_back_kernel(sizes, tok_ref, g_ref, b_ref, kx_ref, mid_ref, q_ref, k_ref, v_ref, o_ref, ag_ref, lx_ref,
                       wq_ref, wk_ref, wv_ref, whg_ref, wrg_ref, wog_ref,
                       tg_ref, sq_ref, sums_ref, qvs_ref, who_ref, wro_ref, woo_ref,
                       n1t, back, kaug, vaug, qaug, oaug, dqt, dq, dk, dv, square, *comm):
    step = pl.program_id(0)
    blocks = [slice(s * 256, (s + 1) * 256) for s in range(TOK // 256)]
    pos = place(sizes)
    groups = ((whg_ref, who_ref), (wrg_ref, wro_ref), (wog_ref, woo_ref))
    pieces, loads, base, at = [], [], 0, 0
    for source, _ in groups:
        count = source.shape[0]
        refs, keep = comm[at : at + 4 * count + 2], comm[at + 4 * count + 2 : at + 4 * count + 4]
        at += 4 * count + 4
        pieces += make_pieces(
            sizes, pos, BACK_ORDERS[base : base + count], [source.at[n] for n in range(count)],
            [keep[0].at[n] for n in range(count)], refs,
        )
        loads += [pltpu.make_async_copy(source.at[n, pos[0]], keep[0].at[n], keep[1].at[n]) for n in range(count)]
        base += count

    def event(index, stage):
        if stage == 0:
            pieces[index].start(0)
            loads[index].start()
        elif stage < 4:
            if stage == 1:
                loads[index].wait()
            pieces[index].advance(stage)
        else:
            total = pieces[index].gather(3)
            if index < 3:
                width = total.shape[1]
                who_ref[:, index * width : (index + 1) * width] = total
            elif index < 6:
                height, width = D // (2 * sizes[1]), FF // (sizes[2] * sizes[3]) // 3
                wro_ref[:, (index - 3) * width : (index - 2) * width] = unfold_block(total, height, width)
            else:
                woo_ref[...] = unfold_block(total, *woo_ref.shape, odd=pos[0] == 1)

    def finish():
        for part in pieces:
            part.drain()

    table = {(0, 0): [functools.partial(greet, sizes, pos, True, True)]}
    for when, index, stage in BACK_PLAN:
        if when < 2:
            key = (0, when)
        elif when < 26:
            key = ((when - 2) // 8, 2 + (when - 2) % 8)
        else:
            key = (2, 10)
        table.setdefault(key, []).append(functools.partial(event, index, stage))
    table.setdefault((2, 10), []).append(finish)
    run_events(step, table, (0,))

    @pl.when(step == 0)
    def _():
        for rs in blocks:
            hat, _ = norm_stats(tok_ref[rs, :].astype(F32))
            n1t[:, rs] = (hat * g_ref[...] + b_ref[...]).astype(BF).T
            back[rs, :] = jnp.zeros((256, D), F32)

    run_events(step, table, (1,))
    lane = lax.broadcasted_iota(jnp.int32, (NPATCH, 128), 1)
    low = lane < HD
    ones = jnp.where((lane >= 4) & (lane < 7), 1.0, 0.0).astype(BF)
    for i, rs in enumerate(blocks):
        kaug[rs, 128:256] = jnp.broadcast_to(kx_ref[i : i + 1, :], (NPATCH, 128)).astype(BF)
        vaug[rs, 128:256] = ones
    pick_row = lax.broadcasted_iota(jnp.int32, (256, 256), 0) % 128 // HD
    pick_col = lax.broadcasted_iota(jnp.int32, (256, 256), 1) // 128
    pick = jnp.where(pick_row == pick_col, 1.0, 0.0).astype(BF)
    for pair in range(2):
        cs = slice(pair * 128, (pair + 1) * 128)
        kaug[:, 0:128] = k_ref[:, cs]
        vaug[:, 0:128] = v_ref[:, cs]
        kt = k_ref[:, cs].T
        for rs in blocks:
            qp = q_ref[rs, cs]
            gp = ag_ref[rs, cs]
            prod = gp.astype(F32) * o_ref[rs, cs].astype(F32)
            hi = prod.astype(BF)
            both = jnp.concatenate([hi, (prod - hi.astype(F32)).astype(BF)], axis=1)
            dots = mm(both, pick)
            for h in range(2):
                mine = low if h == 0 else ~low
                qaug[h, rs, 0:128] = jnp.where(mine, qp, jnp.zeros_like(qp))
                qaug[h, rs, 128:256] = lx_ref[pair * 2 + h, rs, :]
                oaug[h, rs, 0:128] = jnp.where(mine, gp, jnp.zeros_like(gp))
                oaug[h, rs, 128:256] = minus_terms(dots[:, h * 128 : (h + 1) * 128], lane, jnp.zeros((NPATCH, 128), F32))
        for j, rs in enumerate(blocks):
            span = slice(j * NPATCH, TOK)
            parts_k, parts_v = [], []
            for h in range(2):
                probs = jnp.exp(mm_t(kaug[rs, :], qaug[h, span, :]))
                rise = mm_t(vaug[rs, :], oaug[h, span, :])
                grad = (probs * rise).astype(BF)
                probs_low = probs.astype(BF)
                parts_v.append(mm(probs_low, ag_ref[span, cs]))
                parts_k.append(mm(grad, q_ref[span, cs]))
                hs = slice(h * HD, (h + 1) * HD)
                part = mm(kt[hs, rs], grad)
                if j == 0:
                    dqt[hs, :] = part
                else:
                    dqt[hs, span] += part
            dk[rs, cs] = jnp.where(low, parts_k[0], parts_k[1]).astype(BF)
            dv[rs, cs] = jnp.where(low, parts_v[0], parts_v[1]).astype(BF)
            run_events(step, table, (2 + pair * 4 + j,))
        dq[:, cs] = (dqt[...].T * 0.125).astype(BF)
    qvs_ref[0:1, :] = col_sum(dq[...].astype(F32))
    qvs_ref[1:2, :] = col_sum(dv[...].astype(F32))
    for n, part in enumerate((dq, dk, dv)):
        square[n, step] = mm(n1t[...], part[...]).astype(BF)
    for rs in blocks:
        back[rs, :] += (
            mm_t(dq[rs, :], wq_ref[...]) + mm_t(dk[rs, :], wk_ref[...]) + mm_t(dv[rs, :], wv_ref[...])
        )

    @pl.when(step == pl.num_programs(0) - 1)
    def _():
        gsum = jnp.zeros((1, D), F32)
        bsum = jnp.zeros((1, D), F32)
        for rs in blocks:
            hat, inv = norm_stats(tok_ref[rs, :].astype(F32))
            e = back[rs, :]
            gsum = gsum + col_sum(e * hat)
            bsum = bsum + col_sum(e)
            tg_ref[rs, :] = (mid_ref[rs, :] + norm_back(e, hat, inv, g_ref[...])).astype(BF)
        sums_ref[0:1, :] = gsum
        sums_ref[1:2, :] = bsum
        for n in range(3):
            store_square(sq_ref, n, jnp.concatenate([square[n, g] for g in range(D // 256)], axis=1))

    run_events(step, table, (10,))


BACK_ORDERS = (
    (2, 3, 1), (2, 1, 3), (3, 2, 1), (1, 2, 3), (1, 2, 3), (1, 2, 3),
    (1, 2, 3),
)
BACK_PLAN = (
    (0, 1, 0), (0, 5, 0), (0, 2, 0), (0, 3, 0), (0, 4, 0), (0, 0, 0), (0, 6, 0), (2, 1, 1), (2, 5, 1),
    (3, 2, 1), (4, 4, 1), (6, 0, 1), (6, 3, 1), (8, 5, 2), (13, 0, 2), (13, 4, 2), (14, 6, 1), (14, 1, 2),
    (15, 2, 2), (16, 4, 3), (16, 5, 3), (17, 3, 2), (18, 6, 2), (18, 2, 3), (21, 3, 3), (22, 1, 3), (22, 0, 3),
    (24, 6, 3), (24, 5, 4), (26, 4, 4), (28, 2, 4), (29, 0, 4), (29, 1, 4), (29, 6, 4), (29, 3, 4),
)


def attend_back(tokens, gain, shift, kx, mid, q, k, v, o, ag, lx, wq, wk, wv, whg, wrg, wog, sizes):
    squares = (3,) + sizes + wog.shape[5:]
    col = pl.BlockSpec((D, 256), lambda g: (0, g))
    part = pl.BlockSpec((TOK, 256), lambda g: (0, g))
    far = pl.BlockSpec(memory_space=pl.ANY)
    items, rows = sizes[2] * sizes[3], 2 * sizes[1]
    outs = [(D // items, FF // rows), (D // rows, FF // items), (D // items, D // rows)]
    return pl.pallas_call(
        functools.partial(attend_back_kernel, sizes),
        name="attend_back",
        grid=(D // 256,),
        in_specs=[whole((TOK, D)), whole((1, D)), whole((1, D)), whole(kx.shape), whole((TOK, D)),
                  part, part, part, part, part, pl.BlockSpec((4, TOK, 128), lambda g: (g, 0, 0)),
                  col, col, col, far, far, far],
        out_specs=(whole((TOK, D)), whole(squares), whole((8, D)), pl.BlockSpec((8, 256), lambda g: (0, g)))
        + tuple(whole(shape) for shape in outs),
        out_shape=(
            jax.ShapeDtypeStruct((TOK, D), BF),
            jax.ShapeDtypeStruct(squares, BF),
            jax.ShapeDtypeStruct((8, D), F32),
            jax.ShapeDtypeStruct((8, D), F32),
        ) + tuple(jax.ShapeDtypeStruct(shape, F32) for shape in outs),
        scratch_shapes=[
            pltpu.VMEM((D, TOK), BF), pltpu.VMEM((TOK, D), F32),
            pltpu.VMEM((TOK, 256), BF), pltpu.VMEM((TOK, 256), BF),
            pltpu.VMEM((2, TOK, 256), BF), pltpu.VMEM((2, TOK, 256), BF),
            pltpu.VMEM((128, TOK), F32),
            pltpu.VMEM((TOK, 256), BF), pltpu.VMEM((TOK, 256), BF), pltpu.VMEM((TOK, 256), BF),
            pltpu.VMEM((3, D // 256, D, 256), BF),
        ]
        + piece_scratch(sizes, BACK_ORDERS[0:3], whg.shape[5:]) + own_scratch(sizes, 3, whg.shape[5:])
        + piece_scratch(sizes, BACK_ORDERS[3:6], wrg.shape[5:]) + own_scratch(sizes, 3, wrg.shape[5:])
        + piece_scratch(sizes, BACK_ORDERS[6:7], wog.shape[5:]) + own_scratch(sizes, 1, wog.shape[5:]),
        compiler_params=params(collective_id=1, has_side_effects=True),
    )(tokens, gain, shift, kx, mid, q, k, v, o, ag, lx, wq, wk, wv, whg, wrg, wog)


EARLY = 80
FINISH_STEPS = 2 * STEPS + CIN
LAST = FINISH_STEPS - 1
FINISH_ORDERS = (
    (3, 1, 2), (1, 3, 2), (2, 1, 3), (2, 1, 3), (1, 3, 2), (2, 1, 3),
    (1, 2, 3), (2, 1, 3), (2, 1, 3), (2, 3, 1), (3, 1, 2),
)
FINISH_PLAN = (
    (0, 9, 0), (0, 10, 0), (0, 8, 0), (1, 9, 1), (1, 10, 1), (2, 8, 1), (3, 10, 2), (3, 9, 2), (4, 8, 2),
    (5, 11, 0), (5, 0, 0), (6, 1, 0), (6, 10, 3), (6, 0, 1), (7, 2, 0), (7, 11, 1), (7, 1, 1), (8, 3, 0),
    (8, 2, 1), (9, 4, 0), (9, 3, 1), (10, 4, 1), (10, 5, 0), (11, 6, 0), (11, 5, 1), (11, 11, 2), (11, 1, 2),
    (12, 7, 0), (12, 6, 1), (13, 7, 1), (13, 2, 2), (13, 8, 3), (14, 3, 2), (14, 4, 2), (15, 8, 4), (16, 5, 2),
    (16, 6, 2), (16, 10, 4), (17, 11, 3), (17, 3, 3), (17, 9, 3), (18, 7, 2), (18, 4, 3), (18, 2, 3), (19, 1, 3),
    (19, 0, 2), (19, 6, 3), (19, 11, 4), (20, 12, 0), (20, 5, 3), (20, 0, 3), (21, 12, 1), (21, 7, 3), (22, 12, 2),
    (23, 12, 3), (23, 2, 4), (24, 4, 4), (24, 1, 4), (24, 0, 4), (25, 9, 4), (26, 3, 4), (28, 5, 4), (29, 6, 4),
    (29, 7, 4), (29, 12, 4),
)


def finish_kernel(sizes, tg_ref, saved_ref, w_ref, xt_ref, t_ref, sel_ref, sq_ref, early_ref,
                  pw_ref, sq0_ref, sq1_ref, sq2_ref, ig_ref, earlyo_ref, tapso_ref,
                  tgc, tgt, dxa, pg, cw, lines, flat, grads, edge, edge_send, edge_recv, got, send, recv, *comm):
    t = pl.program_id(0)
    nc, nx, ny, nz = sizes
    items, rows = ny * nz, nc * nx
    tokens = tgc.shape[0]
    group = tokens // NP
    count, _, height, width = ig_ref.shape
    nrow = height // PATCH
    pos = place(sizes)
    item, row = lax.axis_index("items"), lax.axis_index("rows")
    final_row = lax.axis_size("rows") - 1
    at = 4 * STEPS + 2
    patch = make_pieces(
        sizes, pos, FINISH_ORDERS[0:STEPS], [grads.at[q % 2] for q in range(STEPS)],
        [grads.at[q % 2, pos[0]] for q in range(STEPS)], comm[0:at],
    )
    keep = comm[at + 14 : at + 16]
    square = make_pieces(
        sizes, pos, FINISH_ORDERS[STEPS : STEPS + 3], [sq_ref.at[n] for n in range(3)],
        [keep[0].at[n] for n in range(3)], comm[at : at + 14],
    )
    loads = [pltpu.make_async_copy(sq_ref.at[n, pos[0]], keep[0].at[n], keep[1].at[n]) for n in range(3)]
    at += 16
    early = SmallSum(sizes, pos, comm[at : at + 4], comm[at + 4], comm[at + 5])
    late = SmallSum(sizes, pos, comm[at + 6 : at + 10], comm[at + 10], comm[at + 11])

    def edge_copy(n):
        step = -1 if n == 0 else 1
        return pltpu.make_async_remote_copy(
            src_ref=edge.at[n], dst_ref=edge.at[2 + n], send_sem=edge_send.at[n], recv_sem=edge_recv.at[n],
            device_id=(item, row + step), device_id_type=MESH,
        )

    share, per = tokens // nx, group // nx
    turns = [turn_of(sizes, pos, xg) * share for xg in range(nx)]

    def spread(j, c):
        return jnp.concatenate(
            [dxa[j, pl.ds(pl.multiple_of(turns[xg] + c * per, per), per), :] for xg in range(nx)], axis=0
        )

    def parcel(k):
        to = lax.rem(row + k, rows)
        return pltpu.make_async_remote_copy(
            src_ref=tg_ref.at[:, to], dst_ref=got.at[row], send_sem=send.at[k - 1], recv_sem=recv.at[row],
            device_id=(item, to), device_id_type=MESH,
        )

    def arrive():
        got[row] = tg_ref[:, row]
        for k in range(1, rows):
            source = lax.rem(row + k, rows)
            pltpu.make_async_remote_copy(
                src_ref=tg_ref.at[:, source], dst_ref=got.at[source], send_sem=send.at[k - 1], recv_sem=recv.at[source],
                device_id=(item, source), device_id_type=MESH,
            ).wait_recv()

    def put_lines(j):
        low = lax.broadcasted_iota(jnp.int32, (group, 2 * HALF), 1) < HALF
        for pair in range(NP // 2):
            a, b = spread(j, 2 * pair), spread(j, 2 * pair + 1)
            cs = slice(pair * 128, (pair + 1) * 128)
            lines[2 * j * group : (2 * j + 1) * group, cs] = jnp.where(low, a, pltpu.roll(b, HALF, 1)).astype(BF)
            lines[(2 * j + 1) * group : (2 * j + 2) * group, cs] = jnp.where(low, pltpu.roll(a, HALF, 1), b).astype(BF)

    def event(index, stage):
        if index < STEPS:
            if stage == 0:
                patch[index].start(0)
            elif stage < 4:
                patch[index].advance(stage)
            else:
                total = unfold_block(patch[index].gather(3), D // rows, FEAT // items)
                for c in range(CH // items):
                    at = c * PATCH * PATCH + index * 2 * PATCH
                    pw_ref[:, at : at + 2 * PATCH] = total[:, c * 2 * PATCH : (c + 1) * 2 * PATCH]
        elif index < STEPS + 3:
            n = index - STEPS
            if stage == 0:
                loads[n].start()
                square[n].start(0)
                return
            if stage == 1:
                loads[n].wait()
            if stage < 4:
                square[n].advance(stage)
            else:
                out = (sq0_ref, sq1_ref, sq2_ref)[n]
                out[...] = unfold_block(square[n].gather(3), *out.shape, odd=pos[0] == 1)
        else:
            part, out = ((early, earlyo_ref), (late, tapso_ref))[index - STEPS - 3]
            if stage < 4:
                part.advance(stage)
            else:
                out[...] = part.gather(3)

    opening, table = [], {}
    for when, index, stage in FINISH_PLAN:
        if stage > 0 or index < STEPS + 3:
            call = functools.partial(event, index, stage)
            if when < 5:
                opening.append(call)
            else:
                table.setdefault((min(when - 5, LAST), 0), []).append(call)

    @pl.when(t == 0)
    def _():
        @pl.when(row == final_row)
        def _():
            edge[2] = jnp.zeros(edge.shape[1:], BF)

        @pl.when(row == 0)
        def _():
            edge[3] = jnp.zeros(edge.shape[1:], BF)

        greet(sizes, pos, True, True)
        for k in range(1, rows):
            parcel(k).start()
        for call in opening:
            call()
        arrive()
        for k in range(D // 128):
            dxa[k] = got[:, :, :, k * 128 : (k + 1) * 128].reshape(tokens, 128).astype(F32)
        total = jnp.zeros((1, D), F32)
        for c in range(NP):
            part = jnp.concatenate([dxa[k, pl.ds(c, group, stride=NP), :] for k in range(D // 128)], axis=1)
            total = total + col_sum(part)
            low = part.astype(BF)
            for xg in range(nx):
                tgc[pl.ds(pl.multiple_of(turns[xg] + c * per, per), per), :] = low[xg * per : (xg + 1) * per]
        for s in range(tokens // 256):
            rs = slice(s * 256, (s + 1) * 256)
            tgt[:, rs] = tgc[rs, :].T
        bias = [total[:, k * 128 : (k + 1) * 128] for k in range(D // 128)]
        early.start(0, jnp.concatenate([early_ref[...]] + bias + [jnp.zeros((2, 128), F32)], axis=0))

    @pl.when(t < STEPS)
    def _():
        for q in range(2, STEPS):
            @pl.when(t == q)
            def _(q=q):
                patch[q - 2].drain((0,))

        feats = FEAT // items
        slot = t % 2
        for n in range(FEAT // 256):
            grad = mm(tgt[...], saved_ref[0, 0, :, n * 256 : (n + 1) * 256]).astype(BF)
            for c in range(256 // feats):
                i = n * (256 // feats) + c
                for r in range(rows):
                    block = grad[r * (D // rows) : (r + 1) * (D // rows), c * feats : (c + 1) * feats]
                    grads[slot, r % 2, r // 2, i % ny, i // ny] = fold_block(block)

    @pl.when((t >= STEPS) & (t < 2 * STEPS))
    def _():
        p = t - STEPS
        weight = w_ref[...].reshape(FEAT, D)

        @pl.when(p == 0)
        def _():
            cw[...] = jnp.zeros_like(cw)
            dxa[0] = jnp.zeros((tokens, 128), F32)

        for s in range(tokens // 256):
            rs = slice(s * 256, (s + 1) * 256)
            for n in range(FEAT // 256):
                cs = slice(n * 256, (n + 1) * 256)
                da = mm_t(tgc[rs, :], weight[cs, :])
                pg[rs, cs] = (saved_ref[0, 0, rs, cs].astype(F32) * da).astype(BF)
            back = mm_t(pg[rs, :], t_ref[...])
            dxa[p, rs, :] += back[:, 0:128]
            dxa[p + 1, rs, :] = back[:, 128:256]
        xt = jnp.concatenate([xt_ref[p], xt_ref[p + 1]], axis=0)
        cw[...] += mm(xt, pg[...])

        @pl.when(p == 0)
        def _():
            put_lines(0)
            for ch in range(CIN):
                head = mm_t(lines[0:group], sel_ref[ch * width : (ch + 1) * width, :])
                edge[0, ch] = (pltpu.roll(head, nrow - 1, 0) if nrow > 1 else head).astype(BF)

            @pl.when(row > 0)
            def _():
                edge_copy(0).start()

        @pl.when(p == STEPS - 1)
        def _():
            put_lines(SLABS - 1)
            for ch in range(CIN):
                tail = mm_t(lines[(WIN - 1) * group : WIN * group], sel_ref[ch * width : (ch + 1) * width, :])
                edge[1, ch] = (pltpu.roll(tail, group - nrow + 1, 0) if nrow > 1 else tail).astype(BF)

            @pl.when(row < final_row)
            def _():
                edge_copy(1).start()

            late.start(0, tap_grad_rows(cw[...]))

    @pl.when(t >= 2 * STEPS)
    def _():
        ch = t - 2 * STEPS

        @pl.when(t == 2 * STEPS)
        def _():
            for j in range(1, SLABS - 1):
                put_lines(j)

            @pl.when(row < final_row)
            def _():
                edge_copy(0).wait_recv()

            @pl.when(row > 0)
            def _():
                edge_copy(1).wait_recv()

        patch_row = lax.broadcasted_iota(jnp.int32, (group, width), 0) % nrow
        res = mm_t(lines[...], sel_ref[pl.ds(pl.multiple_of(ch * width, width), width), :])
        head = res[0:group]
        tail = res[(PATCH + 1) * group : (PATCH + 2) * group]
        for r in range(PATCH):
            v = res[(r + 1) * group : (r + 2) * group]
            if r == 0:
                v = v + jnp.where(patch_row == 0, edge[3, ch].astype(F32), pltpu.roll(tail, 1, 0))
            if r == PATCH - 1:
                v = v + jnp.where(patch_row == nrow - 1, edge[2, ch].astype(F32), pltpu.roll(head, group - 1, 0))
            flat[0, pl.ds(r, group, stride=PATCH), :] = v[:, 0:128]
            flat[1, pl.ds(r, group, stride=PATCH), :] = v[:, 128:256]
        for n in range(count):
            at = slice(n * height, (n + 1) * height)
            ig_ref[n, 0, :, 0:128] = flat[0, at, :]
            ig_ref[n, 0, :, 128:256] = flat[1, at, :]

    def close():
        for part in square:
            part.drain()
        for q, part in enumerate(patch):
            part.drain((1, 2, 3) if q < STEPS - 2 else (0, 1, 2, 3))
        early.drain()
        late.drain()
        for k in range(1, rows):
            parcel(k).wait_send()

        @pl.when(row > 0)
        def _():
            edge_copy(0).wait_send()

        @pl.when(row < final_row)
        def _():
            edge_copy(1).wait_send()

    table.setdefault((LAST, 0), []).append(close)
    run_events(t, table, (0,))


def finish(tg, saved, weight, xt, taps, sel, squares, early, count, height, sizes):
    nc, nx, ny, nz = sizes
    items, rows = ny * nz, nc * nx
    group = count * height // PATCH
    tokens = group * NP
    feats = FEAT // items
    square = squares.shape[5:]

    def clip(v, low, high):
        return jnp.minimum(jnp.maximum(v, low), high)

    return pl.pallas_call(
        functools.partial(finish_kernel, sizes),
        name="finish",
        grid=(FINISH_STEPS,),
        in_specs=[
            whole(tg.shape),
            pl.BlockSpec(
                (1, 1, tokens, FEAT),
                lambda t: (jnp.where(t < 2 * STEPS, t % STEPS, STEPS - 1), jnp.where(t < STEPS, 0, 1), 0, 0),
            ),
            pl.BlockSpec((CH, 1, 2 * PATCH, D), lambda t: (0, clip(t - STEPS, 0, STEPS - 1), 0, 0)),
            whole(xt.shape),
            whole(taps.shape),
            whole(sel.shape),
            pl.BlockSpec(memory_space=pl.ANY),
            whole(early.shape),
        ],
        out_specs=(
            whole((D // rows, PF // items)),
            whole((D // items, D // rows)),
            whole((D // items, D // rows)),
            whole((D // items, D // rows)),
            pl.BlockSpec((count, 1, height, IMG), lambda t: (0, clip(t - 2 * STEPS, 0, CIN - 1), 0, 0)),
            whole((EARLY, 128)),
            whole((32, 128)),
        ),
        out_shape=(
            jax.ShapeDtypeStruct((D // rows, PF // items), F32),
            jax.ShapeDtypeStruct((D // items, D // rows), F32),
            jax.ShapeDtypeStruct((D // items, D // rows), F32),
            jax.ShapeDtypeStruct((D // items, D // rows), F32),
            jax.ShapeDtypeStruct((count, CIN, height, IMG), F32),
            jax.ShapeDtypeStruct((EARLY, 128), F32),
            jax.ShapeDtypeStruct((32, 128), F32),
        ),
        scratch_shapes=[
            pltpu.VMEM((tokens, D), BF),
            pltpu.VMEM((D, tokens), BF),
            pltpu.VMEM((SLABS, tokens, 128), F32),
            pltpu.VMEM((tokens, FEAT), BF),
            pltpu.VMEM((4 * HALF, FEAT), F32),
            pltpu.VMEM((WIN * group, NP * HALF), BF),
            pltpu.VMEM((2, group * PATCH, 128), F32),
            pltpu.VMEM((2,) + sizes + folded_shape(D // rows, feats), BF),
            pltpu.VMEM((4, CIN, group, IMG), BF),
            pltpu.SemaphoreType.DMA((2,)),
            pltpu.SemaphoreType.DMA((2,)),
            pltpu.VMEM((rows, SEQ_ITEMS, tokens // rows // SEQ_ITEMS, D), BF),
            pltpu.SemaphoreType.DMA((rows - 1,)),
            pltpu.SemaphoreType.DMA((rows,)),
        ]
        + piece_scratch(sizes, FINISH_ORDERS[0:STEPS], folded_shape(D // rows, feats))
        + piece_scratch(sizes, FINISH_ORDERS[STEPS : STEPS + 3], square) + own_scratch(sizes, 3, square)
        + small_scratch(sizes, EARLY)
        + small_scratch(sizes, 32),
        compiler_params=params(collective_id=2, has_side_effects=True),
    )(tg, saved, weight, xt, taps, sel, squares, early)


def feature_parts(rows):
    feat = lax.broadcasted_iota(jnp.int32, (rows, FEAT), 1)
    return feat // (2 * PATCH), feat // PATCH % 2, feat % PATCH


def tap_rows(wide, ch, r, b, half):
    parts = []
    for r2 in range(2):
        a = r - r2
        parts.append(wide[9 * ch + 3 * a + b : 9 * ch + 3 * a + b + 1, :] if 0 <= a < 3 else jnp.zeros((1, FEAT), F32))
    return jnp.where(half == 0, parts[0], parts[1])


def tap_matrix(cw_ref, t_ref):
    chan, _, _ = feature_parts(32)
    expand = jnp.where(chan == lax.broadcasted_iota(jnp.int32, (32, FEAT), 0), 1.0, 0.0).astype(BF)
    wide = mm(cw_ref[...], expand)
    _, half, spot = feature_parts(1)
    line = lax.broadcasted_iota(jnp.int32, (HALF, FEAT), 0)
    for r in range(4):
        block = jnp.zeros((HALF, FEAT), F32)
        if r == 0:
            block = jnp.where(line == ONE_LANE, wide[27:28, :], block)
        for ch in range(CIN):
            for b in range(3):
                block = jnp.where(line == WIN * ch + b + spot, tap_rows(wide, ch, r, b, half), block)
        t_ref[r * HALF : (r + 1) * HALF, :] = block.astype(BF)


def tap_grad_rows(full):
    chan, half, spot = feature_parts(1)
    line = lax.broadcasted_iota(jnp.int32, (HALF, FEAT), 0)
    sums = [[None] * 3 for _ in range(9)]
    for r in range(4):
        block = full[r * HALF : (r + 1) * HALF]
        for ch in range(CIN):
            for b in range(3):
                line_sum = jnp.sum(jnp.where(line == WIN * ch + b + spot, block, 0.0), axis=0, keepdims=True)
                for a in range(3):
                    if 0 <= r - a < 2:
                        part = jnp.where(half == r - a, line_sum, 0.0)
                        old = sums[3 * ch + b][a]
                        sums[3 * ch + b][a] = part if old is None else old + part
    lines = [sums[3 * ch + b][a] for ch in range(CIN) for a in range(3) for b in range(3)]
    lines.append(full[ONE_LANE : ONE_LANE + 1])
    lines.append(jnp.zeros((4, FEAT), F32))
    table = jnp.concatenate(lines, axis=0)
    chan, _, _ = feature_parts(128)
    expand = jnp.where(chan == lax.broadcasted_iota(jnp.int32, (128, FEAT), 0), 1.0, 0.0).astype(BF)
    hi, mid, lo = three_terms(table)
    return mm_t(hi, expand) + (mm_t(mid, expand) + mm_t(lo, expand))


def on_device(
    images, item_segment, conv_weight, conv_bias, patch_weight, patch_bias, norm1_gain, norm1_bias,
    query_weight, query_bias, key_weight, value_weight, value_bias, output_weight, output_bias,
    norm2_gain, norm2_bias, hidden_weight, hidden_bias, result_weight, result_bias, cotangent,
):
    items, rows = lax.axis_size("items"), lax.axis_size("rows")
    sizes = grid_sizes(items, rows)
    count, _, height, _ = images.shape
    nrow = height // PATCH

    def vec(v):
        return v.astype(F32).reshape(1, -1)

    segments = lax.dynamic_slice_in_dim(item_segment, lax.axis_index("rows") * SEQ_ITEMS, SEQ_ITEMS)
    lanes = jnp.arange(128)[None, :]
    same = lanes == segments[:, None]
    qx = jnp.where(same, 1.0, 0.0).astype(F32)
    kx = jnp.where((lanes < 4) & ~same, -1e30, 0.0) + jnp.where((lanes >= 4) & (lanes < 7), 1.0, 0.0)
    kx = kx.astype(F32)

    cw = jnp.concatenate([conv_weight.reshape(CH, 27), conv_bias[:, None], jnp.zeros((CH, 4), BF)], axis=1).T
    weight4 = patch_weight.reshape(CH, STEPS, 2 * PATCH, D)
    tokens, saved, xt, sel, taps = stem_forward(images, cw, weight4, vec(patch_bias), sizes)
    tokens = tokens.reshape(TOK, D)
    gain1, shift1 = vec(norm1_gain), vec(norm1_bias)
    q, k, v, attended, lx = attend(
        tokens, gain1, shift1, qx, kx, query_weight, key_weight, value_weight, vec(query_bias), vec(value_bias)
    )
    vecs = jnp.concatenate([vec(output_bias), vec(norm2_gain), vec(norm2_bias), vec(result_bias)], axis=0)
    block_out, middle_grad, attended_grad, wo_grad, wh_grad, wr_grad, sums2, hb_grad = mixer(
        tokens, attended, cotangent, output_weight, vecs, hidden_weight, vec(hidden_bias), result_weight, sizes
    )
    token_grad, squares, sums1, qvs, wh_grad, wr_grad, wo_grad = attend_back(
        tokens, gain1, shift1, kx, middle_grad, q, k, v, attended, attended_grad, lx,
        query_weight, key_weight, value_weight, wh_grad, wr_grad, wo_grad, sizes,
    )
    token_grad = token_grad.reshape(SEQ_ITEMS, rows, nrow * NP, D)
    early = jnp.concatenate([v.reshape(-1, 128) for v in (sums2[0:4], hb_grad, sums1[0:2], qvs[0:2])], axis=0)
    pw_grad, wq_grad, wk_grad, wv_grad, image_grad, sums, tap_grads = finish(
        token_grad, saved, weight4, xt, taps, sel, squares, early, count, height, sizes
    )
    wide = D // 128

    def row_of(at):
        return sums[at * wide : (at + 1) * wide].reshape(D)

    return (
        block_out,
        image_grad,
        tap_grads[0:27, 0:CH].T.reshape(conv_weight.shape),
        tap_grads[27, 0:CH],
        pw_grad.T,
        row_of(12),
        row_of(8),
        row_of(9),
        wq_grad,
        row_of(10),
        wk_grad,
        wv_grad,
        row_of(11),
        wo_grad,
        row_of(2),
        row_of(0),
        row_of(1),
        wh_grad,
        sums[4 * wide : 8 * wide].reshape(FF),
        wr_grad.T,
        row_of(3),
    )


def solution(mesh):
    split = P("items", "rows")
    flat = P(("items", "rows"), None)
    image = P("items", None, "rows", None)
    return jax.shard_map(
        on_device,
        mesh=mesh,
        in_specs=(image, P("items")) + (P(),) * 19 + (flat,),
        out_specs=(
            flat, image, P(), P(), split, P(), P(), P(), split, P(), split, split,
            P(), split, P(), P(), P(), split, P(), split, P(),
        ),
        check_vma=False,
    )
```

```python
import functools

import jax
import jax.numpy as jnp
from jax import lax
from jax.experimental import pallas as pl
from jax.experimental.pallas import tpu as pltpu
from jax.sharding import PartitionSpec as P

BF = jnp.bfloat16
F32 = jnp.float32
D = 768
HEADS = 12
HD = 64
FF = 3072
IMG = 256
PATCH = 16
CH = 32
CIN = 3
SEQ_ITEMS = 4
NPATCH = 256
TOK = 1024
NP = IMG // PATCH
PF = CH * PATCH * PATCH
HALF = 64
WIN = PATCH + 2
ONE_LANE = CIN * WIN
SLABS = (PATCH + 2) // 2
STEPS = PATCH // 2
FEAT = PF // STEPS
GELU_A = 0.7978845608028654
GELU_B = GELU_A * 0.044715
VMEM_CAP = 60 * 1024 * 1024


def mm(left, right):
    return jnp.dot(left, right, preferred_element_type=F32)


def mm_t(left, right):
    return lax.dot_general(left, right, (((1,), (1,)), ((), ())), preferred_element_type=F32)


def params(**extra):
    return pltpu.CompilerParams(vmem_limit_bytes=VMEM_CAP, **extra)


def whole(shape):
    zeros = (0,) * len(shape)
    return pl.BlockSpec(shape, lambda *_: zeros, pipeline_mode=pl.Buffered(1))


def gelu_pair(v):
    square = v * v
    gate = 0.5 + 0.5 * jnp.tanh(v * (GELU_A + GELU_B * square))
    act = v * gate
    slope = gate + act * (1.0 - gate) * (2.0 * GELU_A + (6.0 * GELU_B) * square)
    return act, slope


MESH = pl.DeviceIdType.MESH


def grid_sizes(items, rows):
    nx = rows // 2
    ny = nx if items % nx == 0 else 1
    return (2, nx, ny, items // ny)


def place(sizes):
    item, row = lax.axis_index("items"), lax.axis_index("rows")
    return (row % 2, row // 2, item % sizes[2], item // sizes[2])


def peer(sizes, pos, axis, k):
    moved = list(pos)
    moved[axis] = lax.rem(pos[axis] + k, sizes[axis])
    return (moved[3] * sizes[2] + moved[2], moved[1] * 2 + moved[0]), moved[axis]


def greet(sizes, pos, near, far):
    barrier = pltpu.get_barrier_semaphore()
    item, row, rows = lax.axis_index("items"), lax.axis_index("rows"), 2 * sizes[1]
    peers = [(item, lax.rem(row + k, rows)) for k in range(1, rows)] if near else []
    for axis in (2, 3) if far else ():
        peers += [peer(sizes, pos, axis, k)[0] for k in range(1, sizes[axis])]
    for device in peers:
        pl.semaphore_signal(barrier, inc=1, device_id=device, device_id_type=MESH)
    pl.semaphore_wait(barrier, len(peers))


def turn_of(sizes, pos, x):
    return lax.rem(x + 2 * sizes[1] - 1 - pos[1], sizes[1])


def add_up(first, rest):
    total = first.astype(F32)
    for term in rest:
        total = total + term.astype(F32)
    return total


class Piece:
    def __init__(self, sizes, pos, order, source, own, bufs, send, recv):
        self.sizes, self.pos = sizes, pos
        self.source, self.own, self.bufs = source, own, bufs
        self.send, self.recv = send, recv
        self.axes = (0,) + order

    def at(self, stage, where):
        left = sorted(self.axes[stage:])
        return (slice(None),) * left.index(self.axes[stage]) + (where,)

    def copies(self, stage):
        out = []
        for k in range(1, self.sizes[self.axes[stage]]):
            device, there = peer(self.sizes, self.pos, self.axes[stage], k)
            if stage == 0:
                src, dst = self.source.at[there], self.bufs[0]
            else:
                held = self.at(stage, there)
                src = self.bufs[0].at[held] if stage == 1 else self.bufs[stage - 1].at[(0,) + held]
                dst = self.bufs[stage].at[k - 1]
            out.append(
                pltpu.make_async_remote_copy(
                    src_ref=src, dst_ref=dst, send_sem=self.send.at[stage, k - 1], recv_sem=self.recv.at[stage, k - 1],
                    device_id=device, device_id_type=MESH,
                )
            )
        return out

    def start(self, stage):
        for copy in self.copies(stage):
            copy.start()

    def gather(self, stage):
        for copy in self.copies(stage):
            copy.wait_recv()
        bufs = self.bufs
        if stage == 0:
            bufs[0][...] = bufs[0][...] + self.own[...]
            return None
        held = self.at(stage, self.pos[self.axes[stage]])
        base = bufs[0][held] if stage == 1 else bufs[stage - 1][(0,) + held]
        terms = self.sizes[self.axes[stage]] - 1
        if stage < 3 and terms == 1:
            bufs[stage][0] = base + bufs[stage][0]
            return None
        total = add_up(base, [bufs[stage][k] for k in range(terms)])
        if stage == 3:
            return total
        bufs[stage][0] = total.astype(BF)

    def advance(self, stage):
        self.gather(stage - 1)
        self.start(stage)

    def drain(self, stages=(0, 1, 2, 3)):
        for stage in stages:
            for copy in self.copies(stage):
                copy.wait_send()


def piece_scratch(sizes, orders, shape):
    out = []
    for order in orders:
        out.append(pltpu.VMEM(sizes[1:] + shape, BF))
        for stage in range(3):
            left = tuple(sizes[axis] for axis in sorted(order[stage + 1 :]))
            out.append(pltpu.VMEM((sizes[order[stage]] - 1,) + left + shape, BF))
    sems = pltpu.SemaphoreType.DMA((len(orders), 4, max(sizes) - 1))
    return out + [sems, sems]


def own_scratch(sizes, count, shape):
    return [pltpu.VMEM((count,) + sizes[1:] + shape, BF), pltpu.SemaphoreType.DMA((count,))]


def make_pieces(sizes, pos, orders, sources, owns, refs):
    count = len(orders)
    return [
        Piece(sizes, pos, orders[n], sources[n], owns[n], refs[4 * n : 4 * n + 4], refs[4 * count].at[n], refs[4 * count + 1].at[n])
        for n in range(count)
    ]


class SmallSum:
    def __init__(self, sizes, pos, bufs, send, recv):
        self.sizes, self.pos, self.bufs, self.send, self.recv = sizes, pos, bufs, send, recv

    def copies(self, axis, receive):
        buf, here = self.bufs[axis], self.pos[axis]
        out = []
        for k in range(1, self.sizes[axis]):
            device, _ = peer(self.sizes, self.pos, axis, k)
            slot = lax.rem(here + self.sizes[axis] - k, self.sizes[axis]) if receive else here
            out.append(
                pltpu.make_async_remote_copy(
                    src_ref=buf.at[here], dst_ref=buf.at[slot], send_sem=self.send.at[axis, k - 1],
                    recv_sem=self.recv.at[axis, k - 1], device_id=device, device_id_type=MESH,
                )
            )
        return out

    def start(self, axis, value):
        self.bufs[axis][self.pos[axis]] = value
        for copy in self.copies(axis, False):
            copy.start()

    def gather(self, axis):
        for copy in self.copies(axis, True):
            copy.wait_recv()
        total = self.bufs[axis][0]
        for k in range(1, self.sizes[axis]):
            total = total + self.bufs[axis][k]
        return total

    def advance(self, axis):
        self.start(axis, self.gather(axis - 1))

    def drain(self):
        for axis in range(4):
            for copy in self.copies(axis, False):
                copy.wait_send()


def small_scratch(sizes, height):
    return [pltpu.VMEM((size, height, 128), F32) for size in sizes] + [
        pltpu.SemaphoreType.DMA((4, max(sizes) - 1)),
        pltpu.SemaphoreType.DMA((4, max(sizes) - 1)),
    ]


def folds(width):
    return width % 128 == HALF and width > 128


def narrow(width):
    return 128 // width if width < 128 and 128 % width == 0 else 1


def folded_shape(height, width):
    if folds(width) or narrow(width) > 1:
        return (height * width // 128, 128)
    return (height, width)


def fold_block(block):
    height, width = block.shape
    if narrow(width) > 1:
        part = height // narrow(width)
        return jnp.concatenate([block[k * part : (k + 1) * part] for k in range(narrow(width))], axis=1)
    return block


def unfold_block(block, height, width, odd=False):
    if narrow(width) > 1:
        return jnp.concatenate([block[:, k * width : (k + 1) * width] for k in range(narrow(width))], axis=0)
    if not folds(width):
        return block
    main, side = block[:height], block[height:]
    side = jnp.concatenate([side[:, :HALF], side[:, HALF:]], axis=0)
    return jnp.where(odd, jnp.concatenate([side, main], axis=1), jnp.concatenate([main, side], axis=1))


def run_events(step, table, slots):
    for (when, slot), todo in table.items():
        if slot in slots:
            @pl.when(step == when)
            def _(todo=todo):
                for call in todo:
                    call()


def make_windows(sizes, pos, img_ref, edge, edge_copies, x, xt_ref, sel_ref, pix, lines):
    items, _, height, width = img_ref.shape
    nrow = height // PATCH
    group = items * nrow
    row, final_row = lax.axis_index("rows"), lax.axis_size("rows") - 1
    for ch in range(CIN):
        for item in range(items):
            full = img_ref[item, ch].astype(F32)
            for k in range(width // 128):
                pix[ch, k, item * height : (item + 1) * height, :] = full[:, k * 128 : (k + 1) * 128]

    def line(ch, r):
        return jnp.concatenate([pix[ch, k, pl.ds(r, group, stride=PATCH), :] for k in range(width // 128)], axis=1)

    for ch in range(CIN):
        first, final = line(ch, 0), line(ch, PATCH - 1)
        edge[0, ch] = pltpu.roll(first, nrow - 1, 0).astype(BF)
        edge[1, ch] = pltpu.roll(final, group - nrow + 1, 0).astype(BF)

    @pl.when(row > 0)
    def _():
        edge_copies[0].start()

    @pl.when(row < final_row)
    def _():
        edge_copies[1].start()

    for ch in range(CIN):
        cols = slice(ch * width, (ch + 1) * width)
        for r in range(PATCH):
            lines[(r + 1) * group : (r + 2) * group, cols] = line(ch, r).astype(BF)
    lane = lax.broadcasted_iota(jnp.int32, (1, NP * HALF), 1)
    col, spot = lane // HALF, lane % HALF
    for ch in range(CIN):
        inside = (spot >= WIN * ch) & (spot < WIN * (ch + 1))
        want = jnp.where(inside, PATCH * col + spot - WIN * ch - 1, -5)
        here = lax.broadcasted_iota(jnp.int32, (width, NP * HALF), 0)
        sel_ref[ch * width : (ch + 1) * width, :] = jnp.where(here == want, 1.0, 0.0).astype(BF)

    @pl.when(row < final_row)
    def _():
        edge_copies[0].wait_recv()

    @pl.when(row > 0)
    def _():
        edge_copies[1].wait_recv()

    patch_row = lax.broadcasted_iota(jnp.int32, (group, width), 0) % nrow
    for ch in range(CIN):
        cols = slice(ch * width, (ch + 1) * width)
        up = jnp.where(patch_row == 0, edge[3, ch].astype(F32), pltpu.roll(line(ch, PATCH - 1), 1, 0))
        lines[0:group, cols] = up.astype(BF)
        down = jnp.where(patch_row == nrow - 1, edge[2, ch].astype(F32), pltpu.roll(line(ch, 0), group - 1, 0))
        lines[(PATCH + 1) * group : (PATCH + 2) * group, cols] = down.astype(BF)
    lane = lax.broadcasted_iota(jnp.int32, (group, 2 * HALF), 1)
    low = lane < HALF
    ones = (lane % HALF) == ONE_LANE
    nx = sizes[1]
    share, per = items * nrow * NP // nx, group // nx
    turns = [turn_of(sizes, pos, xg) * share for xg in range(nx)]

    def put(j, c, block):
        low_bits = block.astype(BF)
        for xg in range(nx):
            x[j, pl.ds(pl.multiple_of(turns[xg] + c * per, per), per), :] = low_bits[xg * per : (xg + 1) * per]

    for quarter in range(NP * HALF // 256):
        res = mm(lines[...], sel_ref[:, quarter * 256 : (quarter + 1) * 256])
        for j in range(SLABS):
            first = res[2 * j * group : (2 * j + 1) * group]
            second = res[(2 * j + 1) * group : (2 * j + 2) * group]
            for pair in range(2):
                a = first[:, pair * 128 : (pair + 1) * 128]
                b = second[:, pair * 128 : (pair + 1) * 128]
                put(j, quarter * 4 + pair * 2, jnp.where(ones, 1.0, jnp.where(low, a, pltpu.roll(b, HALF, 1))))
                put(j, quarter * 4 + pair * 2 + 1, jnp.where(ones, 1.0, jnp.where(low, pltpu.roll(a, HALF, 1), b)))
    for j in range(SLABS):
        xt_ref[j] = x[j].T


def stem_kernel(sizes, img_ref, cw_ref, w_ref, pb_ref, tok_ref, saved_ref, xt_ref, sel_ref, t_ref,
                x, pix, lines, edge, edge_send, edge_recv, acc, nat, parcel, got, send, recv):
    t = pl.program_id(0)
    p = t % STEPS
    nx = sizes[1]
    rows = 2 * nx
    pos = place(sizes)
    item, row, final_row = lax.axis_index("items"), lax.axis_index("rows"), lax.axis_size("rows") - 1
    share = acc.shape[0]
    per = share // NP

    def edge_copy(n):
        return pltpu.make_async_remote_copy(
            src_ref=edge.at[n], dst_ref=edge.at[2 + n], send_sem=edge_send.at[n], recv_sem=edge_recv.at[n],
            device_id=(item, row + (2 * n - 1)), device_id_type=MESH,
        )

    @pl.when(t == 0)
    def _():
        @pl.when(row == final_row)
        def _():
            edge[2] = jnp.zeros(edge.shape[1:], BF)

        @pl.when(row == 0)
        def _():
            edge[3] = jnp.zeros(edge.shape[1:], BF)

        greet(sizes, pos, True, False)
        tap_matrix(cw_ref, pb_ref, t_ref)
        make_windows(sizes, pos, img_ref, edge, [edge_copy(0), edge_copy(1)], x, xt_ref, sel_ref, pix, lines)

    @pl.when(p == 0)
    def _():
        acc[...] = jnp.broadcast_to(pb_ref[2:3, :], acc.shape)

    weight = w_ref[...].reshape(FEAT, D)
    for s in range(share // 256):
        rs = slice(s * 256, (s + 1) * 256)
        here = pl.ds(pl.multiple_of(t // STEPS * share + s * 256, 256), 256)
        xs = jnp.concatenate([x[p, here, :], x[p + 1, here, :]], axis=1)
        for n in range(FEAT // 256):
            cs = slice(n * 256, (n + 1) * 256)
            act, slope = gelu_pair(mm(xs, t_ref[:, cs]))
            saved_ref[0, 0, rs, cs] = act.astype(BF)
            saved_ref[0, 1, rs, cs] = slope.astype(BF)
        acc[rs, :] += mm(saved_ref[0, 0, rs, :], weight)

    @pl.when(p == STEPS - 1)
    def _():
        for c in range(NP):
            for k in range(D // 128):
                nat[k, pl.ds(c, per, stride=NP), :] = acc[c * per : (c + 1) * per, k * 128 : (k + 1) * 128]

    def parcel_copy(turn, core, slot):
        to = lax.rem(pos[1] + 1 + turn, nx) * 2 + core
        return pltpu.make_async_remote_copy(
            src_ref=parcel.at[turn, core], dst_ref=got.at[:, row], send_sem=send.at[turn, slot], recv_sem=recv.at[row],
            device_id=(item, to), device_id_type=MESH,
        )

    for turn in range(nx):
        @pl.when(t == turn * STEPS + STEPS - 1)
        def _(turn=turn):
            for k in range(D // 128):
                cut = nat[k].astype(BF).reshape(parcel.shape[1:4] + (128,))
                parcel[turn, :, :, :, k * 128 : (k + 1) * 128] = cut
            if turn < nx - 1:
                for core in range(2):
                    parcel_copy(turn, core, core).start()
            else:
                parcel_copy(turn, 1 - pos[0], 0).start()
                got[:, row] = parcel[turn, pos[0]]

    @pl.when(t == nx * STEPS - 1)
    def _():
        for k in range(1, rows):
            source = lax.rem(row + k, rows)
            pltpu.make_async_remote_copy(
                src_ref=parcel.at[0, 0], dst_ref=got.at[:, source], send_sem=send.at[0, 0], recv_sem=recv.at[source],
                device_id=(item, source), device_id_type=MESH,
            ).wait_recv()
        tok_ref[...] = got[...]
        for turn in range(nx - 1):
            for core in range(2):
                parcel_copy(turn, core, core).wait_send()
        parcel_copy(nx - 1, 1 - pos[0], 0).wait_send()

        @pl.when(row > 0)
        def _():
            edge_copy(0).wait_send()

        @pl.when(row < final_row)
        def _():
            edge_copy(1).wait_send()


def stem_forward(images, cw, weight, bias, sizes):
    count, _, height, width = images.shape
    nx = sizes[1]
    nrow = height // PATCH
    group = count * nrow
    tokens = group * NP
    share = tokens // nx
    arrived = (SEQ_ITEMS, 2 * nx, nrow * NP, D)
    return pl.pallas_call(
        functools.partial(stem_kernel, sizes),
        name="stem_forward",
        grid=(nx * STEPS,),
        in_specs=[
            whole(images.shape),
            whole(cw.shape),
            pl.BlockSpec((CH, 1, 2 * PATCH, D), lambda t: (0, t % STEPS, 0, 0)),
            whole(bias.shape),
        ],
        out_specs=(
            whole(arrived),
            pl.BlockSpec((1, 2, share, FEAT), lambda t: (t % STEPS, 0, t // STEPS, 0)),
            whole((SLABS, 128, tokens)),
            whole((CIN * width, NP * HALF)),
            whole((4 * HALF, FEAT)),
        ),
        out_shape=(
            jax.ShapeDtypeStruct(arrived, BF),
            jax.ShapeDtypeStruct((STEPS, 2, tokens, FEAT), BF),
            jax.ShapeDtypeStruct((SLABS, 128, tokens), BF),
            jax.ShapeDtypeStruct((CIN * width, NP * HALF), BF),
            jax.ShapeDtypeStruct((4 * HALF, FEAT), BF),
        ),
        scratch_shapes=[
            pltpu.VMEM((SLABS, tokens, 128), BF),
            pltpu.VMEM((CIN, width // 128, count * height, 128), F32),
            pltpu.VMEM((WIN * group, CIN * width), BF),
            pltpu.VMEM((4, CIN, group, width), BF),
            pltpu.SemaphoreType.DMA((2,)),
            pltpu.SemaphoreType.DMA((2,)),
            pltpu.VMEM((share, D), F32),
            pltpu.VMEM((D // 128, share, 128), F32),
            pltpu.VMEM((nx, 2, SEQ_ITEMS, nrow * NP, D), BF),
            pltpu.VMEM(arrived, BF),
            pltpu.SemaphoreType.DMA((nx, 2)),
            pltpu.SemaphoreType.DMA((2 * nx,)),
        ],
        compiler_params=params(collective_id=0, has_side_effects=True),
    )(images, cw, weight, bias)


def norm_stats(v):
    centred = v - jnp.mean(v, axis=-1, keepdims=True)
    inv = lax.rsqrt(jnp.mean(centred * centred, axis=-1, keepdims=True) + 1e-06)
    return centred * inv, inv


def three_terms(v):
    hi = v.astype(BF)
    rest = v - hi.astype(F32)
    mid = rest.astype(BF)
    lo = (rest - mid.astype(F32)).astype(BF)
    return hi, mid, lo


def minus_terms(v, lane, base):
    hi, mid, lo = three_terms(-v)
    out = jnp.where(lane == 4, hi.astype(F32), base)
    out = jnp.where(lane == 5, mid.astype(F32), out)
    return jnp.where(lane == 6, lo.astype(F32), out).astype(BF)


def attend_kernel(tok_ref, vec_ref, seg_ref, wq_ref, wk_ref, wv_ref,
                  q_ref, k_ref, v_ref, o_ref, lx_ref, kx_ref, n1, kaug, vaug):
    step = pl.program_id(0)
    line = lax.broadcasted_iota(jnp.int32, (1, 128), 1)
    first_item = lax.axis_index("rows") * SEQ_ITEMS
    same = [line == seg_ref[first_item + i] for i in range(SEQ_ITEMS)]
    terms = jnp.where((line >= 4) & (line < 7), 1.0, 0.0)
    keys_in = [jnp.where((line < 4) & ~one, -1e30, terms) for one in same]

    @pl.when(step == 0)
    def _():
        kx_ref[...] = jnp.concatenate(keys_in + [jnp.zeros((8 - SEQ_ITEMS, 128), F32)], axis=0)
        for s in range(TOK // 128):
            rs = slice(s * 128, (s + 1) * 128)
            hat, _ = norm_stats(tok_ref[rs, :].astype(F32))
            n1[rs, :] = (hat * vec_ref[0:1, :] + vec_ref[1:2, :]).astype(BF)

    own = pl.ds(pl.multiple_of(step * 256, 256), 256)
    q_ref[...] = ((mm(n1[...], wq_ref[...]) + vec_ref[3:4, own]).astype(BF) * 0.125).astype(BF)
    k_ref[...] = mm(n1[...], wk_ref[...]).astype(BF)
    v_ref[...] = (mm(n1[...], wv_ref[...]) + vec_ref[4:5, own]).astype(BF)
    lane = lax.broadcasted_iota(jnp.int32, (NPATCH, 128), 1)
    low = lane < HD
    for i in range(SEQ_ITEMS):
        rs = slice(i * NPATCH, (i + 1) * NPATCH)
        kaug[rs, 128:256] = jnp.broadcast_to(keys_in[i], (NPATCH, 128)).astype(BF)
        vaug[rs, 128:256] = jnp.ones((NPATCH, 128), BF)
    for pair in range(2):
        cs = slice(pair * 128, (pair + 1) * 128)
        kaug[:, 0:128] = k_ref[:, cs]
        vaug[:, 0:128] = v_ref[:, cs]
        for i in range(SEQ_ITEMS):
            rs = slice(i * NPATCH, (i + 1) * NPATCH)
            span = slice(0, (i + 1) * NPATCH)
            qp = q_ref[rs, cs]
            qx = jnp.broadcast_to(jnp.where(same[i], 1.0, 0.0), (NPATCH, 128))
            halves = []
            for h in range(2):
                mine = low if h == 0 else ~low
                qaug = jnp.concatenate([jnp.where(mine, qp, jnp.zeros_like(qp)), qx.astype(BF)], axis=1)
                scores = mm_t(qaug, kaug[span, :])
                top = jnp.max(scores, axis=1, keepdims=True)
                raised = jnp.exp(scores - top).astype(BF)
                out = mm(raised, vaug[span, :])
                total = out[:, 128:256]
                halves.append(out[:, 0:128] / total)
                lx_ref[pair * 2 + h, rs, :] = minus_terms(top + jnp.log(total), lane, qx)
            o_ref[rs, cs] = jnp.where(low, halves[0], halves[1]).astype(BF)


def attend(tokens, vecs, segments, wq, wk, wv):
    col = pl.BlockSpec((D, 256), lambda g: (0, g))
    out = pl.BlockSpec((TOK, 256), lambda g: (0, g))
    return pl.pallas_call(
        attend_kernel,
        name="attend",
        grid=(D // 256,),
        in_specs=[whole((TOK, D)), whole(vecs.shape), pl.BlockSpec(memory_space=pltpu.SMEM), col, col, col],
        out_specs=(out, out, out, out, pl.BlockSpec((4, TOK, 128), lambda g: (g, 0, 0)), whole((8, 128))),
        out_shape=(jax.ShapeDtypeStruct((TOK, D), BF),) * 4
        + (jax.ShapeDtypeStruct((HEADS, TOK, 128), BF), jax.ShapeDtypeStruct((8, 128), F32)),
        scratch_shapes=[pltpu.VMEM((TOK, D), BF), pltpu.VMEM((TOK, 256), BF), pltpu.VMEM((TOK, 256), BF)],
        compiler_params=params(),
    )(tokens, vecs, segments, wq, wk, wv)


def norm_back(e, hat, inv, gain):
    f = e * gain
    return inv * (f - jnp.mean(f, axis=-1, keepdims=True) - hat * jnp.mean(f * hat, axis=-1, keepdims=True))


def col_sum(v):
    return jnp.sum(v, axis=0, keepdims=True)


def store_square(ref, n, grad):
    _, _, nx, ny, nz, _, _ = ref.shape
    height, width = D // (ny * nz), D // (2 * nx)
    if not folds(width):
        for r in range(2 * nx):
            part = grad[:, r * width : (r + 1) * width]
            for i in range(ny * nz):
                ref[n, r % 2, r // 2, i % ny, i // ny] = part[i * height : (i + 1) * height]
        return
    half = height // 2
    low = lax.broadcasted_iota(jnp.int32, (half, 128), 1) < HALF
    for x in range(nx):
        base = 2 * x * width
        shared = grad[:, base + 128 : base + 256]
        turned = jnp.concatenate([shared[:, HALF:], shared[:, :HALF]], axis=1)
        for i in range(ny * nz):
            top, end = i * height, (i + 1) * height
            mid = top + half
            ref[n, 0, x, i % ny, i // ny, 0:height] = grad[top:end, base : base + 128]
            ref[n, 0, x, i % ny, i // ny, height:] = jnp.where(low, shared[top:mid], turned[mid:end])
            ref[n, 1, x, i % ny, i // ny, 0:height] = grad[top:end, base + 256 : base + 384]
            ref[n, 1, x, i % ny, i // ny, height:] = jnp.where(low, turned[top:mid], shared[mid:end])


def mixer_kernel(tok_ref, att_ref, cot_ref, wo_ref, vec_ref, wh_ref, wr_ref,
                 out_ref, mid_ref, ag_ref, wog_ref, whg_ref, wrg_ref, sums_ref, hbg_ref,
                 middle, n2, n2t, cott, acc, back, act, hg):
    step = pl.program_id(0)
    last = pl.num_programs(0) - 1
    chunk = wh_ref.shape[1]
    tile = 2 if chunk % 256 == 0 else 3
    blocks = [slice(s * 256, (s + 1) * 256) for s in range(TOK // 256)]

    @pl.when(step == 0)
    def _():
        for rs in blocks:
            row = tok_ref[rs, :].astype(F32) + mm(att_ref[rs, :], wo_ref[...]) + vec_ref[5:6, :]
            middle[rs, :] = row
            acc[rs, :] = row + vec_ref[8:9, :]
            back[rs, :] = jnp.zeros((256, D), F32)
            hat, _ = norm_stats(row)
            low = (hat * vec_ref[6:7, :] + vec_ref[7:8, :]).astype(BF)
            n2[rs, :] = low
            n2t[:, rs] = low.T
            cott[:, rs] = cot_ref[rs, :].T

    at = step * chunk
    hidden_bias = vec_ref[pl.ds(9 + at // D, 1), pl.ds(pl.multiple_of(at % D, 128), chunk)]
    hsum = jnp.zeros((1, chunk), F32)
    for rs in blocks:
        for n in range(chunk // 128 // tile):
            cs = slice(n * 128 * tile, (n + 1) * 128 * tile)
            pre = mm(n2[rs, :], wh_ref[:, cs]) + hidden_bias[:, cs]
            up = mm_t(cot_ref[rs, :], wr_ref[cs, :])
            a, slope = gelu_pair(pre)
            act[rs, cs] = a.astype(BF)
            hg[rs, cs] = (slope * up).astype(BF)
        acc[rs, :] += mm(act[rs, :], wr_ref[...])
        back[rs, :] += mm_t(hg[rs, :], wh_ref[...])
        hsum = hsum + col_sum(hg[rs, :].astype(F32))
    hbg_ref[...] = hsum
    _, _, nx, ny, nz, height, _ = whg_ref.shape
    for n in range(3):
        width = chunk // 3
        grad = mm(n2t[...], hg[:, n * width : (n + 1) * width]).astype(BF)
        for i in range(ny * nz):
            whg_ref[n, 0, 0, i % ny, i // ny] = grad[i * height : (i + 1) * height]
    _, _, nx, ny, _, _, _ = wrg_ref.shape
    height, width = D // (2 * nx), chunk // ny // 3
    for y in range(ny):
        grad = mm(cott[...], act[:, y * 3 * width : (y + 1) * 3 * width]).astype(BF)
        for n in range(3):
            for r in range(2 * nx):
                part = grad[r * height : (r + 1) * height, n * width : (n + 1) * width]
                wrg_ref[n, r % 2, r // 2, y, 0] = fold_block(part)

    @pl.when(step == last)
    def _():
        gsum = jnp.zeros((1, D), F32)
        bsum = jnp.zeros((1, D), F32)
        osum = jnp.zeros((1, D), F32)
        rsum = jnp.zeros((1, D), F32)
        for rs in blocks:
            out_ref[rs, :] = acc[rs, :].astype(BF)
            hat, inv = norm_stats(middle[rs, :])
            e = back[rs, :]
            gsum = gsum + col_sum(e * hat)
            bsum = bsum + col_sum(e)
            cot = cot_ref[rs, :].astype(F32)
            rsum = rsum + col_sum(cot)
            mid = cot + norm_back(e, hat, inv, vec_ref[6:7, :])
            mid_ref[rs, :] = mid
            low = mid.astype(BF)
            osum = osum + col_sum(low.astype(F32))
            n2[rs, :] = low
            n2t[:, rs] = att_ref[rs, :].T
            ag_ref[rs, :] = mm_t(low, wo_ref[...]).astype(BF)
        store_square(wog_ref, 0, mm(n2t[...], n2[...]).astype(BF))
        sums_ref[0:1, :] = gsum
        sums_ref[1:2, :] = bsum
        sums_ref[2:3, :] = osum
        sums_ref[3:4, :] = rsum


def mixer(tokens, attended, cotangent, wo, vecs, wh, wr, sizes):
    nc, nx, ny, nz = sizes
    rows, items = nc * nx, ny * nz
    chunk = FF // rows
    square = (1,) + sizes + folded_shape(D // items, D // rows)
    return pl.pallas_call(
        mixer_kernel,
        name="mixer",
        grid=(rows,),
        in_specs=[
            whole((TOK, D)), whole((TOK, D)), whole((TOK, D)), whole((D, D)), whole(vecs.shape),
            pl.BlockSpec((D, chunk), lambda r: (0, r)),
            pl.BlockSpec((chunk, D), lambda r: (r, 0)),
        ],
        out_specs=(
            whole((TOK, D)), whole((TOK, D)), whole((TOK, D)), whole(square),
            pl.BlockSpec((3, 1, 1, ny, nz, D // items, chunk // 3), lambda r: (0, r % 2, r // 2, 0, 0, 0, 0)),
            pl.BlockSpec((3, nc, nx, ny, 1) + folded_shape(D // rows, FF // items // 3), lambda r: (0, 0, 0, 0, r, 0, 0)),
            whole((8, D)),
            pl.BlockSpec((1, chunk), lambda r: (0, r)),
        ),
        out_shape=(
            jax.ShapeDtypeStruct((TOK, D), BF),
            jax.ShapeDtypeStruct((TOK, D), F32),
            jax.ShapeDtypeStruct((TOK, D), BF),
            jax.ShapeDtypeStruct(square, BF),
            jax.ShapeDtypeStruct((3,) + sizes + (D // items, chunk // 3), BF),
            jax.ShapeDtypeStruct((3,) + sizes + folded_shape(D // rows, FF // items // 3), BF),
            jax.ShapeDtypeStruct((8, D), F32),
            jax.ShapeDtypeStruct((1, FF), F32),
        ),
        scratch_shapes=[
            pltpu.VMEM((TOK, D), F32), pltpu.VMEM((TOK, D), BF), pltpu.VMEM((D, TOK), BF),
            pltpu.VMEM((D, TOK), BF), pltpu.VMEM((TOK, D), F32), pltpu.VMEM((TOK, D), F32),
            pltpu.VMEM((TOK, chunk), BF), pltpu.VMEM((TOK, chunk), BF),
        ],
        compiler_params=params(),
    )(tokens, attended, cotangent, wo, vecs, wh, wr)


def attend_back_kernel(sizes, tok_ref, vec_ref, kx_ref, mid_ref, q_ref, k_ref, v_ref, o_ref, ag_ref, lx_ref,
                       wq_ref, wk_ref, wv_ref, whg_ref, wrg_ref, wog_ref,
                       tg_ref, sq_ref, sums_ref, qvs_ref, who_ref, wro_ref, woo_ref,
                       n1t, back, kaug, vaug, qaug, oaug, dqt, dq, dk, dv, square, *comm):
    step = pl.program_id(0)
    blocks = [slice(s * 256, (s + 1) * 256) for s in range(TOK // 256)]
    pos = place(sizes)
    groups = ((whg_ref, who_ref), (wrg_ref, wro_ref), (wog_ref, woo_ref))
    pieces, loads, base, at = [], [], 0, 0
    for source, _ in groups:
        count = source.shape[0]
        refs, keep = comm[at : at + 4 * count + 2], comm[at + 4 * count + 2 : at + 4 * count + 4]
        at += 4 * count + 4
        pieces += make_pieces(
            sizes, pos, BACK_ORDERS[base : base + count], [source.at[n] for n in range(count)],
            [keep[0].at[n] for n in range(count)], refs,
        )
        loads += [pltpu.make_async_copy(source.at[n, pos[0]], keep[0].at[n], keep[1].at[n]) for n in range(count)]
        base += count

    def event(index, stage):
        if stage == 0:
            pieces[index].start(0)
            loads[index].start()
        elif stage < 4:
            if stage == 1:
                loads[index].wait()
            pieces[index].advance(stage)
        else:
            total = pieces[index].gather(3)
            if index < 3:
                width = total.shape[1]
                who_ref[:, index * width : (index + 1) * width] = total
            elif index < 6:
                height, width = D // (2 * sizes[1]), FF // (sizes[2] * sizes[3]) // 3
                wro_ref[:, (index - 3) * width : (index - 2) * width] = unfold_block(total, height, width)
            else:
                woo_ref[...] = unfold_block(total, *woo_ref.shape, odd=pos[0] == 1)

    def finish():
        for part in pieces:
            part.drain()

    table = {(0, 0): [functools.partial(greet, sizes, pos, True, True)]}
    for when, index, stage in BACK_PLAN:
        if when < 2:
            key = (0, when)
        elif when < 26:
            key = ((when - 2) // 8, 2 + (when - 2) % 8)
        else:
            key = (2, 10)
        table.setdefault(key, []).append(functools.partial(event, index, stage))
    table.setdefault((2, 10), []).append(finish)
    run_events(step, table, (0,))

    @pl.when(step == 0)
    def _():
        for rs in blocks:
            hat, _ = norm_stats(tok_ref[rs, :].astype(F32))
            n1t[:, rs] = (hat * vec_ref[0:1, :] + vec_ref[1:2, :]).astype(BF).T
            back[rs, :] = jnp.zeros((256, D), F32)

    run_events(step, table, (1,))
    lane = lax.broadcasted_iota(jnp.int32, (NPATCH, 128), 1)
    low = lane < HD
    ones = jnp.where((lane >= 4) & (lane < 7), 1.0, 0.0).astype(BF)
    for i, rs in enumerate(blocks):
        kaug[rs, 128:256] = jnp.broadcast_to(kx_ref[i : i + 1, :], (NPATCH, 128)).astype(BF)
        vaug[rs, 128:256] = ones
    pick_row = lax.broadcasted_iota(jnp.int32, (256, 256), 0) % 128 // HD
    pick_col = lax.broadcasted_iota(jnp.int32, (256, 256), 1) // 128
    pick = jnp.where(pick_row == pick_col, 1.0, 0.0).astype(BF)
    for pair in range(2):
        cs = slice(pair * 128, (pair + 1) * 128)
        kaug[:, 0:128] = k_ref[:, cs]
        vaug[:, 0:128] = v_ref[:, cs]
        kt = k_ref[:, cs].T
        for rs in blocks:
            qp = q_ref[rs, cs]
            gp = ag_ref[rs, cs]
            prod = gp.astype(F32) * o_ref[rs, cs].astype(F32)
            hi = prod.astype(BF)
            both = jnp.concatenate([hi, (prod - hi.astype(F32)).astype(BF)], axis=1)
            dots = mm(both, pick)
            for h in range(2):
                mine = low if h == 0 else ~low
                qaug[h, rs, 0:128] = jnp.where(mine, qp, jnp.zeros_like(qp))
                qaug[h, rs, 128:256] = lx_ref[pair * 2 + h, rs, :]
                oaug[h, rs, 0:128] = jnp.where(mine, gp, jnp.zeros_like(gp))
                oaug[h, rs, 128:256] = minus_terms(dots[:, h * 128 : (h + 1) * 128], lane, jnp.zeros((NPATCH, 128), F32))
        for j, rs in enumerate(blocks):
            span = slice(j * NPATCH, TOK)
            parts_k, parts_v = [], []
            for h in range(2):
                probs = jnp.exp(mm_t(kaug[rs, :], qaug[h, span, :]))
                rise = mm_t(vaug[rs, :], oaug[h, span, :])
                grad = (probs * rise).astype(BF)
                probs_low = probs.astype(BF)
                parts_v.append(mm(probs_low, ag_ref[span, cs]))
                parts_k.append(mm(grad, q_ref[span, cs]))
                hs = slice(h * HD, (h + 1) * HD)
                part = mm(kt[hs, rs], grad)
                if j == 0:
                    dqt[hs, :] = part
                else:
                    dqt[hs, span] += part
            dk[rs, cs] = jnp.where(low, parts_k[0], parts_k[1]).astype(BF)
            dv[rs, cs] = jnp.where(low, parts_v[0], parts_v[1]).astype(BF)
            run_events(step, table, (2 + pair * 4 + j,))
        dq[:, cs] = (dqt[...].T * 0.125).astype(BF)
    qvs_ref[0:1, :] = col_sum(dq[...].astype(F32))
    qvs_ref[1:2, :] = col_sum(dv[...].astype(F32))
    for n, part in enumerate((dq, dk, dv)):
        square[n, step] = mm(n1t[...], part[...]).astype(BF)
    for rs in blocks:
        back[rs, :] += (
            mm_t(dq[rs, :], wq_ref[...]) + mm_t(dk[rs, :], wk_ref[...]) + mm_t(dv[rs, :], wv_ref[...])
        )

    @pl.when(step == pl.num_programs(0) - 1)
    def _():
        gsum = jnp.zeros((1, D), F32)
        bsum = jnp.zeros((1, D), F32)
        for rs in blocks:
            hat, inv = norm_stats(tok_ref[rs, :].astype(F32))
            e = back[rs, :]
            gsum = gsum + col_sum(e * hat)
            bsum = bsum + col_sum(e)
            tg_ref[rs, :] = (mid_ref[rs, :] + norm_back(e, hat, inv, vec_ref[0:1, :])).astype(BF)
        sums_ref[0:1, :] = gsum
        sums_ref[1:2, :] = bsum
        for n in range(3):
            store_square(sq_ref, n, jnp.concatenate([square[n, g] for g in range(D // 256)], axis=1))

    run_events(step, table, (10,))


BACK_ORDERS = (
    (2, 3, 1), (2, 1, 3), (3, 2, 1), (1, 2, 3), (1, 2, 3), (1, 2, 3),
    (1, 2, 3),
)
BACK_PLAN = (
    (0, 1, 0), (0, 5, 0), (0, 2, 0), (0, 3, 0), (0, 4, 0), (0, 0, 0), (0, 6, 0), (2, 1, 1), (2, 5, 1),
    (3, 2, 1), (4, 4, 1), (6, 0, 1), (6, 3, 1), (8, 5, 2), (13, 0, 2), (13, 4, 2), (14, 6, 1), (14, 1, 2),
    (15, 2, 2), (16, 4, 3), (16, 5, 3), (17, 3, 2), (18, 6, 2), (18, 2, 3), (21, 3, 3), (22, 1, 3), (22, 0, 3),
    (24, 6, 3), (24, 5, 4), (26, 4, 4), (28, 2, 4), (29, 0, 4), (29, 1, 4), (29, 6, 4), (29, 3, 4),
)


def attend_back(tokens, vecs, kx, mid, q, k, v, o, ag, lx, wq, wk, wv, whg, wrg, wog, sizes):
    squares = (3,) + sizes + wog.shape[5:]
    col = pl.BlockSpec((D, 256), lambda g: (0, g))
    part = pl.BlockSpec((TOK, 256), lambda g: (0, g))
    far = pl.BlockSpec(memory_space=pl.ANY)
    items, rows = sizes[2] * sizes[3], 2 * sizes[1]
    outs = [(D // items, FF // rows), (D // rows, FF // items), (D // items, D // rows)]
    return pl.pallas_call(
        functools.partial(attend_back_kernel, sizes),
        name="attend_back",
        grid=(D // 256,),
        in_specs=[whole((TOK, D)), whole(vecs.shape), whole(kx.shape), whole((TOK, D)),
                  part, part, part, part, part, pl.BlockSpec((4, TOK, 128), lambda g: (g, 0, 0)),
                  col, col, col, far, far, far],
        out_specs=(whole((TOK, D)), whole(squares), whole((8, D)), pl.BlockSpec((8, 256), lambda g: (0, g)))
        + tuple(whole(shape) for shape in outs),
        out_shape=(
            jax.ShapeDtypeStruct((TOK, D), BF),
            jax.ShapeDtypeStruct(squares, BF),
            jax.ShapeDtypeStruct((8, D), F32),
            jax.ShapeDtypeStruct((8, D), F32),
        ) + tuple(jax.ShapeDtypeStruct(shape, F32) for shape in outs),
        scratch_shapes=[
            pltpu.VMEM((D, TOK), BF), pltpu.VMEM((TOK, D), F32),
            pltpu.VMEM((TOK, 256), BF), pltpu.VMEM((TOK, 256), BF),
            pltpu.VMEM((2, TOK, 256), BF), pltpu.VMEM((2, TOK, 256), BF),
            pltpu.VMEM((128, TOK), F32),
            pltpu.VMEM((TOK, 256), BF), pltpu.VMEM((TOK, 256), BF), pltpu.VMEM((TOK, 256), BF),
            pltpu.VMEM((3, D // 256, D, 256), BF),
        ]
        + piece_scratch(sizes, BACK_ORDERS[0:3], whg.shape[5:]) + own_scratch(sizes, 3, whg.shape[5:])
        + piece_scratch(sizes, BACK_ORDERS[3:6], wrg.shape[5:]) + own_scratch(sizes, 3, wrg.shape[5:])
        + piece_scratch(sizes, BACK_ORDERS[6:7], wog.shape[5:]) + own_scratch(sizes, 1, wog.shape[5:]),
        compiler_params=params(collective_id=1, has_side_effects=True),
    )(tokens, vecs, kx, mid, q, k, v, o, ag, lx, wq, wk, wv, whg, wrg, wog)


EARLY = 80
FINISH_ORDERS = (
    (3, 2, 1), (2, 3, 1), (1, 2, 3), (1, 2, 3), (2, 3, 1), (2, 1, 3),
    (1, 2, 3), (1, 2, 3), (2, 3, 1), (3, 1, 2), (2, 3, 1),
)
FINISH_PLAN = (
    (0, 9, 0), (0, 10, 0), (0, 8, 0), (1, 9, 1), (1, 10, 1), (1, 8, 1), (5, 10, 2), (8, 8, 2), (9, 0, 0),
    (9, 11, 0), (9, 10, 3), (10, 1, 0), (10, 0, 1), (11, 2, 0), (11, 1, 1), (11, 9, 2), (12, 3, 0), (12, 2, 1),
    (13, 4, 0), (13, 4, 1), (13, 11, 1), (13, 3, 1), (14, 5, 0), (14, 1, 2), (14, 11, 2), (15, 5, 1), (15, 6, 0),
    (16, 7, 0), (16, 6, 1), (16, 4, 2), (16, 2, 2), (17, 7, 1), (19, 11, 3), (20, 3, 2), (20, 5, 2), (21, 6, 2),
    (21, 0, 2), (21, 8, 3), (21, 2, 3), (22, 9, 3), (22, 4, 3), (22, 3, 3), (23, 1, 3), (24, 12, 0), (24, 6, 3),
    (24, 7, 2), (25, 5, 3), (25, 2, 4), (26, 12, 1), (26, 12, 2), (26, 7, 3), (26, 12, 3), (26, 0, 3), (26, 5, 4),
    (27, 4, 4), (27, 1, 4), (28, 8, 4), (28, 9, 4), (30, 3, 4), (31, 10, 4), (31, 0, 4), (33, 11, 4), (33, 6, 4),
    (33, 7, 4), (33, 12, 4),
)


def finish_kernel(sizes, tg_ref, act_ref, slope_ref, w_ref, xt_ref, t_ref, sel_ref, sq_ref, sums2_ref, hbg_ref, sums1_ref, qvs_ref,
                  pw_ref, sq0_ref, sq1_ref, sq2_ref, ig_ref, earlyo_ref, tapso_ref,
                  tgc, tgt, dxa, pg, cw, lines, flat, grads, edge, edge_send, edge_recv, got, send, recv, nat, *comm):
    t = pl.program_id(0)
    nc, nx, ny, nz = sizes
    items, rows = ny * nz, nc * nx
    tokens = tgc.shape[0]
    group = tokens // NP
    count, _, height, width = ig_ref.shape
    nrow = height // PATCH
    pos = place(sizes)
    item, row = lax.axis_index("items"), lax.axis_index("rows")
    final_row = lax.axis_size("rows") - 1
    far_steps = STEPS * (nx - 1)
    image_step = 2 * STEPS + far_steps
    final_step = image_step + CIN - 1
    at = 4 * STEPS + 2
    patch = make_pieces(
        sizes, pos, FINISH_ORDERS[0:STEPS], [grads.at[q % 2] for q in range(STEPS)],
        [grads.at[q % 2, pos[0]] for q in range(STEPS)], comm[0:at],
    )
    keep = comm[at + 14 : at + 16]
    square = make_pieces(
        sizes, pos, FINISH_ORDERS[STEPS : STEPS + 3], [sq_ref.at[n] for n in range(3)],
        [keep[0].at[n] for n in range(3)], comm[at : at + 14],
    )
    loads = [pltpu.make_async_copy(sq_ref.at[n, pos[0]], keep[0].at[n], keep[1].at[n]) for n in range(3)]
    at += 16
    early = SmallSum(sizes, pos, comm[at : at + 4], comm[at + 4], comm[at + 5])
    late = SmallSum(sizes, pos, comm[at + 6 : at + 10], comm[at + 10], comm[at + 11])

    def edge_copy(n):
        step = -1 if n == 0 else 1
        return pltpu.make_async_remote_copy(
            src_ref=edge.at[n], dst_ref=edge.at[2 + n], send_sem=edge_send.at[n], recv_sem=edge_recv.at[n],
            device_id=(item, row + step), device_id_type=MESH,
        )

    share, per = tokens // nx, group // nx
    turns = [turn_of(sizes, pos, xg) * share for xg in range(nx)]

    def spread(j, c):
        return jnp.concatenate(
            [dxa[j, pl.ds(pl.multiple_of(turns[xg] + c * per, per), per), :] for xg in range(nx)], axis=0
        )

    def parcel(k):
        to = lax.rem(row + k, rows)
        return pltpu.make_async_remote_copy(
            src_ref=tg_ref.at[:, to], dst_ref=got.at[row], send_sem=send.at[k - 1], recv_sem=recv.at[row],
            device_id=(item, to), device_id_type=MESH,
        )

    def arrived(source):
        pltpu.make_async_remote_copy(
            src_ref=tg_ref.at[:, source], dst_ref=got.at[source], send_sem=send.at[0], recv_sem=recv.at[source],
            device_id=(item, source), device_id_type=MESH,
        ).wait_recv()

    def unpack(xg, turn):
        for k in range(D // 128):
            cut = got[pl.ds(2 * xg, 2), :, :, k * 128 : (k + 1) * 128]
            nat[k] = cut.reshape(share, 128).astype(F32)
        for c in range(NP):
            part = jnp.concatenate([nat[k, pl.ds(c, per, stride=NP), :] for k in range(D // 128)], axis=1)
            tgc[turn * share + c * per : turn * share + (c + 1) * per, :] = part.astype(BF)

    def put_lines(j):
        low = lax.broadcasted_iota(jnp.int32, (group, 2 * HALF), 1) < HALF
        for pair in range(NP // 2):
            a, b = spread(j, 2 * pair), spread(j, 2 * pair + 1)
            cs = slice(pair * 128, (pair + 1) * 128)
            lines[2 * j * group : (2 * j + 1) * group, cs] = jnp.where(low, a, pltpu.roll(b, HALF, 1)).astype(BF)
            lines[(2 * j + 1) * group : (2 * j + 2) * group, cs] = jnp.where(low, pltpu.roll(a, HALF, 1), b).astype(BF)

    def event(index, stage):
        if index < STEPS:
            if stage == 0:
                patch[index].start(0)
            elif stage < 4:
                patch[index].advance(stage)
            else:
                total = unfold_block(patch[index].gather(3), D // rows, FEAT // items)
                for c in range(CH // items):
                    at = c * PATCH * PATCH + index * 2 * PATCH
                    pw_ref[:, at : at + 2 * PATCH] = total[:, c * 2 * PATCH : (c + 1) * 2 * PATCH]
        elif index < STEPS + 3:
            n = index - STEPS
            if stage == 0:
                loads[n].start()
                square[n].start(0)
                return
            if stage == 1:
                loads[n].wait()
            if stage < 4:
                square[n].advance(stage)
            else:
                out = (sq0_ref, sq1_ref, sq2_ref)[n]
                out[...] = unfold_block(square[n].gather(3), *out.shape, odd=pos[0] == 1)
        else:
            part, out = ((early, earlyo_ref), (late, tapso_ref))[index - STEPS - 3]
            if stage < 4:
                part.advance(stage)
            else:
                out[...] = part.gather(3)

    opening, table = [], {}
    for when, index, stage in FINISH_PLAN:
        if stage > 0 or index < STEPS + 3:
            call = functools.partial(event, index, stage)
            if when == 0:
                opening.append(call)
            else:
                later = when - 1 + (far_steps - STEPS if when > 3 * STEPS else 0)
                table.setdefault((min(later, final_step), 0), []).append(call)

    @pl.when(t == 0)
    def _():
        @pl.when(row == final_row)
        def _():
            edge[2] = jnp.zeros(edge.shape[1:], BF)

        @pl.when(row == 0)
        def _():
            edge[3] = jnp.zeros(edge.shape[1:], BF)

        greet(sizes, pos, True, True)
        for k in range(1, rows):
            parcel(k).start()
        for call in opening:
            call()
        got[row] = tg_ref[:, row]
        arrived(2 * pos[1] + 1 - pos[0])
        unpack(pos[1], nx - 1)
        cw[...] = jnp.zeros_like(cw)

    @pl.when(t == STEPS)
    def _():
        for turn in range(nx - 1):
            xg = lax.rem(pos[1] + 1 + turn, nx)
            arrived(2 * xg)
            arrived(2 * xg + 1)
            unpack(xg, turn)
        total = jnp.zeros((1, D), F32)
        for s in range(tokens // 256):
            rs = slice(s * 256, (s + 1) * 256)
            total = total + col_sum(tgc[rs, :].astype(F32))
            tgt[:, rs] = tgc[rs, :].T
        lines_in = [sums2_ref[0:1], sums2_ref[1:2], sums2_ref[2:3], sums2_ref[3:4]]
        lines_in += [hbg_ref[:, n * D : (n + 1) * D] for n in range(FF // D)]
        lines_in += [sums1_ref[0:1], sums1_ref[1:2], qvs_ref[0:1], qvs_ref[1:2], total]
        cells = [one[:, k * 128 : (k + 1) * 128] for one in lines_in for k in range(D // 128)]
        early.start(0, jnp.concatenate(cells + [jnp.zeros((EARLY - len(cells), 128), F32)], axis=0))

    @pl.when((t >= STEPS) & (t < 2 * STEPS))
    def _():
        for q in range(2, STEPS):
            @pl.when(t == STEPS + q)
            def _(q=q):
                patch[q - 2].drain((0,))

        feats = FEAT // items
        slot = t % 2
        for n in range(FEAT // 256):
            grad = mm(tgt[...], act_ref[0, 0, :, n * 256 : (n + 1) * 256]).astype(BF)
            for c in range(256 // feats):
                i = n * (256 // feats) + c
                for r in range(rows):
                    block = grad[r * (D // rows) : (r + 1) * (D // rows), c * feats : (c + 1) * feats]
                    grads[slot, r % 2, r // 2, i % ny, i // ny] = fold_block(block)

    def stem_part(p, turn):
        weight = w_ref[...].reshape(FEAT, D)

        def at(s, size):
            return pl.ds(pl.multiple_of(turn * share + s * 256, 256), size)

        @pl.when(p == 0)
        def _():
            dxa[0, at(0, share), :] = jnp.zeros((share, 128), F32)

        for s in range(share // 256):
            rs = slice(s * 256, (s + 1) * 256)
            for n in range(FEAT // 256):
                cs = slice(n * 256, (n + 1) * 256)
                da = mm_t(tgc[at(s, 256), :], weight[cs, :])
                pg[rs, cs] = (slope_ref[0, 0, rs, cs].astype(F32) * da).astype(BF)
            back = mm_t(pg[rs, :], t_ref[...])
            dxa[p, at(s, 256), :] += back[:, 0:128]
            dxa[p + 1, at(s, 256), :] = back[:, 128:256]
        xt = jnp.concatenate([xt_ref[p, :, at(0, share)], xt_ref[p + 1, :, at(0, share)]], axis=0)
        cw[...] += mm(xt, pg[...])

    near, far = t < STEPS, (t >= 2 * STEPS) & (t < image_step)

    @pl.when(near | far)
    def _():
        stem_part(t % STEPS, jnp.where(near, nx - 1, t // STEPS - 2))

    @pl.when((t >= image_step - STEPS) & (t < image_step))
    def _():
        p = t % STEPS

        @pl.when(p == 0)
        def _():
            put_lines(0)
            for ch in range(CIN):
                head = mm_t(lines[0:group], sel_ref[ch * width : (ch + 1) * width, :])
                edge[0, ch] = (pltpu.roll(head, nrow - 1, 0) if nrow > 1 else head).astype(BF)

            @pl.when(row > 0)
            def _():
                edge_copy(0).start()

        @pl.when(p == STEPS - 1)
        def _():
            put_lines(SLABS - 1)
            for ch in range(CIN):
                tail = mm_t(lines[(WIN - 1) * group : WIN * group], sel_ref[ch * width : (ch + 1) * width, :])
                edge[1, ch] = (pltpu.roll(tail, group - nrow + 1, 0) if nrow > 1 else tail).astype(BF)

            @pl.when(row < final_row)
            def _():
                edge_copy(1).start()

            late.start(0, tap_grad_rows(cw[...]))

    @pl.when(t >= image_step)
    def _():
        ch = t - image_step

        @pl.when(t == image_step)
        def _():
            for j in range(1, SLABS - 1):
                put_lines(j)

            @pl.when(row < final_row)
            def _():
                edge_copy(0).wait_recv()

            @pl.when(row > 0)
            def _():
                edge_copy(1).wait_recv()

        patch_row = lax.broadcasted_iota(jnp.int32, (group, width), 0) % nrow
        res = mm_t(lines[...], sel_ref[pl.ds(pl.multiple_of(ch * width, width), width), :])
        head = res[0:group]
        tail = res[(PATCH + 1) * group : (PATCH + 2) * group]
        for r in range(PATCH):
            v = res[(r + 1) * group : (r + 2) * group]
            if r == 0:
                v = v + jnp.where(patch_row == 0, edge[3, ch].astype(F32), pltpu.roll(tail, 1, 0))
            if r == PATCH - 1:
                v = v + jnp.where(patch_row == nrow - 1, edge[2, ch].astype(F32), pltpu.roll(head, group - 1, 0))
            flat[0, pl.ds(r, group, stride=PATCH), :] = v[:, 0:128]
            flat[1, pl.ds(r, group, stride=PATCH), :] = v[:, 128:256]
        for n in range(count):
            at = slice(n * height, (n + 1) * height)
            ig_ref[n, 0, :, 0:128] = flat[0, at, :]
            ig_ref[n, 0, :, 128:256] = flat[1, at, :]

    def close():
        for part in square:
            part.drain()
        for q, part in enumerate(patch):
            part.drain((1, 2, 3) if q < STEPS - 2 else (0, 1, 2, 3))
        early.drain()
        late.drain()
        for k in range(1, rows):
            parcel(k).wait_send()

        @pl.when(row > 0)
        def _():
            edge_copy(0).wait_send()

        @pl.when(row < final_row)
        def _():
            edge_copy(1).wait_send()

    table.setdefault((final_step, 0), []).append(close)
    run_events(t, table, (0,))


def finish(tg, saved, weight, xt, taps, sel, squares, sums2, hbg, sums1, qvs, count, height, sizes):
    nc, nx, ny, nz = sizes
    items, rows = ny * nz, nc * nx
    group = count * height // PATCH
    tokens = group * NP
    feats = FEAT // items
    square = squares.shape[5:]
    share = tokens // nx
    image_step = STEPS * (nx + 1)

    def clip(v, low, high):
        return jnp.minimum(jnp.maximum(v, low), high)

    def sub(t):
        held = jnp.where(t < STEPS, t, jnp.where(t < 2 * STEPS, 0, t % STEPS))
        return jnp.where(t < image_step, held, STEPS - 1)

    def turn(t):
        return jnp.where(t < STEPS, nx - 1, clip(t // STEPS - 2, 0, nx - 2))

    return pl.pallas_call(
        functools.partial(finish_kernel, sizes),
        name="finish",
        grid=(image_step + CIN,),
        in_specs=[
            whole(tg.shape),
            pl.BlockSpec((1, 1, tokens, FEAT), lambda t: (clip(t - STEPS, 0, STEPS - 1), 0, 0, 0)),
            pl.BlockSpec((1, 1, share, FEAT), lambda t: (sub(t), 1, turn(t), 0)),
            pl.BlockSpec((CH, 1, 2 * PATCH, D), lambda t: (0, sub(t), 0, 0)),
            whole(xt.shape),
            whole(taps.shape),
            whole(sel.shape),
            pl.BlockSpec(memory_space=pl.ANY),
            whole(sums2.shape), whole(hbg.shape), whole(sums1.shape), whole(qvs.shape),
        ],
        out_specs=(
            whole((D // rows, PF // items)),
            whole((D // items, D // rows)),
            whole((D // items, D // rows)),
            whole((D // items, D // rows)),
            pl.BlockSpec((count, 1, height, IMG), lambda t: (0, clip(t - image_step, 0, CIN - 1), 0, 0)),
            whole((EARLY, 128)),
            whole((32, 128)),
        ),
        out_shape=(
            jax.ShapeDtypeStruct((D // rows, PF // items), F32),
            jax.ShapeDtypeStruct((D // items, D // rows), F32),
            jax.ShapeDtypeStruct((D // items, D // rows), F32),
            jax.ShapeDtypeStruct((D // items, D // rows), F32),
            jax.ShapeDtypeStruct((count, CIN, height, IMG), F32),
            jax.ShapeDtypeStruct((EARLY, 128), F32),
            jax.ShapeDtypeStruct((32, 128), F32),
        ),
        scratch_shapes=[
            pltpu.VMEM((tokens, D), BF),
            pltpu.VMEM((D, tokens), BF),
            pltpu.VMEM((SLABS, tokens, 128), F32),
            pltpu.VMEM((share, FEAT), BF),
            pltpu.VMEM((4 * HALF, FEAT), F32),
            pltpu.VMEM((WIN * group, NP * HALF), BF),
            pltpu.VMEM((2, group * PATCH, 128), F32),
            pltpu.VMEM((2,) + sizes + folded_shape(D // rows, feats), BF),
            pltpu.VMEM((4, CIN, group, IMG), BF),
            pltpu.SemaphoreType.DMA((2,)),
            pltpu.SemaphoreType.DMA((2,)),
            pltpu.VMEM((rows, SEQ_ITEMS, tokens // rows // SEQ_ITEMS, D), BF),
            pltpu.SemaphoreType.DMA((rows - 1,)),
            pltpu.SemaphoreType.DMA((rows,)),
            pltpu.VMEM((D // 128, share, 128), F32),
        ]
        + piece_scratch(sizes, FINISH_ORDERS[0:STEPS], folded_shape(D // rows, feats))
        + piece_scratch(sizes, FINISH_ORDERS[STEPS : STEPS + 3], square) + own_scratch(sizes, 3, square)
        + small_scratch(sizes, EARLY)
        + small_scratch(sizes, 32),
        compiler_params=params(collective_id=2, has_side_effects=True),
    )(tg, saved, saved, weight, xt, taps, sel, squares, sums2, hbg, sums1, qvs)


def feature_parts(rows):
    feat = lax.broadcasted_iota(jnp.int32, (rows, FEAT), 1)
    return feat // (2 * PATCH), feat // PATCH % 2, feat % PATCH


def tap_rows(wide, ch, r, b, half):
    parts = []
    for r2 in range(2):
        a = r - r2
        parts.append(wide[9 * ch + 3 * a + b : 9 * ch + 3 * a + b + 1, :] if 0 <= a < 3 else jnp.zeros((1, FEAT), F32))
    return jnp.where(half == 0, parts[0], parts[1])


def tap_matrix(cw_ref, vec_ref, t_ref):
    chan, _, _ = feature_parts(32)
    expand = jnp.where(chan == lax.broadcasted_iota(jnp.int32, (32, FEAT), 0), 1.0, 0.0).astype(BF)
    wide = lax.dot_general(cw_ref[...], expand, (((0,), (0,)), ((), ())), preferred_element_type=F32)
    bias = mm(jnp.broadcast_to(vec_ref[13:14, 0:CH], (8, CH)).astype(BF), expand)
    _, half, spot = feature_parts(1)
    line = lax.broadcasted_iota(jnp.int32, (HALF, FEAT), 0)
    for r in range(4):
        block = jnp.zeros((HALF, FEAT), F32)
        if r == 0:
            block = jnp.where(line == ONE_LANE, bias[0:1, :], block)
        for ch in range(CIN):
            for b in range(3):
                block = jnp.where(line == WIN * ch + b + spot, tap_rows(wide, ch, r, b, half), block)
        t_ref[r * HALF : (r + 1) * HALF, :] = block.astype(BF)


def tap_grad_rows(full):
    chan, half, spot = feature_parts(1)
    line = lax.broadcasted_iota(jnp.int32, (HALF, FEAT), 0)
    sums = [[None] * 3 for _ in range(9)]
    for r in range(4):
        block = full[r * HALF : (r + 1) * HALF]
        for ch in range(CIN):
            for b in range(3):
                line_sum = jnp.sum(jnp.where(line == WIN * ch + b + spot, block, 0.0), axis=0, keepdims=True)
                for a in range(3):
                    if 0 <= r - a < 2:
                        part = jnp.where(half == r - a, line_sum, 0.0)
                        old = sums[3 * ch + b][a]
                        sums[3 * ch + b][a] = part if old is None else old + part
    lines = [sums[3 * ch + b][a] for ch in range(CIN) for a in range(3) for b in range(3)]
    lines.append(full[ONE_LANE : ONE_LANE + 1])
    lines.append(jnp.zeros((4, FEAT), F32))
    table = jnp.concatenate(lines, axis=0)
    chan, _, _ = feature_parts(128)
    expand = jnp.where(chan == lax.broadcasted_iota(jnp.int32, (128, FEAT), 0), 1.0, 0.0).astype(BF)
    hi, mid, lo = three_terms(table)
    return mm_t(hi, expand) + (mm_t(mid, expand) + mm_t(lo, expand))


def on_device(
    images, item_segment, conv_weight, conv_bias, patch_weight, patch_bias, norm1_gain, norm1_bias,
    query_weight, query_bias, key_weight, value_weight, value_bias, output_weight, output_bias,
    norm2_gain, norm2_bias, hidden_weight, hidden_bias, result_weight, result_bias, cotangent,
):
    items, rows = lax.axis_size("items"), lax.axis_size("rows")
    sizes = grid_sizes(items, rows)
    count, _, height, _ = images.shape
    nrow = height // PATCH

    lines = (norm1_gain, norm1_bias, patch_bias, query_bias, value_bias, output_bias, norm2_gain, norm2_bias, result_bias)
    lines += (hidden_bias, conv_bias, jnp.zeros((D - CH,), BF))
    vecs = jnp.concatenate(lines).astype(F32).reshape(-1, D)
    cw = conv_weight.reshape(CH, 27)
    weight4 = patch_weight.reshape(CH, STEPS, 2 * PATCH, D)
    tokens, saved, xt, sel, taps = stem_forward(images, cw, weight4, vecs, sizes)
    tokens = tokens.reshape(TOK, D)
    q, k, v, attended, lx, kx = attend(tokens, vecs, item_segment, query_weight, key_weight, value_weight)
    block_out, middle_grad, attended_grad, wo_grad, wh_grad, wr_grad, sums2, hb_grad = mixer(
        tokens, attended, cotangent, output_weight, vecs, hidden_weight, result_weight, sizes
    )
    token_grad, squares, sums1, qvs, wh_grad, wr_grad, wo_grad = attend_back(
        tokens, vecs, kx, middle_grad, q, k, v, attended, attended_grad, lx,
        query_weight, key_weight, value_weight, wh_grad, wr_grad, wo_grad, sizes,
    )
    token_grad = token_grad.reshape(SEQ_ITEMS, rows, nrow * NP, D)
    pw_grad, wq_grad, wk_grad, wv_grad, image_grad, sums, tap_grads = finish(
        token_grad, saved, weight4, xt, taps, sel, squares, sums2, hb_grad, sums1, qvs, count, height, sizes
    )
    wide = D // 128

    def row_of(at):
        return sums[at * wide : (at + 1) * wide].reshape(D)

    return (
        block_out,
        image_grad,
        tap_grads[0:27, 0:CH].T.reshape(conv_weight.shape),
        tap_grads[27, 0:CH],
        pw_grad.T,
        row_of(12),
        row_of(8),
        row_of(9),
        wq_grad,
        row_of(10),
        wk_grad,
        wv_grad,
        row_of(11),
        wo_grad,
        row_of(2),
        row_of(0),
        row_of(1),
        wh_grad,
        sums[4 * wide : 8 * wide].reshape(FF),
        wr_grad.T,
        row_of(3),
    )


def solution(mesh):
    split = P("items", "rows")
    flat = P(("items", "rows"), None)
    image = P("items", None, "rows", None)
    return jax.shard_map(
        on_device,
        mesh=mesh,
        in_specs=(image, P("items")) + (P(),) * 19 + (flat,),
        out_specs=(
            flat, image, P(), P(), split, P(), P(), P(), split, P(), split, split,
            P(), split, P(), P(), P(), split, P(), split, P(),
        ),
        check_vma=False,
    )
```

```python
import functools

import jax
import jax.numpy as jnp
from jax import lax
from jax.experimental import pallas as pl
from jax.experimental.pallas import tpu as pltpu
from jax.sharding import PartitionSpec as P

BF = jnp.bfloat16
F32 = jnp.float32
D = 768
HEADS = 12
HD = 64
FF = 3072
IMG = 256
PATCH = 16
CH = 32
CIN = 3
SEQ_ITEMS = 4
NPATCH = 256
TOK = 1024
NP = IMG // PATCH
PF = CH * PATCH * PATCH
HALF = 64
WIN = PATCH + 2
ONE_LANE = CIN * WIN
SLABS = (PATCH + 2) // 2
STEPS = PATCH // 2
FEAT = PF // STEPS
GELU_A = 0.7978845608028654
GELU_B = GELU_A * 0.044715
VMEM_CAP = 60 * 1024 * 1024


def mm(left, right):
    return jnp.dot(left, right, preferred_element_type=F32)


def mm_t(left, right):
    return lax.dot_general(left, right, (((1,), (1,)), ((), ())), preferred_element_type=F32)


def params(**extra):
    return pltpu.CompilerParams(vmem_limit_bytes=VMEM_CAP, **extra)


def whole(shape):
    zeros = (0,) * len(shape)
    return pl.BlockSpec(shape, lambda *_: zeros, pipeline_mode=pl.Buffered(1))


def gelu_pair_low(v):
    bend = jnp.tanh((v * (GELU_A + GELU_B * (v * v))).astype(BF))
    low = v.astype(BF)
    gate = bend * BF(0.5) + BF(0.5)
    act = low * gate
    slope = gate + act * (BF(1.0) - gate) * (BF(2.0 * GELU_A) + BF(6.0 * GELU_B) * (low * low))
    return act, slope


def as_row(ref, at=None):
    line = ref[...] if at is None else ref[at]
    return line.astype(F32).reshape(1, line.shape[0])


def gelu_pair(v):
    square = v * v
    gate = 0.5 + 0.5 * jnp.tanh(v * (GELU_A + GELU_B * square))
    act = v * gate
    slope = gate + act * (1.0 - gate) * (2.0 * GELU_A + (6.0 * GELU_B) * square)
    return act, slope


MESH = pl.DeviceIdType.MESH


def grid_sizes(items, rows):
    nx = rows // 2
    ny = nx if items % nx == 0 else 1
    return (2, nx, ny, items // ny)


def place(sizes):
    item, row = lax.axis_index("items"), lax.axis_index("rows")
    return (row % 2, row // 2, item % sizes[2], item // sizes[2])


def peer(sizes, pos, axis, k):
    moved = list(pos)
    moved[axis] = lax.rem(pos[axis] + k, sizes[axis])
    return (moved[3] * sizes[2] + moved[2], moved[1] * 2 + moved[0]), moved[axis]


def greet(sizes, pos, near, far):
    barrier = pltpu.get_barrier_semaphore()
    item, row, rows = lax.axis_index("items"), lax.axis_index("rows"), 2 * sizes[1]
    peers = [(item, lax.rem(row + k, rows)) for k in range(1, rows)] if near else []
    for axis in (2, 3) if far else ():
        peers += [peer(sizes, pos, axis, k)[0] for k in range(1, sizes[axis])]
    for device in peers:
        pl.semaphore_signal(barrier, inc=1, device_id=device, device_id_type=MESH)
    pl.semaphore_wait(barrier, len(peers))


def turn_of(sizes, pos, x):
    return lax.rem(x + 2 * sizes[1] - 1 - pos[1], sizes[1])


def add_up(first, rest):
    total = first.astype(F32)
    for term in rest:
        total = total + term.astype(F32)
    return total


class Piece:
    def __init__(self, sizes, pos, order, source, own, bufs, send, recv):
        self.sizes, self.pos = sizes, pos
        self.source, self.own, self.bufs = source, own, bufs
        self.send, self.recv = send, recv
        self.axes = (0,) + order

    def at(self, stage, where):
        left = sorted(self.axes[stage:])
        return (slice(None),) * left.index(self.axes[stage]) + (where,)

    def copies(self, stage):
        out = []
        for k in range(1, self.sizes[self.axes[stage]]):
            device, there = peer(self.sizes, self.pos, self.axes[stage], k)
            if stage == 0:
                src, dst = self.source.at[there], self.bufs[0]
            else:
                held = self.at(stage, there)
                src = self.bufs[0].at[held] if stage == 1 else self.bufs[stage - 1].at[(0,) + held]
                dst = self.bufs[stage].at[k - 1]
            out.append(
                pltpu.make_async_remote_copy(
                    src_ref=src, dst_ref=dst, send_sem=self.send.at[stage, k - 1], recv_sem=self.recv.at[stage, k - 1],
                    device_id=device, device_id_type=MESH,
                )
            )
        return out

    def start(self, stage):
        for copy in self.copies(stage):
            copy.start()

    def gather(self, stage):
        for copy in self.copies(stage):
            copy.wait_recv()
        bufs = self.bufs
        if stage == 0:
            bufs[0][...] = bufs[0][...] + self.own[...]
            return None
        held = self.at(stage, self.pos[self.axes[stage]])
        base = bufs[0][held] if stage == 1 else bufs[stage - 1][(0,) + held]
        terms = self.sizes[self.axes[stage]] - 1
        if stage < 3 and terms == 1:
            bufs[stage][0] = base + bufs[stage][0]
            return None
        total = add_up(base, [bufs[stage][k] for k in range(terms)])
        if stage == 3:
            return total
        bufs[stage][0] = total.astype(BF)

    def advance(self, stage):
        self.gather(stage - 1)
        self.start(stage)

    def drain(self, stages=(0, 1, 2, 3)):
        for stage in stages:
            for copy in self.copies(stage):
                copy.wait_send()


def piece_scratch(sizes, orders, shape):
    out = []
    for order in orders:
        out.append(pltpu.VMEM(sizes[1:] + shape, BF))
        for stage in range(3):
            left = tuple(sizes[axis] for axis in sorted(order[stage + 1 :]))
            out.append(pltpu.VMEM((sizes[order[stage]] - 1,) + left + shape, BF))
    sems = pltpu.SemaphoreType.DMA((len(orders), 4, max(sizes) - 1))
    return out + [sems, sems]


def own_scratch(sizes, count, shape):
    return [pltpu.VMEM((count,) + sizes[1:] + shape, BF), pltpu.SemaphoreType.DMA((count,))]


def make_pieces(sizes, pos, orders, sources, owns, refs):
    count = len(orders)
    return [
        Piece(sizes, pos, orders[n], sources[n], owns[n], refs[4 * n : 4 * n + 4], refs[4 * count].at[n], refs[4 * count + 1].at[n])
        for n in range(count)
    ]


class SmallSum:
    def __init__(self, sizes, pos, bufs, send, recv):
        self.sizes, self.pos, self.bufs, self.send, self.recv = sizes, pos, bufs, send, recv

    def copies(self, axis, receive):
        buf, here = self.bufs[axis], self.pos[axis]
        out = []
        for k in range(1, self.sizes[axis]):
            device, _ = peer(self.sizes, self.pos, axis, k)
            slot = lax.rem(here + self.sizes[axis] - k, self.sizes[axis]) if receive else here
            out.append(
                pltpu.make_async_remote_copy(
                    src_ref=buf.at[here], dst_ref=buf.at[slot], send_sem=self.send.at[axis, k - 1],
                    recv_sem=self.recv.at[axis, k - 1], device_id=device, device_id_type=MESH,
                )
            )
        return out

    def start(self, axis, value):
        self.bufs[axis][self.pos[axis]] = value
        for copy in self.copies(axis, False):
            copy.start()

    def gather(self, axis):
        for copy in self.copies(axis, True):
            copy.wait_recv()
        total = self.bufs[axis][0]
        for k in range(1, self.sizes[axis]):
            total = total + self.bufs[axis][k]
        return total

    def advance(self, axis):
        self.start(axis, self.gather(axis - 1))

    def drain(self):
        for axis in range(4):
            for copy in self.copies(axis, False):
                copy.wait_send()


def small_scratch(sizes, height):
    return [pltpu.VMEM((size, height, 128), F32) for size in sizes] + [
        pltpu.SemaphoreType.DMA((4, max(sizes) - 1)),
        pltpu.SemaphoreType.DMA((4, max(sizes) - 1)),
    ]


def folds(width):
    return width % 128 == HALF and width > 128


def narrow(width):
    return 128 // width if width < 128 and 128 % width == 0 else 1


def folded_shape(height, width):
    if folds(width) or narrow(width) > 1:
        return (height * width // 128, 128)
    return (height, width)


def fold_block(block):
    height, width = block.shape
    if narrow(width) > 1:
        part = height // narrow(width)
        return jnp.concatenate([block[k * part : (k + 1) * part] for k in range(narrow(width))], axis=1)
    return block


def unfold_block(block, height, width, odd=False):
    if narrow(width) > 1:
        return jnp.concatenate([block[:, k * width : (k + 1) * width] for k in range(narrow(width))], axis=0)
    if not folds(width):
        return block
    main, side = block[:height], block[height:]
    side = jnp.concatenate([side[:, :HALF], side[:, HALF:]], axis=0)
    return jnp.where(odd, jnp.concatenate([side, main], axis=1), jnp.concatenate([main, side], axis=1))


def run_events(step, table, slots):
    for (when, slot), todo in table.items():
        if slot in slots:
            @pl.when(step == when)
            def _(todo=todo):
                for call in todo:
                    call()


def make_windows(sizes, pos, img_ref, edge, edge_copies, x, xt_ref, sel_ref, pix, lines):
    items, _, height, width = img_ref.shape
    nrow = height // PATCH
    group = items * nrow
    row, final_row = lax.axis_index("rows"), lax.axis_size("rows") - 1
    for ch in range(CIN):
        for item in range(items):
            full = img_ref[item, ch].astype(F32)
            for k in range(width // 128):
                pix[ch, k, item * height : (item + 1) * height, :] = full[:, k * 128 : (k + 1) * 128]

    def line(ch, r):
        return jnp.concatenate([pix[ch, k, pl.ds(r, group, stride=PATCH), :] for k in range(width // 128)], axis=1)

    for ch in range(CIN):
        first, final = line(ch, 0), line(ch, PATCH - 1)
        edge[0, ch] = pltpu.roll(first, nrow - 1, 0).astype(BF)
        edge[1, ch] = pltpu.roll(final, group - nrow + 1, 0).astype(BF)

    @pl.when(row > 0)
    def _():
        edge_copies[0].start()

    @pl.when(row < final_row)
    def _():
        edge_copies[1].start()

    for ch in range(CIN):
        cols = slice(ch * width, (ch + 1) * width)
        for r in range(PATCH):
            lines[(r + 1) * group : (r + 2) * group, cols] = line(ch, r).astype(BF)
    lane = lax.broadcasted_iota(jnp.int32, (1, NP * HALF), 1)
    col, spot = lane // HALF, lane % HALF
    for ch in range(CIN):
        inside = (spot >= WIN * ch) & (spot < WIN * (ch + 1))
        want = jnp.where(inside, PATCH * col + spot - WIN * ch - 1, -5)
        here = lax.broadcasted_iota(jnp.int32, (width, NP * HALF), 0)
        sel_ref[ch * width : (ch + 1) * width, :] = jnp.where(here == want, 1.0, 0.0).astype(BF)

    @pl.when(row < final_row)
    def _():
        edge_copies[0].wait_recv()

    @pl.when(row > 0)
    def _():
        edge_copies[1].wait_recv()

    patch_row = lax.broadcasted_iota(jnp.int32, (group, width), 0) % nrow
    for ch in range(CIN):
        cols = slice(ch * width, (ch + 1) * width)
        up = jnp.where(patch_row == 0, edge[3, ch].astype(F32), pltpu.roll(line(ch, PATCH - 1), 1, 0))
        lines[0:group, cols] = up.astype(BF)
        down = jnp.where(patch_row == nrow - 1, edge[2, ch].astype(F32), pltpu.roll(line(ch, 0), group - 1, 0))
        lines[(PATCH + 1) * group : (PATCH + 2) * group, cols] = down.astype(BF)
    lane = lax.broadcasted_iota(jnp.int32, (group, 2 * HALF), 1)
    low = lane < HALF
    ones = (lane % HALF) == ONE_LANE
    nx = sizes[1]
    share, per = items * nrow * NP // nx, group // nx
    turns = [turn_of(sizes, pos, xg) * share for xg in range(nx)]

    def put(j, c, block):
        low_bits = block.astype(BF)
        for xg in range(nx):
            x[j, pl.ds(pl.multiple_of(turns[xg] + c * per, per), per), :] = low_bits[xg * per : (xg + 1) * per]

    for quarter in range(NP * HALF // 256):
        res = mm(lines[...], sel_ref[:, quarter * 256 : (quarter + 1) * 256])
        for j in range(SLABS):
            first = res[2 * j * group : (2 * j + 1) * group]
            second = res[(2 * j + 1) * group : (2 * j + 2) * group]
            for pair in range(2):
                a = first[:, pair * 128 : (pair + 1) * 128]
                b = second[:, pair * 128 : (pair + 1) * 128]
                put(j, quarter * 4 + pair * 2, jnp.where(ones, 1.0, jnp.where(low, a, pltpu.roll(b, HALF, 1))))
                put(j, quarter * 4 + pair * 2 + 1, jnp.where(ones, 1.0, jnp.where(low, pltpu.roll(a, HALF, 1), b)))
    for j in range(SLABS):
        xt_ref[j] = x[j].T


def stem_kernel(sizes, img_ref, cw_ref, cb_ref, w_ref, pb_ref, tok_ref, saved_ref, xt_ref, sel_ref, t_ref,
                x, pix, lines, edge, edge_send, edge_recv, acc, nat, parcel, got, send, recv):
    t = pl.program_id(0)
    p = t % STEPS
    nx = sizes[1]
    rows = 2 * nx
    pos = place(sizes)
    item, row, final_row = lax.axis_index("items"), lax.axis_index("rows"), lax.axis_size("rows") - 1
    share = acc.shape[0]
    per = share // NP

    def edge_copy(n):
        return pltpu.make_async_remote_copy(
            src_ref=edge.at[n], dst_ref=edge.at[2 + n], send_sem=edge_send.at[n], recv_sem=edge_recv.at[n],
            device_id=(item, row + (2 * n - 1)), device_id_type=MESH,
        )

    @pl.when(t == 0)
    def _():
        @pl.when(row == final_row)
        def _():
            edge[2] = jnp.zeros(edge.shape[1:], BF)

        @pl.when(row == 0)
        def _():
            edge[3] = jnp.zeros(edge.shape[1:], BF)

        greet(sizes, pos, True, False)
        tap_matrix(cw_ref, cb_ref, t_ref)
        make_windows(sizes, pos, img_ref, edge, [edge_copy(0), edge_copy(1)], x, xt_ref, sel_ref, pix, lines)

    @pl.when(p == 0)
    def _():
        acc[...] = jnp.broadcast_to(as_row(pb_ref), acc.shape)

    weight = w_ref[...].reshape(FEAT, D)
    for s in range(share // 256):
        rs = slice(s * 256, (s + 1) * 256)
        here = pl.ds(pl.multiple_of(t // STEPS * share + s * 256, 256), 256)
        xs = jnp.concatenate([x[p, here, :], x[p + 1, here, :]], axis=1)
        for n in range(FEAT // 256):
            cs = slice(n * 256, (n + 1) * 256)
            act, slope = gelu_pair_low(mm(xs, t_ref[:, cs]))
            saved_ref[0, 0, rs, cs] = act
            saved_ref[0, 1, rs, cs] = slope
        acc[rs, :] += mm(saved_ref[0, 0, rs, :], weight)

    @pl.when(p == STEPS - 1)
    def _():
        for c in range(NP):
            for k in range(D // 128):
                nat[k, pl.ds(c, per, stride=NP), :] = acc[c * per : (c + 1) * per, k * 128 : (k + 1) * 128]

    def parcel_copy(turn, core, slot):
        to = lax.rem(pos[1] + 1 + turn, nx) * 2 + core
        return pltpu.make_async_remote_copy(
            src_ref=parcel.at[turn, core], dst_ref=got.at[:, row], send_sem=send.at[turn, slot], recv_sem=recv.at[row],
            device_id=(item, to), device_id_type=MESH,
        )

    for turn in range(nx):
        @pl.when(t == turn * STEPS + STEPS - 1)
        def _(turn=turn):
            for k in range(D // 128):
                cut = nat[k].astype(BF).reshape(parcel.shape[1:4] + (128,))
                parcel[turn, :, :, :, k * 128 : (k + 1) * 128] = cut
            if turn < nx - 1:
                for core in range(2):
                    parcel_copy(turn, core, core).start()
            else:
                parcel_copy(turn, 1 - pos[0], 0).start()
                got[:, row] = parcel[turn, pos[0]]

    @pl.when(t == nx * STEPS - 1)
    def _():
        for k in range(1, rows):
            source = lax.rem(row + k, rows)
            pltpu.make_async_remote_copy(
                src_ref=parcel.at[0, 0], dst_ref=got.at[:, source], send_sem=send.at[0, 0], recv_sem=recv.at[source],
                device_id=(item, source), device_id_type=MESH,
            ).wait_recv()
        tok_ref[...] = got[...]
        for turn in range(nx - 1):
            for core in range(2):
                parcel_copy(turn, core, core).wait_send()
        parcel_copy(nx - 1, 1 - pos[0], 0).wait_send()

        @pl.when(row > 0)
        def _():
            edge_copy(0).wait_send()

        @pl.when(row < final_row)
        def _():
            edge_copy(1).wait_send()


def stem_forward(images, cw, cb, weight, bias, sizes):
    count, _, height, width = images.shape
    nx = sizes[1]
    nrow = height // PATCH
    group = count * nrow
    tokens = group * NP
    share = tokens // nx
    arrived = (SEQ_ITEMS, 2 * nx, nrow * NP, D)
    return pl.pallas_call(
        functools.partial(stem_kernel, sizes),
        name="stem_forward",
        grid=(nx * STEPS,),
        in_specs=[
            whole(images.shape),
            whole(cw.shape),
            whole(cb.shape),
            pl.BlockSpec((CH, 1, 2 * PATCH, D), lambda t: (0, t % STEPS, 0, 0)),
            whole(bias.shape),
        ],
        out_specs=(
            whole(arrived),
            pl.BlockSpec((1, 2, share, FEAT), lambda t: (t % STEPS, 0, t // STEPS, 0)),
            whole((SLABS, 128, tokens)),
            whole((CIN * width, NP * HALF)),
            whole((4 * HALF, FEAT)),
        ),
        out_shape=(
            jax.ShapeDtypeStruct(arrived, BF),
            jax.ShapeDtypeStruct((STEPS, 2, tokens, FEAT), BF),
            jax.ShapeDtypeStruct((SLABS, 128, tokens), BF),
            jax.ShapeDtypeStruct((CIN * width, NP * HALF), BF),
            jax.ShapeDtypeStruct((4 * HALF, FEAT), BF),
        ),
        scratch_shapes=[
            pltpu.VMEM((SLABS, tokens, 128), BF),
            pltpu.VMEM((CIN, width // 128, count * height, 128), F32),
            pltpu.VMEM((WIN * group, CIN * width), BF),
            pltpu.VMEM((4, CIN, group, width), BF),
            pltpu.SemaphoreType.DMA((2,)),
            pltpu.SemaphoreType.DMA((2,)),
            pltpu.VMEM((share, D), F32),
            pltpu.VMEM((D // 128, share, 128), F32),
            pltpu.VMEM((nx, 2, SEQ_ITEMS, nrow * NP, D), BF),
            pltpu.VMEM(arrived, BF),
            pltpu.SemaphoreType.DMA((nx, 2)),
            pltpu.SemaphoreType.DMA((2 * nx,)),
        ],
        compiler_params=params(collective_id=0, has_side_effects=True),
    )(images, cw, cb, weight, bias)


def norm_stats(v):
    centred = v - jnp.mean(v, axis=-1, keepdims=True)
    inv = lax.rsqrt(jnp.mean(centred * centred, axis=-1, keepdims=True) + 1e-06)
    return centred * inv, inv


def three_terms(v):
    hi = v.astype(BF)
    rest = v - hi.astype(F32)
    mid = rest.astype(BF)
    lo = (rest - mid.astype(F32)).astype(BF)
    return hi, mid, lo


def minus_terms(v, lane, base):
    hi, mid, lo = three_terms(-v)
    out = jnp.where(lane == 4, hi.astype(F32), base)
    out = jnp.where(lane == 5, mid.astype(F32), out)
    return jnp.where(lane == 6, lo.astype(F32), out).astype(BF)


def attend_kernel(tok_ref, g_ref, b_ref, qb_ref, vb_ref, seg_ref, wq_ref, wk_ref, wv_ref,
                  q_ref, k_ref, v_ref, o_ref, o32_ref, lx_ref, kx_ref, n1, kaug, vaug):
    step = pl.program_id(0)
    line = lax.broadcasted_iota(jnp.int32, (1, 128), 1)
    first_item = lax.axis_index("rows") * SEQ_ITEMS
    same = [line == seg_ref[first_item + i] for i in range(SEQ_ITEMS)]
    terms = jnp.where((line >= 4) & (line < 7), 1.0, 0.0)
    keys_in = [jnp.where((line < 4) & ~one, -1e30, terms) for one in same]

    @pl.when(step == 0)
    def _():
        kx_ref[...] = jnp.concatenate(keys_in + [jnp.zeros((8 - SEQ_ITEMS, 128), F32)], axis=0)
        for s in range(TOK // 128):
            rs = slice(s * 128, (s + 1) * 128)
            hat, _ = norm_stats(tok_ref[rs, :].astype(F32))
            n1[rs, :] = (hat * as_row(g_ref) + as_row(b_ref)).astype(BF)

    own = pl.ds(pl.multiple_of(step * 256, 256), 256)
    q_ref[...] = ((mm(n1[...], wq_ref[...]) + as_row(qb_ref, own)).astype(BF) * 0.125).astype(BF)
    k_ref[...] = mm(n1[...], wk_ref[...]).astype(BF)
    v_ref[...] = (mm(n1[...], wv_ref[...]) + as_row(vb_ref, own)).astype(BF)
    lane = lax.broadcasted_iota(jnp.int32, (NPATCH, 128), 1)
    low = lane < HD
    for i in range(SEQ_ITEMS):
        rs = slice(i * NPATCH, (i + 1) * NPATCH)
        kaug[rs, 128:256] = jnp.broadcast_to(keys_in[i], (NPATCH, 128)).astype(BF)
        vaug[rs, 128:256] = jnp.ones((NPATCH, 128), BF)
    for pair in range(2):
        cs = slice(pair * 128, (pair + 1) * 128)
        kaug[:, 0:128] = k_ref[:, cs]
        vaug[:, 0:128] = v_ref[:, cs]
        for i in range(SEQ_ITEMS):
            rs = slice(i * NPATCH, (i + 1) * NPATCH)
            span = slice(0, (i + 1) * NPATCH)
            qp = q_ref[rs, cs]
            qx = jnp.broadcast_to(jnp.where(same[i], 1.0, 0.0), (NPATCH, 128))
            halves = []
            for h in range(2):
                mine = low if h == 0 else ~low
                qaug = jnp.concatenate([jnp.where(mine, qp, jnp.zeros_like(qp)), qx.astype(BF)], axis=1)
                scores = mm_t(qaug, kaug[span, :])
                top = jnp.max(scores, axis=1, keepdims=True)
                raised = jnp.exp(scores - top).astype(BF)
                out = mm(raised, vaug[span, :])
                total = out[:, 128:256]
                halves.append(out[:, 0:128] / total)
                lx_ref[pair * 2 + h, rs, :] = minus_terms(top + jnp.log(total), lane, qx)
            out = jnp.where(low, halves[0], halves[1])
            o32_ref[rs, cs] = out
            o_ref[rs, cs] = out.astype(BF)


def attend(tokens, vecs, segments, wq, wk, wv):
    lines = [whole(vec.shape) for vec in vecs]
    col = pl.BlockSpec((D, 256), lambda g: (0, g))
    out = pl.BlockSpec((TOK, 256), lambda g: (0, g))
    return pl.pallas_call(
        attend_kernel,
        name="attend",
        grid=(D // 256,),
        in_specs=[whole((TOK, D))] + lines + [pl.BlockSpec(memory_space=pltpu.SMEM), col, col, col],
        out_specs=(out, out, out, out, out, pl.BlockSpec((4, TOK, 128), lambda g: (g, 0, 0)), whole((8, 128))),
        out_shape=(jax.ShapeDtypeStruct((TOK, D), BF),) * 4
        + (
            jax.ShapeDtypeStruct((TOK, D), F32),
            jax.ShapeDtypeStruct((HEADS, TOK, 128), BF),
            jax.ShapeDtypeStruct((8, 128), F32),
        ),
        scratch_shapes=[pltpu.VMEM((TOK, D), BF), pltpu.VMEM((TOK, 256), BF), pltpu.VMEM((TOK, 256), BF)],
        compiler_params=params(),
    )(tokens, *vecs, segments, wq, wk, wv)


def norm_back(e, hat, inv, gain):
    f = e * gain
    return inv * (f - jnp.mean(f, axis=-1, keepdims=True) - hat * jnp.mean(f * hat, axis=-1, keepdims=True))


def col_sum(v):
    return jnp.sum(v, axis=0, keepdims=True)


def store_square(ref, n, grad):
    _, _, nx, ny, nz, _, _ = ref.shape
    height, width = D // (ny * nz), D // (2 * nx)
    if not folds(width):
        for r in range(2 * nx):
            part = grad[:, r * width : (r + 1) * width]
            for i in range(ny * nz):
                ref[n, r % 2, r // 2, i % ny, i // ny] = part[i * height : (i + 1) * height]
        return
    half = height // 2
    low = lax.broadcasted_iota(jnp.int32, (half, 128), 1) < HALF
    for x in range(nx):
        base = 2 * x * width
        shared = grad[:, base + 128 : base + 256]
        turned = jnp.concatenate([shared[:, HALF:], shared[:, :HALF]], axis=1)
        for i in range(ny * nz):
            top, end = i * height, (i + 1) * height
            mid = top + half
            ref[n, 0, x, i % ny, i // ny, 0:height] = grad[top:end, base : base + 128]
            ref[n, 0, x, i % ny, i // ny, height:] = jnp.where(low, shared[top:mid], turned[mid:end])
            ref[n, 1, x, i % ny, i // ny, 0:height] = grad[top:end, base + 256 : base + 384]
            ref[n, 1, x, i % ny, i // ny, height:] = jnp.where(low, turned[top:mid], shared[mid:end])


def mixer_kernel(tok_ref, att_ref, cot_ref, wo_ref, ob_ref, g_ref, b_ref, rb_ref, hb_ref, wh_ref, wr_ref,
                 out_ref, mid_ref, ag_ref, wog_ref, whg_ref, wrg_ref, sums_ref, hbg_ref,
                 middle, n2, n2t, cott, acc, back, act, hg, hidden_row):
    step = pl.program_id(0)
    last = pl.num_programs(0) - 1
    chunk = wh_ref.shape[1]
    tile = 2 if chunk % 256 == 0 else 3
    blocks = [slice(s * 256, (s + 1) * 256) for s in range(TOK // 256)]

    @pl.when(step == 0)
    def _():
        hidden_row[...] = as_row(hb_ref)
        for rs in blocks:
            row = tok_ref[rs, :].astype(F32) + mm(att_ref[rs, :], wo_ref[...]) + as_row(ob_ref)
            middle[rs, :] = row
            acc[rs, :] = row + as_row(rb_ref)
            back[rs, :] = jnp.zeros((256, D), F32)
            hat, _ = norm_stats(row)
            low = (hat * as_row(g_ref) + as_row(b_ref)).astype(BF)
            n2[rs, :] = low
            n2t[:, rs] = low.T
            cott[:, rs] = cot_ref[rs, :].T

    hidden_bias = hidden_row[0:1, pl.ds(pl.multiple_of(step * chunk, 128), chunk)]
    hsum = jnp.zeros((1, chunk), F32)
    for rs in blocks:
        for n in range(chunk // 128 // tile):
            cs = slice(n * 128 * tile, (n + 1) * 128 * tile)
            pre = mm(n2[rs, :], wh_ref[:, cs]) + hidden_bias[:, cs]
            up = mm_t(cot_ref[rs, :], wr_ref[cs, :])
            a, slope = gelu_pair(pre)
            act[rs, cs] = a.astype(BF)
            hg[rs, cs] = (slope * up).astype(BF)
        acc[rs, :] += mm(act[rs, :], wr_ref[...])
        back[rs, :] += mm_t(hg[rs, :], wh_ref[...])
        hsum = hsum + col_sum(hg[rs, :].astype(F32))
    hbg_ref[...] = hsum
    _, _, nx, ny, nz, height, _ = whg_ref.shape
    for n in range(3):
        width = chunk // 3
        grad = mm(n2t[...], hg[:, n * width : (n + 1) * width]).astype(BF)
        for i in range(ny * nz):
            whg_ref[n, 0, 0, i % ny, i // ny] = grad[i * height : (i + 1) * height]
    _, _, nx, ny, _, _, _ = wrg_ref.shape
    height, width = D // (2 * nx), chunk // ny // 3
    for y in range(ny):
        grad = mm(cott[...], act[:, y * 3 * width : (y + 1) * 3 * width]).astype(BF)
        for n in range(3):
            for r in range(2 * nx):
                part = grad[r * height : (r + 1) * height, n * width : (n + 1) * width]
                wrg_ref[n, r % 2, r // 2, y, 0] = fold_block(part)

    @pl.when(step == last)
    def _():
        gsum = jnp.zeros((1, D), F32)
        bsum = jnp.zeros((1, D), F32)
        osum = jnp.zeros((1, D), F32)
        rsum = jnp.zeros((1, D), F32)
        for rs in blocks:
            out_ref[rs, :] = acc[rs, :].astype(BF)
            hat, inv = norm_stats(middle[rs, :])
            e = back[rs, :]
            gsum = gsum + col_sum(e * hat)
            bsum = bsum + col_sum(e)
            cot = cot_ref[rs, :].astype(F32)
            rsum = rsum + col_sum(cot)
            mid = cot + norm_back(e, hat, inv, as_row(g_ref))
            mid_ref[rs, :] = mid
            low = mid.astype(BF)
            osum = osum + col_sum(low.astype(F32))
            n2[rs, :] = low
            n2t[:, rs] = att_ref[rs, :].T
            ag_ref[rs, :] = mm_t(low, wo_ref[...]).astype(BF)
        store_square(wog_ref, 0, mm(n2t[...], n2[...]).astype(BF))
        sums_ref[0:1, :] = gsum
        sums_ref[1:2, :] = bsum
        sums_ref[2:3, :] = osum
        sums_ref[3:4, :] = rsum


def mixer(tokens, attended, cotangent, wo, vecs, wh, wr, sizes):
    nc, nx, ny, nz = sizes
    rows, items = nc * nx, ny * nz
    chunk = FF // rows
    square = (1,) + sizes + folded_shape(D // items, D // rows)
    return pl.pallas_call(
        mixer_kernel,
        name="mixer",
        grid=(rows,),
        in_specs=[
            whole((TOK, D)), whole((TOK, D)), whole((TOK, D)), whole((D, D)),
            whole((D,)), whole((D,)), whole((D,)), whole((D,)), whole((FF,)),
            pl.BlockSpec((D, chunk), lambda r: (0, r)),
            pl.BlockSpec((chunk, D), lambda r: (r, 0)),
        ],
        out_specs=(
            whole((TOK, D)), whole((TOK, D)), whole((TOK, D)), whole(square),
            pl.BlockSpec((3, 1, 1, ny, nz, D // items, chunk // 3), lambda r: (0, r % 2, r // 2, 0, 0, 0, 0)),
            pl.BlockSpec((3, nc, nx, ny, 1) + folded_shape(D // rows, FF // items // 3), lambda r: (0, 0, 0, 0, r, 0, 0)),
            whole((8, D)),
            pl.BlockSpec((1, chunk), lambda r: (0, r)),
        ),
        out_shape=(
            jax.ShapeDtypeStruct((TOK, D), BF),
            jax.ShapeDtypeStruct((TOK, D), F32),
            jax.ShapeDtypeStruct((TOK, D), BF),
            jax.ShapeDtypeStruct(square, BF),
            jax.ShapeDtypeStruct((3,) + sizes + (D // items, chunk // 3), BF),
            jax.ShapeDtypeStruct((3,) + sizes + folded_shape(D // rows, FF // items // 3), BF),
            jax.ShapeDtypeStruct((8, D), F32),
            jax.ShapeDtypeStruct((1, FF), F32),
        ),
        scratch_shapes=[
            pltpu.VMEM((TOK, D), F32), pltpu.VMEM((TOK, D), BF), pltpu.VMEM((D, TOK), BF),
            pltpu.VMEM((D, TOK), BF), pltpu.VMEM((TOK, D), F32), pltpu.VMEM((TOK, D), F32),
            pltpu.VMEM((TOK, chunk), BF), pltpu.VMEM((TOK, chunk), BF), pltpu.VMEM((1, FF), F32),
        ],
        compiler_params=params(),
    )(tokens, attended, cotangent, wo, *vecs, wh, wr)


def attend_back_kernel(sizes, tok_ref, g_ref, b_ref, kx_ref, mid_ref, q_ref, k_ref, v_ref, o_ref, ag_ref, lx_ref,
                       wq_ref, wk_ref, wv_ref, whg_ref, wrg_ref, wog_ref,
                       tg_ref, sq_ref, sums_ref, qvs_ref, who_ref, wro_ref, woo_ref,
                       n1t, back, kaug, vaug, qaug, oaug, dqt, dq, dk, dv, square, *comm):
    step = pl.program_id(0)
    blocks = [slice(s * 256, (s + 1) * 256) for s in range(TOK // 256)]
    pos = place(sizes)
    groups = ((whg_ref, who_ref), (wrg_ref, wro_ref), (wog_ref, woo_ref))
    pieces, loads, base, at = [], [], 0, 0
    for source, _ in groups:
        count = source.shape[0]
        refs, keep = comm[at : at + 4 * count + 2], comm[at + 4 * count + 2 : at + 4 * count + 4]
        at += 4 * count + 4
        pieces += make_pieces(
            sizes, pos, BACK_ORDERS[base : base + count], [source.at[n] for n in range(count)],
            [keep[0].at[n] for n in range(count)], refs,
        )
        loads += [pltpu.make_async_copy(source.at[n, pos[0]], keep[0].at[n], keep[1].at[n]) for n in range(count)]
        base += count

    def event(index, stage):
        if stage == 0:
            pieces[index].start(0)
            loads[index].start()
        elif stage < 4:
            if stage == 1:
                loads[index].wait()
            pieces[index].advance(stage)
        else:
            total = pieces[index].gather(3)
            if index < 3:
                width = total.shape[1]
                who_ref[:, index * width : (index + 1) * width] = total
            elif index < 6:
                height, width = D // (2 * sizes[1]), FF // (sizes[2] * sizes[3]) // 3
                wro_ref[:, (index - 3) * width : (index - 2) * width] = unfold_block(total, height, width)
            else:
                woo_ref[...] = unfold_block(total, *woo_ref.shape, odd=pos[0] == 1)

    def finish():
        for part in pieces:
            part.drain()

    table = {(0, 0): [functools.partial(greet, sizes, pos, True, True)]}
    for when, index, stage in BACK_PLAN:
        if when < 2:
            key = (0, when)
        elif when < 26:
            key = ((when - 2) // 8, 2 + (when - 2) % 8)
        else:
            key = (2, 10)
        table.setdefault(key, []).append(functools.partial(event, index, stage))
    table.setdefault((2, 10), []).append(finish)
    run_events(step, table, (0,))

    @pl.when(step == 0)
    def _():
        for rs in blocks:
            hat, _ = norm_stats(tok_ref[rs, :].astype(F32))
            n1t[:, rs] = (hat * as_row(g_ref) + as_row(b_ref)).astype(BF).T
            back[rs, :] = jnp.zeros((256, D), F32)

    run_events(step, table, (1,))
    lane = lax.broadcasted_iota(jnp.int32, (NPATCH, 128), 1)
    low = lane < HD
    ones = jnp.where((lane >= 4) & (lane < 7), 1.0, 0.0).astype(BF)
    for i, rs in enumerate(blocks):
        kaug[rs, 128:256] = jnp.broadcast_to(kx_ref[i : i + 1, :], (NPATCH, 128)).astype(BF)
        vaug[rs, 128:256] = ones
    pick_row = lax.broadcasted_iota(jnp.int32, (256, 256), 0) % 128 // HD
    pick_col = lax.broadcasted_iota(jnp.int32, (256, 256), 1) // 128
    pick = jnp.where(pick_row == pick_col, 1.0, 0.0).astype(BF)
    for pair in range(2):
        cs = slice(pair * 128, (pair + 1) * 128)
        kaug[:, 0:128] = k_ref[:, cs]
        vaug[:, 0:128] = v_ref[:, cs]
        kt = k_ref[:, cs].T
        for rs in blocks:
            qp = q_ref[rs, cs]
            gp = ag_ref[rs, cs]
            prod = gp.astype(F32) * o_ref[rs, cs]
            hi = prod.astype(BF)
            both = jnp.concatenate([hi, (prod - hi.astype(F32)).astype(BF)], axis=1)
            dots = mm(both, pick)
            for h in range(2):
                mine = low if h == 0 else ~low
                qaug[h, rs, 0:128] = jnp.where(mine, qp, jnp.zeros_like(qp))
                qaug[h, rs, 128:256] = lx_ref[pair * 2 + h, rs, :]
                oaug[h, rs, 0:128] = jnp.where(mine, gp, jnp.zeros_like(gp))
                oaug[h, rs, 128:256] = minus_terms(dots[:, h * 128 : (h + 1) * 128], lane, jnp.zeros((NPATCH, 128), F32))
        for j, rs in enumerate(blocks):
            span = slice(j * NPATCH, TOK)
            parts_k, parts_v = [], []
            for h in range(2):
                probs = jnp.exp(mm_t(kaug[rs, :], qaug[h, span, :]))
                rise = mm_t(vaug[rs, :], oaug[h, span, :])
                grad = (probs * rise).astype(BF)
                probs_low = probs.astype(BF)
                parts_v.append(mm(probs_low, ag_ref[span, cs]))
                parts_k.append(mm(grad, q_ref[span, cs]))
                hs = slice(h * HD, (h + 1) * HD)
                part = mm(kt[hs, rs], grad)
                if j == 0:
                    dqt[hs, :] = part
                else:
                    dqt[hs, span] += part
            dk[rs, cs] = jnp.where(low, parts_k[0], parts_k[1]).astype(BF)
            dv[rs, cs] = jnp.where(low, parts_v[0], parts_v[1]).astype(BF)
            run_events(step, table, (2 + pair * 4 + j,))
        dq[:, cs] = (dqt[...].T * 0.125).astype(BF)
    qvs_ref[0:1, :] = col_sum(dq[...].astype(F32))
    qvs_ref[1:2, :] = col_sum(dv[...].astype(F32))
    for n, part in enumerate((dq, dk, dv)):
        square[n, step] = mm(n1t[...], part[...]).astype(BF)
    for rs in blocks:
        back[rs, :] += (
            mm_t(dq[rs, :], wq_ref[...]) + mm_t(dk[rs, :], wk_ref[...]) + mm_t(dv[rs, :], wv_ref[...])
        )

    @pl.when(step == pl.num_programs(0) - 1)
    def _():
        gsum = jnp.zeros((1, D), F32)
        bsum = jnp.zeros((1, D), F32)
        for rs in blocks:
            hat, inv = norm_stats(tok_ref[rs, :].astype(F32))
            e = back[rs, :]
            gsum = gsum + col_sum(e * hat)
            bsum = bsum + col_sum(e)
            tg_ref[rs, :] = (mid_ref[rs, :] + norm_back(e, hat, inv, as_row(g_ref))).astype(BF)
        sums_ref[0:1, :] = gsum
        sums_ref[1:2, :] = bsum
        for n in range(3):
            store_square(sq_ref, n, jnp.concatenate([square[n, g] for g in range(D // 256)], axis=1))

    run_events(step, table, (10,))


BACK_ORDERS = (
    (3, 2, 1), (2, 3, 1), (1, 2, 3), (1, 2, 3), (1, 2, 3), (1, 2, 3),
    (2, 1, 3),
)
BACK_PLAN = (
    (0, 3, 0), (0, 0, 0), (0, 1, 0), (0, 5, 0), (0, 4, 0), (0, 2, 0), (0, 6, 0), (1, 3, 1), (1, 0, 1),
    (1, 1, 1), (4, 5, 1), (6, 6, 1), (6, 2, 1), (7, 1, 2), (9, 3, 2), (9, 4, 1), (10, 5, 2), (15, 3, 3),
    (16, 2, 2), (16, 0, 2), (16, 5, 3), (17, 6, 2), (18, 3, 4), (18, 2, 3), (19, 4, 2), (19, 0, 3), (20, 1, 3),
    (21, 6, 3), (23, 4, 3), (26, 6, 4), (26, 1, 4), (26, 5, 4), (27, 0, 4), (28, 2, 4), (29, 4, 4),
)


def attend_back(tokens, gain, shift, kx, mid, q, k, v, o, ag, lx, wq, wk, wv, whg, wrg, wog, sizes):
    squares = (3,) + sizes + wog.shape[5:]
    col = pl.BlockSpec((D, 256), lambda g: (0, g))
    part = pl.BlockSpec((TOK, 256), lambda g: (0, g))
    far = pl.BlockSpec(memory_space=pl.ANY)
    items, rows = sizes[2] * sizes[3], 2 * sizes[1]
    outs = [(D // items, FF // rows), (D // rows, FF // items), (D // items, D // rows)]
    return pl.pallas_call(
        functools.partial(attend_back_kernel, sizes),
        name="attend_back",
        grid=(D // 256,),
        in_specs=[whole((TOK, D)), whole((D,)), whole((D,)), whole(kx.shape), whole((TOK, D)),
                  part, part, part, part, part, pl.BlockSpec((4, TOK, 128), lambda g: (g, 0, 0)),
                  col, col, col, far, far, far],
        out_specs=(whole((TOK, D)), whole(squares), whole((8, D)), pl.BlockSpec((8, 256), lambda g: (0, g)))
        + tuple(whole(shape) for shape in outs),
        out_shape=(
            jax.ShapeDtypeStruct((TOK, D), BF),
            jax.ShapeDtypeStruct(squares, BF),
            jax.ShapeDtypeStruct((8, D), F32),
            jax.ShapeDtypeStruct((8, D), F32),
        ) + tuple(jax.ShapeDtypeStruct(shape, F32) for shape in outs),
        scratch_shapes=[
            pltpu.VMEM((D, TOK), BF), pltpu.VMEM((TOK, D), F32),
            pltpu.VMEM((TOK, 256), BF), pltpu.VMEM((TOK, 256), BF),
            pltpu.VMEM((2, TOK, 256), BF), pltpu.VMEM((2, TOK, 256), BF),
            pltpu.VMEM((128, TOK), F32),
            pltpu.VMEM((TOK, 256), BF), pltpu.VMEM((TOK, 256), BF), pltpu.VMEM((TOK, 256), BF),
            pltpu.VMEM((3, D // 256, D, 256), BF),
        ]
        + piece_scratch(sizes, BACK_ORDERS[0:3], whg.shape[5:]) + own_scratch(sizes, 3, whg.shape[5:])
        + piece_scratch(sizes, BACK_ORDERS[3:6], wrg.shape[5:]) + own_scratch(sizes, 3, wrg.shape[5:])
        + piece_scratch(sizes, BACK_ORDERS[6:7], wog.shape[5:]) + own_scratch(sizes, 1, wog.shape[5:]),
        compiler_params=params(collective_id=1, has_side_effects=True),
    )(tokens, gain, shift, kx, mid, q, k, v, o, ag, lx, wq, wk, wv, whg, wrg, wog)


EARLY = 80
FINISH_ORDERS = (
    (1, 2, 3), (2, 1, 3), (3, 2, 1), (1, 2, 3), (2, 3, 1), (1, 2, 3),
    (2, 1, 3), (1, 2, 3), (2, 3, 1), (3, 1, 2), (2, 3, 1),
)
FINISH_PLAN = (
    (0, 8, 0), (0, 10, 0), (0, 9, 0), (1, 10, 1), (2, 9, 1), (3, 8, 1), (7, 10, 2), (9, 0, 0), (9, 11, 0),
    (9, 8, 2), (10, 1, 0), (10, 0, 1), (11, 2, 0), (11, 1, 1), (12, 3, 0), (12, 2, 1), (12, 3, 1), (13, 4, 0),
    (13, 0, 2), (14, 5, 0), (14, 1, 2), (14, 4, 1), (15, 6, 0), (15, 5, 1), (16, 7, 0), (16, 0, 3), (16, 6, 1),
    (16, 3, 2), (17, 7, 1), (18, 4, 2), (18, 1, 3), (19, 10, 3), (20, 5, 2), (20, 2, 2), (21, 8, 3), (22, 11, 1),
    (22, 6, 2), (22, 3, 3), (23, 4, 3), (24, 0, 4), (24, 11, 2), (24, 12, 0), (24, 5, 3), (25, 7, 2), (25, 12, 1),
    (25, 6, 3), (25, 9, 2), (26, 10, 4), (26, 12, 2), (28, 11, 3), (28, 12, 3), (28, 5, 4), (28, 2, 3), (29, 7, 3),
    (29, 1, 4), (30, 8, 4), (31, 9, 3), (31, 4, 4), (32, 11, 4), (33, 2, 4), (33, 3, 4), (33, 9, 4), (33, 6, 4),
    (33, 12, 4), (33, 7, 4),
)


def finish_kernel(sizes, tg_ref, act_ref, slope_ref, w_ref, xt_ref, t_ref, sel_ref, sq_ref, sums2_ref, hbg_ref, sums1_ref, qvs_ref,
                  pw_ref, sq0_ref, sq1_ref, sq2_ref, ig_ref, earlyo_ref, tapso_ref,
                  tgc, tgt, dxa, pg, cw, lines, flat, grads, edge, edge_send, edge_recv, got, send, recv, nat, *comm):
    t = pl.program_id(0)
    nc, nx, ny, nz = sizes
    items, rows = ny * nz, nc * nx
    tokens = tgc.shape[0]
    group = tokens // NP
    count, _, height, width = ig_ref.shape
    nrow = height // PATCH
    pos = place(sizes)
    item, row = lax.axis_index("items"), lax.axis_index("rows")
    final_row = lax.axis_size("rows") - 1
    far_steps = STEPS * (nx - 1)
    image_step = 2 * STEPS + far_steps
    final_step = image_step + CIN - 1
    at = 4 * STEPS + 2
    patch = make_pieces(
        sizes, pos, FINISH_ORDERS[0:STEPS], [grads.at[q % 2] for q in range(STEPS)],
        [grads.at[q % 2, pos[0]] for q in range(STEPS)], comm[0:at],
    )
    keep = comm[at + 14 : at + 16]
    square = make_pieces(
        sizes, pos, FINISH_ORDERS[STEPS : STEPS + 3], [sq_ref.at[n] for n in range(3)],
        [keep[0].at[n] for n in range(3)], comm[at : at + 14],
    )
    loads = [pltpu.make_async_copy(sq_ref.at[n, pos[0]], keep[0].at[n], keep[1].at[n]) for n in range(3)]
    at += 16
    early = SmallSum(sizes, pos, comm[at : at + 4], comm[at + 4], comm[at + 5])
    late = SmallSum(sizes, pos, comm[at + 6 : at + 10], comm[at + 10], comm[at + 11])

    def edge_copy(n):
        step = -1 if n == 0 else 1
        return pltpu.make_async_remote_copy(
            src_ref=edge.at[n], dst_ref=edge.at[2 + n], send_sem=edge_send.at[n], recv_sem=edge_recv.at[n],
            device_id=(item, row + step), device_id_type=MESH,
        )

    share, per = tokens // nx, group // nx
    turns = [turn_of(sizes, pos, xg) * share for xg in range(nx)]

    def spread(j, c):
        return jnp.concatenate(
            [dxa[j, pl.ds(pl.multiple_of(turns[xg] + c * per, per), per), :] for xg in range(nx)], axis=0
        )

    def parcel(k):
        to = lax.rem(row + k, rows)
        return pltpu.make_async_remote_copy(
            src_ref=tg_ref.at[:, to], dst_ref=got.at[row], send_sem=send.at[k - 1], recv_sem=recv.at[row],
            device_id=(item, to), device_id_type=MESH,
        )

    def arrived(source):
        pltpu.make_async_remote_copy(
            src_ref=tg_ref.at[:, source], dst_ref=got.at[source], send_sem=send.at[0], recv_sem=recv.at[source],
            device_id=(item, source), device_id_type=MESH,
        ).wait_recv()

    def unpack(xg, turn):
        for k in range(D // 128):
            cut = got[pl.ds(2 * xg, 2), :, :, k * 128 : (k + 1) * 128]
            nat[k] = cut.reshape(share, 128).astype(F32)
        for c in range(NP):
            part = jnp.concatenate([nat[k, pl.ds(c, per, stride=NP), :] for k in range(D // 128)], axis=1)
            tgc[turn * share + c * per : turn * share + (c + 1) * per, :] = part.astype(BF)

    def put_lines(j):
        low = lax.broadcasted_iota(jnp.int32, (group, 2 * HALF), 1) < HALF
        for pair in range(NP // 2):
            a, b = spread(j, 2 * pair), spread(j, 2 * pair + 1)
            cs = slice(pair * 128, (pair + 1) * 128)
            lines[2 * j * group : (2 * j + 1) * group, cs] = jnp.where(low, a, pltpu.roll(b, HALF, 1)).astype(BF)
            lines[(2 * j + 1) * group : (2 * j + 2) * group, cs] = jnp.where(low, pltpu.roll(a, HALF, 1), b).astype(BF)

    def event(index, stage):
        if index < STEPS:
            if stage == 0:
                patch[index].start(0)
            elif stage < 4:
                patch[index].advance(stage)
            else:
                total = unfold_block(patch[index].gather(3), D // rows, FEAT // items)
                for c in range(CH // items):
                    at = c * PATCH * PATCH + index * 2 * PATCH
                    pw_ref[:, at : at + 2 * PATCH] = total[:, c * 2 * PATCH : (c + 1) * 2 * PATCH]
        elif index < STEPS + 3:
            n = index - STEPS
            if stage == 0:
                loads[n].start()
                square[n].start(0)
                return
            if stage == 1:
                loads[n].wait()
            if stage < 4:
                square[n].advance(stage)
            else:
                out = (sq0_ref, sq1_ref, sq2_ref)[n]
                out[...] = unfold_block(square[n].gather(3), *out.shape, odd=pos[0] == 1)
        else:
            part, out = ((early, earlyo_ref), (late, tapso_ref))[index - STEPS - 3]
            if stage < 4:
                part.advance(stage)
            else:
                out[...] = part.gather(3)

    opening, table = [], {}
    for when, index, stage in FINISH_PLAN:
        if stage > 0 or index < STEPS + 3:
            call = functools.partial(event, index, stage)
            if when == 0:
                opening.append(call)
            else:
                later = when - 1 + (far_steps - STEPS if when > 3 * STEPS else 0)
                table.setdefault((min(later, final_step), 0), []).append(call)

    @pl.when(t == 0)
    def _():
        @pl.when(row == final_row)
        def _():
            edge[2] = jnp.zeros(edge.shape[1:], BF)

        @pl.when(row == 0)
        def _():
            edge[3] = jnp.zeros(edge.shape[1:], BF)

        greet(sizes, pos, True, True)
        for k in range(1, rows):
            parcel(k).start()
        for call in opening:
            call()
        got[row] = tg_ref[:, row]
        arrived(2 * pos[1] + 1 - pos[0])
        unpack(pos[1], nx - 1)
        cw[...] = jnp.zeros_like(cw)

    @pl.when(t == STEPS)
    def _():
        for turn in range(nx - 1):
            xg = lax.rem(pos[1] + 1 + turn, nx)
            arrived(2 * xg)
            arrived(2 * xg + 1)
            unpack(xg, turn)
        total = jnp.zeros((1, D), F32)
        for s in range(tokens // 256):
            rs = slice(s * 256, (s + 1) * 256)
            total = total + col_sum(tgc[rs, :].astype(F32))
            tgt[:, rs] = tgc[rs, :].T
        lines_in = [sums2_ref[0:1], sums2_ref[1:2], sums2_ref[2:3], sums2_ref[3:4]]
        lines_in += [hbg_ref[:, n * D : (n + 1) * D] for n in range(FF // D)]
        lines_in += [sums1_ref[0:1], sums1_ref[1:2], qvs_ref[0:1], qvs_ref[1:2], total]
        cells = [one[:, k * 128 : (k + 1) * 128] for one in lines_in for k in range(D // 128)]
        early.start(0, jnp.concatenate(cells + [jnp.zeros((EARLY - len(cells), 128), F32)], axis=0))

    @pl.when((t >= STEPS) & (t < 2 * STEPS))
    def _():
        for q in range(2, STEPS):
            @pl.when(t == STEPS + q)
            def _(q=q):
                patch[q - 2].drain((0,))

        feats = FEAT // items
        slot = t % 2
        for n in range(FEAT // 256):
            grad = mm(tgt[...], act_ref[0, 0, :, n * 256 : (n + 1) * 256]).astype(BF)
            for c in range(256 // feats):
                i = n * (256 // feats) + c
                for r in range(rows):
                    block = grad[r * (D // rows) : (r + 1) * (D // rows), c * feats : (c + 1) * feats]
                    grads[slot, r % 2, r // 2, i % ny, i // ny] = fold_block(block)

    def stem_part(p, turn):
        weight = w_ref[...].reshape(FEAT, D)

        def at(s, size):
            return pl.ds(pl.multiple_of(turn * share + s * 256, 256), size)

        @pl.when(p == 0)
        def _():
            dxa[0, at(0, share), :] = jnp.zeros((share, 128), F32)

        for s in range(share // 256):
            rs = slice(s * 256, (s + 1) * 256)
            for n in range(FEAT // 256):
                cs = slice(n * 256, (n + 1) * 256)
                da = mm_t(tgc[at(s, 256), :], weight[cs, :])
                pg[rs, cs] = (slope_ref[0, 0, rs, cs].astype(F32) * da).astype(BF)
            back = mm_t(pg[rs, :], t_ref[...])
            dxa[p, at(s, 256), :] += back[:, 0:128]
            dxa[p + 1, at(s, 256), :] = back[:, 128:256]
        xt = jnp.concatenate([xt_ref[p, :, at(0, share)], xt_ref[p + 1, :, at(0, share)]], axis=0)
        cw[...] += mm(xt, pg[...])

    near, far = t < STEPS, (t >= 2 * STEPS) & (t < image_step)

    @pl.when(near | far)
    def _():
        stem_part(t % STEPS, jnp.where(near, nx - 1, t // STEPS - 2))

    @pl.when((t >= image_step - STEPS) & (t < image_step))
    def _():
        p = t % STEPS

        @pl.when(p == 0)
        def _():
            put_lines(0)
            for ch in range(CIN):
                head = mm_t(lines[0:group], sel_ref[ch * width : (ch + 1) * width, :])
                edge[0, ch] = (pltpu.roll(head, nrow - 1, 0) if nrow > 1 else head).astype(BF)

            @pl.when(row > 0)
            def _():
                edge_copy(0).start()

        @pl.when(p == STEPS - 1)
        def _():
            put_lines(SLABS - 1)
            for ch in range(CIN):
                tail = mm_t(lines[(WIN - 1) * group : WIN * group], sel_ref[ch * width : (ch + 1) * width, :])
                edge[1, ch] = (pltpu.roll(tail, group - nrow + 1, 0) if nrow > 1 else tail).astype(BF)

            @pl.when(row < final_row)
            def _():
                edge_copy(1).start()

            late.start(0, tap_grad_rows(cw[...]))

    @pl.when(t >= image_step)
    def _():
        ch = t - image_step

        @pl.when(t == image_step)
        def _():
            for j in range(1, SLABS - 1):
                put_lines(j)

            @pl.when(row < final_row)
            def _():
                edge_copy(0).wait_recv()

            @pl.when(row > 0)
            def _():
                edge_copy(1).wait_recv()

        patch_row = lax.broadcasted_iota(jnp.int32, (group, width), 0) % nrow
        res = mm_t(lines[...], sel_ref[pl.ds(pl.multiple_of(ch * width, width), width), :])
        head = res[0:group]
        tail = res[(PATCH + 1) * group : (PATCH + 2) * group]
        for r in range(PATCH):
            v = res[(r + 1) * group : (r + 2) * group]
            if r == 0:
                v = v + jnp.where(patch_row == 0, edge[3, ch].astype(F32), pltpu.roll(tail, 1, 0))
            if r == PATCH - 1:
                v = v + jnp.where(patch_row == nrow - 1, edge[2, ch].astype(F32), pltpu.roll(head, group - 1, 0))
            flat[0, pl.ds(r, group, stride=PATCH), :] = v[:, 0:128]
            flat[1, pl.ds(r, group, stride=PATCH), :] = v[:, 128:256]
        for n in range(count):
            at = slice(n * height, (n + 1) * height)
            ig_ref[n, 0, :, 0:128] = flat[0, at, :]
            ig_ref[n, 0, :, 128:256] = flat[1, at, :]

    def close():
        for part in square:
            part.drain()
        for q, part in enumerate(patch):
            part.drain((1, 2, 3) if q < STEPS - 2 else (0, 1, 2, 3))
        early.drain()
        late.drain()
        for k in range(1, rows):
            parcel(k).wait_send()

        @pl.when(row > 0)
        def _():
            edge_copy(0).wait_send()

        @pl.when(row < final_row)
        def _():
            edge_copy(1).wait_send()

    table.setdefault((final_step, 0), []).append(close)
    run_events(t, table, (0,))


def finish(tg, saved, weight, xt, taps, sel, squares, sums2, hbg, sums1, qvs, count, height, sizes):
    nc, nx, ny, nz = sizes
    items, rows = ny * nz, nc * nx
    group = count * height // PATCH
    tokens = group * NP
    feats = FEAT // items
    square = squares.shape[5:]
    share = tokens // nx
    image_step = STEPS * (nx + 1)

    def clip(v, low, high):
        return jnp.minimum(jnp.maximum(v, low), high)

    def sub(t):
        held = jnp.where(t < STEPS, t, jnp.where(t < 2 * STEPS, 0, t % STEPS))
        return jnp.where(t < image_step, held, STEPS - 1)

    def turn(t):
        return jnp.where(t < STEPS, nx - 1, clip(t // STEPS - 2, 0, nx - 2))

    return pl.pallas_call(
        functools.partial(finish_kernel, sizes),
        name="finish",
        grid=(image_step + CIN,),
        in_specs=[
            whole(tg.shape),
            pl.BlockSpec((1, 1, tokens, FEAT), lambda t: (clip(t - STEPS, 0, STEPS - 1), 0, 0, 0)),
            pl.BlockSpec((1, 1, share, FEAT), lambda t: (sub(t), 1, turn(t), 0)),
            pl.BlockSpec((CH, 1, 2 * PATCH, D), lambda t: (0, sub(t), 0, 0)),
            whole(xt.shape),
            whole(taps.shape),
            whole(sel.shape),
            pl.BlockSpec(memory_space=pl.ANY),
            whole(sums2.shape), whole(hbg.shape), whole(sums1.shape), whole(qvs.shape),
        ],
        out_specs=(
            whole((D // rows, PF // items)),
            whole((D // items, D // rows)),
            whole((D // items, D // rows)),
            whole((D // items, D // rows)),
            pl.BlockSpec((count, 1, height, IMG), lambda t: (0, clip(t - image_step, 0, CIN - 1), 0, 0)),
            whole((EARLY, 128)),
            whole((32, 128)),
        ),
        out_shape=(
            jax.ShapeDtypeStruct((D // rows, PF // items), F32),
            jax.ShapeDtypeStruct((D // items, D // rows), F32),
            jax.ShapeDtypeStruct((D // items, D // rows), F32),
            jax.ShapeDtypeStruct((D // items, D // rows), F32),
            jax.ShapeDtypeStruct((count, CIN, height, IMG), F32),
            jax.ShapeDtypeStruct((EARLY, 128), F32),
            jax.ShapeDtypeStruct((32, 128), F32),
        ),
        scratch_shapes=[
            pltpu.VMEM((tokens, D), BF),
            pltpu.VMEM((D, tokens), BF),
            pltpu.VMEM((SLABS, tokens, 128), F32),
            pltpu.VMEM((share, FEAT), BF),
            pltpu.VMEM((4 * HALF, FEAT), F32),
            pltpu.VMEM((WIN * group, NP * HALF), BF),
            pltpu.VMEM((2, group * PATCH, 128), F32),
            pltpu.VMEM((2,) + sizes + folded_shape(D // rows, feats), BF),
            pltpu.VMEM((4, CIN, group, IMG), BF),
            pltpu.SemaphoreType.DMA((2,)),
            pltpu.SemaphoreType.DMA((2,)),
            pltpu.VMEM((rows, SEQ_ITEMS, tokens // rows // SEQ_ITEMS, D), BF),
            pltpu.SemaphoreType.DMA((rows - 1,)),
            pltpu.SemaphoreType.DMA((rows,)),
            pltpu.VMEM((D // 128, share, 128), F32),
        ]
        + piece_scratch(sizes, FINISH_ORDERS[0:STEPS], folded_shape(D // rows, feats))
        + piece_scratch(sizes, FINISH_ORDERS[STEPS : STEPS + 3], square) + own_scratch(sizes, 3, square)
        + small_scratch(sizes, EARLY)
        + small_scratch(sizes, 32),
        compiler_params=params(collective_id=2, has_side_effects=True),
    )(tg, saved, saved, weight, xt, taps, sel, squares, sums2, hbg, sums1, qvs)


def feature_parts(rows):
    feat = lax.broadcasted_iota(jnp.int32, (rows, FEAT), 1)
    return feat // (2 * PATCH), feat // PATCH % 2, feat % PATCH


def tap_rows(wide, ch, r, b, half):
    parts = []
    for r2 in range(2):
        a = r - r2
        parts.append(wide[9 * ch + 3 * a + b : 9 * ch + 3 * a + b + 1, :] if 0 <= a < 3 else jnp.zeros((1, FEAT), F32))
    return jnp.where(half == 0, parts[0], parts[1])


def tap_matrix(cw_ref, cb_ref, t_ref):
    chan, _, _ = feature_parts(32)
    expand = jnp.where(chan == lax.broadcasted_iota(jnp.int32, (32, FEAT), 0), 1.0, 0.0).astype(BF)
    wide = lax.dot_general(cw_ref[...], expand, (((0,), (0,)), ((), ())), preferred_element_type=F32)
    bias = mm(jnp.broadcast_to(as_row(cb_ref), (8, CH)).astype(BF), expand)
    _, half, spot = feature_parts(1)
    line = lax.broadcasted_iota(jnp.int32, (HALF, FEAT), 0)
    for r in range(4):
        block = jnp.zeros((HALF, FEAT), F32)
        if r == 0:
            block = jnp.where(line == ONE_LANE, bias[0:1, :], block)
        for ch in range(CIN):
            for b in range(3):
                block = jnp.where(line == WIN * ch + b + spot, tap_rows(wide, ch, r, b, half), block)
        t_ref[r * HALF : (r + 1) * HALF, :] = block.astype(BF)


def tap_grad_rows(full):
    chan, half, spot = feature_parts(1)
    line = lax.broadcasted_iota(jnp.int32, (HALF, FEAT), 0)
    sums = [[None] * 3 for _ in range(9)]
    for r in range(4):
        block = full[r * HALF : (r + 1) * HALF]
        for ch in range(CIN):
            for b in range(3):
                line_sum = jnp.sum(jnp.where(line == WIN * ch + b + spot, block, 0.0), axis=0, keepdims=True)
                for a in range(3):
                    if 0 <= r - a < 2:
                        part = jnp.where(half == r - a, line_sum, 0.0)
                        old = sums[3 * ch + b][a]
                        sums[3 * ch + b][a] = part if old is None else old + part
    lines = [sums[3 * ch + b][a] for ch in range(CIN) for a in range(3) for b in range(3)]
    lines.append(full[ONE_LANE : ONE_LANE + 1])
    lines.append(jnp.zeros((4, FEAT), F32))
    table = jnp.concatenate(lines, axis=0)
    chan, _, _ = feature_parts(128)
    expand = jnp.where(chan == lax.broadcasted_iota(jnp.int32, (128, FEAT), 0), 1.0, 0.0).astype(BF)
    hi, mid, lo = three_terms(table)
    return mm_t(hi, expand) + (mm_t(mid, expand) + mm_t(lo, expand))


def on_device(
    images, item_segment, conv_weight, conv_bias, patch_weight, patch_bias, norm1_gain, norm1_bias,
    query_weight, query_bias, key_weight, value_weight, value_bias, output_weight, output_bias,
    norm2_gain, norm2_bias, hidden_weight, hidden_bias, result_weight, result_bias, cotangent,
):
    items, rows = lax.axis_size("items"), lax.axis_size("rows")
    sizes = grid_sizes(items, rows)
    count, _, height, _ = images.shape
    nrow = height // PATCH

    cw = conv_weight.reshape(CH, 27)
    weight4 = patch_weight.reshape(CH, STEPS, 2 * PATCH, D)
    tokens, saved, xt, sel, taps = stem_forward(images, cw, conv_bias, weight4, patch_bias, sizes)
    tokens = tokens.reshape(TOK, D)
    q, k, v, attended, attended32, lx, kx = attend(
        tokens, (norm1_gain, norm1_bias, query_bias, value_bias), item_segment, query_weight, key_weight, value_weight)
    block_out, middle_grad, attended_grad, wo_grad, wh_grad, wr_grad, sums2, hb_grad = mixer(
        tokens, attended, cotangent, output_weight,
        (output_bias, norm2_gain, norm2_bias, result_bias, hidden_bias), hidden_weight, result_weight, sizes,
    )
    token_grad, squares, sums1, qvs, wh_grad, wr_grad, wo_grad = attend_back(
        tokens, norm1_gain, norm1_bias, kx, middle_grad, q, k, v, attended32, attended_grad, lx,
        query_weight, key_weight, value_weight, wh_grad, wr_grad, wo_grad, sizes,
    )
    token_grad = token_grad.reshape(SEQ_ITEMS, rows, nrow * NP, D)
    pw_grad, wq_grad, wk_grad, wv_grad, image_grad, sums, tap_grads = finish(
        token_grad, saved, weight4, xt, taps, sel, squares, sums2, hb_grad, sums1, qvs, count, height, sizes
    )
    wide = D // 128

    def row_of(at):
        return sums[at * wide : (at + 1) * wide].reshape(D)

    return (
        block_out,
        image_grad,
        tap_grads[0:27, 0:CH].T.reshape(conv_weight.shape),
        tap_grads[27, 0:CH],
        pw_grad.T,
        row_of(12),
        row_of(8),
        row_of(9),
        wq_grad,
        row_of(10),
        wk_grad,
        wv_grad,
        row_of(11),
        wo_grad,
        row_of(2),
        row_of(0),
        row_of(1),
        wh_grad,
        sums[4 * wide : 8 * wide].reshape(FF),
        wr_grad.T,
        row_of(3),
    )


def solution(mesh):
    split = P("items", "rows")
    flat = P(("items", "rows"), None)
    image = P("items", None, "rows", None)
    return jax.shard_map(
        on_device,
        mesh=mesh,
        in_specs=(image, P("items")) + (P(),) * 19 + (flat,),
        out_specs=(
            flat, image, P(), P(), split, P(), P(), P(), split, P(), split, split,
            P(), split, P(), P(), P(), split, P(), split, P(),
        ),
        check_vma=False,
    )
```

```python
import functools

import jax
import jax.numpy as jnp
from jax import lax
from jax.experimental import pallas as pl
from jax.experimental.pallas import tpu as pltpu
from jax.sharding import PartitionSpec as P

BF = jnp.bfloat16
F32 = jnp.float32
D = 768
HEADS = 12
HD = 64
FF = 3072
IMG = 256
PATCH = 16
CH = 32
CIN = 3
SEQ_ITEMS = 4
NPATCH = 256
TOK = 1024
NP = IMG // PATCH
PF = CH * PATCH * PATCH
HALF = 64
WIN = PATCH + 2
ONE_LANE = CIN * WIN
SLABS = (PATCH + 2) // 2
STEPS = PATCH // 2
FEAT = PF // STEPS
GELU_A = 0.7978845608028654
GELU_B = GELU_A * 0.044715
VMEM_CAP = 60 * 1024 * 1024


def mm(left, right):
    return jnp.dot(left, right, preferred_element_type=F32)


def mm_t(left, right):
    return lax.dot_general(left, right, (((1,), (1,)), ((), ())), preferred_element_type=F32)


def params(**extra):
    return pltpu.CompilerParams(vmem_limit_bytes=VMEM_CAP, **extra)


def whole(shape):
    zeros = (0,) * len(shape)
    return pl.BlockSpec(shape, lambda *_: zeros, pipeline_mode=pl.Buffered(1))


def gelu_pair_low(v):
    bend = jnp.tanh((v * (GELU_A + GELU_B * (v * v))).astype(BF))
    low = v.astype(BF)
    gate = bend * BF(0.5) + BF(0.5)
    act = low * gate
    slope = gate + act * (BF(1.0) - gate) * (BF(2.0 * GELU_A) + BF(6.0 * GELU_B) * (low * low))
    return act, slope


def as_row(ref, at=None):
    line = ref[...] if at is None else ref[at]
    return line.astype(F32).reshape(1, line.shape[0])


def gelu_pair(v):
    square = v * v
    gate = 0.5 + 0.5 * jnp.tanh(v * (GELU_A + GELU_B * square))
    act = v * gate
    slope = gate + act * (1.0 - gate) * (2.0 * GELU_A + (6.0 * GELU_B) * square)
    return act, slope


MESH = pl.DeviceIdType.MESH


def grid_sizes(items, rows):
    nx = rows // 2
    ny = nx if items % nx == 0 else 1
    return (2, nx, ny, items // ny)


def place(sizes):
    item, row = lax.axis_index("items"), lax.axis_index("rows")
    return (row % 2, row // 2, item % sizes[2], item // sizes[2])


def peer(sizes, pos, axis, k):
    moved = list(pos)
    moved[axis] = lax.rem(pos[axis] + k, sizes[axis])
    return (moved[3] * sizes[2] + moved[2], moved[1] * 2 + moved[0]), moved[axis]


def greet(sizes, pos, near, far):
    barrier = pltpu.get_barrier_semaphore()
    item, row, rows = lax.axis_index("items"), lax.axis_index("rows"), 2 * sizes[1]
    peers = [(item, lax.rem(row + k, rows)) for k in range(1, rows)] if near else []
    for axis in (2, 3) if far else ():
        peers += [peer(sizes, pos, axis, k)[0] for k in range(1, sizes[axis])]
    for device in peers:
        pl.semaphore_signal(barrier, inc=1, device_id=device, device_id_type=MESH)
    pl.semaphore_wait(barrier, len(peers))


def turn_of(sizes, pos, x):
    return lax.rem(x + 2 * sizes[1] - 1 - pos[1], sizes[1])


def add_up(first, rest):
    total = first.astype(F32)
    for term in rest:
        total = total + term.astype(F32)
    return total


class Piece:
    def __init__(self, sizes, pos, order, source, own, bufs, send, recv):
        self.sizes, self.pos = sizes, pos
        self.source, self.own, self.bufs = source, own, bufs
        self.send, self.recv = send, recv
        self.axes = (0,) + order

    def at(self, stage, where):
        left = sorted(self.axes[stage:])
        return (slice(None),) * left.index(self.axes[stage]) + (where,)

    def copies(self, stage):
        out = []
        for k in range(1, self.sizes[self.axes[stage]]):
            device, there = peer(self.sizes, self.pos, self.axes[stage], k)
            if stage == 0:
                src, dst = self.source.at[there], self.bufs[0]
            else:
                held = self.at(stage, there)
                src = self.bufs[0].at[held] if stage == 1 else self.bufs[stage - 1].at[(0,) + held]
                dst = self.bufs[stage].at[k - 1]
            out.append(
                pltpu.make_async_remote_copy(
                    src_ref=src, dst_ref=dst, send_sem=self.send.at[stage, k - 1], recv_sem=self.recv.at[stage, k - 1],
                    device_id=device, device_id_type=MESH,
                )
            )
        return out

    def start(self, stage):
        for copy in self.copies(stage):
            copy.start()

    def gather(self, stage):
        for copy in self.copies(stage):
            copy.wait_recv()
        bufs = self.bufs
        if stage == 0:
            bufs[0][...] = bufs[0][...] + self.own[...]
            return None
        held = self.at(stage, self.pos[self.axes[stage]])
        base = bufs[0][held] if stage == 1 else bufs[stage - 1][(0,) + held]
        terms = self.sizes[self.axes[stage]] - 1
        if stage < 3 and terms == 1:
            bufs[stage][0] = base + bufs[stage][0]
            return None
        total = add_up(base, [bufs[stage][k] for k in range(terms)])
        if stage == 3:
            return total
        bufs[stage][0] = total.astype(BF)

    def advance(self, stage):
        self.gather(stage - 1)
        self.start(stage)

    def drain(self, stages=(0, 1, 2, 3)):
        for stage in stages:
            for copy in self.copies(stage):
                copy.wait_send()


def piece_scratch(sizes, orders, shape):
    out = []
    for order in orders:
        out.append(pltpu.VMEM(sizes[1:] + shape, BF))
        for stage in range(3):
            left = tuple(sizes[axis] for axis in sorted(order[stage + 1 :]))
            out.append(pltpu.VMEM((sizes[order[stage]] - 1,) + left + shape, BF))
    sems = pltpu.SemaphoreType.DMA((len(orders), 4, max(sizes) - 1))
    return out + [sems, sems]


def own_scratch(sizes, count, shape):
    return [pltpu.VMEM((count,) + sizes[1:] + shape, BF), pltpu.SemaphoreType.DMA((count,))]


def make_pieces(sizes, pos, orders, sources, owns, refs):
    count = len(orders)
    return [
        Piece(sizes, pos, orders[n], sources[n], owns[n], refs[4 * n : 4 * n + 4], refs[4 * count].at[n], refs[4 * count + 1].at[n])
        for n in range(count)
    ]


class SmallSum:
    def __init__(self, sizes, pos, bufs, send, recv):
        self.sizes, self.pos, self.bufs, self.send, self.recv = sizes, pos, bufs, send, recv

    def copies(self, axis, receive):
        buf, here = self.bufs[axis], self.pos[axis]
        out = []
        for k in range(1, self.sizes[axis]):
            device, _ = peer(self.sizes, self.pos, axis, k)
            slot = lax.rem(here + self.sizes[axis] - k, self.sizes[axis]) if receive else here
            out.append(
                pltpu.make_async_remote_copy(
                    src_ref=buf.at[here], dst_ref=buf.at[slot], send_sem=self.send.at[axis, k - 1],
                    recv_sem=self.recv.at[axis, k - 1], device_id=device, device_id_type=MESH,
                )
            )
        return out

    def start(self, axis, value):
        self.bufs[axis][self.pos[axis]] = value
        for copy in self.copies(axis, False):
            copy.start()

    def gather(self, axis):
        for copy in self.copies(axis, True):
            copy.wait_recv()
        total = self.bufs[axis][0]
        for k in range(1, self.sizes[axis]):
            total = total + self.bufs[axis][k]
        return total

    def advance(self, axis):
        self.start(axis, self.gather(axis - 1))

    def drain(self):
        for axis in range(4):
            for copy in self.copies(axis, False):
                copy.wait_send()


def small_scratch(sizes, shape):
    return [pltpu.VMEM((size,) + shape, F32) for size in sizes] + [
        pltpu.SemaphoreType.DMA((4, max(sizes) - 1)),
        pltpu.SemaphoreType.DMA((4, max(sizes) - 1)),
    ]


def folds(width):
    return width % 128 == HALF and width > 128


def narrow(width):
    return 128 // width if width < 128 and 128 % width == 0 else 1


def folded_shape(height, width):
    if folds(width) or narrow(width) > 1:
        return (height * width // 128, 128)
    return (height, width)


def fold_block(block):
    height, width = block.shape
    if narrow(width) > 1:
        part = height // narrow(width)
        return jnp.concatenate([block[k * part : (k + 1) * part] for k in range(narrow(width))], axis=1)
    return block


def unfold_block(block, height, width, odd=False):
    if narrow(width) > 1:
        return jnp.concatenate([block[:, k * width : (k + 1) * width] for k in range(narrow(width))], axis=0)
    if not folds(width):
        return block
    main, side = block[:height], block[height:]
    side = jnp.concatenate([side[:, :HALF], side[:, HALF:]], axis=0)
    return jnp.where(odd, jnp.concatenate([side, main], axis=1), jnp.concatenate([main, side], axis=1))


def run_events(step, table, slots):
    for (when, slot), todo in table.items():
        if slot in slots:
            @pl.when(step == when)
            def _(todo=todo):
                for call in todo:
                    call()


def make_windows(sizes, pos, img_ref, edge, edge_copies, x, xt_ref, sel_ref, pix, lines):
    items, _, height, width = img_ref.shape
    nrow = height // PATCH
    group = items * nrow
    row, final_row = lax.axis_index("rows"), lax.axis_size("rows") - 1
    for ch in range(CIN):
        for item in range(items):
            full = img_ref[item, ch].astype(F32)
            for k in range(width // 128):
                pix[ch, k, item * height : (item + 1) * height, :] = full[:, k * 128 : (k + 1) * 128]

    def line(ch, r):
        return jnp.concatenate([pix[ch, k, pl.ds(r, group, stride=PATCH), :] for k in range(width // 128)], axis=1)

    for ch in range(CIN):
        first, final = line(ch, 0), line(ch, PATCH - 1)
        edge[0, ch] = pltpu.roll(first, nrow - 1, 0).astype(BF)
        edge[1, ch] = pltpu.roll(final, group - nrow + 1, 0).astype(BF)

    @pl.when(row > 0)
    def _():
        edge_copies[0].start()

    @pl.when(row < final_row)
    def _():
        edge_copies[1].start()

    for ch in range(CIN):
        cols = slice(ch * width, (ch + 1) * width)
        for r in range(PATCH):
            lines[(r + 1) * group : (r + 2) * group, cols] = line(ch, r).astype(BF)
    lane = lax.broadcasted_iota(jnp.int32, (1, NP * HALF), 1)
    col, spot = lane // HALF, lane % HALF
    for ch in range(CIN):
        inside = (spot >= WIN * ch) & (spot < WIN * (ch + 1))
        want = jnp.where(inside, PATCH * col + spot - WIN * ch - 1, -5)
        here = lax.broadcasted_iota(jnp.int32, (width, NP * HALF), 0)
        sel_ref[ch * width : (ch + 1) * width, :] = jnp.where(here == want, 1.0, 0.0).astype(BF)

    @pl.when(row < final_row)
    def _():
        edge_copies[0].wait_recv()

    @pl.when(row > 0)
    def _():
        edge_copies[1].wait_recv()

    patch_row = lax.broadcasted_iota(jnp.int32, (group, width), 0) % nrow
    for ch in range(CIN):
        cols = slice(ch * width, (ch + 1) * width)
        up = jnp.where(patch_row == 0, edge[3, ch].astype(F32), pltpu.roll(line(ch, PATCH - 1), 1, 0))
        lines[0:group, cols] = up.astype(BF)
        down = jnp.where(patch_row == nrow - 1, edge[2, ch].astype(F32), pltpu.roll(line(ch, 0), group - 1, 0))
        lines[(PATCH + 1) * group : (PATCH + 2) * group, cols] = down.astype(BF)
    lane = lax.broadcasted_iota(jnp.int32, (group, 2 * HALF), 1)
    low = lane < HALF
    ones = (lane % HALF) == ONE_LANE
    nx = sizes[1]
    share, per = items * nrow * NP // nx, group // nx
    turns = [turn_of(sizes, pos, xg) * share for xg in range(nx)]

    def put(j, c, block):
        low_bits = block.astype(BF)
        for xg in range(nx):
            x[j, pl.ds(pl.multiple_of(turns[xg] + c * per, per), per), :] = low_bits[xg * per : (xg + 1) * per]

    for quarter in range(NP * HALF // 256):
        res = mm(lines[...], sel_ref[:, quarter * 256 : (quarter + 1) * 256])
        for j in range(SLABS):
            first = res[2 * j * group : (2 * j + 1) * group]
            second = res[(2 * j + 1) * group : (2 * j + 2) * group]
            for pair in range(2):
                a = first[:, pair * 128 : (pair + 1) * 128]
                b = second[:, pair * 128 : (pair + 1) * 128]
                put(j, quarter * 4 + pair * 2, jnp.where(ones, 1.0, jnp.where(low, a, pltpu.roll(b, HALF, 1))))
                put(j, quarter * 4 + pair * 2 + 1, jnp.where(ones, 1.0, jnp.where(low, pltpu.roll(a, HALF, 1), b)))
    for j in range(SLABS):
        xt_ref[j] = x[j].T


def stem_kernel(sizes, img_ref, cw_ref, cb_ref, w_ref, pb_ref, tok_ref, saved_ref, xt_ref, sel_ref, t_ref,
                x, pix, lines, edge, edge_send, edge_recv, acc, nat, parcel, got, send, recv):
    t = pl.program_id(0)
    p = t % STEPS
    nx = sizes[1]
    rows = 2 * nx
    pos = place(sizes)
    item, row, final_row = lax.axis_index("items"), lax.axis_index("rows"), lax.axis_size("rows") - 1
    share = acc.shape[0]
    per = share // NP

    def edge_copy(n):
        return pltpu.make_async_remote_copy(
            src_ref=edge.at[n], dst_ref=edge.at[2 + n], send_sem=edge_send.at[n], recv_sem=edge_recv.at[n],
            device_id=(item, row + (2 * n - 1)), device_id_type=MESH,
        )

    @pl.when(t == 0)
    def _():
        @pl.when(row == final_row)
        def _():
            edge[2] = jnp.zeros(edge.shape[1:], BF)

        @pl.when(row == 0)
        def _():
            edge[3] = jnp.zeros(edge.shape[1:], BF)

        greet(sizes, pos, True, False)
        tap_matrix(cw_ref, cb_ref, t_ref)
        make_windows(sizes, pos, img_ref, edge, [edge_copy(0), edge_copy(1)], x, xt_ref, sel_ref, pix, lines)

    @pl.when(p == 0)
    def _():
        acc[...] = jnp.broadcast_to(as_row(pb_ref), acc.shape)

    weight = w_ref[...].reshape(FEAT, D)
    for s in range(share // 256):
        rs = slice(s * 256, (s + 1) * 256)
        here = pl.ds(pl.multiple_of(t // STEPS * share + s * 256, 256), 256)
        xs = jnp.concatenate([x[p, here, :], x[p + 1, here, :]], axis=1)
        for n in range(FEAT // 256):
            cs = slice(n * 256, (n + 1) * 256)
            act, slope = gelu_pair_low(mm(xs, t_ref[:, cs]))
            saved_ref[0, 0, rs, cs] = act
            saved_ref[0, 1, rs, cs] = slope
        acc[rs, :] += mm(saved_ref[0, 0, rs, :], weight)

    @pl.when(p == STEPS - 1)
    def _():
        for c in range(NP):
            for k in range(D // 128):
                nat[k, pl.ds(c, per, stride=NP), :] = acc[c * per : (c + 1) * per, k * 128 : (k + 1) * 128]

    def parcel_copy(turn, core, slot):
        to = lax.rem(pos[1] + 1 + turn, nx) * 2 + core
        return pltpu.make_async_remote_copy(
            src_ref=parcel.at[turn, core], dst_ref=got.at[:, row], send_sem=send.at[turn, slot], recv_sem=recv.at[row],
            device_id=(item, to), device_id_type=MESH,
        )

    for turn in range(nx):
        @pl.when(t == turn * STEPS + STEPS - 1)
        def _(turn=turn):
            for k in range(D // 128):
                cut = nat[k].astype(BF).reshape(parcel.shape[1:4] + (128,))
                parcel[turn, :, :, :, k * 128 : (k + 1) * 128] = cut
            if turn < nx - 1:
                for core in range(2):
                    parcel_copy(turn, core, core).start()
            else:
                parcel_copy(turn, 1 - pos[0], 0).start()
                got[:, row] = parcel[turn, pos[0]]

    @pl.when(t == nx * STEPS - 1)
    def _():
        for k in range(1, rows):
            source = lax.rem(row + k, rows)
            pltpu.make_async_remote_copy(
                src_ref=parcel.at[0, 0], dst_ref=got.at[:, source], send_sem=send.at[0, 0], recv_sem=recv.at[source],
                device_id=(item, source), device_id_type=MESH,
            ).wait_recv()
        tok_ref[...] = got[...]
        for turn in range(nx - 1):
            for core in range(2):
                parcel_copy(turn, core, core).wait_send()
        parcel_copy(nx - 1, 1 - pos[0], 0).wait_send()

        @pl.when(row > 0)
        def _():
            edge_copy(0).wait_send()

        @pl.when(row < final_row)
        def _():
            edge_copy(1).wait_send()


def stem_forward(images, cw, cb, weight, bias, sizes):
    count, _, height, width = images.shape
    nx = sizes[1]
    nrow = height // PATCH
    group = count * nrow
    tokens = group * NP
    share = tokens // nx
    arrived = (SEQ_ITEMS, 2 * nx, nrow * NP, D)
    return pl.pallas_call(
        functools.partial(stem_kernel, sizes),
        name="stem_forward",
        grid=(nx * STEPS,),
        in_specs=[
            whole(images.shape),
            whole(cw.shape),
            whole(cb.shape),
            pl.BlockSpec((CH, 1, 2 * PATCH, D), lambda t: (0, t % STEPS, 0, 0)),
            whole(bias.shape),
        ],
        out_specs=(
            whole(arrived),
            pl.BlockSpec((1, 2, share, FEAT), lambda t: (t % STEPS, 0, t // STEPS, 0)),
            whole((SLABS, 128, tokens)),
            whole((CIN * width, NP * HALF)),
            whole((4 * HALF, FEAT)),
        ),
        out_shape=(
            jax.ShapeDtypeStruct(arrived, BF),
            jax.ShapeDtypeStruct((STEPS, 2, tokens, FEAT), BF),
            jax.ShapeDtypeStruct((SLABS, 128, tokens), BF),
            jax.ShapeDtypeStruct((CIN * width, NP * HALF), BF),
            jax.ShapeDtypeStruct((4 * HALF, FEAT), BF),
        ),
        scratch_shapes=[
            pltpu.VMEM((SLABS, tokens, 128), BF),
            pltpu.VMEM((CIN, width // 128, count * height, 128), F32),
            pltpu.VMEM((WIN * group, CIN * width), BF),
            pltpu.VMEM((4, CIN, group, width), BF),
            pltpu.SemaphoreType.DMA((2,)),
            pltpu.SemaphoreType.DMA((2,)),
            pltpu.VMEM((share, D), F32),
            pltpu.VMEM((D // 128, share, 128), F32),
            pltpu.VMEM((nx, 2, SEQ_ITEMS, nrow * NP, D), BF),
            pltpu.VMEM(arrived, BF),
            pltpu.SemaphoreType.DMA((nx, 2)),
            pltpu.SemaphoreType.DMA((2 * nx,)),
        ],
        compiler_params=params(collective_id=0, has_side_effects=True),
    )(images, cw, cb, weight, bias)


def norm_stats(v):
    centred = v - jnp.mean(v, axis=-1, keepdims=True)
    inv = lax.rsqrt(jnp.mean(centred * centred, axis=-1, keepdims=True) + 1e-06)
    return centred * inv, inv


def three_terms(v):
    hi = v.astype(BF)
    rest = v - hi.astype(F32)
    mid = rest.astype(BF)
    lo = (rest - mid.astype(F32)).astype(BF)
    return hi, mid, lo


def minus_terms(v, lane, base):
    rest = -v - (-v).astype(BF).astype(F32)
    return jnp.where(lane == 4, -v, jnp.where(lane == 5, rest, base)).astype(BF)


def attend_kernel(tok_ref, g_ref, b_ref, qb_ref, vb_ref, seg_ref, wq_ref, wk_ref, wv_ref,
                  q_ref, k_ref, v_ref, o_ref, o32_ref, lx_ref, kx_ref, n1, kaug, vaug):
    step = pl.program_id(0)
    line = lax.broadcasted_iota(jnp.int32, (1, 128), 1)
    first_item = lax.axis_index("rows") * SEQ_ITEMS
    same = [line == seg_ref[first_item + i] for i in range(SEQ_ITEMS)]
    terms = jnp.where((line >= 4) & (line < 6), 1.0, 0.0)
    keys_in = [jnp.where((line < 4) & ~one, -1e30, terms) for one in same]

    @pl.when(step == 0)
    def _():
        kx_ref[...] = jnp.concatenate(keys_in + [jnp.zeros((8 - SEQ_ITEMS, 128), F32)], axis=0)
        for s in range(TOK // 128):
            rs = slice(s * 128, (s + 1) * 128)
            hat, _ = norm_stats(tok_ref[rs, :].astype(F32))
            n1[rs, :] = (hat * as_row(g_ref) + as_row(b_ref)).astype(BF)

    own = pl.ds(pl.multiple_of(step * 256, 256), 256)
    q_ref[...] = ((mm(n1[...], wq_ref[...]) + as_row(qb_ref, own)).astype(BF) * 0.125).astype(BF)
    k_ref[...] = mm(n1[...], wk_ref[...]).astype(BF)
    v_ref[...] = (mm(n1[...], wv_ref[...]) + as_row(vb_ref, own)).astype(BF)
    lane = lax.broadcasted_iota(jnp.int32, (NPATCH, 128), 1)
    low = lane < HD
    for i in range(SEQ_ITEMS):
        rs = slice(i * NPATCH, (i + 1) * NPATCH)
        kaug[rs, 128:256] = jnp.broadcast_to(keys_in[i], (NPATCH, 128)).astype(BF)
        vaug[rs, 128:256] = jnp.ones((NPATCH, 128), BF)
    for pair in range(2):
        cs = slice(pair * 128, (pair + 1) * 128)
        kaug[:, 0:128] = k_ref[:, cs]
        vaug[:, 0:128] = v_ref[:, cs]
        for i in range(SEQ_ITEMS):
            rs = slice(i * NPATCH, (i + 1) * NPATCH)
            span = slice(0, (i + 1) * NPATCH)
            qp = q_ref[rs, cs]
            qx = jnp.broadcast_to(jnp.where(same[i], 1.0, 0.0), (NPATCH, 128))
            halves = []
            for h in range(2):
                mine = low if h == 0 else ~low
                qaug = jnp.concatenate([jnp.where(mine, qp, jnp.zeros_like(qp)), qx.astype(BF)], axis=1)
                scores = mm_t(qaug, kaug[span, :])
                top = jnp.max(scores, axis=1, keepdims=True)
                raised = jnp.exp(scores - top).astype(BF)
                out = mm(raised, vaug[span, :])
                total = out[:, 128:256]
                halves.append(out[:, 0:128] / total)
                lx_ref[pair * 2 + h, rs, :] = minus_terms(top + jnp.log(total), lane, qx)
            out = jnp.where(low, halves[0], halves[1])
            o32_ref[rs, cs] = out
            o_ref[rs, cs] = out.astype(BF)


def attend(tokens, vecs, segments, wq, wk, wv):
    lines = [whole(vec.shape) for vec in vecs]
    col = pl.BlockSpec((D, 256), lambda g: (0, g))
    out = pl.BlockSpec((TOK, 256), lambda g: (0, g))
    return pl.pallas_call(
        attend_kernel,
        name="attend",
        grid=(D // 256,),
        in_specs=[whole((TOK, D))] + lines + [pl.BlockSpec(memory_space=pltpu.SMEM), col, col, col],
        out_specs=(out, out, out, out, out, pl.BlockSpec((4, TOK, 128), lambda g: (g, 0, 0)), whole((8, 128))),
        out_shape=(jax.ShapeDtypeStruct((TOK, D), BF),) * 4
        + (
            jax.ShapeDtypeStruct((TOK, D), F32),
            jax.ShapeDtypeStruct((HEADS, TOK, 128), BF),
            jax.ShapeDtypeStruct((8, 128), F32),
        ),
        scratch_shapes=[pltpu.VMEM((TOK, D), BF), pltpu.VMEM((TOK, 256), BF), pltpu.VMEM((TOK, 256), BF)],
        compiler_params=params(),
    )(tokens, *vecs, segments, wq, wk, wv)


def norm_back(e, hat, inv, gain):
    f = e * gain
    return inv * (f - jnp.mean(f, axis=-1, keepdims=True) - hat * jnp.mean(f * hat, axis=-1, keepdims=True))


def col_sum(v):
    return jnp.sum(v, axis=0, keepdims=True)


def store_square(ref, n, grad):
    _, _, nx, ny, nz, _, _ = ref.shape
    height, width = D // (ny * nz), D // (2 * nx)
    if not folds(width):
        for r in range(2 * nx):
            part = grad[:, r * width : (r + 1) * width]
            for i in range(ny * nz):
                ref[n, r % 2, r // 2, i % ny, i // ny] = part[i * height : (i + 1) * height]
        return
    half = height // 2
    low = lax.broadcasted_iota(jnp.int32, (half, 128), 1) < HALF
    for x in range(nx):
        base = 2 * x * width
        shared = grad[:, base + 128 : base + 256]
        turned = jnp.concatenate([shared[:, HALF:], shared[:, :HALF]], axis=1)
        for i in range(ny * nz):
            top, end = i * height, (i + 1) * height
            mid = top + half
            ref[n, 0, x, i % ny, i // ny, 0:height] = grad[top:end, base : base + 128]
            ref[n, 0, x, i % ny, i // ny, height:] = jnp.where(low, shared[top:mid], turned[mid:end])
            ref[n, 1, x, i % ny, i // ny, 0:height] = grad[top:end, base + 256 : base + 384]
            ref[n, 1, x, i % ny, i // ny, height:] = jnp.where(low, turned[top:mid], shared[mid:end])


def mixer_kernel(tok_ref, att_ref, cot_ref, wo_ref, ob_ref, g_ref, b_ref, rb_ref, hb_ref, wh_ref, wr_ref,
                 out_ref, mid_ref, ag_ref, wog_ref, whg_ref, wrg_ref, sums_ref, hbg_ref,
                 middle, n2, n2t, cott, acc, back, act, hg, hidden_row):
    step = pl.program_id(0)
    last = pl.num_programs(0) - 1
    chunk = wh_ref.shape[1]
    tile = 2 if chunk % 256 == 0 else 3
    blocks = [slice(s * 256, (s + 1) * 256) for s in range(TOK // 256)]

    @pl.when(step == 0)
    def _():
        hidden_row[...] = as_row(hb_ref)
        for rs in blocks:
            row = tok_ref[rs, :].astype(F32) + mm(att_ref[rs, :], wo_ref[...]) + as_row(ob_ref)
            middle[rs, :] = row
            acc[rs, :] = row + as_row(rb_ref)
            back[rs, :] = jnp.zeros((256, D), F32)
            hat, _ = norm_stats(row)
            low = (hat * as_row(g_ref) + as_row(b_ref)).astype(BF)
            n2[rs, :] = low
            n2t[:, rs] = low.T
            cott[:, rs] = cot_ref[rs, :].T

    hidden_bias = hidden_row[0:1, pl.ds(pl.multiple_of(step * chunk, 128), chunk)]
    hsum = jnp.zeros((1, chunk), F32)
    for rs in blocks:
        for n in range(chunk // 128 // tile):
            cs = slice(n * 128 * tile, (n + 1) * 128 * tile)
            pre = mm(n2[rs, :], wh_ref[:, cs]) + hidden_bias[:, cs]
            up = mm_t(cot_ref[rs, :], wr_ref[cs, :])
            a, slope = gelu_pair(pre)
            act[rs, cs] = a.astype(BF)
            hg[rs, cs] = (slope * up).astype(BF)
        acc[rs, :] += mm(act[rs, :], wr_ref[...])
        back[rs, :] += mm_t(hg[rs, :], wh_ref[...])
        hsum = hsum + col_sum(hg[rs, :].astype(F32))
    hbg_ref[...] = hsum
    _, _, nx, ny, nz, height, _ = whg_ref.shape
    for n in range(3):
        width = chunk // 3
        grad = mm(n2t[...], hg[:, n * width : (n + 1) * width]).astype(BF)
        for i in range(ny * nz):
            whg_ref[n, 0, 0, i % ny, i // ny] = grad[i * height : (i + 1) * height]
    _, _, nx, ny, _, _, _ = wrg_ref.shape
    height, width = D // (2 * nx), chunk // ny // 3
    for y in range(ny):
        grad = mm(cott[...], act[:, y * 3 * width : (y + 1) * 3 * width]).astype(BF)
        for n in range(3):
            for r in range(2 * nx):
                part = grad[r * height : (r + 1) * height, n * width : (n + 1) * width]
                wrg_ref[n, r % 2, r // 2, y, 0] = fold_block(part)

    @pl.when(step == last)
    def _():
        gsum = jnp.zeros((1, D), F32)
        bsum = jnp.zeros((1, D), F32)
        osum = jnp.zeros((1, D), F32)
        rsum = jnp.zeros((1, D), F32)
        for rs in blocks:
            out_ref[rs, :] = acc[rs, :].astype(BF)
            hat, inv = norm_stats(middle[rs, :])
            e = back[rs, :]
            gsum = gsum + col_sum(e * hat)
            bsum = bsum + col_sum(e)
            cot = cot_ref[rs, :].astype(F32)
            rsum = rsum + col_sum(cot)
            mid = cot + norm_back(e, hat, inv, as_row(g_ref))
            mid_ref[rs, :] = mid
            low = mid.astype(BF)
            osum = osum + col_sum(low.astype(F32))
            n2[rs, :] = low
            n2t[:, rs] = att_ref[rs, :].T
            ag_ref[rs, :] = mm_t(low, wo_ref[...]).astype(BF)
        store_square(wog_ref, 0, mm(n2t[...], n2[...]).astype(BF))
        sums_ref[0:1, :] = gsum
        sums_ref[1:2, :] = bsum
        sums_ref[2:3, :] = osum
        sums_ref[3:4, :] = rsum


def mixer(tokens, attended, cotangent, wo, vecs, wh, wr, sizes):
    nc, nx, ny, nz = sizes
    rows, items = nc * nx, ny * nz
    chunk = FF // rows
    square = (1,) + sizes + folded_shape(D // items, D // rows)
    return pl.pallas_call(
        mixer_kernel,
        name="mixer",
        grid=(rows,),
        in_specs=[
            whole((TOK, D)), whole((TOK, D)), whole((TOK, D)), whole((D, D)),
            whole((D,)), whole((D,)), whole((D,)), whole((D,)), whole((FF,)),
            pl.BlockSpec((D, chunk), lambda r: (0, r)),
            pl.BlockSpec((chunk, D), lambda r: (r, 0)),
        ],
        out_specs=(
            whole((TOK, D)), whole((TOK, D)), whole((TOK, D)), whole(square),
            pl.BlockSpec((3, 1, 1, ny, nz, D // items, chunk // 3), lambda r: (0, r % 2, r // 2, 0, 0, 0, 0)),
            pl.BlockSpec((3, nc, nx, ny, 1) + folded_shape(D // rows, FF // items // 3), lambda r: (0, 0, 0, 0, r, 0, 0)),
            whole((8, D)),
            pl.BlockSpec((1, chunk), lambda r: (0, r)),
        ),
        out_shape=(
            jax.ShapeDtypeStruct((TOK, D), BF),
            jax.ShapeDtypeStruct((TOK, D), F32),
            jax.ShapeDtypeStruct((TOK, D), BF),
            jax.ShapeDtypeStruct(square, BF),
            jax.ShapeDtypeStruct((3,) + sizes + (D // items, chunk // 3), BF),
            jax.ShapeDtypeStruct((3,) + sizes + folded_shape(D // rows, FF // items // 3), BF),
            jax.ShapeDtypeStruct((8, D), F32),
            jax.ShapeDtypeStruct((1, FF), F32),
        ),
        scratch_shapes=[
            pltpu.VMEM((TOK, D), F32), pltpu.VMEM((TOK, D), BF), pltpu.VMEM((D, TOK), BF),
            pltpu.VMEM((D, TOK), BF), pltpu.VMEM((TOK, D), F32), pltpu.VMEM((TOK, D), F32),
            pltpu.VMEM((TOK, chunk), BF), pltpu.VMEM((TOK, chunk), BF), pltpu.VMEM((1, FF), F32),
        ],
        compiler_params=params(),
    )(tokens, attended, cotangent, wo, *vecs, wh, wr)


def attend_back_kernel(sizes, tok_ref, g_ref, b_ref, kx_ref, mid_ref, q_ref, k_ref, v_ref, o_ref, ag_ref, lx_ref,
                       wq_ref, wk_ref, wv_ref, whg_ref, wrg_ref, wog_ref,
                       tg_ref, sq_ref, sums_ref, qvs_ref, who_ref, wro_ref, woo_ref,
                       n1t, back, kaug, vaug, qaug, oaug, dqt, dq, dk, dv, square, *comm):
    step = pl.program_id(0)
    blocks = [slice(s * 256, (s + 1) * 256) for s in range(TOK // 256)]
    pos = place(sizes)
    groups = ((whg_ref, who_ref), (wrg_ref, wro_ref), (wog_ref, woo_ref))
    pieces, loads, base, at = [], [], 0, 0
    for source, _ in groups:
        count = source.shape[0]
        refs, keep = comm[at : at + 4 * count + 2], comm[at + 4 * count + 2 : at + 4 * count + 4]
        at += 4 * count + 4
        pieces += make_pieces(
            sizes, pos, BACK_ORDERS[base : base + count], [source.at[n] for n in range(count)],
            [keep[0].at[n] for n in range(count)], refs,
        )
        loads += [pltpu.make_async_copy(source.at[n, pos[0]], keep[0].at[n], keep[1].at[n]) for n in range(count)]
        base += count

    def event(index, stage):
        if stage == 0:
            pieces[index].start(0)
            loads[index].start()
        elif stage < 4:
            if stage == 1:
                loads[index].wait()
            pieces[index].advance(stage)
        else:
            total = pieces[index].gather(3)
            if index < 3:
                width = total.shape[1]
                who_ref[:, index * width : (index + 1) * width] = total
            elif index < 6:
                height, width = D // (2 * sizes[1]), FF // (sizes[2] * sizes[3]) // 3
                wro_ref[:, (index - 3) * width : (index - 2) * width] = unfold_block(total, height, width)
            else:
                woo_ref[...] = unfold_block(total, *woo_ref.shape, odd=pos[0] == 1)

    def finish():
        for part in pieces:
            part.drain()

    table = {(0, 0): [functools.partial(greet, sizes, pos, True, True)]}
    for when, index, stage in BACK_PLAN:
        if when < 2:
            key = (0, when)
        elif when < 26:
            key = ((when - 2) // 8, 2 + (when - 2) % 8)
        else:
            key = (2, 10)
        table.setdefault(key, []).append(functools.partial(event, index, stage))
    table.setdefault((2, 10), []).append(finish)
    run_events(step, table, (0,))

    @pl.when(step == 0)
    def _():
        for rs in blocks:
            hat, _ = norm_stats(tok_ref[rs, :].astype(F32))
            n1t[:, rs] = (hat * as_row(g_ref) + as_row(b_ref)).astype(BF).T
            back[rs, :] = jnp.zeros((256, D), F32)

    run_events(step, table, (1,))
    lane = lax.broadcasted_iota(jnp.int32, (NPATCH, 128), 1)
    low = lane < HD
    ones = jnp.where((lane >= 4) & (lane < 6), 1.0, 0.0).astype(BF)
    for i, rs in enumerate(blocks):
        kaug[rs, 128:256] = jnp.broadcast_to(kx_ref[i : i + 1, :], (NPATCH, 128)).astype(BF)
        vaug[rs, 128:256] = ones
    pick_row = lax.broadcasted_iota(jnp.int32, (256, 256), 0) % 128 // HD
    pick_col = lax.broadcasted_iota(jnp.int32, (256, 256), 1) // 128
    pick = jnp.where(pick_row == pick_col, 1.0, 0.0).astype(BF)
    for pair in range(2):
        cs = slice(pair * 128, (pair + 1) * 128)
        kaug[:, 0:128] = k_ref[:, cs]
        vaug[:, 0:128] = v_ref[:, cs]
        kt = k_ref[:, cs].T
        for rs in blocks:
            qp = q_ref[rs, cs]
            gp = ag_ref[rs, cs]
            prod = gp.astype(F32) * o_ref[rs, cs]
            hi = prod.astype(BF)
            both = jnp.concatenate([hi, (prod - hi.astype(F32)).astype(BF)], axis=1)
            dots = mm(both, pick)
            for h in range(2):
                mine = low if h == 0 else ~low
                qaug[h, rs, 0:128] = jnp.where(mine, qp, jnp.zeros_like(qp))
                qaug[h, rs, 128:256] = lx_ref[pair * 2 + h, rs, :]
                oaug[h, rs, 0:128] = jnp.where(mine, gp, jnp.zeros_like(gp))
                oaug[h, rs, 128:256] = minus_terms(dots[:, h * 128 : (h + 1) * 128], lane, jnp.zeros((NPATCH, 128), F32))
        for j, rs in enumerate(blocks):
            span = slice(j * NPATCH, TOK)
            parts_k, parts_v = [], []
            for h in range(2):
                probs = jnp.exp(mm_t(kaug[rs, :], qaug[h, span, :]))
                rise = mm_t(vaug[rs, :], oaug[h, span, :])
                grad = (probs * rise).astype(BF)
                probs_low = probs.astype(BF)
                parts_v.append(mm(probs_low, ag_ref[span, cs]))
                parts_k.append(mm(grad, q_ref[span, cs]))
                hs = slice(h * HD, (h + 1) * HD)
                part = mm(kt[hs, rs], grad)
                if j == 0:
                    dqt[hs, :] = part
                else:
                    dqt[hs, span] += part
            dk[rs, cs] = jnp.where(low, parts_k[0], parts_k[1]).astype(BF)
            dv[rs, cs] = jnp.where(low, parts_v[0], parts_v[1]).astype(BF)
            run_events(step, table, (2 + pair * 4 + j,))
        dq[:, cs] = (dqt[...].T * 0.125).astype(BF)
    qvs_ref[0:1, :] = col_sum(dq[...].astype(F32))
    qvs_ref[1:2, :] = col_sum(dv[...].astype(F32))
    for n, part in enumerate((dq, dk, dv)):
        square[n, step] = mm(n1t[...], part[...]).astype(BF)
    for rs in blocks:
        back[rs, :] += (
            mm_t(dq[rs, :], wq_ref[...]) + mm_t(dk[rs, :], wk_ref[...]) + mm_t(dv[rs, :], wv_ref[...])
        )

    @pl.when(step == pl.num_programs(0) - 1)
    def _():
        gsum = jnp.zeros((1, D), F32)
        bsum = jnp.zeros((1, D), F32)
        for rs in blocks:
            hat, inv = norm_stats(tok_ref[rs, :].astype(F32))
            e = back[rs, :]
            gsum = gsum + col_sum(e * hat)
            bsum = bsum + col_sum(e)
            tg_ref[rs, :] = (mid_ref[rs, :] + norm_back(e, hat, inv, as_row(g_ref))).astype(BF)
        sums_ref[0:1, :] = gsum
        sums_ref[1:2, :] = bsum
        for n in range(3):
            store_square(sq_ref, n, jnp.concatenate([square[n, g] for g in range(D // 256)], axis=1))

    run_events(step, table, (10,))


BACK_ORDERS = (
    (3, 2, 1), (2, 3, 1), (1, 2, 3), (1, 2, 3), (1, 2, 3), (1, 2, 3),
    (2, 1, 3),
)
BACK_PLAN = (
    (0, 3, 0), (0, 0, 0), (0, 1, 0), (0, 5, 0), (0, 4, 0), (0, 2, 0), (0, 6, 0), (1, 3, 1), (1, 0, 1),
    (1, 1, 1), (4, 5, 1), (6, 6, 1), (6, 2, 1), (7, 1, 2), (9, 3, 2), (9, 4, 1), (10, 5, 2), (15, 3, 3),
    (16, 2, 2), (16, 0, 2), (16, 5, 3), (17, 6, 2), (18, 3, 4), (18, 2, 3), (19, 4, 2), (19, 0, 3), (20, 1, 3),
    (21, 6, 3), (23, 4, 3), (26, 6, 4), (26, 1, 4), (26, 5, 4), (27, 0, 4), (28, 2, 4), (29, 4, 4),
)


def attend_back(tokens, gain, shift, kx, mid, q, k, v, o, ag, lx, wq, wk, wv, whg, wrg, wog, sizes):
    squares = (3,) + sizes + wog.shape[5:]
    col = pl.BlockSpec((D, 256), lambda g: (0, g))
    part = pl.BlockSpec((TOK, 256), lambda g: (0, g))
    far = pl.BlockSpec(memory_space=pl.ANY)
    items, rows = sizes[2] * sizes[3], 2 * sizes[1]
    outs = [(D // items, FF // rows), (D // rows, FF // items), (D // items, D // rows)]
    return pl.pallas_call(
        functools.partial(attend_back_kernel, sizes),
        name="attend_back",
        grid=(D // 256,),
        in_specs=[whole((TOK, D)), whole((D,)), whole((D,)), whole(kx.shape), whole((TOK, D)),
                  part, part, part, part, part, pl.BlockSpec((4, TOK, 128), lambda g: (g, 0, 0)),
                  col, col, col, far, far, far],
        out_specs=(whole((TOK, D)), whole(squares), whole((8, D)), pl.BlockSpec((8, 256), lambda g: (0, g)))
        + tuple(whole(shape) for shape in outs),
        out_shape=(
            jax.ShapeDtypeStruct((TOK, D), BF),
            jax.ShapeDtypeStruct(squares, BF),
            jax.ShapeDtypeStruct((8, D), F32),
            jax.ShapeDtypeStruct((8, D), F32),
        ) + tuple(jax.ShapeDtypeStruct(shape, F32) for shape in outs),
        scratch_shapes=[
            pltpu.VMEM((D, TOK), BF), pltpu.VMEM((TOK, D), F32),
            pltpu.VMEM((TOK, 256), BF), pltpu.VMEM((TOK, 256), BF),
            pltpu.VMEM((2, TOK, 256), BF), pltpu.VMEM((2, TOK, 256), BF),
            pltpu.VMEM((128, TOK), F32),
            pltpu.VMEM((TOK, 256), BF), pltpu.VMEM((TOK, 256), BF), pltpu.VMEM((TOK, 256), BF),
            pltpu.VMEM((3, D // 256, D, 256), BF),
        ]
        + piece_scratch(sizes, BACK_ORDERS[0:3], whg.shape[5:]) + own_scratch(sizes, 3, whg.shape[5:])
        + piece_scratch(sizes, BACK_ORDERS[3:6], wrg.shape[5:]) + own_scratch(sizes, 3, wrg.shape[5:])
        + piece_scratch(sizes, BACK_ORDERS[6:7], wog.shape[5:]) + own_scratch(sizes, 1, wog.shape[5:]),
        compiler_params=params(collective_id=1, has_side_effects=True),
    )(tokens, gain, shift, kx, mid, q, k, v, o, ag, lx, wq, wk, wv, whg, wrg, wog)


EARLY = 16
FINISH_ORDERS = (
    (1, 2, 3), (2, 1, 3), (3, 2, 1), (1, 2, 3), (2, 3, 1), (1, 2, 3),
    (2, 1, 3), (1, 2, 3), (2, 3, 1), (3, 1, 2), (2, 3, 1),
)
FINISH_PLAN = (
    (0, 8, 0), (0, 10, 0), (0, 9, 0), (1, 10, 1), (2, 9, 1), (3, 8, 1), (7, 10, 2), (9, 0, 0), (9, 11, 0),
    (9, 8, 2), (10, 1, 0), (10, 0, 1), (11, 2, 0), (11, 1, 1), (12, 3, 0), (12, 2, 1), (12, 3, 1), (13, 4, 0),
    (13, 0, 2), (14, 5, 0), (14, 1, 2), (14, 4, 1), (15, 6, 0), (15, 5, 1), (16, 7, 0), (16, 0, 3), (16, 6, 1),
    (16, 3, 2), (17, 7, 1), (18, 4, 2), (18, 1, 3), (19, 10, 3), (20, 5, 2), (20, 2, 2), (21, 8, 3), (22, 11, 1),
    (22, 6, 2), (22, 3, 3), (23, 4, 3), (24, 0, 4), (24, 11, 2), (24, 12, 0), (24, 5, 3), (25, 7, 2), (25, 12, 1),
    (25, 6, 3), (25, 9, 2), (26, 10, 4), (26, 12, 2), (28, 11, 3), (28, 12, 3), (28, 5, 4), (28, 2, 3), (29, 7, 3),
    (29, 1, 4), (30, 8, 4), (31, 9, 3), (31, 4, 4), (32, 11, 4), (33, 2, 4), (33, 3, 4), (33, 9, 4), (33, 6, 4),
    (33, 12, 4), (33, 7, 4),
)


def finish_kernel(sizes, tg_ref, act_ref, slope_ref, w_ref, xt_ref, t_ref, sel_ref, sq_ref, sums2_ref, hbg_ref, sums1_ref, qvs_ref, wh_ref, wo_ref,
                  pw_ref, table_ref, ig_ref, small_ref,
                  tgc, tgt, dxa, pg, cw, lines, flat, grads, edge, edge_send, edge_recv, got, send, recv, nat, *comm):
    t = pl.program_id(0)
    nc, nx, ny, nz = sizes
    items, rows = ny * nz, nc * nx
    tokens = tgc.shape[0]
    group = tokens // NP
    count, _, height, width = ig_ref.shape
    nrow = height // PATCH
    pos = place(sizes)
    item, row = lax.axis_index("items"), lax.axis_index("rows")
    final_row = lax.axis_size("rows") - 1
    far_steps = STEPS * (nx - 1)
    image_step = 2 * STEPS + far_steps
    final_step = image_step + CIN - 1
    at = 4 * STEPS + 2
    patch = make_pieces(
        sizes, pos, FINISH_ORDERS[0:STEPS], [grads.at[q % 2] for q in range(STEPS)],
        [grads.at[q % 2, pos[0]] for q in range(STEPS)], comm[0:at],
    )
    keep = comm[at + 14 : at + 16]
    square = make_pieces(
        sizes, pos, FINISH_ORDERS[STEPS : STEPS + 3], [sq_ref.at[n] for n in range(3)],
        [keep[0].at[n] for n in range(3)], comm[at : at + 14],
    )
    loads = [pltpu.make_async_copy(sq_ref.at[n, pos[0]], keep[0].at[n], keep[1].at[n]) for n in range(3)]
    at += 16
    early = SmallSum(sizes, pos, comm[at : at + 4], comm[at + 4], comm[at + 5])
    late = SmallSum(sizes, pos, comm[at + 6 : at + 10], comm[at + 10], comm[at + 11])

    def edge_copy(n):
        step = -1 if n == 0 else 1
        return pltpu.make_async_remote_copy(
            src_ref=edge.at[n], dst_ref=edge.at[2 + n], send_sem=edge_send.at[n], recv_sem=edge_recv.at[n],
            device_id=(item, row + step), device_id_type=MESH,
        )

    share, per = tokens // nx, group // nx
    turns = [turn_of(sizes, pos, xg) * share for xg in range(nx)]

    def spread(j, c):
        return jnp.concatenate(
            [dxa[j, pl.ds(pl.multiple_of(turns[xg] + c * per, per), per), :] for xg in range(nx)], axis=0
        )

    def parcel(k):
        to = lax.rem(row + k, rows)
        return pltpu.make_async_remote_copy(
            src_ref=tg_ref.at[:, to], dst_ref=got.at[row], send_sem=send.at[k - 1], recv_sem=recv.at[row],
            device_id=(item, to), device_id_type=MESH,
        )

    def arrived(source):
        pltpu.make_async_remote_copy(
            src_ref=tg_ref.at[:, source], dst_ref=got.at[source], send_sem=send.at[0], recv_sem=recv.at[source],
            device_id=(item, source), device_id_type=MESH,
        ).wait_recv()

    def unpack(xg, turn):
        for k in range(D // 128):
            cut = got[pl.ds(2 * xg, 2), :, :, k * 128 : (k + 1) * 128]
            nat[k] = cut.reshape(share, 128).astype(F32)
        for c in range(NP):
            part = jnp.concatenate([nat[k, pl.ds(c, per, stride=NP), :] for k in range(D // 128)], axis=1)
            tgc[turn * share + c * per : turn * share + (c + 1) * per, :] = part.astype(BF)

    def turn_over(turn):
        for s in range(share // 256):
            rs = slice(turn * share + s * 256, turn * share + (s + 1) * 256)
            tgt[:, rs] = tgc[rs, :].T

    def put_lines(j):
        low = lax.broadcasted_iota(jnp.int32, (group, 2 * HALF), 1) < HALF
        for pair in range(NP // 2):
            a, b = spread(j, 2 * pair), spread(j, 2 * pair + 1)
            cs = slice(pair * 128, (pair + 1) * 128)
            lines[2 * j * group : (2 * j + 1) * group, cs] = jnp.where(low, a, pltpu.roll(b, HALF, 1)).astype(BF)
            lines[(2 * j + 1) * group : (2 * j + 2) * group, cs] = jnp.where(low, pltpu.roll(a, HALF, 1), b).astype(BF)

    def event(index, stage):
        if index < STEPS:
            if stage == 0:
                patch[index].start(0)
            elif stage < 4:
                patch[index].advance(stage)
            else:
                total = unfold_block(patch[index].gather(3), D // rows, FEAT // items)
                for c in range(CH // items):
                    at = c * PATCH * PATCH + index * 2 * PATCH
                    pw_ref[:, at : at + 2 * PATCH] = total[:, c * 2 * PATCH : (c + 1) * 2 * PATCH]
        elif index < STEPS + 3:
            n = index - STEPS
            if stage == 0:
                loads[n].start()
                square[n].start(0)
                return
            if stage == 1:
                loads[n].wait()
            if stage < 4:
                square[n].advance(stage)
            else:
                high, wide = wo_ref.shape
                block = unfold_block(square[n].gather(3), high, wide, odd=pos[0] == 1)
                table_ref[high : 2 * high, n * wide : (n + 1) * wide] = block
        else:
            part = (early, late)[index - STEPS - 3]
            if stage < 4:
                part.advance(stage)
            elif part is early:
                small_ref[0:EARLY, :] = part.gather(3)
            else:
                small_ref[EARLY : EARLY + 32, 0:128] = part.gather(3)

    opening, table = [], {}
    for when, index, stage in FINISH_PLAN:
        if stage > 0 or index < STEPS + 3:
            call = functools.partial(event, index, stage)
            if when == 0:
                opening.append(call)
            else:
                later = when - 1 + (far_steps - STEPS if when > 3 * STEPS else 0)
                table.setdefault((min(later, final_step), 0), []).append(call)

    @pl.when(t == 0)
    def _():
        @pl.when(row == final_row)
        def _():
            edge[2] = jnp.zeros(edge.shape[1:], BF)

        @pl.when(row == 0)
        def _():
            edge[3] = jnp.zeros(edge.shape[1:], BF)

        greet(sizes, pos, True, True)
        for k in range(1, rows):
            parcel(k).start()
        for call in opening:
            call()
        got[row] = tg_ref[:, row]
        arrived(2 * pos[1] + 1 - pos[0])
        unpack(pos[1], nx - 1)
        turn_over(nx - 1)
        cw[...] = jnp.zeros_like(cw)
        high, wide = wo_ref.shape
        table_ref[0:high, :] = wh_ref[...]
        table_ref[high : 2 * high, 3 * wide : 4 * wide] = wo_ref[...]
        small_ref[EARLY:, :] = jnp.zeros((32, D), F32)

    @pl.when(t == STEPS)
    def _():
        for turn in range(nx - 1):
            xg = lax.rem(pos[1] + 1 + turn, nx)
            arrived(2 * xg)
            arrived(2 * xg + 1)
            unpack(xg, turn)
            turn_over(turn)

    @pl.when(t == STEPS + 1)
    def _():
        total = jnp.zeros((1, D), F32)
        for s in range(tokens // 256):
            total = total + col_sum(tgc[s * 256 : (s + 1) * 256, :].astype(F32))
        lines_in = [sums2_ref[0:1], sums2_ref[1:2], sums2_ref[2:3], sums2_ref[3:4]]
        lines_in += [hbg_ref[:, n * D : (n + 1) * D] for n in range(FF // D)]
        lines_in += [sums1_ref[0:1], sums1_ref[1:2], qvs_ref[0:1], qvs_ref[1:2], total]
        early.start(0, jnp.concatenate(lines_in + [jnp.zeros((EARLY - len(lines_in), D), F32)], axis=0))

    @pl.when((t >= STEPS) & (t < 2 * STEPS))
    def _():
        for q in range(2, STEPS):
            @pl.when(t == STEPS + q)
            def _(q=q):
                patch[q - 2].drain((0,))

        feats = FEAT // items
        slot = t % 2
        for n in range(FEAT // 256):
            grad = mm(tgt[...], act_ref[0, 0, :, n * 256 : (n + 1) * 256]).astype(BF)
            for c in range(256 // feats):
                i = n * (256 // feats) + c
                for r in range(rows):
                    block = grad[r * (D // rows) : (r + 1) * (D // rows), c * feats : (c + 1) * feats]
                    grads[slot, r % 2, r // 2, i % ny, i // ny] = fold_block(block)

    def stem_part(p, turn):
        weight = w_ref[...].reshape(FEAT, D)

        def at(s, size):
            return pl.ds(pl.multiple_of(turn * share + s * 256, 256), size)

        @pl.when(p == 0)
        def _():
            dxa[0, at(0, share), :] = jnp.zeros((share, 128), F32)

        for s in range(share // 256):
            rs = slice(s * 256, (s + 1) * 256)
            for n in range(FEAT // 256):
                cs = slice(n * 256, (n + 1) * 256)
                da = mm_t(tgc[at(s, 256), :], weight[cs, :])
                pg[rs, cs] = (slope_ref[0, 0, rs, cs].astype(F32) * da).astype(BF)
            back = mm_t(pg[rs, :], t_ref[...])
            dxa[p, at(s, 256), :] += back[:, 0:128]
            dxa[p + 1, at(s, 256), :] = back[:, 128:256]
        xt = jnp.concatenate([xt_ref[p, :, at(0, share)], xt_ref[p + 1, :, at(0, share)]], axis=0)
        cw[...] += mm(xt, pg[...])

    near, far = t < STEPS, (t >= 2 * STEPS) & (t < image_step)

    @pl.when(near | far)
    def _():
        stem_part(t % STEPS, jnp.where(near, nx - 1, t // STEPS - 2))

    @pl.when((t >= image_step - STEPS) & (t < image_step))
    def _():
        p = t % STEPS

        @pl.when(p == 0)
        def _():
            put_lines(0)
            for ch in range(CIN):
                head = mm_t(lines[0:group], sel_ref[ch * width : (ch + 1) * width, :])
                edge[0, ch] = (pltpu.roll(head, nrow - 1, 0) if nrow > 1 else head).astype(BF)

            @pl.when(row > 0)
            def _():
                edge_copy(0).start()

        @pl.when(p == STEPS - 1)
        def _():
            put_lines(SLABS - 1)
            for ch in range(CIN):
                tail = mm_t(lines[(WIN - 1) * group : WIN * group], sel_ref[ch * width : (ch + 1) * width, :])
                edge[1, ch] = (pltpu.roll(tail, group - nrow + 1, 0) if nrow > 1 else tail).astype(BF)

            @pl.when(row < final_row)
            def _():
                edge_copy(1).start()

            late.start(0, tap_grad_rows(cw[...]))

    @pl.when(t >= image_step)
    def _():
        ch = t - image_step

        @pl.when(t == image_step)
        def _():
            for j in range(1, SLABS - 1):
                put_lines(j)

            @pl.when(row < final_row)
            def _():
                edge_copy(0).wait_recv()

            @pl.when(row > 0)
            def _():
                edge_copy(1).wait_recv()

        patch_row = lax.broadcasted_iota(jnp.int32, (group, width), 0) % nrow
        res = mm_t(lines[...], sel_ref[pl.ds(pl.multiple_of(ch * width, width), width), :])
        head = res[0:group]
        tail = res[(PATCH + 1) * group : (PATCH + 2) * group]
        for r in range(PATCH):
            v = res[(r + 1) * group : (r + 2) * group]
            if r == 0:
                v = v + jnp.where(patch_row == 0, edge[3, ch].astype(F32), pltpu.roll(tail, 1, 0))
            if r == PATCH - 1:
                v = v + jnp.where(patch_row == nrow - 1, edge[2, ch].astype(F32), pltpu.roll(head, group - 1, 0))
            flat[0, pl.ds(r, group, stride=PATCH), :] = v[:, 0:128]
            flat[1, pl.ds(r, group, stride=PATCH), :] = v[:, 128:256]
        for n in range(count):
            at = slice(n * height, (n + 1) * height)
            ig_ref[n, 0, :, 0:128] = flat[0, at, :]
            ig_ref[n, 0, :, 128:256] = flat[1, at, :]

    def close():
        for part in square:
            part.drain()
        for q, part in enumerate(patch):
            part.drain((1, 2, 3) if q < STEPS - 2 else (0, 1, 2, 3))
        early.drain()
        late.drain()
        for k in range(1, rows):
            parcel(k).wait_send()

        @pl.when(row > 0)
        def _():
            edge_copy(0).wait_send()

        @pl.when(row < final_row)
        def _():
            edge_copy(1).wait_send()

    table.setdefault((final_step, 0), []).append(close)
    run_events(t, table, (0,))


def finish(tg, saved, weight, xt, taps, sel, squares, sums2, hbg, sums1, qvs, wh, wo, count, height, sizes):
    nc, nx, ny, nz = sizes
    items, rows = ny * nz, nc * nx
    group = count * height // PATCH
    tokens = group * NP
    feats = FEAT // items
    square = squares.shape[5:]
    share = tokens // nx
    image_step = STEPS * (nx + 1)

    def clip(v, low, high):
        return jnp.minimum(jnp.maximum(v, low), high)

    def sub(t):
        held = jnp.where(t < STEPS, t, jnp.where(t < 2 * STEPS, 0, t % STEPS))
        return jnp.where(t < image_step, held, STEPS - 1)

    def turn(t):
        return jnp.where(t < STEPS, nx - 1, clip(t // STEPS - 2, 0, nx - 2))

    return pl.pallas_call(
        functools.partial(finish_kernel, sizes),
        name="finish",
        grid=(image_step + CIN,),
        in_specs=[
            whole(tg.shape),
            pl.BlockSpec((1, 1, tokens, FEAT), lambda t: (clip(t - STEPS, 0, STEPS - 1), 0, 0, 0)),
            pl.BlockSpec((1, 1, share, FEAT), lambda t: (sub(t), 1, turn(t), 0)),
            pl.BlockSpec((CH, 1, 2 * PATCH, D), lambda t: (0, sub(t), 0, 0)),
            whole(xt.shape),
            whole(taps.shape),
            whole(sel.shape),
            pl.BlockSpec(memory_space=pl.ANY),
            whole(sums2.shape), whole(hbg.shape), whole(sums1.shape), whole(qvs.shape), whole(wh.shape), whole(wo.shape),
        ],
        out_specs=(
            whole((D // rows, PF // items)),
            whole((2 * D // items, FF // rows)),
            pl.BlockSpec((count, 1, height, IMG), lambda t: (0, clip(t - image_step, 0, CIN - 1), 0, 0)),
            whole((EARLY + 32, D)),
        ),
        out_shape=(
            jax.ShapeDtypeStruct((D // rows, PF // items), F32),
            jax.ShapeDtypeStruct((2 * D // items, FF // rows), F32),
            jax.ShapeDtypeStruct((count, CIN, height, IMG), F32),
            jax.ShapeDtypeStruct((EARLY + 32, D), F32),
        ),
        scratch_shapes=[
            pltpu.VMEM((tokens, D), BF),
            pltpu.VMEM((D, tokens), BF),
            pltpu.VMEM((SLABS, tokens, 128), F32),
            pltpu.VMEM((share, FEAT), BF),
            pltpu.VMEM((4 * HALF, FEAT), F32),
            pltpu.VMEM((WIN * group, NP * HALF), BF),
            pltpu.VMEM((2, group * PATCH, 128), F32),
            pltpu.VMEM((2,) + sizes + folded_shape(D // rows, feats), BF),
            pltpu.VMEM((4, CIN, group, IMG), BF),
            pltpu.SemaphoreType.DMA((2,)),
            pltpu.SemaphoreType.DMA((2,)),
            pltpu.VMEM((rows, SEQ_ITEMS, tokens // rows // SEQ_ITEMS, D), BF),
            pltpu.SemaphoreType.DMA((rows - 1,)),
            pltpu.SemaphoreType.DMA((rows,)),
            pltpu.VMEM((D // 128, share, 128), F32),
        ]
        + piece_scratch(sizes, FINISH_ORDERS[0:STEPS], folded_shape(D // rows, feats))
        + piece_scratch(sizes, FINISH_ORDERS[STEPS : STEPS + 3], square) + own_scratch(sizes, 3, square)
        + small_scratch(sizes, (EARLY, D))
        + small_scratch(sizes, (32, 128)),
        compiler_params=params(collective_id=2, has_side_effects=True),
    )(tg, saved, saved, weight, xt, taps, sel, squares, sums2, hbg, sums1, qvs, wh, wo)


def feature_parts(rows):
    feat = lax.broadcasted_iota(jnp.int32, (rows, FEAT), 1)
    return feat // (2 * PATCH), feat // PATCH % 2, feat % PATCH


def tap_rows(wide, ch, r, b, half):
    parts = []
    for r2 in range(2):
        a = r - r2
        parts.append(wide[9 * ch + 3 * a + b : 9 * ch + 3 * a + b + 1, :] if 0 <= a < 3 else jnp.zeros((1, FEAT), F32))
    return jnp.where(half == 0, parts[0], parts[1])


def tap_matrix(cw_ref, cb_ref, t_ref):
    chan, _, _ = feature_parts(32)
    expand = jnp.where(chan == lax.broadcasted_iota(jnp.int32, (32, FEAT), 0), 1.0, 0.0).astype(BF)
    wide = lax.dot_general(cw_ref[...], expand, (((0,), (0,)), ((), ())), preferred_element_type=F32)
    bias = mm(jnp.broadcast_to(as_row(cb_ref), (8, CH)).astype(BF), expand)
    _, half, spot = feature_parts(1)
    line = lax.broadcasted_iota(jnp.int32, (HALF, FEAT), 0)
    for r in range(4):
        block = jnp.zeros((HALF, FEAT), F32)
        if r == 0:
            block = jnp.where(line == ONE_LANE, bias[0:1, :], block)
        for ch in range(CIN):
            for b in range(3):
                block = jnp.where(line == WIN * ch + b + spot, tap_rows(wide, ch, r, b, half), block)
        t_ref[r * HALF : (r + 1) * HALF, :] = block.astype(BF)


def tap_grad_rows(full):
    chan, half, spot = feature_parts(1)
    line = lax.broadcasted_iota(jnp.int32, (HALF, FEAT), 0)
    sums = [[None] * 3 for _ in range(9)]
    for r in range(4):
        block = full[r * HALF : (r + 1) * HALF]
        for ch in range(CIN):
            for b in range(3):
                line_sum = jnp.sum(jnp.where(line == WIN * ch + b + spot, block, 0.0), axis=0, keepdims=True)
                for a in range(3):
                    if 0 <= r - a < 2:
                        part = jnp.where(half == r - a, line_sum, 0.0)
                        old = sums[3 * ch + b][a]
                        sums[3 * ch + b][a] = part if old is None else old + part
    lines = [sums[3 * ch + b][a] for ch in range(CIN) for a in range(3) for b in range(3)]
    lines.append(full[ONE_LANE : ONE_LANE + 1])
    lines.append(jnp.zeros((4, FEAT), F32))
    table = jnp.concatenate(lines, axis=0)
    chan, _, _ = feature_parts(128)
    expand = jnp.where(chan == lax.broadcasted_iota(jnp.int32, (128, FEAT), 0), 1.0, 0.0).astype(BF)
    hi, mid, lo = three_terms(table)
    return mm_t(hi, expand) + (mm_t(mid, expand) + mm_t(lo, expand))


def on_device(
    images, item_segment, conv_weight, conv_bias, patch_weight, patch_bias, norm1_gain, norm1_bias,
    query_weight, query_bias, key_weight, value_weight, value_bias, output_weight, output_bias,
    norm2_gain, norm2_bias, hidden_weight, hidden_bias, result_weight, result_bias, cotangent,
):
    items, rows = lax.axis_size("items"), lax.axis_size("rows")
    sizes = grid_sizes(items, rows)
    count, _, height, _ = images.shape
    nrow = height // PATCH

    cw = conv_weight.reshape(CH, 27)
    weight4 = patch_weight.reshape(CH, STEPS, 2 * PATCH, D)
    tokens, saved, xt, sel, taps = stem_forward(images, cw, conv_bias, weight4, patch_bias, sizes)
    tokens = tokens.reshape(TOK, D)
    q, k, v, attended, attended32, lx, kx = attend(
        tokens, (norm1_gain, norm1_bias, query_bias, value_bias), item_segment, query_weight, key_weight, value_weight)
    block_out, middle_grad, attended_grad, wo_grad, wh_grad, wr_grad, sums2, hb_grad = mixer(
        tokens, attended, cotangent, output_weight,
        (output_bias, norm2_gain, norm2_bias, result_bias, hidden_bias), hidden_weight, result_weight, sizes,
    )
    token_grad, squares, sums1, qvs, wh_grad, wr_grad, wo_grad = attend_back(
        tokens, norm1_gain, norm1_bias, kx, middle_grad, q, k, v, attended32, attended_grad, lx,
        query_weight, key_weight, value_weight, wh_grad, wr_grad, wo_grad, sizes,
    )
    token_grad = token_grad.reshape(SEQ_ITEMS, rows, nrow * NP, D)
    pw_grad, table, image_grad, small = finish(
        token_grad, saved, weight4, xt, taps, sel, squares, sums2, hb_grad, sums1, qvs, wh_grad, wo_grad,
        count, height, sizes,
    )
    high, wide = D // items, D // rows
    wq_grad, wk_grad, wv_grad, wo_grad = (table[high:, n * wide : (n + 1) * wide] for n in range(4))
    wh_grad = table[:high]
    tap_grads = small[EARLY:, 0:128]

    def row_of(at):
        return small[at]

    return (
        block_out,
        image_grad,
        tap_grads[0:27, 0:CH].T.reshape(conv_weight.shape),
        tap_grads[27, 0:CH],
        pw_grad.T,
        row_of(12),
        row_of(8),
        row_of(9),
        wq_grad,
        row_of(10),
        wk_grad,
        wv_grad,
        row_of(11),
        wo_grad,
        row_of(2),
        row_of(0),
        row_of(1),
        wh_grad,
        small[4:8].reshape(FF),
        wr_grad.T,
        row_of(3),
    )


def solution(mesh):
    split = P("items", "rows")
    flat = P(("items", "rows"), None)
    image = P("items", None, "rows", None)
    return jax.shard_map(
        on_device,
        mesh=mesh,
        in_specs=(image, P("items")) + (P(),) * 19 + (flat,),
        out_specs=(
            flat, image, P(), P(), split, P(), P(), P(), split, P(), split, split,
            P(), split, P(), P(), P(), split, P(), split, P(),
        ),
        check_vma=False,
    )
```

```python
import functools

import jax
import jax.numpy as jnp
from jax import lax
from jax.experimental import pallas as pl
from jax.experimental.pallas import tpu as pltpu
from jax.sharding import PartitionSpec as P

BF = jnp.bfloat16
F32 = jnp.float32
D = 768
HEADS = 12
HD = 64
FF = 3072
IMG = 256
PATCH = 16
CH = 32
CIN = 3
SEQ_ITEMS = 4
NPATCH = 256
TOK = 1024
NP = IMG // PATCH
PF = CH * PATCH * PATCH
HALF = 64
WIN = PATCH + 2
ONE_LANE = CIN * WIN
SLABS = (PATCH + 2) // 2
STEPS = PATCH // 2
FEAT = PF // STEPS
GELU_A = 0.7978845608028654
GELU_B = GELU_A * 0.044715
VMEM_CAP = 60 * 1024 * 1024


def mm(left, right):
    return jnp.dot(left, right, preferred_element_type=F32)


def mm_t(left, right):
    return lax.dot_general(left, right, (((1,), (1,)), ((), ())), preferred_element_type=F32)


def params(**extra):
    return pltpu.CompilerParams(vmem_limit_bytes=VMEM_CAP, **extra)


def whole(shape):
    zeros = (0,) * len(shape)
    return pl.BlockSpec(shape, lambda *_: zeros, pipeline_mode=pl.Buffered(1))


def gelu_pair_low(v):
    bend = jnp.tanh((v * (GELU_A + GELU_B * (v * v))).astype(BF))
    low = v.astype(BF)
    gate = bend * BF(0.5) + BF(0.5)
    act = low * gate
    slope = gate + act * (BF(1.0) - gate) * (BF(2.0 * GELU_A) + BF(6.0 * GELU_B) * (low * low))
    return act, slope


def as_row(ref, at=None):
    line = ref[...] if at is None else ref[at]
    return line.astype(F32).reshape(1, line.shape[0])


def gelu_pair(v):
    square = v * v
    gate = 0.5 + 0.5 * jnp.tanh(v * (GELU_A + GELU_B * square))
    act = v * gate
    slope = gate + act * (1.0 - gate) * (2.0 * GELU_A + (6.0 * GELU_B) * square)
    return act, slope


MESH = pl.DeviceIdType.MESH


def grid_sizes(items, rows):
    nx = rows // 2
    ny = nx if items % nx == 0 else 1
    return (2, nx, ny, items // ny)


def place(sizes):
    item, row = lax.axis_index("items"), lax.axis_index("rows")
    return (row % 2, row // 2, item % sizes[2], item // sizes[2])


def peer(sizes, pos, axis, k):
    moved = list(pos)
    moved[axis] = lax.rem(pos[axis] + k, sizes[axis])
    return (moved[3] * sizes[2] + moved[2], moved[1] * 2 + moved[0]), moved[axis]


def greet(sizes, pos, near, far):
    barrier = pltpu.get_barrier_semaphore()
    item, row, rows = lax.axis_index("items"), lax.axis_index("rows"), 2 * sizes[1]
    peers = [(item, lax.rem(row + k, rows)) for k in range(1, rows)] if near else []
    for axis in (2, 3) if far else ():
        peers += [peer(sizes, pos, axis, k)[0] for k in range(1, sizes[axis])]
    for device in peers:
        pl.semaphore_signal(barrier, inc=1, device_id=device, device_id_type=MESH)
    pl.semaphore_wait(barrier, len(peers))


def turn_of(sizes, pos, x):
    return lax.rem(x + 2 * sizes[1] - 1 - pos[1], sizes[1])


def add_up(first, rest):
    total = first.astype(F32)
    for term in rest:
        total = total + term.astype(F32)
    return total


class Piece:
    def __init__(self, sizes, pos, order, source, own, bufs, send, recv):
        self.sizes, self.pos = sizes, pos
        self.source, self.own, self.bufs = source, own, bufs
        self.send, self.recv = send, recv
        self.axes = (0,) + order

    def at(self, stage, where):
        left = sorted(self.axes[stage:])
        return (slice(None),) * left.index(self.axes[stage]) + (where,)

    def copies(self, stage):
        out = []
        for k in range(1, self.sizes[self.axes[stage]]):
            device, there = peer(self.sizes, self.pos, self.axes[stage], k)
            if stage == 0:
                src, dst = self.source.at[there], self.bufs[0]
            else:
                held = self.at(stage, there)
                src = self.bufs[0].at[held] if stage == 1 else self.bufs[stage - 1].at[(0,) + held]
                dst = self.bufs[stage].at[k - 1]
            out.append(
                pltpu.make_async_remote_copy(
                    src_ref=src, dst_ref=dst, send_sem=self.send.at[stage, k - 1], recv_sem=self.recv.at[stage, k - 1],
                    device_id=device, device_id_type=MESH,
                )
            )
        return out

    def start(self, stage):
        for copy in self.copies(stage):
            copy.start()

    def gather(self, stage):
        for copy in self.copies(stage):
            copy.wait_recv()
        bufs = self.bufs
        if stage == 0:
            bufs[0][...] = bufs[0][...] + self.own[...]
            return None
        held = self.at(stage, self.pos[self.axes[stage]])
        base = bufs[0][held] if stage == 1 else bufs[stage - 1][(0,) + held]
        terms = self.sizes[self.axes[stage]] - 1
        if stage < 3 and terms == 1:
            bufs[stage][0] = base + bufs[stage][0]
            return None
        total = add_up(base, [bufs[stage][k] for k in range(terms)])
        if stage == 3:
            return total
        bufs[stage][0] = total.astype(BF)

    def advance(self, stage):
        self.gather(stage - 1)
        self.start(stage)

    def drain(self, stages=(0, 1, 2, 3)):
        for stage in stages:
            for copy in self.copies(stage):
                copy.wait_send()


def piece_scratch(sizes, orders, shape):
    out = []
    for order in orders:
        out.append(pltpu.VMEM(sizes[1:] + shape, BF))
        for stage in range(3):
            left = tuple(sizes[axis] for axis in sorted(order[stage + 1 :]))
            out.append(pltpu.VMEM((sizes[order[stage]] - 1,) + left + shape, BF))
    sems = pltpu.SemaphoreType.DMA((len(orders), 4, max(sizes) - 1))
    return out + [sems, sems]


def own_scratch(sizes, count, shape):
    return [pltpu.VMEM((count,) + sizes[1:] + shape, BF), pltpu.SemaphoreType.DMA((count,))]


def make_pieces(sizes, pos, orders, sources, owns, refs):
    count = len(orders)
    return [
        Piece(sizes, pos, orders[n], sources[n], owns[n], refs[4 * n : 4 * n + 4], refs[4 * count].at[n], refs[4 * count + 1].at[n])
        for n in range(count)
    ]


class SmallSum:
    def __init__(self, sizes, pos, bufs, send, recv):
        self.sizes, self.pos, self.bufs, self.send, self.recv = sizes, pos, bufs, send, recv

    def copies(self, axis, receive):
        buf, here = self.bufs[axis], self.pos[axis]
        out = []
        for k in range(1, self.sizes[axis]):
            device, _ = peer(self.sizes, self.pos, axis, k)
            slot = lax.rem(here + self.sizes[axis] - k, self.sizes[axis]) if receive else here
            out.append(
                pltpu.make_async_remote_copy(
                    src_ref=buf.at[here], dst_ref=buf.at[slot], send_sem=self.send.at[axis, k - 1],
                    recv_sem=self.recv.at[axis, k - 1], device_id=device, device_id_type=MESH,
                )
            )
        return out

    def start(self, axis, value):
        self.bufs[axis][self.pos[axis]] = value
        for copy in self.copies(axis, False):
            copy.start()

    def gather(self, axis):
        for copy in self.copies(axis, True):
            copy.wait_recv()
        total = self.bufs[axis][0]
        for k in range(1, self.sizes[axis]):
            total = total + self.bufs[axis][k]
        return total

    def advance(self, axis):
        self.start(axis, self.gather(axis - 1))

    def drain(self):
        for axis in range(4):
            for copy in self.copies(axis, False):
                copy.wait_send()


def small_scratch(sizes, height):
    return [pltpu.VMEM((size, height, 128), F32) for size in sizes] + [
        pltpu.SemaphoreType.DMA((4, max(sizes) - 1)),
        pltpu.SemaphoreType.DMA((4, max(sizes) - 1)),
    ]


def folds(width):
    return width % 128 == HALF and width > 128


def narrow(width):
    return 128 // width if width < 128 and 128 % width == 0 else 1


def folded_shape(height, width):
    if folds(width) or narrow(width) > 1:
        return (height * width // 128, 128)
    return (height, width)


def fold_block(block):
    height, width = block.shape
    if narrow(width) > 1:
        part = height // narrow(width)
        return jnp.concatenate([block[k * part : (k + 1) * part] for k in range(narrow(width))], axis=1)
    return block


def unfold_block(block, height, width, odd=False):
    if narrow(width) > 1:
        return jnp.concatenate([block[:, k * width : (k + 1) * width] for k in range(narrow(width))], axis=0)
    if not folds(width):
        return block
    main, side = block[:height], block[height:]
    side = jnp.concatenate([side[:, :HALF], side[:, HALF:]], axis=0)
    return jnp.where(odd, jnp.concatenate([side, main], axis=1), jnp.concatenate([main, side], axis=1))


def run_events(step, table, slots):
    for (when, slot), todo in table.items():
        if slot in slots:
            @pl.when(step == when)
            def _(todo=todo):
                for call in todo:
                    call()


def make_windows(sizes, pos, img_ref, edge, edge_copies, x, xt_ref, sel_ref, pix, lines):
    items, _, height, width = img_ref.shape
    nrow = height // PATCH
    group = items * nrow
    row, final_row = lax.axis_index("rows"), lax.axis_size("rows") - 1
    for ch in range(CIN):
        for item in range(items):
            full = img_ref[item, ch].astype(F32)
            for k in range(width // 128):
                pix[ch, k, item * height : (item + 1) * height, :] = full[:, k * 128 : (k + 1) * 128]

    def line(ch, r):
        return jnp.concatenate([pix[ch, k, pl.ds(r, group, stride=PATCH), :] for k in range(width // 128)], axis=1)

    for ch in range(CIN):
        first, final = line(ch, 0), line(ch, PATCH - 1)
        edge[0, ch] = pltpu.roll(first, nrow - 1, 0).astype(BF)
        edge[1, ch] = pltpu.roll(final, group - nrow + 1, 0).astype(BF)

    @pl.when(row > 0)
    def _():
        edge_copies[0].start()

    @pl.when(row < final_row)
    def _():
        edge_copies[1].start()

    for ch in range(CIN):
        cols = slice(ch * width, (ch + 1) * width)
        for r in range(PATCH):
            lines[(r + 1) * group : (r + 2) * group, cols] = line(ch, r).astype(BF)
    lane = lax.broadcasted_iota(jnp.int32, (1, NP * HALF), 1)
    col, spot = lane // HALF, lane % HALF
    for ch in range(CIN):
        inside = (spot >= WIN * ch) & (spot < WIN * (ch + 1))
        want = jnp.where(inside, PATCH * col + spot - WIN * ch - 1, -5)
        here = lax.broadcasted_iota(jnp.int32, (width, NP * HALF), 0)
        sel_ref[ch * width : (ch + 1) * width, :] = jnp.where(here == want, 1.0, 0.0).astype(BF)

    @pl.when(row < final_row)
    def _():
        edge_copies[0].wait_recv()

    @pl.when(row > 0)
    def _():
        edge_copies[1].wait_recv()

    patch_row = lax.broadcasted_iota(jnp.int32, (group, width), 0) % nrow
    for ch in range(CIN):
        cols = slice(ch * width, (ch + 1) * width)
        up = jnp.where(patch_row == 0, edge[3, ch].astype(F32), pltpu.roll(line(ch, PATCH - 1), 1, 0))
        lines[0:group, cols] = up.astype(BF)
        down = jnp.where(patch_row == nrow - 1, edge[2, ch].astype(F32), pltpu.roll(line(ch, 0), group - 1, 0))
        lines[(PATCH + 1) * group : (PATCH + 2) * group, cols] = down.astype(BF)
    lane = lax.broadcasted_iota(jnp.int32, (group, 2 * HALF), 1)
    low = lane < HALF
    ones = (lane % HALF) == ONE_LANE
    nx = sizes[1]
    share, per = items * nrow * NP // nx, group // nx
    turns = [turn_of(sizes, pos, xg) * share for xg in range(nx)]

    def put(j, c, block):
        low_bits = block.astype(BF)
        for xg in range(nx):
            x[j, pl.ds(pl.multiple_of(turns[xg] + c * per, per), per), :] = low_bits[xg * per : (xg + 1) * per]

    for quarter in range(NP * HALF // 256):
        res = mm(lines[...], sel_ref[:, quarter * 256 : (quarter + 1) * 256])
        for j in range(SLABS):
            first = res[2 * j * group : (2 * j + 1) * group]
            second = res[(2 * j + 1) * group : (2 * j + 2) * group]
            for pair in range(2):
                a = first[:, pair * 128 : (pair + 1) * 128]
                b = second[:, pair * 128 : (pair + 1) * 128]
                put(j, quarter * 4 + pair * 2, jnp.where(ones, 1.0, jnp.where(low, a, pltpu.roll(b, HALF, 1))))
                put(j, quarter * 4 + pair * 2 + 1, jnp.where(ones, 1.0, jnp.where(low, pltpu.roll(a, HALF, 1), b)))
    for j in range(SLABS):
        xt_ref[j] = x[j].T


def stem_kernel(sizes, img_ref, cw_ref, cb_ref, w_ref, pb_ref, tok_ref, saved_ref, xt_ref, sel_ref, t_ref,
                x, pix, lines, edge, edge_send, edge_recv, acc, nat, parcel, got, send, recv):
    t = pl.program_id(0)
    p = t % STEPS
    nx = sizes[1]
    rows = 2 * nx
    pos = place(sizes)
    item, row, final_row = lax.axis_index("items"), lax.axis_index("rows"), lax.axis_size("rows") - 1
    share = acc.shape[0]
    per = share // NP

    def edge_copy(n):
        return pltpu.make_async_remote_copy(
            src_ref=edge.at[n], dst_ref=edge.at[2 + n], send_sem=edge_send.at[n], recv_sem=edge_recv.at[n],
            device_id=(item, row + (2 * n - 1)), device_id_type=MESH,
        )

    @pl.when(t == 0)
    def _():
        @pl.when(row == final_row)
        def _():
            edge[2] = jnp.zeros(edge.shape[1:], BF)

        @pl.when(row == 0)
        def _():
            edge[3] = jnp.zeros(edge.shape[1:], BF)

        greet(sizes, pos, True, False)
        tap_matrix(cw_ref, cb_ref, t_ref)
        make_windows(sizes, pos, img_ref, edge, [edge_copy(0), edge_copy(1)], x, xt_ref, sel_ref, pix, lines)

    @pl.when(p == 0)
    def _():
        acc[...] = jnp.broadcast_to(as_row(pb_ref), acc.shape)

    weight = w_ref[...].reshape(FEAT, D)
    for s in range(share // 256):
        rs = slice(s * 256, (s + 1) * 256)
        here = pl.ds(pl.multiple_of(t // STEPS * share + s * 256, 256), 256)
        xs = jnp.concatenate([x[p, here, :], x[p + 1, here, :]], axis=1)
        for n in range(FEAT // 256):
            cs = slice(n * 256, (n + 1) * 256)
            act, slope = gelu_pair_low(mm(xs, t_ref[:, cs]))
            saved_ref[0, 0, rs, cs] = act
            saved_ref[0, 1, rs, cs] = slope
        acc[rs, :] += mm(saved_ref[0, 0, rs, :], weight)

    @pl.when(p == STEPS - 1)
    def _():
        for c in range(NP):
            for k in range(D // 128):
                nat[k, pl.ds(c, per, stride=NP), :] = acc[c * per : (c + 1) * per, k * 128 : (k + 1) * 128]

    def parcel_copy(turn, core, slot):
        to = lax.rem(pos[1] + 1 + turn, nx) * 2 + core
        return pltpu.make_async_remote_copy(
            src_ref=parcel.at[turn, core], dst_ref=got.at[:, row], send_sem=send.at[turn, slot], recv_sem=recv.at[row],
            device_id=(item, to), device_id_type=MESH,
        )

    for turn in range(nx):
        @pl.when(t == turn * STEPS + STEPS - 1)
        def _(turn=turn):
            for k in range(D // 128):
                cut = nat[k].astype(BF).reshape(parcel.shape[1:4] + (128,))
                parcel[turn, :, :, :, k * 128 : (k + 1) * 128] = cut
            if turn < nx - 1:
                for core in range(2):
                    parcel_copy(turn, core, core).start()
            else:
                parcel_copy(turn, 1 - pos[0], 0).start()
                got[:, row] = parcel[turn, pos[0]]

    @pl.when(t == nx * STEPS - 1)
    def _():
        for k in range(1, rows):
            source = lax.rem(row + k, rows)
            pltpu.make_async_remote_copy(
                src_ref=parcel.at[0, 0], dst_ref=got.at[:, source], send_sem=send.at[0, 0], recv_sem=recv.at[source],
                device_id=(item, source), device_id_type=MESH,
            ).wait_recv()
        tok_ref[...] = got[...]
        for turn in range(nx - 1):
            for core in range(2):
                parcel_copy(turn, core, core).wait_send()
        parcel_copy(nx - 1, 1 - pos[0], 0).wait_send()

        @pl.when(row > 0)
        def _():
            edge_copy(0).wait_send()

        @pl.when(row < final_row)
        def _():
            edge_copy(1).wait_send()


def stem_forward(images, cw, cb, weight, bias, sizes):
    count, _, height, width = images.shape
    nx = sizes[1]
    nrow = height // PATCH
    group = count * nrow
    tokens = group * NP
    share = tokens // nx
    arrived = (SEQ_ITEMS, 2 * nx, nrow * NP, D)
    return pl.pallas_call(
        functools.partial(stem_kernel, sizes),
        name="stem_forward",
        grid=(nx * STEPS,),
        in_specs=[
            whole(images.shape),
            whole(cw.shape),
            whole(cb.shape),
            pl.BlockSpec((CH, 1, 2 * PATCH, D), lambda t: (0, t % STEPS, 0, 0)),
            whole(bias.shape),
        ],
        out_specs=(
            whole(arrived),
            pl.BlockSpec((1, 2, share, FEAT), lambda t: (t % STEPS, 0, t // STEPS, 0)),
            whole((SLABS, 128, tokens)),
            whole((CIN * width, NP * HALF)),
            whole((4 * HALF, FEAT)),
        ),
        out_shape=(
            jax.ShapeDtypeStruct(arrived, BF),
            jax.ShapeDtypeStruct((STEPS, 2, tokens, FEAT), BF),
            jax.ShapeDtypeStruct((SLABS, 128, tokens), BF),
            jax.ShapeDtypeStruct((CIN * width, NP * HALF), BF),
            jax.ShapeDtypeStruct((4 * HALF, FEAT), BF),
        ),
        scratch_shapes=[
            pltpu.VMEM((SLABS, tokens, 128), BF),
            pltpu.VMEM((CIN, width // 128, count * height, 128), F32),
            pltpu.VMEM((WIN * group, CIN * width), BF),
            pltpu.VMEM((4, CIN, group, width), BF),
            pltpu.SemaphoreType.DMA((2,)),
            pltpu.SemaphoreType.DMA((2,)),
            pltpu.VMEM((share, D), F32),
            pltpu.VMEM((D // 128, share, 128), F32),
            pltpu.VMEM((nx, 2, SEQ_ITEMS, nrow * NP, D), BF),
            pltpu.VMEM(arrived, BF),
            pltpu.SemaphoreType.DMA((nx, 2)),
            pltpu.SemaphoreType.DMA((2 * nx,)),
        ],
        compiler_params=params(collective_id=0, has_side_effects=True),
    )(images, cw, cb, weight, bias)


def norm_stats(v):
    centred = v - jnp.mean(v, axis=-1, keepdims=True)
    inv = lax.rsqrt(jnp.mean(centred * centred, axis=-1, keepdims=True) + 1e-06)
    return centred * inv, inv


def three_terms(v):
    hi = v.astype(BF)
    rest = v - hi.astype(F32)
    mid = rest.astype(BF)
    lo = (rest - mid.astype(F32)).astype(BF)
    return hi, mid, lo


def minus_terms(v, lane, base):
    rest = -v - (-v).astype(BF).astype(F32)
    return jnp.where(lane == 4, -v, jnp.where(lane == 5, rest, base)).astype(BF)


def attend_kernel(tok_ref, g_ref, b_ref, qb_ref, vb_ref, seg_ref, wq_ref, wk_ref, wv_ref,
                  q_ref, k_ref, v_ref, o_ref, o32_ref, lx_ref, kx_ref, n1, kaug, vaug):
    step = pl.program_id(0)
    line = lax.broadcasted_iota(jnp.int32, (1, 128), 1)
    first_item = lax.axis_index("rows") * SEQ_ITEMS
    same = [line == seg_ref[first_item + i] for i in range(SEQ_ITEMS)]
    terms = jnp.where((line >= 4) & (line < 6), 1.0, 0.0)
    keys_in = [jnp.where((line < 4) & ~one, -1e30, terms) for one in same]

    @pl.when(step == 0)
    def _():
        kx_ref[...] = jnp.concatenate(keys_in + [jnp.zeros((8 - SEQ_ITEMS, 128), F32)], axis=0)
        for s in range(TOK // 128):
            rs = slice(s * 128, (s + 1) * 128)
            hat, _ = norm_stats(tok_ref[rs, :].astype(F32))
            n1[rs, :] = (hat * as_row(g_ref) + as_row(b_ref)).astype(BF)

    own = pl.ds(pl.multiple_of(step * 256, 256), 256)
    q_ref[...] = ((mm(n1[...], wq_ref[...]) + as_row(qb_ref, own)).astype(BF) * 0.125).astype(BF)
    k_ref[...] = mm(n1[...], wk_ref[...]).astype(BF)
    v_ref[...] = (mm(n1[...], wv_ref[...]) + as_row(vb_ref, own)).astype(BF)
    lane = lax.broadcasted_iota(jnp.int32, (NPATCH, 128), 1)
    low = lane < HD
    for i in range(SEQ_ITEMS):
        rs = slice(i * NPATCH, (i + 1) * NPATCH)
        kaug[rs, 128:256] = jnp.broadcast_to(keys_in[i], (NPATCH, 128)).astype(BF)
        vaug[rs, 128:256] = jnp.ones((NPATCH, 128), BF)
    for pair in range(2):
        cs = slice(pair * 128, (pair + 1) * 128)
        kaug[:, 0:128] = k_ref[:, cs]
        vaug[:, 0:128] = v_ref[:, cs]
        for i in range(SEQ_ITEMS):
            rs = slice(i * NPATCH, (i + 1) * NPATCH)
            span = slice(0, (i + 1) * NPATCH)
            qp = q_ref[rs, cs]
            qx = jnp.broadcast_to(jnp.where(same[i], 1.0, 0.0), (NPATCH, 128))
            halves = []
            for h in range(2):
                mine = low if h == 0 else ~low
                qaug = jnp.concatenate([jnp.where(mine, qp, jnp.zeros_like(qp)), qx.astype(BF)], axis=1)
                scores = mm_t(qaug, kaug[span, :])
                top = jnp.max(scores, axis=1, keepdims=True)
                raised = jnp.exp(scores - top).astype(BF)
                out = mm(raised, vaug[span, :])
                total = out[:, 128:256]
                halves.append(out[:, 0:128] / total)
                lx_ref[pair * 2 + h, rs, :] = minus_terms(top + jnp.log(total), lane, qx)
            out = jnp.where(low, halves[0], halves[1])
            o32_ref[rs, cs] = out
            o_ref[rs, cs] = out.astype(BF)


def attend(tokens, vecs, segments, wq, wk, wv):
    lines = [whole(vec.shape) for vec in vecs]
    col = pl.BlockSpec((D, 256), lambda g: (0, g))
    out = pl.BlockSpec((TOK, 256), lambda g: (0, g))
    return pl.pallas_call(
        attend_kernel,
        name="attend",
        grid=(D // 256,),
        in_specs=[whole((TOK, D))] + lines + [pl.BlockSpec(memory_space=pltpu.SMEM), col, col, col],
        out_specs=(out, out, out, out, out, pl.BlockSpec((4, TOK, 128), lambda g: (g, 0, 0)), whole((8, 128))),
        out_shape=(jax.ShapeDtypeStruct((TOK, D), BF),) * 4
        + (
            jax.ShapeDtypeStruct((TOK, D), F32),
            jax.ShapeDtypeStruct((HEADS, TOK, 128), BF),
            jax.ShapeDtypeStruct((8, 128), F32),
        ),
        scratch_shapes=[pltpu.VMEM((TOK, D), BF), pltpu.VMEM((TOK, 256), BF), pltpu.VMEM((TOK, 256), BF)],
        compiler_params=params(),
    )(tokens, *vecs, segments, wq, wk, wv)


def norm_back(e, hat, inv, gain):
    f = e * gain
    return inv * (f - jnp.mean(f, axis=-1, keepdims=True) - hat * jnp.mean(f * hat, axis=-1, keepdims=True))


def col_sum(v):
    return jnp.sum(v, axis=0, keepdims=True)


def store_square(ref, n, grad):
    _, _, nx, ny, nz, _, _ = ref.shape
    height, width = D // (ny * nz), D // (2 * nx)
    if not folds(width):
        for r in range(2 * nx):
            part = grad[:, r * width : (r + 1) * width]
            for i in range(ny * nz):
                ref[n, r % 2, r // 2, i % ny, i // ny] = part[i * height : (i + 1) * height]
        return
    half = height // 2
    low = lax.broadcasted_iota(jnp.int32, (half, 128), 1) < HALF
    for x in range(nx):
        base = 2 * x * width
        shared = grad[:, base + 128 : base + 256]
        turned = jnp.concatenate([shared[:, HALF:], shared[:, :HALF]], axis=1)
        for i in range(ny * nz):
            top, end = i * height, (i + 1) * height
            mid = top + half
            ref[n, 0, x, i % ny, i // ny, 0:height] = grad[top:end, base : base + 128]
            ref[n, 0, x, i % ny, i // ny, height:] = jnp.where(low, shared[top:mid], turned[mid:end])
            ref[n, 1, x, i % ny, i // ny, 0:height] = grad[top:end, base + 256 : base + 384]
            ref[n, 1, x, i % ny, i // ny, height:] = jnp.where(low, turned[top:mid], shared[mid:end])


def mixer_kernel(tok_ref, att_ref, cot_ref, wo_ref, ob_ref, g_ref, b_ref, rb_ref, hb_ref, wh_ref, wr_ref,
                 out_ref, mid_ref, ag_ref, wog_ref, whg_ref, wrg_ref, sums_ref, hbg_ref,
                 middle, n2, n2t, cott, acc, back, act, hg, hidden_row):
    step = pl.program_id(0)
    last = pl.num_programs(0) - 1
    chunk = wh_ref.shape[1]
    tile = 2 if chunk % 256 == 0 else 3
    blocks = [slice(s * 256, (s + 1) * 256) for s in range(TOK // 256)]

    @pl.when(step == 0)
    def _():
        hidden_row[...] = as_row(hb_ref)
        for rs in blocks:
            row = tok_ref[rs, :].astype(F32) + mm(att_ref[rs, :], wo_ref[...]) + as_row(ob_ref)
            middle[rs, :] = row
            acc[rs, :] = row + as_row(rb_ref)
            back[rs, :] = jnp.zeros((256, D), F32)
            hat, _ = norm_stats(row)
            low = (hat * as_row(g_ref) + as_row(b_ref)).astype(BF)
            n2[rs, :] = low
            n2t[:, rs] = low.T
            cott[:, rs] = cot_ref[rs, :].T

    hidden_bias = hidden_row[0:1, pl.ds(pl.multiple_of(step * chunk, 128), chunk)]
    hsum = jnp.zeros((1, chunk), F32)
    for rs in blocks:
        for n in range(chunk // 128 // tile):
            cs = slice(n * 128 * tile, (n + 1) * 128 * tile)
            pre = mm(n2[rs, :], wh_ref[:, cs]) + hidden_bias[:, cs]
            up = mm_t(cot_ref[rs, :], wr_ref[cs, :])
            a, slope = gelu_pair(pre)
            act[rs, cs] = a.astype(BF)
            hg[rs, cs] = (slope * up).astype(BF)
        acc[rs, :] += mm(act[rs, :], wr_ref[...])
        back[rs, :] += mm_t(hg[rs, :], wh_ref[...])
        hsum = hsum + col_sum(hg[rs, :].astype(F32))
    hbg_ref[...] = hsum
    _, _, nx, ny, nz, height, _ = whg_ref.shape
    for n in range(3):
        width = chunk // 3
        grad = mm(n2t[...], hg[:, n * width : (n + 1) * width]).astype(BF)
        for i in range(ny * nz):
            whg_ref[n, 0, 0, i % ny, i // ny] = grad[i * height : (i + 1) * height]
    _, _, nx, ny, _, _, _ = wrg_ref.shape
    height, width = D // (2 * nx), chunk // ny // 3
    for y in range(ny):
        grad = mm(cott[...], act[:, y * 3 * width : (y + 1) * 3 * width]).astype(BF)
        for n in range(3):
            for r in range(2 * nx):
                part = grad[r * height : (r + 1) * height, n * width : (n + 1) * width]
                wrg_ref[n, r % 2, r // 2, y, 0] = fold_block(part)

    @pl.when(step == last)
    def _():
        gsum = jnp.zeros((1, D), F32)
        bsum = jnp.zeros((1, D), F32)
        osum = jnp.zeros((1, D), F32)
        rsum = jnp.zeros((1, D), F32)
        for rs in blocks:
            out_ref[rs, :] = acc[rs, :].astype(BF)
            hat, inv = norm_stats(middle[rs, :])
            e = back[rs, :]
            gsum = gsum + col_sum(e * hat)
            bsum = bsum + col_sum(e)
            cot = cot_ref[rs, :].astype(F32)
            rsum = rsum + col_sum(cot)
            mid = cot + norm_back(e, hat, inv, as_row(g_ref))
            mid_ref[rs, :] = mid
            low = mid.astype(BF)
            osum = osum + col_sum(low.astype(F32))
            n2[rs, :] = low
            n2t[:, rs] = att_ref[rs, :].T
            ag_ref[rs, :] = mm_t(low, wo_ref[...]).astype(BF)
        store_square(wog_ref, 0, mm(n2t[...], n2[...]).astype(BF))
        sums_ref[0:1, :] = gsum
        sums_ref[1:2, :] = bsum
        sums_ref[2:3, :] = osum
        sums_ref[3:4, :] = rsum


def mixer(tokens, attended, cotangent, wo, vecs, wh, wr, sizes):
    nc, nx, ny, nz = sizes
    rows, items = nc * nx, ny * nz
    chunk = FF // rows
    square = (1,) + sizes + folded_shape(D // items, D // rows)
    return pl.pallas_call(
        mixer_kernel,
        name="mixer",
        grid=(rows,),
        in_specs=[
            whole((TOK, D)), whole((TOK, D)), whole((TOK, D)), whole((D, D)),
            whole((D,)), whole((D,)), whole((D,)), whole((D,)), whole((FF,)),
            pl.BlockSpec((D, chunk), lambda r: (0, r)),
            pl.BlockSpec((chunk, D), lambda r: (r, 0)),
        ],
        out_specs=(
            whole((TOK, D)), whole((TOK, D)), whole((TOK, D)), whole(square),
            pl.BlockSpec((3, 1, 1, ny, nz, D // items, chunk // 3), lambda r: (0, r % 2, r // 2, 0, 0, 0, 0)),
            pl.BlockSpec((3, nc, nx, ny, 1) + folded_shape(D // rows, FF // items // 3), lambda r: (0, 0, 0, 0, r, 0, 0)),
            whole((8, D)),
            pl.BlockSpec((1, chunk), lambda r: (0, r)),
        ),
        out_shape=(
            jax.ShapeDtypeStruct((TOK, D), BF),
            jax.ShapeDtypeStruct((TOK, D), F32),
            jax.ShapeDtypeStruct((TOK, D), BF),
            jax.ShapeDtypeStruct(square, BF),
            jax.ShapeDtypeStruct((3,) + sizes + (D // items, chunk // 3), BF),
            jax.ShapeDtypeStruct((3,) + sizes + folded_shape(D // rows, FF // items // 3), BF),
            jax.ShapeDtypeStruct((8, D), F32),
            jax.ShapeDtypeStruct((1, FF), F32),
        ),
        scratch_shapes=[
            pltpu.VMEM((TOK, D), F32), pltpu.VMEM((TOK, D), BF), pltpu.VMEM((D, TOK), BF),
            pltpu.VMEM((D, TOK), BF), pltpu.VMEM((TOK, D), F32), pltpu.VMEM((TOK, D), F32),
            pltpu.VMEM((TOK, chunk), BF), pltpu.VMEM((TOK, chunk), BF), pltpu.VMEM((1, FF), F32),
        ],
        compiler_params=params(),
    )(tokens, attended, cotangent, wo, *vecs, wh, wr)


def attend_back_kernel(sizes, tok_ref, g_ref, b_ref, kx_ref, mid_ref, q_ref, k_ref, v_ref, o_ref, ag_ref, lx_ref,
                       wq_ref, wk_ref, wv_ref, whg_ref, wrg_ref, wog_ref,
                       tg_ref, sq_ref, sums_ref, qvs_ref, who_ref, wro_ref, woo_ref,
                       n1t, back, kaug, vaug, qaug, oaug, dqt, dq, dk, dv, square, *comm):
    step = pl.program_id(0)
    blocks = [slice(s * 256, (s + 1) * 256) for s in range(TOK // 256)]
    pos = place(sizes)
    groups = ((whg_ref, who_ref), (wrg_ref, wro_ref), (wog_ref, woo_ref))
    pieces, loads, base, at = [], [], 0, 0
    for source, _ in groups:
        count = source.shape[0]
        refs, keep = comm[at : at + 4 * count + 2], comm[at + 4 * count + 2 : at + 4 * count + 4]
        at += 4 * count + 4
        pieces += make_pieces(
            sizes, pos, BACK_ORDERS[base : base + count], [source.at[n] for n in range(count)],
            [keep[0].at[n] for n in range(count)], refs,
        )
        loads += [pltpu.make_async_copy(source.at[n, pos[0]], keep[0].at[n], keep[1].at[n]) for n in range(count)]
        base += count

    def event(index, stage):
        if stage == 0:
            pieces[index].start(0)
            loads[index].start()
        elif stage < 4:
            if stage == 1:
                loads[index].wait()
            pieces[index].advance(stage)
        else:
            total = pieces[index].gather(3)
            if index < 3:
                width = total.shape[1]
                who_ref[:, index * width : (index + 1) * width] = total
            elif index < 6:
                height, width = D // (2 * sizes[1]), FF // (sizes[2] * sizes[3]) // 3
                wro_ref[:, (index - 3) * width : (index - 2) * width] = unfold_block(total, height, width)
            else:
                woo_ref[...] = unfold_block(total, *woo_ref.shape, odd=pos[0] == 1)

    def finish():
        for part in pieces:
            part.drain()

    table = {(0, 0): [functools.partial(greet, sizes, pos, True, True)]}
    for when, index, stage in BACK_PLAN:
        if when < 2:
            key = (0, when)
        elif when < 26:
            key = ((when - 2) // 8, 2 + (when - 2) % 8)
        else:
            key = (2, 10)
        table.setdefault(key, []).append(functools.partial(event, index, stage))
    table.setdefault((2, 10), []).append(finish)
    run_events(step, table, (0,))

    @pl.when(step == 0)
    def _():
        for rs in blocks:
            hat, _ = norm_stats(tok_ref[rs, :].astype(F32))
            n1t[:, rs] = (hat * as_row(g_ref) + as_row(b_ref)).astype(BF).T
            back[rs, :] = jnp.zeros((256, D), F32)

    run_events(step, table, (1,))
    lane = lax.broadcasted_iota(jnp.int32, (NPATCH, 128), 1)
    low = lane < HD
    ones = jnp.where((lane >= 4) & (lane < 6), 1.0, 0.0).astype(BF)
    for i, rs in enumerate(blocks):
        kaug[rs, 128:256] = jnp.broadcast_to(kx_ref[i : i + 1, :], (NPATCH, 128)).astype(BF)
        vaug[rs, 128:256] = ones
    pick_row = lax.broadcasted_iota(jnp.int32, (256, 256), 0) % 128 // HD
    pick_col = lax.broadcasted_iota(jnp.int32, (256, 256), 1) // 128
    pick = jnp.where(pick_row == pick_col, 1.0, 0.0).astype(BF)
    for pair in range(2):
        cs = slice(pair * 128, (pair + 1) * 128)
        kaug[:, 0:128] = k_ref[:, cs]
        vaug[:, 0:128] = v_ref[:, cs]
        kt = k_ref[:, cs].T
        for rs in blocks:
            qp = q_ref[rs, cs]
            gp = ag_ref[rs, cs]
            prod = gp.astype(F32) * o_ref[rs, cs]
            hi = prod.astype(BF)
            both = jnp.concatenate([hi, (prod - hi.astype(F32)).astype(BF)], axis=1)
            dots = mm(both, pick)
            for h in range(2):
                mine = low if h == 0 else ~low
                qaug[h, rs, 0:128] = jnp.where(mine, qp, jnp.zeros_like(qp))
                qaug[h, rs, 128:256] = lx_ref[pair * 2 + h, rs, :]
                oaug[h, rs, 0:128] = jnp.where(mine, gp, jnp.zeros_like(gp))
                oaug[h, rs, 128:256] = minus_terms(dots[:, h * 128 : (h + 1) * 128], lane, jnp.zeros((NPATCH, 128), F32))
        for j, rs in enumerate(blocks):
            span = slice(j * NPATCH, TOK)
            parts_k, parts_v = [], []
            for h in range(2):
                probs = jnp.exp(mm_t(kaug[rs, :], qaug[h, span, :]))
                rise = mm_t(vaug[rs, :], oaug[h, span, :])
                grad = (probs * rise).astype(BF)
                probs_low = probs.astype(BF)
                parts_v.append(mm(probs_low, ag_ref[span, cs]))
                parts_k.append(mm(grad, q_ref[span, cs]))
                hs = slice(h * HD, (h + 1) * HD)
                part = mm(kt[hs, rs], grad)
                if j == 0:
                    dqt[hs, :] = part
                else:
                    dqt[hs, span] += part
            dk[rs, cs] = jnp.where(low, parts_k[0], parts_k[1]).astype(BF)
            dv[rs, cs] = jnp.where(low, parts_v[0], parts_v[1]).astype(BF)
            run_events(step, table, (2 + pair * 4 + j,))
        dq[:, cs] = (dqt[...].T * 0.125).astype(BF)
    qvs_ref[0:1, :] = col_sum(dq[...].astype(F32))
    qvs_ref[1:2, :] = col_sum(dv[...].astype(F32))
    for n, part in enumerate((dq, dk, dv)):
        square[n, step] = mm(n1t[...], part[...]).astype(BF)
    for rs in blocks:
        back[rs, :] += (
            mm_t(dq[rs, :], wq_ref[...]) + mm_t(dk[rs, :], wk_ref[...]) + mm_t(dv[rs, :], wv_ref[...])
        )

    @pl.when(step == pl.num_programs(0) - 1)
    def _():
        gsum = jnp.zeros((1, D), F32)
        bsum = jnp.zeros((1, D), F32)
        for rs in blocks:
            hat, inv = norm_stats(tok_ref[rs, :].astype(F32))
            e = back[rs, :]
            gsum = gsum + col_sum(e * hat)
            bsum = bsum + col_sum(e)
            tg_ref[rs, :] = (mid_ref[rs, :] + norm_back(e, hat, inv, as_row(g_ref))).astype(BF)
        sums_ref[0:1, :] = gsum
        sums_ref[1:2, :] = bsum
        for n in range(3):
            store_square(sq_ref, n, jnp.concatenate([square[n, g] for g in range(D // 256)], axis=1))

    run_events(step, table, (10,))


BACK_ORDERS = (
    (3, 2, 1), (2, 3, 1), (1, 2, 3), (1, 2, 3), (1, 2, 3), (1, 2, 3),
    (2, 1, 3),
)
BACK_PLAN = (
    (0, 3, 0), (0, 0, 0), (0, 1, 0), (0, 5, 0), (0, 4, 0), (0, 2, 0), (0, 6, 0), (1, 3, 1), (1, 0, 1),
    (1, 1, 1), (4, 5, 1), (6, 6, 1), (6, 2, 1), (7, 1, 2), (9, 3, 2), (9, 4, 1), (10, 5, 2), (15, 3, 3),
    (16, 2, 2), (16, 0, 2), (16, 5, 3), (17, 6, 2), (18, 3, 4), (18, 2, 3), (19, 4, 2), (19, 0, 3), (20, 1, 3),
    (21, 6, 3), (23, 4, 3), (26, 6, 4), (26, 1, 4), (26, 5, 4), (27, 0, 4), (28, 2, 4), (29, 4, 4),
)


def attend_back(tokens, gain, shift, kx, mid, q, k, v, o, ag, lx, wq, wk, wv, whg, wrg, wog, sizes):
    squares = (3,) + sizes + wog.shape[5:]
    col = pl.BlockSpec((D, 256), lambda g: (0, g))
    part = pl.BlockSpec((TOK, 256), lambda g: (0, g))
    far = pl.BlockSpec(memory_space=pl.ANY)
    items, rows = sizes[2] * sizes[3], 2 * sizes[1]
    outs = [(D // items, FF // rows), (D // rows, FF // items), (D // items, D // rows)]
    return pl.pallas_call(
        functools.partial(attend_back_kernel, sizes),
        name="attend_back",
        grid=(D // 256,),
        in_specs=[whole((TOK, D)), whole((D,)), whole((D,)), whole(kx.shape), whole((TOK, D)),
                  part, part, part, part, part, pl.BlockSpec((4, TOK, 128), lambda g: (g, 0, 0)),
                  col, col, col, far, far, far],
        out_specs=(whole((TOK, D)), whole(squares), whole((8, D)), pl.BlockSpec((8, 256), lambda g: (0, g)))
        + tuple(whole(shape) for shape in outs),
        out_shape=(
            jax.ShapeDtypeStruct((TOK, D), BF),
            jax.ShapeDtypeStruct(squares, BF),
            jax.ShapeDtypeStruct((8, D), F32),
            jax.ShapeDtypeStruct((8, D), F32),
        ) + tuple(jax.ShapeDtypeStruct(shape, F32) for shape in outs),
        scratch_shapes=[
            pltpu.VMEM((D, TOK), BF), pltpu.VMEM((TOK, D), F32),
            pltpu.VMEM((TOK, 256), BF), pltpu.VMEM((TOK, 256), BF),
            pltpu.VMEM((2, TOK, 256), BF), pltpu.VMEM((2, TOK, 256), BF),
            pltpu.VMEM((128, TOK), F32),
            pltpu.VMEM((TOK, 256), BF), pltpu.VMEM((TOK, 256), BF), pltpu.VMEM((TOK, 256), BF),
            pltpu.VMEM((3, D // 256, D, 256), BF),
        ]
        + piece_scratch(sizes, BACK_ORDERS[0:3], whg.shape[5:]) + own_scratch(sizes, 3, whg.shape[5:])
        + piece_scratch(sizes, BACK_ORDERS[3:6], wrg.shape[5:]) + own_scratch(sizes, 3, wrg.shape[5:])
        + piece_scratch(sizes, BACK_ORDERS[6:7], wog.shape[5:]) + own_scratch(sizes, 1, wog.shape[5:]),
        compiler_params=params(collective_id=1, has_side_effects=True),
    )(tokens, gain, shift, kx, mid, q, k, v, o, ag, lx, wq, wk, wv, whg, wrg, wog)


EARLY = 80
FINISH_ORDERS = (
    (1, 2, 3), (2, 1, 3), (3, 2, 1), (1, 2, 3), (2, 3, 1), (1, 2, 3),
    (2, 1, 3), (1, 2, 3), (2, 3, 1), (3, 1, 2), (2, 3, 1),
)
FINISH_PLAN = (
    (0, 8, 0), (0, 10, 0), (0, 9, 0), (1, 10, 1), (2, 9, 1), (3, 8, 1), (7, 10, 2), (9, 0, 0), (9, 8, 2),
    (10, 11, 0), (10, 1, 0), (10, 0, 1), (11, 2, 0), (11, 1, 1), (12, 3, 0), (12, 2, 1), (12, 3, 1), (13, 4, 0),
    (13, 0, 2), (14, 4, 1), (14, 5, 0), (14, 1, 2), (14, 11, 1), (15, 6, 0), (15, 5, 1), (16, 7, 0), (16, 0, 3),
    (16, 6, 1), (16, 3, 2), (17, 7, 1), (18, 4, 2), (18, 1, 3), (19, 10, 3), (19, 11, 2), (20, 5, 2), (20, 2, 2),
    (21, 8, 3), (22, 6, 2), (22, 3, 3), (22, 0, 4), (23, 4, 3), (23, 11, 3), (24, 12, 0), (24, 5, 3), (25, 7, 2),
    (25, 12, 1), (25, 6, 3), (25, 9, 2), (26, 12, 2), (26, 2, 3), (26, 10, 4), (28, 12, 3), (28, 5, 4), (29, 7, 3),
    (29, 1, 4), (30, 8, 4), (30, 2, 4), (31, 9, 3), (32, 11, 4), (32, 4, 4), (33, 3, 4), (33, 9, 4), (33, 6, 4),
    (33, 12, 4), (33, 7, 4),
)


def finish_kernel(sizes, tg_ref, act_ref, slope_ref, w_ref, xt_ref, t_ref, sel_ref, sq_ref, sums2_ref, hbg_ref, sums1_ref, qvs_ref,
                  pw_ref, sq0_ref, sq1_ref, sq2_ref, ig_ref, earlyo_ref, tapso_ref,
                  tgc, tgt, dxa, pg, cw, lines, flat, grads, edge, edge_send, edge_recv, got, send, recv, nat, *comm):
    t = pl.program_id(0)
    nc, nx, ny, nz = sizes
    items, rows = ny * nz, nc * nx
    tokens = tgc.shape[0]
    group = tokens // NP
    count, _, height, width = ig_ref.shape
    nrow = height // PATCH
    pos = place(sizes)
    item, row = lax.axis_index("items"), lax.axis_index("rows")
    final_row = lax.axis_size("rows") - 1
    far_steps = STEPS * (nx - 1)
    image_step = 2 * STEPS + far_steps
    final_step = image_step + CIN - 1
    at = 4 * STEPS + 2
    patch = make_pieces(
        sizes, pos, FINISH_ORDERS[0:STEPS], [grads.at[q % 2] for q in range(STEPS)],
        [grads.at[q % 2, pos[0]] for q in range(STEPS)], comm[0:at],
    )
    keep = comm[at + 14 : at + 16]
    square = make_pieces(
        sizes, pos, FINISH_ORDERS[STEPS : STEPS + 3], [sq_ref.at[n] for n in range(3)],
        [keep[0].at[n] for n in range(3)], comm[at : at + 14],
    )
    loads = [pltpu.make_async_copy(sq_ref.at[n, pos[0]], keep[0].at[n], keep[1].at[n]) for n in range(3)]
    at += 16
    early = SmallSum(sizes, pos, comm[at : at + 4], comm[at + 4], comm[at + 5])
    late = SmallSum(sizes, pos, comm[at + 6 : at + 10], comm[at + 10], comm[at + 11])

    def edge_copy(n):
        step = -1 if n == 0 else 1
        return pltpu.make_async_remote_copy(
            src_ref=edge.at[n], dst_ref=edge.at[2 + n], send_sem=edge_send.at[n], recv_sem=edge_recv.at[n],
            device_id=(item, row + step), device_id_type=MESH,
        )

    share, per = tokens // nx, group // nx
    turns = [turn_of(sizes, pos, xg) * share for xg in range(nx)]

    def spread(j, c):
        return jnp.concatenate(
            [dxa[j, pl.ds(pl.multiple_of(turns[xg] + c * per, per), per), :] for xg in range(nx)], axis=0
        )

    def parcel(k):
        to = lax.rem(row + k, rows)
        return pltpu.make_async_remote_copy(
            src_ref=tg_ref.at[:, to], dst_ref=got.at[row], send_sem=send.at[k - 1], recv_sem=recv.at[row],
            device_id=(item, to), device_id_type=MESH,
        )

    def arrived(source):
        pltpu.make_async_remote_copy(
            src_ref=tg_ref.at[:, source], dst_ref=got.at[source], send_sem=send.at[0], recv_sem=recv.at[source],
            device_id=(item, source), device_id_type=MESH,
        ).wait_recv()

    def unpack(xg, turn):
        for k in range(D // 128):
            cut = got[pl.ds(2 * xg, 2), :, :, k * 128 : (k + 1) * 128]
            nat[k] = cut.reshape(share, 128).astype(F32)
        for c in range(NP):
            part = jnp.concatenate([nat[k, pl.ds(c, per, stride=NP), :] for k in range(D // 128)], axis=1)
            tgc[turn * share + c * per : turn * share + (c + 1) * per, :] = part.astype(BF)

    def turn_over(turn):
        for s in range(share // 256):
            rs = slice(turn * share + s * 256, turn * share + (s + 1) * 256)
            tgt[:, rs] = tgc[rs, :].T

    def put_lines(j):
        low = lax.broadcasted_iota(jnp.int32, (group, 2 * HALF), 1) < HALF
        for pair in range(NP // 2):
            a, b = spread(j, 2 * pair), spread(j, 2 * pair + 1)
            cs = slice(pair * 128, (pair + 1) * 128)
            lines[2 * j * group : (2 * j + 1) * group, cs] = jnp.where(low, a, pltpu.roll(b, HALF, 1)).astype(BF)
            lines[(2 * j + 1) * group : (2 * j + 2) * group, cs] = jnp.where(low, pltpu.roll(a, HALF, 1), b).astype(BF)

    def event(index, stage):
        if index < STEPS:
            if stage == 0:
                patch[index].start(0)
            elif stage < 4:
                patch[index].advance(stage)
            else:
                total = unfold_block(patch[index].gather(3), D // rows, FEAT // items)
                for c in range(CH // items):
                    at = c * PATCH * PATCH + index * 2 * PATCH
                    pw_ref[:, at : at + 2 * PATCH] = total[:, c * 2 * PATCH : (c + 1) * 2 * PATCH]
        elif index < STEPS + 3:
            n = index - STEPS
            if stage == 0:
                loads[n].start()
                square[n].start(0)
                return
            if stage == 1:
                loads[n].wait()
            if stage < 4:
                square[n].advance(stage)
            else:
                out = (sq0_ref, sq1_ref, sq2_ref)[n]
                out[...] = unfold_block(square[n].gather(3), *out.shape, odd=pos[0] == 1)
        else:
            part, out = ((early, earlyo_ref), (late, tapso_ref))[index - STEPS - 3]
            if stage < 4:
                part.advance(stage)
            else:
                out[...] = part.gather(3)

    opening, table = [], {}
    for when, index, stage in FINISH_PLAN:
        if stage > 0 or index < STEPS + 3:
            call = functools.partial(event, index, stage)
            if when == 0:
                opening.append(call)
            else:
                later = when - 1 + (far_steps - STEPS if when > 3 * STEPS else 0)
                table.setdefault((min(later, final_step), 0), []).append(call)

    @pl.when(t == 0)
    def _():
        @pl.when(row == final_row)
        def _():
            edge[2] = jnp.zeros(edge.shape[1:], BF)

        @pl.when(row == 0)
        def _():
            edge[3] = jnp.zeros(edge.shape[1:], BF)

        greet(sizes, pos, True, True)
        for k in range(1, rows):
            parcel(k).start()
        for call in opening:
            call()
        got[row] = tg_ref[:, row]
        arrived(2 * pos[1] + 1 - pos[0])
        unpack(pos[1], nx - 1)
        turn_over(nx - 1)
        cw[...] = jnp.zeros_like(cw)

    @pl.when(t == STEPS)
    def _():
        for turn in range(nx - 1):
            xg = lax.rem(pos[1] + 1 + turn, nx)
            arrived(2 * xg)
            arrived(2 * xg + 1)
            unpack(xg, turn)
            turn_over(turn)

    @pl.when(t == STEPS + 1)
    def _():
        total = jnp.zeros((1, D), F32)
        for s in range(tokens // 256):
            total = total + col_sum(tgc[s * 256 : (s + 1) * 256, :].astype(F32))
        lines_in = [sums2_ref[0:1], sums2_ref[1:2], sums2_ref[2:3], sums2_ref[3:4]]
        lines_in += [hbg_ref[:, n * D : (n + 1) * D] for n in range(FF // D)]
        lines_in += [sums1_ref[0:1], sums1_ref[1:2], qvs_ref[0:1], qvs_ref[1:2], total]
        cells = [one[:, k * 128 : (k + 1) * 128] for one in lines_in for k in range(D // 128)]
        early.start(0, jnp.concatenate(cells + [jnp.zeros((EARLY - len(cells), 128), F32)], axis=0))

    @pl.when((t >= STEPS) & (t < 2 * STEPS))
    def _():
        for q in range(2, STEPS):
            @pl.when(t == STEPS + q)
            def _(q=q):
                patch[q - 2].drain((0,))

        feats = FEAT // items
        slot = t % 2
        for n in range(FEAT // 256):
            grad = mm(tgt[...], act_ref[0, 0, :, n * 256 : (n + 1) * 256]).astype(BF)
            for c in range(256 // feats):
                i = n * (256 // feats) + c
                for r in range(rows):
                    block = grad[r * (D // rows) : (r + 1) * (D // rows), c * feats : (c + 1) * feats]
                    grads[slot, r % 2, r // 2, i % ny, i // ny] = fold_block(block)

    def stem_part(p, turn):
        weight = w_ref[...].reshape(FEAT, D)

        def at(s, size):
            return pl.ds(pl.multiple_of(turn * share + s * 256, 256), size)

        @pl.when(p == 0)
        def _():
            dxa[0, at(0, share), :] = jnp.zeros((share, 128), F32)

        for s in range(share // 256):
            rs = slice(s * 256, (s + 1) * 256)
            for n in range(FEAT // 256):
                cs = slice(n * 256, (n + 1) * 256)
                da = mm_t(tgc[at(s, 256), :], weight[cs, :])
                pg[rs, cs] = (slope_ref[0, 0, rs, cs].astype(F32) * da).astype(BF)
            back = mm_t(pg[rs, :], t_ref[...])
            dxa[p, at(s, 256), :] += back[:, 0:128]
            dxa[p + 1, at(s, 256), :] = back[:, 128:256]
        xt = jnp.concatenate([xt_ref[p, :, at(0, share)], xt_ref[p + 1, :, at(0, share)]], axis=0)
        cw[...] += mm(xt, pg[...])

    near, far = t < STEPS, (t >= 2 * STEPS) & (t < image_step)

    @pl.when(near | far)
    def _():
        stem_part(t % STEPS, jnp.where(near, nx - 1, t // STEPS - 2))

    @pl.when((t >= image_step - STEPS) & (t < image_step))
    def _():
        p = t % STEPS

        @pl.when(p == 0)
        def _():
            put_lines(0)
            for ch in range(CIN):
                head = mm_t(lines[0:group], sel_ref[ch * width : (ch + 1) * width, :])
                edge[0, ch] = (pltpu.roll(head, nrow - 1, 0) if nrow > 1 else head).astype(BF)

            @pl.when(row > 0)
            def _():
                edge_copy(0).start()

        @pl.when(p == STEPS - 1)
        def _():
            put_lines(SLABS - 1)
            for ch in range(CIN):
                tail = mm_t(lines[(WIN - 1) * group : WIN * group], sel_ref[ch * width : (ch + 1) * width, :])
                edge[1, ch] = (pltpu.roll(tail, group - nrow + 1, 0) if nrow > 1 else tail).astype(BF)

            @pl.when(row < final_row)
            def _():
                edge_copy(1).start()

            late.start(0, tap_grad_rows(cw[...]))

    @pl.when(t >= image_step)
    def _():
        ch = t - image_step

        @pl.when(t == image_step)
        def _():
            for j in range(1, SLABS - 1):
                put_lines(j)

            @pl.when(row < final_row)
            def _():
                edge_copy(0).wait_recv()

            @pl.when(row > 0)
            def _():
                edge_copy(1).wait_recv()

        patch_row = lax.broadcasted_iota(jnp.int32, (group, width), 0) % nrow
        res = mm_t(lines[...], sel_ref[pl.ds(pl.multiple_of(ch * width, width), width), :])
        head = res[0:group]
        tail = res[(PATCH + 1) * group : (PATCH + 2) * group]
        for r in range(PATCH):
            v = res[(r + 1) * group : (r + 2) * group]
            if r == 0:
                v = v + jnp.where(patch_row == 0, edge[3, ch].astype(F32), pltpu.roll(tail, 1, 0))
            if r == PATCH - 1:
                v = v + jnp.where(patch_row == nrow - 1, edge[2, ch].astype(F32), pltpu.roll(head, group - 1, 0))
            flat[0, pl.ds(r, group, stride=PATCH), :] = v[:, 0:128]
            flat[1, pl.ds(r, group, stride=PATCH), :] = v[:, 128:256]
        for n in range(count):
            at = slice(n * height, (n + 1) * height)
            ig_ref[n, 0, :, 0:128] = flat[0, at, :]
            ig_ref[n, 0, :, 128:256] = flat[1, at, :]

    def close():
        for part in square:
            part.drain()
        for q, part in enumerate(patch):
            part.drain((1, 2, 3) if q < STEPS - 2 else (0, 1, 2, 3))
        early.drain()
        late.drain()
        for k in range(1, rows):
            parcel(k).wait_send()

        @pl.when(row > 0)
        def _():
            edge_copy(0).wait_send()

        @pl.when(row < final_row)
        def _():
            edge_copy(1).wait_send()

    table.setdefault((final_step, 0), []).append(close)
    run_events(t, table, (0,))


def finish(tg, saved, weight, xt, taps, sel, squares, sums2, hbg, sums1, qvs, count, height, sizes):
    nc, nx, ny, nz = sizes
    items, rows = ny * nz, nc * nx
    group = count * height // PATCH
    tokens = group * NP
    feats = FEAT // items
    square = squares.shape[5:]
    share = tokens // nx
    image_step = STEPS * (nx + 1)

    def clip(v, low, high):
        return jnp.minimum(jnp.maximum(v, low), high)

    def sub(t):
        held = jnp.where(t < STEPS, t, jnp.where(t < 2 * STEPS, 0, t % STEPS))
        return jnp.where(t < image_step, held, STEPS - 1)

    def turn(t):
        return jnp.where(t < STEPS, nx - 1, clip(t // STEPS - 2, 0, nx - 2))

    return pl.pallas_call(
        functools.partial(finish_kernel, sizes),
        name="finish",
        grid=(image_step + CIN,),
        in_specs=[
            whole(tg.shape),
            pl.BlockSpec((1, 1, tokens, FEAT), lambda t: (clip(t - STEPS, 0, STEPS - 1), 0, 0, 0)),
            pl.BlockSpec((1, 1, share, FEAT), lambda t: (sub(t), 1, turn(t), 0)),
            pl.BlockSpec((CH, 1, 2 * PATCH, D), lambda t: (0, sub(t), 0, 0)),
            whole(xt.shape),
            whole(taps.shape),
            whole(sel.shape),
            pl.BlockSpec(memory_space=pl.ANY),
            whole(sums2.shape), whole(hbg.shape), whole(sums1.shape), whole(qvs.shape),
        ],
        out_specs=(
            whole((D // rows, PF // items)),
            whole((D // items, D // rows)),
            whole((D // items, D // rows)),
            whole((D // items, D // rows)),
            pl.BlockSpec((count, 1, height, IMG), lambda t: (0, clip(t - image_step, 0, CIN - 1), 0, 0)),
            whole((EARLY, 128)),
            whole((32, 128)),
        ),
        out_shape=(
            jax.ShapeDtypeStruct((D // rows, PF // items), F32),
            jax.ShapeDtypeStruct((D // items, D // rows), F32),
            jax.ShapeDtypeStruct((D // items, D // rows), F32),
            jax.ShapeDtypeStruct((D // items, D // rows), F32),
            jax.ShapeDtypeStruct((count, CIN, height, IMG), F32),
            jax.ShapeDtypeStruct((EARLY, 128), F32),
            jax.ShapeDtypeStruct((32, 128), F32),
        ),
        scratch_shapes=[
            pltpu.VMEM((tokens, D), BF),
            pltpu.VMEM((D, tokens), BF),
            pltpu.VMEM((SLABS, tokens, 128), F32),
            pltpu.VMEM((share, FEAT), BF),
            pltpu.VMEM((4 * HALF, FEAT), F32),
            pltpu.VMEM((WIN * group, NP * HALF), BF),
            pltpu.VMEM((2, group * PATCH, 128), F32),
            pltpu.VMEM((2,) + sizes + folded_shape(D // rows, feats), BF),
            pltpu.VMEM((4, CIN, group, IMG), BF),
            pltpu.SemaphoreType.DMA((2,)),
            pltpu.SemaphoreType.DMA((2,)),
            pltpu.VMEM((rows, SEQ_ITEMS, tokens // rows // SEQ_ITEMS, D), BF),
            pltpu.SemaphoreType.DMA((rows - 1,)),
            pltpu.SemaphoreType.DMA((rows,)),
            pltpu.VMEM((D // 128, share, 128), F32),
        ]
        + piece_scratch(sizes, FINISH_ORDERS[0:STEPS], folded_shape(D // rows, feats))
        + piece_scratch(sizes, FINISH_ORDERS[STEPS : STEPS + 3], square) + own_scratch(sizes, 3, square)
        + small_scratch(sizes, EARLY)
        + small_scratch(sizes, 32),
        compiler_params=params(collective_id=2, has_side_effects=True),
    )(tg, saved, saved, weight, xt, taps, sel, squares, sums2, hbg, sums1, qvs)


def feature_parts(rows):
    feat = lax.broadcasted_iota(jnp.int32, (rows, FEAT), 1)
    return feat // (2 * PATCH), feat // PATCH % 2, feat % PATCH


def tap_rows(wide, ch, r, b, half):
    parts = []
    for r2 in range(2):
        a = r - r2
        parts.append(wide[9 * ch + 3 * a + b : 9 * ch + 3 * a + b + 1, :] if 0 <= a < 3 else jnp.zeros((1, FEAT), F32))
    return jnp.where(half == 0, parts[0], parts[1])


def tap_matrix(cw_ref, cb_ref, t_ref):
    chan, _, _ = feature_parts(32)
    expand = jnp.where(chan == lax.broadcasted_iota(jnp.int32, (32, FEAT), 0), 1.0, 0.0).astype(BF)
    wide = lax.dot_general(cw_ref[...], expand, (((0,), (0,)), ((), ())), preferred_element_type=F32)
    bias = mm(jnp.broadcast_to(as_row(cb_ref), (8, CH)).astype(BF), expand)
    _, half, spot = feature_parts(1)
    line = lax.broadcasted_iota(jnp.int32, (HALF, FEAT), 0)
    for r in range(4):
        block = jnp.zeros((HALF, FEAT), F32)
        if r == 0:
            block = jnp.where(line == ONE_LANE, bias[0:1, :], block)
        for ch in range(CIN):
            for b in range(3):
                block = jnp.where(line == WIN * ch + b + spot, tap_rows(wide, ch, r, b, half), block)
        t_ref[r * HALF : (r + 1) * HALF, :] = block.astype(BF)


def tap_grad_rows(full):
    chan, half, spot = feature_parts(1)
    line = lax.broadcasted_iota(jnp.int32, (HALF, FEAT), 0)
    sums = [[None] * 3 for _ in range(9)]
    for r in range(4):
        block = full[r * HALF : (r + 1) * HALF]
        for ch in range(CIN):
            for b in range(3):
                line_sum = jnp.sum(jnp.where(line == WIN * ch + b + spot, block, 0.0), axis=0, keepdims=True)
                for a in range(3):
                    if 0 <= r - a < 2:
                        part = jnp.where(half == r - a, line_sum, 0.0)
                        old = sums[3 * ch + b][a]
                        sums[3 * ch + b][a] = part if old is None else old + part
    lines = [sums[3 * ch + b][a] for ch in range(CIN) for a in range(3) for b in range(3)]
    lines.append(full[ONE_LANE : ONE_LANE + 1])
    lines.append(jnp.zeros((4, FEAT), F32))
    table = jnp.concatenate(lines, axis=0)
    chan, _, _ = feature_parts(128)
    expand = jnp.where(chan == lax.broadcasted_iota(jnp.int32, (128, FEAT), 0), 1.0, 0.0).astype(BF)
    hi, mid, lo = three_terms(table)
    return mm_t(hi, expand) + (mm_t(mid, expand) + mm_t(lo, expand))


def on_device(
    images, item_segment, conv_weight, conv_bias, patch_weight, patch_bias, norm1_gain, norm1_bias,
    query_weight, query_bias, key_weight, value_weight, value_bias, output_weight, output_bias,
    norm2_gain, norm2_bias, hidden_weight, hidden_bias, result_weight, result_bias, cotangent,
):
    items, rows = lax.axis_size("items"), lax.axis_size("rows")
    sizes = grid_sizes(items, rows)
    count, _, height, _ = images.shape
    nrow = height // PATCH

    cw = conv_weight.reshape(CH, 27)
    weight4 = patch_weight.reshape(CH, STEPS, 2 * PATCH, D)
    tokens, saved, xt, sel, taps = stem_forward(images, cw, conv_bias, weight4, patch_bias, sizes)
    tokens = tokens.reshape(TOK, D)
    q, k, v, attended, attended32, lx, kx = attend(
        tokens, (norm1_gain, norm1_bias, query_bias, value_bias), item_segment, query_weight, key_weight, value_weight)
    block_out, middle_grad, attended_grad, wo_grad, wh_grad, wr_grad, sums2, hb_grad = mixer(
        tokens, attended, cotangent, output_weight,
        (output_bias, norm2_gain, norm2_bias, result_bias, hidden_bias), hidden_weight, result_weight, sizes,
    )
    token_grad, squares, sums1, qvs, wh_grad, wr_grad, wo_grad = attend_back(
        tokens, norm1_gain, norm1_bias, kx, middle_grad, q, k, v, attended32, attended_grad, lx,
        query_weight, key_weight, value_weight, wh_grad, wr_grad, wo_grad, sizes,
    )
    token_grad = token_grad.reshape(SEQ_ITEMS, rows, nrow * NP, D)
    pw_grad, wq_grad, wk_grad, wv_grad, image_grad, sums, tap_grads = finish(
        token_grad, saved, weight4, xt, taps, sel, squares, sums2, hb_grad, sums1, qvs, count, height, sizes
    )
    wide = D // 128

    def row_of(at):
        return sums[at * wide : (at + 1) * wide].reshape(D)

    return (
        block_out,
        image_grad,
        tap_grads[0:27, 0:CH].T.reshape(conv_weight.shape),
        tap_grads[27, 0:CH],
        pw_grad.T,
        row_of(12),
        row_of(8),
        row_of(9),
        wq_grad,
        row_of(10),
        wk_grad,
        wv_grad,
        row_of(11),
        wo_grad,
        row_of(2),
        row_of(0),
        row_of(1),
        wh_grad,
        sums[4 * wide : 8 * wide].reshape(FF),
        wr_grad.T,
        row_of(3),
    )


def solution(mesh):
    split = P("items", "rows")
    flat = P(("items", "rows"), None)
    image = P("items", None, "rows", None)
    return jax.shard_map(
        on_device,
        mesh=mesh,
        in_specs=(image, P("items")) + (P(),) * 19 + (flat,),
        out_specs=(
            flat, image, P(), P(), split, P(), P(), P(), split, P(), split, split,
            P(), split, P(), P(), P(), split, P(), split, P(),
        ),
        check_vma=False,
    )
```

```python
import functools

import jax
import jax.numpy as jnp
from jax import lax
from jax.experimental import pallas as pl
from jax.experimental.pallas import tpu as pltpu
from jax.sharding import PartitionSpec as P

BF = jnp.bfloat16
F32 = jnp.float32
D = 768
HEADS = 12
HD = 64
FF = 3072
IMG = 256
PATCH = 16
CH = 32
CIN = 3
SEQ_ITEMS = 4
NPATCH = 256
TOK = 1024
NP = IMG // PATCH
PF = CH * PATCH * PATCH
HALF = 64
WIN = PATCH + 2
ONE_LANE = CIN * WIN
SLABS = (PATCH + 2) // 2
STEPS = PATCH // 2
FEAT = PF // STEPS
GELU_A = 0.7978845608028654
GELU_B = GELU_A * 0.044715
VMEM_CAP = 60 * 1024 * 1024


def mm(left, right):
    return jnp.dot(left, right, preferred_element_type=F32)


def mm_t(left, right):
    return lax.dot_general(left, right, (((1,), (1,)), ((), ())), preferred_element_type=F32)


def params(**extra):
    return pltpu.CompilerParams(vmem_limit_bytes=VMEM_CAP, **extra)


def whole(shape):
    zeros = (0,) * len(shape)
    return pl.BlockSpec(shape, lambda *_: zeros, pipeline_mode=pl.Buffered(1))


def gelu_pair_low(v):
    bend = jnp.tanh((v * (GELU_A + GELU_B * (v * v))).astype(BF))
    low = v.astype(BF)
    gate = bend * BF(0.5) + BF(0.5)
    act = low * gate
    slope = gate + act * (BF(1.0) - gate) * (BF(2.0 * GELU_A) + BF(6.0 * GELU_B) * (low * low))
    return act, slope


def as_row(ref, at=None):
    line = ref[...] if at is None else ref[at]
    return line.astype(F32).reshape(1, line.shape[0])


def gelu_pair(v):
    square = v * v
    gate = 0.5 + 0.5 * jnp.tanh(v * (GELU_A + GELU_B * square))
    act = v * gate
    slope = gate + act * (1.0 - gate) * (2.0 * GELU_A + (6.0 * GELU_B) * square)
    return act, slope


MESH = pl.DeviceIdType.MESH


def grid_sizes(items, rows):
    nx = rows // 2
    ny = nx if items % nx == 0 else 1
    return (2, nx, ny, items // ny)


def place(sizes):
    item, row = lax.axis_index("items"), lax.axis_index("rows")
    return (row % 2, row // 2, item % sizes[2], item // sizes[2])


def peer(sizes, pos, axis, k):
    moved = list(pos)
    moved[axis] = lax.rem(pos[axis] + k, sizes[axis])
    return (moved[3] * sizes[2] + moved[2], moved[1] * 2 + moved[0]), moved[axis]


def greet(sizes, pos, near, far):
    barrier = pltpu.get_barrier_semaphore()
    item, row, rows = lax.axis_index("items"), lax.axis_index("rows"), 2 * sizes[1]
    peers = [(item, lax.rem(row + k, rows)) for k in range(1, rows)] if near else []
    for axis in (2, 3) if far else ():
        peers += [peer(sizes, pos, axis, k)[0] for k in range(1, sizes[axis])]
    for device in peers:
        pl.semaphore_signal(barrier, inc=1, device_id=device, device_id_type=MESH)
    pl.semaphore_wait(barrier, len(peers))


def turn_of(sizes, pos, x):
    return lax.rem(x + 2 * sizes[1] - 1 - pos[1], sizes[1])


def add_up(first, rest):
    total = first.astype(F32)
    for term in rest:
        total = total + term.astype(F32)
    return total


class Piece:
    def __init__(self, sizes, pos, order, source, own, bufs, send, recv):
        self.sizes, self.pos = sizes, pos
        self.source, self.own, self.bufs = source, own, bufs
        self.send, self.recv = send, recv
        self.axes = (0,) + order

    def at(self, stage, where):
        left = sorted(self.axes[stage:])
        return (slice(None),) * left.index(self.axes[stage]) + (where,)

    def copies(self, stage):
        out = []
        for k in range(1, self.sizes[self.axes[stage]]):
            device, there = peer(self.sizes, self.pos, self.axes[stage], k)
            if stage == 0:
                src, dst = self.source.at[there], self.bufs[0]
            else:
                held = self.at(stage, there)
                src = self.bufs[0].at[held] if stage == 1 else self.bufs[stage - 1].at[(0,) + held]
                dst = self.bufs[stage].at[k - 1]
            out.append(
                pltpu.make_async_remote_copy(
                    src_ref=src, dst_ref=dst, send_sem=self.send.at[stage, k - 1], recv_sem=self.recv.at[stage, k - 1],
                    device_id=device, device_id_type=MESH,
                )
            )
        return out

    def start(self, stage):
        for copy in self.copies(stage):
            copy.start()

    def gather(self, stage):
        for copy in self.copies(stage):
            copy.wait_recv()
        bufs = self.bufs
        if stage == 0:
            bufs[0][...] = bufs[0][...] + self.own[...]
            return None
        held = self.at(stage, self.pos[self.axes[stage]])
        base = bufs[0][held] if stage == 1 else bufs[stage - 1][(0,) + held]
        terms = self.sizes[self.axes[stage]] - 1
        if stage < 3 and terms == 1:
            bufs[stage][0] = base + bufs[stage][0]
            return None
        total = add_up(base, [bufs[stage][k] for k in range(terms)])
        if stage == 3:
            return total
        bufs[stage][0] = total.astype(BF)

    def advance(self, stage):
        self.gather(stage - 1)
        self.start(stage)

    def drain(self, stages=(0, 1, 2, 3)):
        for stage in stages:
            for copy in self.copies(stage):
                copy.wait_send()


def piece_scratch(sizes, orders, shape):
    out = []
    for order in orders:
        out.append(pltpu.VMEM(sizes[1:] + shape, BF))
        for stage in range(3):
            left = tuple(sizes[axis] for axis in sorted(order[stage + 1 :]))
            out.append(pltpu.VMEM((sizes[order[stage]] - 1,) + left + shape, BF))
    sems = pltpu.SemaphoreType.DMA((len(orders), 4, max(sizes) - 1))
    return out + [sems, sems]


def own_scratch(sizes, count, shape):
    return [pltpu.VMEM((count,) + sizes[1:] + shape, BF), pltpu.SemaphoreType.DMA((count,))]


def make_pieces(sizes, pos, orders, sources, owns, refs):
    count = len(orders)
    return [
        Piece(sizes, pos, orders[n], sources[n], owns[n], refs[4 * n : 4 * n + 4], refs[4 * count].at[n], refs[4 * count + 1].at[n])
        for n in range(count)
    ]


class SmallSum:
    def __init__(self, sizes, pos, bufs, send, recv):
        self.sizes, self.pos, self.bufs, self.send, self.recv = sizes, pos, bufs, send, recv

    def copies(self, axis, receive):
        buf, here = self.bufs[axis], self.pos[axis]
        out = []
        for k in range(1, self.sizes[axis]):
            device, _ = peer(self.sizes, self.pos, axis, k)
            slot = lax.rem(here + self.sizes[axis] - k, self.sizes[axis]) if receive else here
            out.append(
                pltpu.make_async_remote_copy(
                    src_ref=buf.at[here], dst_ref=buf.at[slot], send_sem=self.send.at[axis, k - 1],
                    recv_sem=self.recv.at[axis, k - 1], device_id=device, device_id_type=MESH,
                )
            )
        return out

    def start(self, axis, value):
        self.bufs[axis][self.pos[axis]] = value
        for copy in self.copies(axis, False):
            copy.start()

    def gather(self, axis):
        for copy in self.copies(axis, True):
            copy.wait_recv()
        total = self.bufs[axis][0]
        for k in range(1, self.sizes[axis]):
            total = total + self.bufs[axis][k]
        return total

    def advance(self, axis):
        self.start(axis, self.gather(axis - 1))

    def drain(self):
        for axis in range(4):
            for copy in self.copies(axis, False):
                copy.wait_send()


def small_scratch(sizes, height):
    return [pltpu.VMEM((size, height, 128), F32) for size in sizes] + [
        pltpu.SemaphoreType.DMA((4, max(sizes) - 1)),
        pltpu.SemaphoreType.DMA((4, max(sizes) - 1)),
    ]


def folds(width):
    return width % 128 == HALF and width > 128


def narrow(width):
    return 128 // width if width < 128 and 128 % width == 0 else 1


def folded_shape(height, width):
    if folds(width) or narrow(width) > 1:
        return (height * width // 128, 128)
    return (height, width)


def fold_block(block):
    height, width = block.shape
    if narrow(width) > 1:
        part = height // narrow(width)
        return jnp.concatenate([block[k * part : (k + 1) * part] for k in range(narrow(width))], axis=1)
    return block


def unfold_block(block, height, width, odd=False):
    if narrow(width) > 1:
        return jnp.concatenate([block[:, k * width : (k + 1) * width] for k in range(narrow(width))], axis=0)
    if not folds(width):
        return block
    main, side = block[:height], block[height:]
    side = jnp.concatenate([side[:, :HALF], side[:, HALF:]], axis=0)
    return jnp.where(odd, jnp.concatenate([side, main], axis=1), jnp.concatenate([main, side], axis=1))


def run_events(step, table, slots):
    for (when, slot), todo in table.items():
        if slot in slots:
            @pl.when(step == when)
            def _(todo=todo):
                for call in todo:
                    call()


def make_windows(sizes, pos, img_ref, edge, edge_copies, x, xt_ref, sel_ref, pix, lines):
    items, _, height, width = img_ref.shape
    nrow = height // PATCH
    group = items * nrow
    row, final_row = lax.axis_index("rows"), lax.axis_size("rows") - 1
    for ch in range(CIN):
        for item in range(items):
            full = img_ref[item, ch].astype(F32)
            for k in range(width // 128):
                pix[ch, k, item * height : (item + 1) * height, :] = full[:, k * 128 : (k + 1) * 128]

    def line(ch, r):
        return jnp.concatenate([pix[ch, k, pl.ds(r, group, stride=PATCH), :] for k in range(width // 128)], axis=1)

    for ch in range(CIN):
        first, final = line(ch, 0), line(ch, PATCH - 1)
        edge[0, ch] = pltpu.roll(first, nrow - 1, 0).astype(BF)
        edge[1, ch] = pltpu.roll(final, group - nrow + 1, 0).astype(BF)

    @pl.when(row > 0)
    def _():
        edge_copies[0].start()

    @pl.when(row < final_row)
    def _():
        edge_copies[1].start()

    for ch in range(CIN):
        cols = slice(ch * width, (ch + 1) * width)
        for r in range(PATCH):
            lines[(r + 1) * group : (r + 2) * group, cols] = line(ch, r).astype(BF)
    lane = lax.broadcasted_iota(jnp.int32, (1, NP * HALF), 1)
    col, spot = lane // HALF, lane % HALF
    for ch in range(CIN):
        inside = (spot >= WIN * ch) & (spot < WIN * (ch + 1))
        want = jnp.where(inside, PATCH * col + spot - WIN * ch - 1, -5)
        here = lax.broadcasted_iota(jnp.int32, (width, NP * HALF), 0)
        sel_ref[ch * width : (ch + 1) * width, :] = jnp.where(here == want, 1.0, 0.0).astype(BF)

    @pl.when(row < final_row)
    def _():
        edge_copies[0].wait_recv()

    @pl.when(row > 0)
    def _():
        edge_copies[1].wait_recv()

    patch_row = lax.broadcasted_iota(jnp.int32, (group, width), 0) % nrow
    for ch in range(CIN):
        cols = slice(ch * width, (ch + 1) * width)
        up = jnp.where(patch_row == 0, edge[3, ch].astype(F32), pltpu.roll(line(ch, PATCH - 1), 1, 0))
        lines[0:group, cols] = up.astype(BF)
        down = jnp.where(patch_row == nrow - 1, edge[2, ch].astype(F32), pltpu.roll(line(ch, 0), group - 1, 0))
        lines[(PATCH + 1) * group : (PATCH + 2) * group, cols] = down.astype(BF)
    lane = lax.broadcasted_iota(jnp.int32, (group, 2 * HALF), 1)
    low = lane < HALF
    ones = (lane % HALF) == ONE_LANE
    nx = sizes[1]
    share, per = items * nrow * NP // nx, group // nx
    turns = [turn_of(sizes, pos, xg) * share for xg in range(nx)]

    def put(j, c, block):
        low_bits = block.astype(BF)
        for xg in range(nx):
            x[j, pl.ds(pl.multiple_of(turns[xg] + c * per, per), per), :] = low_bits[xg * per : (xg + 1) * per]

    for quarter in range(NP * HALF // 256):
        res = mm(lines[...], sel_ref[:, quarter * 256 : (quarter + 1) * 256])
        for j in range(SLABS):
            first = res[2 * j * group : (2 * j + 1) * group]
            second = res[(2 * j + 1) * group : (2 * j + 2) * group]
            for pair in range(2):
                a = first[:, pair * 128 : (pair + 1) * 128]
                b = second[:, pair * 128 : (pair + 1) * 128]
                put(j, quarter * 4 + pair * 2, jnp.where(ones, 1.0, jnp.where(low, a, pltpu.roll(b, HALF, 1))))
                put(j, quarter * 4 + pair * 2 + 1, jnp.where(ones, 1.0, jnp.where(low, pltpu.roll(a, HALF, 1), b)))
    for j in range(SLABS):
        xt_ref[j] = x[j].T


def stem_kernel(sizes, img_ref, cw_ref, cb_ref, w_ref, pb_ref, tok_ref, saved_ref, xt_ref, sel_ref, t_ref,
                x, pix, lines, edge, edge_send, edge_recv, acc, nat, parcel, got, send, recv):
    t = pl.program_id(0)
    p = t % STEPS
    nx = sizes[1]
    rows = 2 * nx
    pos = place(sizes)
    item, row, final_row = lax.axis_index("items"), lax.axis_index("rows"), lax.axis_size("rows") - 1
    share = acc.shape[0]
    per = share // NP

    def edge_copy(n):
        return pltpu.make_async_remote_copy(
            src_ref=edge.at[n], dst_ref=edge.at[2 + n], send_sem=edge_send.at[n], recv_sem=edge_recv.at[n],
            device_id=(item, row + (2 * n - 1)), device_id_type=MESH,
        )

    @pl.when(t == 0)
    def _():
        @pl.when(row == final_row)
        def _():
            edge[2] = jnp.zeros(edge.shape[1:], BF)

        @pl.when(row == 0)
        def _():
            edge[3] = jnp.zeros(edge.shape[1:], BF)

        greet(sizes, pos, True, False)
        tap_matrix(cw_ref, cb_ref, t_ref)
        make_windows(sizes, pos, img_ref, edge, [edge_copy(0), edge_copy(1)], x, xt_ref, sel_ref, pix, lines)

    @pl.when(p == 0)
    def _():
        acc[...] = jnp.broadcast_to(as_row(pb_ref), acc.shape)

    weight = w_ref[...].reshape(FEAT, D)
    for s in range(share // 256):
        rs = slice(s * 256, (s + 1) * 256)
        here = pl.ds(pl.multiple_of(t // STEPS * share + s * 256, 256), 256)
        xs = jnp.concatenate([x[p, here, :], x[p + 1, here, :]], axis=1)
        for n in range(FEAT // 256):
            cs = slice(n * 256, (n + 1) * 256)
            act, slope = gelu_pair_low(mm(xs, t_ref[:, cs]))
            saved_ref[0, 0, rs, cs] = act
            saved_ref[0, 1, rs, cs] = slope
        acc[rs, :] += mm(saved_ref[0, 0, rs, :], weight)

    @pl.when(p == STEPS - 1)
    def _():
        for c in range(NP):
            for k in range(D // 128):
                nat[k, pl.ds(c, per, stride=NP), :] = acc[c * per : (c + 1) * per, k * 128 : (k + 1) * 128]

    def parcel_copy(turn, core, slot):
        to = lax.rem(pos[1] + 1 + turn, nx) * 2 + core
        return pltpu.make_async_remote_copy(
            src_ref=parcel.at[turn, core], dst_ref=got.at[:, row], send_sem=send.at[turn, slot], recv_sem=recv.at[row],
            device_id=(item, to), device_id_type=MESH,
        )

    for turn in range(nx):
        @pl.when(t == turn * STEPS + STEPS - 1)
        def _(turn=turn):
            for k in range(D // 128):
                cut = nat[k].astype(BF).reshape(parcel.shape[1:4] + (128,))
                parcel[turn, :, :, :, k * 128 : (k + 1) * 128] = cut
            if turn < nx - 1:
                for core in range(2):
                    parcel_copy(turn, core, core).start()
            else:
                parcel_copy(turn, 1 - pos[0], 0).start()
                got[:, row] = parcel[turn, pos[0]]

    @pl.when(t == nx * STEPS - 1)
    def _():
        for k in range(1, rows):
            source = lax.rem(row + k, rows)
            pltpu.make_async_remote_copy(
                src_ref=parcel.at[0, 0], dst_ref=got.at[:, source], send_sem=send.at[0, 0], recv_sem=recv.at[source],
                device_id=(item, source), device_id_type=MESH,
            ).wait_recv()
        tok_ref[...] = got[...]
        for turn in range(nx - 1):
            for core in range(2):
                parcel_copy(turn, core, core).wait_send()
        parcel_copy(nx - 1, 1 - pos[0], 0).wait_send()

        @pl.when(row > 0)
        def _():
            edge_copy(0).wait_send()

        @pl.when(row < final_row)
        def _():
            edge_copy(1).wait_send()


def stem_forward(images, cw, cb, weight, bias, sizes):
    count, _, height, width = images.shape
    nx = sizes[1]
    nrow = height // PATCH
    group = count * nrow
    tokens = group * NP
    share = tokens // nx
    arrived = (SEQ_ITEMS, 2 * nx, nrow * NP, D)
    return pl.pallas_call(
        functools.partial(stem_kernel, sizes),
        name="stem_forward",
        grid=(nx * STEPS,),
        in_specs=[
            whole(images.shape),
            whole(cw.shape),
            whole(cb.shape),
            pl.BlockSpec((CH, 1, 2 * PATCH, D), lambda t: (0, t % STEPS, 0, 0)),
            whole(bias.shape),
        ],
        out_specs=(
            whole(arrived),
            pl.BlockSpec((1, 2, share, FEAT), lambda t: (t % STEPS, 0, t // STEPS, 0)),
            whole((SLABS, 128, tokens)),
            whole((CIN * width, NP * HALF)),
            whole((4 * HALF, FEAT)),
        ),
        out_shape=(
            jax.ShapeDtypeStruct(arrived, BF),
            jax.ShapeDtypeStruct((STEPS, 2, tokens, FEAT), BF),
            jax.ShapeDtypeStruct((SLABS, 128, tokens), BF),
            jax.ShapeDtypeStruct((CIN * width, NP * HALF), BF),
            jax.ShapeDtypeStruct((4 * HALF, FEAT), BF),
        ),
        scratch_shapes=[
            pltpu.VMEM((SLABS, tokens, 128), BF),
            pltpu.VMEM((CIN, width // 128, count * height, 128), F32),
            pltpu.VMEM((WIN * group, CIN * width), BF),
            pltpu.VMEM((4, CIN, group, width), BF),
            pltpu.SemaphoreType.DMA((2,)),
            pltpu.SemaphoreType.DMA((2,)),
            pltpu.VMEM((share, D), F32),
            pltpu.VMEM((D // 128, share, 128), F32),
            pltpu.VMEM((nx, 2, SEQ_ITEMS, nrow * NP, D), BF),
            pltpu.VMEM(arrived, BF),
            pltpu.SemaphoreType.DMA((nx, 2)),
            pltpu.SemaphoreType.DMA((2 * nx,)),
        ],
        compiler_params=params(collective_id=0, has_side_effects=True),
    )(images, cw, cb, weight, bias)


def norm_stats(v):
    centred = v - jnp.mean(v, axis=-1, keepdims=True)
    inv = lax.rsqrt(jnp.mean(centred * centred, axis=-1, keepdims=True) + 1e-06)
    return centred * inv, inv


def three_terms(v):
    hi = v.astype(BF)
    rest = v - hi.astype(F32)
    mid = rest.astype(BF)
    lo = (rest - mid.astype(F32)).astype(BF)
    return hi, mid, lo


def minus_terms(v, lane, base):
    rest = -v - (-v).astype(BF).astype(F32)
    final = rest - rest.astype(BF).astype(F32)
    out = jnp.where(lane == 4, -v, jnp.where(lane == 5, rest, base))
    return jnp.where(lane == 6, final, out).astype(BF)


def attend_kernel(tok_ref, g_ref, b_ref, qb_ref, vb_ref, seg_ref, wq_ref, wk_ref, wv_ref,
                  q_ref, k_ref, v_ref, o_ref, o32_ref, lx_ref, kx_ref, n1, kaug, vaug):
    step = pl.program_id(0)
    line = lax.broadcasted_iota(jnp.int32, (1, 128), 1)
    first_item = lax.axis_index("rows") * SEQ_ITEMS
    same = [line == seg_ref[first_item + i] for i in range(SEQ_ITEMS)]
    terms = jnp.where((line >= 4) & (line < 7), 1.0, 0.0)
    keys_in = [jnp.where((line < 4) & ~one, -1e30, terms) for one in same]

    @pl.when(step == 0)
    def _():
        kx_ref[...] = jnp.concatenate(keys_in + [jnp.zeros((8 - SEQ_ITEMS, 128), F32)], axis=0)
        for s in range(TOK // 128):
            rs = slice(s * 128, (s + 1) * 128)
            hat, _ = norm_stats(tok_ref[rs, :].astype(F32))
            n1[rs, :] = (hat * as_row(g_ref) + as_row(b_ref)).astype(BF)

    own = pl.ds(pl.multiple_of(step * 256, 256), 256)
    q_ref[...] = ((mm(n1[...], wq_ref[...]) + as_row(qb_ref, own)).astype(BF) * 0.125).astype(BF)
    k_ref[...] = mm(n1[...], wk_ref[...]).astype(BF)
    v_ref[...] = (mm(n1[...], wv_ref[...]) + as_row(vb_ref, own)).astype(BF)
    lane = lax.broadcasted_iota(jnp.int32, (NPATCH, 128), 1)
    low = lane < HD
    for i in range(SEQ_ITEMS):
        rs = slice(i * NPATCH, (i + 1) * NPATCH)
        kaug[rs, 128:256] = jnp.broadcast_to(keys_in[i], (NPATCH, 128)).astype(BF)
        vaug[rs, 128:256] = jnp.ones((NPATCH, 128), BF)
    for pair in range(2):
        cs = slice(pair * 128, (pair + 1) * 128)
        kaug[:, 0:128] = k_ref[:, cs]
        vaug[:, 0:128] = v_ref[:, cs]
        for i in range(SEQ_ITEMS):
            rs = slice(i * NPATCH, (i + 1) * NPATCH)
            span = slice(0, (i + 1) * NPATCH)
            qp = q_ref[rs, cs]
            qx = jnp.broadcast_to(jnp.where(same[i], 1.0, 0.0), (NPATCH, 128))
            halves = []
            for h in range(2):
                mine = low if h == 0 else ~low
                qaug = jnp.concatenate([jnp.where(mine, qp, jnp.zeros_like(qp)), qx.astype(BF)], axis=1)
                scores = mm_t(qaug, kaug[span, :])
                top = jnp.max(scores, axis=1, keepdims=True)
                raised = jnp.exp(scores - top).astype(BF)
                out = mm(raised, vaug[span, :])
                total = out[:, 128:256]
                halves.append(out[:, 0:128] / total)
                lx_ref[pair * 2 + h, rs, :] = minus_terms(top + jnp.log(total), lane, qx)
            out = jnp.where(low, halves[0], halves[1])
            o32_ref[rs, cs] = out
            o_ref[rs, cs] = out.astype(BF)


def attend(tokens, vecs, segments, wq, wk, wv):
    lines = [whole(vec.shape) for vec in vecs]
    col = pl.BlockSpec((D, 256), lambda g: (0, g))
    out = pl.BlockSpec((TOK, 256), lambda g: (0, g))
    return pl.pallas_call(
        attend_kernel,
        name="attend",
        grid=(D // 256,),
        in_specs=[whole((TOK, D))] + lines + [pl.BlockSpec(memory_space=pltpu.SMEM), col, col, col],
        out_specs=(out, out, out, out, out, pl.BlockSpec((4, TOK, 128), lambda g: (g, 0, 0)), whole((8, 128))),
        out_shape=(jax.ShapeDtypeStruct((TOK, D), BF),) * 4
        + (
            jax.ShapeDtypeStruct((TOK, D), F32),
            jax.ShapeDtypeStruct((HEADS, TOK, 128), BF),
            jax.ShapeDtypeStruct((8, 128), F32),
        ),
        scratch_shapes=[pltpu.VMEM((TOK, D), BF), pltpu.VMEM((TOK, 256), BF), pltpu.VMEM((TOK, 256), BF)],
        compiler_params=params(),
    )(tokens, *vecs, segments, wq, wk, wv)


def norm_back(e, hat, inv, gain):
    f = e * gain
    return inv * (f - jnp.mean(f, axis=-1, keepdims=True) - hat * jnp.mean(f * hat, axis=-1, keepdims=True))


def col_sum(v):
    return jnp.sum(v, axis=0, keepdims=True)


def store_square(ref, n, grad):
    _, _, nx, ny, nz, _, _ = ref.shape
    height, width = D // (ny * nz), D // (2 * nx)
    if not folds(width):
        for r in range(2 * nx):
            part = grad[:, r * width : (r + 1) * width]
            for i in range(ny * nz):
                ref[n, r % 2, r // 2, i % ny, i // ny] = part[i * height : (i + 1) * height]
        return
    half = height // 2
    low = lax.broadcasted_iota(jnp.int32, (half, 128), 1) < HALF
    for x in range(nx):
        base = 2 * x * width
        shared = grad[:, base + 128 : base + 256]
        turned = jnp.concatenate([shared[:, HALF:], shared[:, :HALF]], axis=1)
        for i in range(ny * nz):
            top, end = i * height, (i + 1) * height
            mid = top + half
            ref[n, 0, x, i % ny, i // ny, 0:height] = grad[top:end, base : base + 128]
            ref[n, 0, x, i % ny, i // ny, height:] = jnp.where(low, shared[top:mid], turned[mid:end])
            ref[n, 1, x, i % ny, i // ny, 0:height] = grad[top:end, base + 256 : base + 384]
            ref[n, 1, x, i % ny, i // ny, height:] = jnp.where(low, turned[top:mid], shared[mid:end])


def mixer_kernel(tok_ref, att_ref, cot_ref, wo_ref, ob_ref, g_ref, b_ref, rb_ref, hb_ref, wh_ref, wr_ref,
                 out_ref, mid_ref, ag_ref, wog_ref, whg_ref, wrg_ref, sums_ref, hbg_ref,
                 middle, n2, n2t, cott, acc, back, act, hg, hidden_row):
    step = pl.program_id(0)
    last = pl.num_programs(0) - 1
    chunk = wh_ref.shape[1]
    tile = 2 if chunk % 256 == 0 else 3
    blocks = [slice(s * 256, (s + 1) * 256) for s in range(TOK // 256)]

    @pl.when(step == 0)
    def _():
        hidden_row[...] = as_row(hb_ref)
        for rs in blocks:
            row = tok_ref[rs, :].astype(F32) + mm(att_ref[rs, :], wo_ref[...]) + as_row(ob_ref)
            middle[rs, :] = row
            acc[rs, :] = row + as_row(rb_ref)
            back[rs, :] = jnp.zeros((256, D), F32)
            hat, _ = norm_stats(row)
            low = (hat * as_row(g_ref) + as_row(b_ref)).astype(BF)
            n2[rs, :] = low
            n2t[:, rs] = low.T
            cott[:, rs] = cot_ref[rs, :].T

    hidden_bias = hidden_row[0:1, pl.ds(pl.multiple_of(step * chunk, 128), chunk)]
    hsum = jnp.zeros((1, chunk), F32)
    for rs in blocks:
        for n in range(chunk // 128 // tile):
            cs = slice(n * 128 * tile, (n + 1) * 128 * tile)
            pre = mm(n2[rs, :], wh_ref[:, cs]) + hidden_bias[:, cs]
            up = mm_t(cot_ref[rs, :], wr_ref[cs, :])
            a, slope = gelu_pair(pre)
            act[rs, cs] = a.astype(BF)
            hg[rs, cs] = (slope * up).astype(BF)
        acc[rs, :] += mm(act[rs, :], wr_ref[...])
        back[rs, :] += mm_t(hg[rs, :], wh_ref[...])
        hsum = hsum + col_sum(hg[rs, :].astype(F32))
    hbg_ref[...] = hsum
    _, _, nx, ny, nz, height, _ = whg_ref.shape
    for n in range(3):
        width = chunk // 3
        grad = mm(n2t[...], hg[:, n * width : (n + 1) * width]).astype(BF)
        for i in range(ny * nz):
            whg_ref[n, 0, 0, i % ny, i // ny] = grad[i * height : (i + 1) * height]
    _, _, nx, ny, _, _, _ = wrg_ref.shape
    height, width = D // (2 * nx), chunk // ny // 3
    for y in range(ny):
        grad = mm(cott[...], act[:, y * 3 * width : (y + 1) * 3 * width]).astype(BF)
        for n in range(3):
            for r in range(2 * nx):
                part = grad[r * height : (r + 1) * height, n * width : (n + 1) * width]
                wrg_ref[n, r % 2, r // 2, y, 0] = fold_block(part)

    @pl.when(step == last)
    def _():
        gsum = jnp.zeros((1, D), F32)
        bsum = jnp.zeros((1, D), F32)
        osum = jnp.zeros((1, D), F32)
        rsum = jnp.zeros((1, D), F32)
        for rs in blocks:
            out_ref[rs, :] = acc[rs, :].astype(BF)
            hat, inv = norm_stats(middle[rs, :])
            e = back[rs, :]
            gsum = gsum + col_sum(e * hat)
            bsum = bsum + col_sum(e)
            cot = cot_ref[rs, :].astype(F32)
            rsum = rsum + col_sum(cot)
            mid = cot + norm_back(e, hat, inv, as_row(g_ref))
            mid_ref[rs, :] = mid
            low = mid.astype(BF)
            osum = osum + col_sum(low.astype(F32))
            n2[rs, :] = low
            n2t[:, rs] = att_ref[rs, :].T
            ag_ref[rs, :] = mm_t(low, wo_ref[...]).astype(BF)
        store_square(wog_ref, 0, mm(n2t[...], n2[...]).astype(BF))
        sums_ref[0:1, :] = gsum
        sums_ref[1:2, :] = bsum
        sums_ref[2:3, :] = osum
        sums_ref[3:4, :] = rsum


def mixer(tokens, attended, cotangent, wo, vecs, wh, wr, sizes):
    nc, nx, ny, nz = sizes
    rows, items = nc * nx, ny * nz
    chunk = FF // rows
    square = (1,) + sizes + folded_shape(D // items, D // rows)
    return pl.pallas_call(
        mixer_kernel,
        name="mixer",
        grid=(rows,),
        in_specs=[
            whole((TOK, D)), whole((TOK, D)), whole((TOK, D)), whole((D, D)),
            whole((D,)), whole((D,)), whole((D,)), whole((D,)), whole((FF,)),
            pl.BlockSpec((D, chunk), lambda r: (0, r)),
            pl.BlockSpec((chunk, D), lambda r: (r, 0)),
        ],
        out_specs=(
            whole((TOK, D)), whole((TOK, D)), whole((TOK, D)), whole(square),
            pl.BlockSpec((3, 1, 1, ny, nz, D // items, chunk // 3), lambda r: (0, r % 2, r // 2, 0, 0, 0, 0)),
            pl.BlockSpec((3, nc, nx, ny, 1) + folded_shape(D // rows, FF // items // 3), lambda r: (0, 0, 0, 0, r, 0, 0)),
            whole((8, D)),
            pl.BlockSpec((1, chunk), lambda r: (0, r)),
        ),
        out_shape=(
            jax.ShapeDtypeStruct((TOK, D), BF),
            jax.ShapeDtypeStruct((TOK, D), F32),
            jax.ShapeDtypeStruct((TOK, D), BF),
            jax.ShapeDtypeStruct(square, BF),
            jax.ShapeDtypeStruct((3,) + sizes + (D // items, chunk // 3), BF),
            jax.ShapeDtypeStruct((3,) + sizes + folded_shape(D // rows, FF // items // 3), BF),
            jax.ShapeDtypeStruct((8, D), F32),
            jax.ShapeDtypeStruct((1, FF), F32),
        ),
        scratch_shapes=[
            pltpu.VMEM((TOK, D), F32), pltpu.VMEM((TOK, D), BF), pltpu.VMEM((D, TOK), BF),
            pltpu.VMEM((D, TOK), BF), pltpu.VMEM((TOK, D), F32), pltpu.VMEM((TOK, D), F32),
            pltpu.VMEM((TOK, chunk), BF), pltpu.VMEM((TOK, chunk), BF), pltpu.VMEM((1, FF), F32),
        ],
        compiler_params=params(),
    )(tokens, attended, cotangent, wo, *vecs, wh, wr)


def attend_back_kernel(sizes, tok_ref, g_ref, b_ref, kx_ref, mid_ref, q_ref, k_ref, v_ref, o_ref, ag_ref, lx_ref,
                       wq_ref, wk_ref, wv_ref, whg_ref, wrg_ref, wog_ref,
                       tg_ref, sq_ref, sums_ref, qvs_ref, who_ref, wro_ref, woo_ref,
                       n1t, back, kaug, vaug, qaug, oaug, dqt, dq, dk, dv, square, *comm):
    step = pl.program_id(0)
    blocks = [slice(s * 256, (s + 1) * 256) for s in range(TOK // 256)]
    pos = place(sizes)
    groups = ((whg_ref, who_ref), (wrg_ref, wro_ref), (wog_ref, woo_ref))
    pieces, loads, base, at = [], [], 0, 0
    for source, _ in groups:
        count = source.shape[0]
        refs, keep = comm[at : at + 4 * count + 2], comm[at + 4 * count + 2 : at + 4 * count + 4]
        at += 4 * count + 4
        pieces += make_pieces(
            sizes, pos, BACK_ORDERS[base : base + count], [source.at[n] for n in range(count)],
            [keep[0].at[n] for n in range(count)], refs,
        )
        loads += [pltpu.make_async_copy(source.at[n, pos[0]], keep[0].at[n], keep[1].at[n]) for n in range(count)]
        base += count

    def event(index, stage):
        if stage == 0:
            pieces[index].start(0)
            loads[index].start()
        elif stage < 4:
            if stage == 1:
                loads[index].wait()
            pieces[index].advance(stage)
        else:
            total = pieces[index].gather(3)
            if index < 3:
                width = total.shape[1]
                who_ref[:, index * width : (index + 1) * width] = total
            elif index < 6:
                height, width = D // (2 * sizes[1]), FF // (sizes[2] * sizes[3]) // 3
                wro_ref[:, (index - 3) * width : (index - 2) * width] = unfold_block(total, height, width)
            else:
                woo_ref[...] = unfold_block(total, *woo_ref.shape, odd=pos[0] == 1)

    def finish():
        for part in pieces:
            part.drain()

    table = {(0, 0): [functools.partial(greet, sizes, pos, True, True)]}
    for when, index, stage in BACK_PLAN:
        if when < 2:
            key = (0, when)
        elif when < 26:
            key = ((when - 2) // 8, 2 + (when - 2) % 8)
        else:
            key = (2, 10)
        table.setdefault(key, []).append(functools.partial(event, index, stage))
    table.setdefault((2, 10), []).append(finish)
    run_events(step, table, (0,))

    @pl.when(step == 0)
    def _():
        for rs in blocks:
            hat, _ = norm_stats(tok_ref[rs, :].astype(F32))
            n1t[:, rs] = (hat * as_row(g_ref) + as_row(b_ref)).astype(BF).T
            back[rs, :] = jnp.zeros((256, D), F32)

    run_events(step, table, (1,))
    lane = lax.broadcasted_iota(jnp.int32, (NPATCH, 128), 1)
    low = lane < HD
    ones = jnp.where((lane >= 4) & (lane < 7), 1.0, 0.0).astype(BF)
    for i, rs in enumerate(blocks):
        kaug[rs, 128:256] = jnp.broadcast_to(kx_ref[i : i + 1, :], (NPATCH, 128)).astype(BF)
        vaug[rs, 128:256] = ones
    pick_row = lax.broadcasted_iota(jnp.int32, (256, 256), 0) % 128 // HD
    pick_col = lax.broadcasted_iota(jnp.int32, (256, 256), 1) // 128
    pick = jnp.where(pick_row == pick_col, 1.0, 0.0).astype(BF)
    for pair in range(2):
        cs = slice(pair * 128, (pair + 1) * 128)
        kaug[:, 0:128] = k_ref[:, cs]
        vaug[:, 0:128] = v_ref[:, cs]
        kt = k_ref[:, cs].T
        for rs in blocks:
            qp = q_ref[rs, cs]
            gp = ag_ref[rs, cs]
            prod = gp.astype(F32) * o_ref[rs, cs]
            hi = prod.astype(BF)
            both = jnp.concatenate([hi, (prod - hi.astype(F32)).astype(BF)], axis=1)
            dots = mm(both, pick)
            for h in range(2):
                mine = low if h == 0 else ~low
                qaug[h, rs, 0:128] = jnp.where(mine, qp, jnp.zeros_like(qp))
                qaug[h, rs, 128:256] = lx_ref[pair * 2 + h, rs, :]
                oaug[h, rs, 0:128] = jnp.where(mine, gp, jnp.zeros_like(gp))
                oaug[h, rs, 128:256] = minus_terms(dots[:, h * 128 : (h + 1) * 128], lane, jnp.zeros((NPATCH, 128), F32))
        for j, rs in enumerate(blocks):
            span = slice(j * NPATCH, TOK)
            parts_k, parts_v = [], []
            for h in range(2):
                probs = jnp.exp(mm_t(kaug[rs, :], qaug[h, span, :]))
                rise = mm_t(vaug[rs, :], oaug[h, span, :])
                grad = (probs * rise).astype(BF)
                probs_low = probs.astype(BF)
                parts_v.append(mm(probs_low, ag_ref[span, cs]))
                parts_k.append(mm(grad, q_ref[span, cs]))
                hs = slice(h * HD, (h + 1) * HD)
                part = mm(kt[hs, rs], grad)
                if j == 0:
                    dqt[hs, :] = part
                else:
                    dqt[hs, span] += part
            dk[rs, cs] = jnp.where(low, parts_k[0], parts_k[1]).astype(BF)
            dv[rs, cs] = jnp.where(low, parts_v[0], parts_v[1]).astype(BF)
            run_events(step, table, (2 + pair * 4 + j,))
        dq[:, cs] = (dqt[...].T * 0.125).astype(BF)
    qvs_ref[0:1, :] = col_sum(dq[...].astype(F32))
    qvs_ref[1:2, :] = col_sum(dv[...].astype(F32))
    for n, part in enumerate((dq, dk, dv)):
        square[n, step] = mm(n1t[...], part[...]).astype(BF)
    for rs in blocks:
        back[rs, :] += (
            mm_t(dq[rs, :], wq_ref[...]) + mm_t(dk[rs, :], wk_ref[...]) + mm_t(dv[rs, :], wv_ref[...])
        )

    @pl.when(step == pl.num_programs(0) - 1)
    def _():
        gsum = jnp.zeros((1, D), F32)
        bsum = jnp.zeros((1, D), F32)
        for rs in blocks:
            hat, inv = norm_stats(tok_ref[rs, :].astype(F32))
            e = back[rs, :]
            gsum = gsum + col_sum(e * hat)
            bsum = bsum + col_sum(e)
            tg_ref[rs, :] = (mid_ref[rs, :] + norm_back(e, hat, inv, as_row(g_ref))).astype(BF)
        sums_ref[0:1, :] = gsum
        sums_ref[1:2, :] = bsum
        for n in range(3):
            store_square(sq_ref, n, jnp.concatenate([square[n, g] for g in range(D // 256)], axis=1))

    run_events(step, table, (10,))


BACK_ORDERS = (
    (3, 2, 1), (2, 3, 1), (1, 2, 3), (1, 2, 3), (1, 2, 3), (1, 2, 3),
    (2, 1, 3),
)
BACK_PLAN = (
    (0, 3, 0), (0, 0, 0), (0, 1, 0), (0, 5, 0), (0, 4, 0), (0, 2, 0), (0, 6, 0), (1, 3, 1), (1, 0, 1),
    (1, 1, 1), (4, 5, 1), (6, 6, 1), (6, 2, 1), (7, 1, 2), (9, 3, 2), (9, 4, 1), (10, 5, 2), (15, 3, 3),
    (16, 2, 2), (16, 0, 2), (16, 5, 3), (17, 6, 2), (18, 3, 4), (18, 2, 3), (19, 4, 2), (19, 0, 3), (20, 1, 3),
    (21, 6, 3), (23, 4, 3), (26, 6, 4), (26, 1, 4), (26, 5, 4), (27, 0, 4), (28, 2, 4), (29, 4, 4),
)


def attend_back(tokens, gain, shift, kx, mid, q, k, v, o, ag, lx, wq, wk, wv, whg, wrg, wog, sizes):
    squares = (3,) + sizes + wog.shape[5:]
    col = pl.BlockSpec((D, 256), lambda g: (0, g))
    part = pl.BlockSpec((TOK, 256), lambda g: (0, g))
    far = pl.BlockSpec(memory_space=pl.ANY)
    items, rows = sizes[2] * sizes[3], 2 * sizes[1]
    outs = [(D // items, FF // rows), (D // rows, FF // items), (D // items, D // rows)]
    return pl.pallas_call(
        functools.partial(attend_back_kernel, sizes),
        name="attend_back",
        grid=(D // 256,),
        in_specs=[whole((TOK, D)), whole((D,)), whole((D,)), whole(kx.shape), whole((TOK, D)),
                  part, part, part, part, part, pl.BlockSpec((4, TOK, 128), lambda g: (g, 0, 0)),
                  col, col, col, far, far, far],
        out_specs=(whole((TOK, D)), whole(squares), whole((8, D)), pl.BlockSpec((8, 256), lambda g: (0, g)))
        + tuple(whole(shape) for shape in outs),
        out_shape=(
            jax.ShapeDtypeStruct((TOK, D), BF),
            jax.ShapeDtypeStruct(squares, BF),
            jax.ShapeDtypeStruct((8, D), F32),
            jax.ShapeDtypeStruct((8, D), F32),
        ) + tuple(jax.ShapeDtypeStruct(shape, F32) for shape in outs),
        scratch_shapes=[
            pltpu.VMEM((D, TOK), BF), pltpu.VMEM((TOK, D), F32),
            pltpu.VMEM((TOK, 256), BF), pltpu.VMEM((TOK, 256), BF),
            pltpu.VMEM((2, TOK, 256), BF), pltpu.VMEM((2, TOK, 256), BF),
            pltpu.VMEM((128, TOK), F32),
            pltpu.VMEM((TOK, 256), BF), pltpu.VMEM((TOK, 256), BF), pltpu.VMEM((TOK, 256), BF),
            pltpu.VMEM((3, D // 256, D, 256), BF),
        ]
        + piece_scratch(sizes, BACK_ORDERS[0:3], whg.shape[5:]) + own_scratch(sizes, 3, whg.shape[5:])
        + piece_scratch(sizes, BACK_ORDERS[3:6], wrg.shape[5:]) + own_scratch(sizes, 3, wrg.shape[5:])
        + piece_scratch(sizes, BACK_ORDERS[6:7], wog.shape[5:]) + own_scratch(sizes, 1, wog.shape[5:]),
        compiler_params=params(collective_id=1, has_side_effects=True),
    )(tokens, gain, shift, kx, mid, q, k, v, o, ag, lx, wq, wk, wv, whg, wrg, wog)


EARLY = 80
FINISH_ORDERS = (
    (1, 2, 3), (2, 1, 3), (3, 2, 1), (1, 2, 3), (2, 3, 1), (1, 2, 3),
    (2, 1, 3), (1, 2, 3), (2, 3, 1), (3, 1, 2), (2, 3, 1),
)
FINISH_PLAN = (
    (0, 8, 0), (0, 10, 0), (0, 9, 0), (1, 10, 1), (2, 9, 1), (3, 8, 1), (7, 10, 2), (9, 0, 0), (9, 8, 2),
    (10, 11, 0), (10, 1, 0), (10, 0, 1), (11, 2, 0), (11, 1, 1), (12, 3, 0), (12, 2, 1), (12, 3, 1), (13, 4, 0),
    (13, 0, 2), (14, 4, 1), (14, 5, 0), (14, 1, 2), (14, 11, 1), (15, 6, 0), (15, 5, 1), (16, 7, 0), (16, 0, 3),
    (16, 6, 1), (16, 3, 2), (17, 7, 1), (18, 4, 2), (18, 1, 3), (19, 10, 3), (19, 11, 2), (20, 5, 2), (20, 2, 2),
    (21, 8, 3), (22, 6, 2), (22, 3, 3), (22, 0, 4), (23, 4, 3), (23, 11, 3), (24, 12, 0), (24, 5, 3), (25, 7, 2),
    (25, 12, 1), (25, 6, 3), (25, 9, 2), (26, 12, 2), (26, 2, 3), (26, 10, 4), (28, 12, 3), (28, 5, 4), (29, 7, 3),
    (29, 1, 4), (30, 8, 4), (30, 2, 4), (31, 9, 3), (32, 11, 4), (32, 4, 4), (33, 3, 4), (33, 9, 4), (33, 6, 4),
    (33, 12, 4), (33, 7, 4),
)


def finish_kernel(sizes, tg_ref, act_ref, slope_ref, w_ref, xt_ref, t_ref, sel_ref, sq_ref, sums2_ref, hbg_ref, sums1_ref, qvs_ref,
                  pw_ref, sq0_ref, sq1_ref, sq2_ref, ig_ref, earlyo_ref, tapso_ref,
                  tgc, tgt, dxa, pg, cw, lines, flat, grads, edge, edge_send, edge_recv, got, send, recv, nat, *comm):
    t = pl.program_id(0)
    nc, nx, ny, nz = sizes
    items, rows = ny * nz, nc * nx
    tokens = tgc.shape[0]
    group = tokens // NP
    count, _, height, width = ig_ref.shape
    nrow = height // PATCH
    pos = place(sizes)
    item, row = lax.axis_index("items"), lax.axis_index("rows")
    final_row = lax.axis_size("rows") - 1
    far_steps = STEPS * (nx - 1)
    image_step = 2 * STEPS + far_steps
    final_step = image_step + CIN - 1
    at = 4 * STEPS + 2
    patch = make_pieces(
        sizes, pos, FINISH_ORDERS[0:STEPS], [grads.at[q % 2] for q in range(STEPS)],
        [grads.at[q % 2, pos[0]] for q in range(STEPS)], comm[0:at],
    )
    keep = comm[at + 14 : at + 16]
    square = make_pieces(
        sizes, pos, FINISH_ORDERS[STEPS : STEPS + 3], [sq_ref.at[n] for n in range(3)],
        [keep[0].at[n] for n in range(3)], comm[at : at + 14],
    )
    loads = [pltpu.make_async_copy(sq_ref.at[n, pos[0]], keep[0].at[n], keep[1].at[n]) for n in range(3)]
    at += 16
    early = SmallSum(sizes, pos, comm[at : at + 4], comm[at + 4], comm[at + 5])
    late = SmallSum(sizes, pos, comm[at + 6 : at + 10], comm[at + 10], comm[at + 11])

    def edge_copy(n):
        step = -1 if n == 0 else 1
        return pltpu.make_async_remote_copy(
            src_ref=edge.at[n], dst_ref=edge.at[2 + n], send_sem=edge_send.at[n], recv_sem=edge_recv.at[n],
            device_id=(item, row + step), device_id_type=MESH,
        )

    share, per = tokens // nx, group // nx
    turns = [turn_of(sizes, pos, xg) * share for xg in range(nx)]

    def spread(j, c):
        return jnp.concatenate(
            [dxa[j, pl.ds(pl.multiple_of(turns[xg] + c * per, per), per), :] for xg in range(nx)], axis=0
        )

    def parcel(k):
        to = lax.rem(row + k, rows)
        return pltpu.make_async_remote_copy(
            src_ref=tg_ref.at[:, to], dst_ref=got.at[row], send_sem=send.at[k - 1], recv_sem=recv.at[row],
            device_id=(item, to), device_id_type=MESH,
        )

    def arrived(source):
        pltpu.make_async_remote_copy(
            src_ref=tg_ref.at[:, source], dst_ref=got.at[source], send_sem=send.at[0], recv_sem=recv.at[source],
            device_id=(item, source), device_id_type=MESH,
        ).wait_recv()

    def unpack(xg, turn):
        for k in range(D // 128):
            cut = got[pl.ds(2 * xg, 2), :, :, k * 128 : (k + 1) * 128]
            nat[k] = cut.reshape(share, 128).astype(F32)
        for c in range(NP):
            part = jnp.concatenate([nat[k, pl.ds(c, per, stride=NP), :] for k in range(D // 128)], axis=1)
            tgc[turn * share + c * per : turn * share + (c + 1) * per, :] = part.astype(BF)

    def turn_over(turn):
        for s in range(share // 256):
            rs = slice(turn * share + s * 256, turn * share + (s + 1) * 256)
            tgt[:, rs] = tgc[rs, :].T

    def put_lines(j):
        low = lax.broadcasted_iota(jnp.int32, (group, 2 * HALF), 1) < HALF
        for pair in range(NP // 2):
            a, b = spread(j, 2 * pair), spread(j, 2 * pair + 1)
            cs = slice(pair * 128, (pair + 1) * 128)
            lines[2 * j * group : (2 * j + 1) * group, cs] = jnp.where(low, a, pltpu.roll(b, HALF, 1)).astype(BF)
            lines[(2 * j + 1) * group : (2 * j + 2) * group, cs] = jnp.where(low, pltpu.roll(a, HALF, 1), b).astype(BF)

    def event(index, stage):
        if index < STEPS:
            if stage == 0:
                patch[index].start(0)
            elif stage < 4:
                patch[index].advance(stage)
            else:
                total = unfold_block(patch[index].gather(3), D // rows, FEAT // items)
                for c in range(CH // items):
                    at = c * PATCH * PATCH + index * 2 * PATCH
                    pw_ref[:, at : at + 2 * PATCH] = total[:, c * 2 * PATCH : (c + 1) * 2 * PATCH]
        elif index < STEPS + 3:
            n = index - STEPS
            if stage == 0:
                loads[n].start()
                square[n].start(0)
                return
            if stage == 1:
                loads[n].wait()
            if stage < 4:
                square[n].advance(stage)
            else:
                out = (sq0_ref, sq1_ref, sq2_ref)[n]
                out[...] = unfold_block(square[n].gather(3), *out.shape, odd=pos[0] == 1)
        else:
            part, out = ((early, earlyo_ref), (late, tapso_ref))[index - STEPS - 3]
            if stage < 4:
                part.advance(stage)
            else:
                out[...] = part.gather(3)

    opening, table = [], {}
    for when, index, stage in FINISH_PLAN:
        if stage > 0 or index < STEPS + 3:
            call = functools.partial(event, index, stage)
            if when == 0:
                opening.append(call)
            else:
                later = when - 1 + (far_steps - STEPS if when > 3 * STEPS else 0)
                table.setdefault((min(later, final_step), 0), []).append(call)

    @pl.when(t == 0)
    def _():
        @pl.when(row == final_row)
        def _():
            edge[2] = jnp.zeros(edge.shape[1:], BF)

        @pl.when(row == 0)
        def _():
            edge[3] = jnp.zeros(edge.shape[1:], BF)

        greet(sizes, pos, True, True)
        for k in range(1, rows):
            parcel(k).start()
        for call in opening:
            call()
        got[row] = tg_ref[:, row]
        arrived(2 * pos[1] + 1 - pos[0])
        unpack(pos[1], nx - 1)
        turn_over(nx - 1)
        cw[...] = jnp.zeros_like(cw)

    @pl.when(t == STEPS)
    def _():
        for turn in range(nx - 1):
            xg = lax.rem(pos[1] + 1 + turn, nx)
            arrived(2 * xg)
            arrived(2 * xg + 1)
            unpack(xg, turn)
            turn_over(turn)

    @pl.when(t == STEPS + 1)
    def _():
        total = jnp.zeros((1, D), F32)
        for s in range(tokens // 256):
            total = total + col_sum(tgc[s * 256 : (s + 1) * 256, :].astype(F32))
        lines_in = [sums2_ref[0:1], sums2_ref[1:2], sums2_ref[2:3], sums2_ref[3:4]]
        lines_in += [hbg_ref[:, n * D : (n + 1) * D] for n in range(FF // D)]
        lines_in += [sums1_ref[0:1], sums1_ref[1:2], qvs_ref[0:1], qvs_ref[1:2], total]
        cells = [one[:, k * 128 : (k + 1) * 128] for one in lines_in for k in range(D // 128)]
        early.start(0, jnp.concatenate(cells + [jnp.zeros((EARLY - len(cells), 128), F32)], axis=0))

    @pl.when((t >= STEPS) & (t < 2 * STEPS))
    def _():
        for q in range(2, STEPS):
            @pl.when(t == STEPS + q)
            def _(q=q):
                patch[q - 2].drain((0,))

        feats = FEAT // items
        slot = t % 2
        for n in range(FEAT // 256):
            grad = mm(tgt[...], act_ref[0, 0, :, n * 256 : (n + 1) * 256]).astype(BF)
            for c in range(256 // feats):
                i = n * (256 // feats) + c
                for r in range(rows):
                    block = grad[r * (D // rows) : (r + 1) * (D // rows), c * feats : (c + 1) * feats]
                    grads[slot, r % 2, r // 2, i % ny, i // ny] = fold_block(block)

    def stem_part(p, turn):
        weight = w_ref[...].reshape(FEAT, D)

        def at(s, size):
            return pl.ds(pl.multiple_of(turn * share + s * 256, 256), size)

        @pl.when(p == 0)
        def _():
            dxa[0, at(0, share), :] = jnp.zeros((share, 128), F32)

        for s in range(share // 256):
            rs = slice(s * 256, (s + 1) * 256)
            for n in range(FEAT // 256):
                cs = slice(n * 256, (n + 1) * 256)
                da = mm_t(tgc[at(s, 256), :], weight[cs, :])
                pg[rs, cs] = (slope_ref[0, 0, rs, cs].astype(F32) * da).astype(BF)
            back = mm_t(pg[rs, :], t_ref[...])
            dxa[p, at(s, 256), :] += back[:, 0:128]
            dxa[p + 1, at(s, 256), :] = back[:, 128:256]
        xt = jnp.concatenate([xt_ref[p, :, at(0, share)], xt_ref[p + 1, :, at(0, share)]], axis=0)
        cw[...] += mm(xt, pg[...])

    near, far = t < STEPS, (t >= 2 * STEPS) & (t < image_step)

    @pl.when(near | far)
    def _():
        stem_part(t % STEPS, jnp.where(near, nx - 1, t // STEPS - 2))

    @pl.when((t >= image_step - STEPS) & (t < image_step))
    def _():
        p = t % STEPS

        @pl.when(p == 0)
        def _():
            put_lines(0)
            for ch in range(CIN):
                head = mm_t(lines[0:group], sel_ref[ch * width : (ch + 1) * width, :])
                edge[0, ch] = (pltpu.roll(head, nrow - 1, 0) if nrow > 1 else head).astype(BF)

            @pl.when(row > 0)
            def _():
                edge_copy(0).start()

        @pl.when(p == STEPS - 1)
        def _():
            put_lines(SLABS - 1)
            for ch in range(CIN):
                tail = mm_t(lines[(WIN - 1) * group : WIN * group], sel_ref[ch * width : (ch + 1) * width, :])
                edge[1, ch] = (pltpu.roll(tail, group - nrow + 1, 0) if nrow > 1 else tail).astype(BF)

            @pl.when(row < final_row)
            def _():
                edge_copy(1).start()

            late.start(0, tap_grad_rows(cw[...]))

    @pl.when(t >= image_step)
    def _():
        ch = t - image_step

        @pl.when(t == image_step)
        def _():
            for j in range(1, SLABS - 1):
                put_lines(j)

            @pl.when(row < final_row)
            def _():
                edge_copy(0).wait_recv()

            @pl.when(row > 0)
            def _():
                edge_copy(1).wait_recv()

        patch_row = lax.broadcasted_iota(jnp.int32, (group, width), 0) % nrow
        res = mm_t(lines[...], sel_ref[pl.ds(pl.multiple_of(ch * width, width), width), :])
        head = res[0:group]
        tail = res[(PATCH + 1) * group : (PATCH + 2) * group]
        for r in range(PATCH):
            v = res[(r + 1) * group : (r + 2) * group]
            if r == 0:
                v = v + jnp.where(patch_row == 0, edge[3, ch].astype(F32), pltpu.roll(tail, 1, 0))
            if r == PATCH - 1:
                v = v + jnp.where(patch_row == nrow - 1, edge[2, ch].astype(F32), pltpu.roll(head, group - 1, 0))
            flat[0, pl.ds(r, group, stride=PATCH), :] = v[:, 0:128]
            flat[1, pl.ds(r, group, stride=PATCH), :] = v[:, 128:256]
        for n in range(count):
            at = slice(n * height, (n + 1) * height)
            ig_ref[n, 0, :, 0:128] = flat[0, at, :]
            ig_ref[n, 0, :, 128:256] = flat[1, at, :]

    def close():
        for part in square:
            part.drain()
        for q, part in enumerate(patch):
            part.drain((1, 2, 3) if q < STEPS - 2 else (0, 1, 2, 3))
        early.drain()
        late.drain()
        for k in range(1, rows):
            parcel(k).wait_send()

        @pl.when(row > 0)
        def _():
            edge_copy(0).wait_send()

        @pl.when(row < final_row)
        def _():
            edge_copy(1).wait_send()

    table.setdefault((final_step, 0), []).append(close)
    run_events(t, table, (0,))


def finish(tg, saved, weight, xt, taps, sel, squares, sums2, hbg, sums1, qvs, count, height, sizes):
    nc, nx, ny, nz = sizes
    items, rows = ny * nz, nc * nx
    group = count * height // PATCH
    tokens = group * NP
    feats = FEAT // items
    square = squares.shape[5:]
    share = tokens // nx
    image_step = STEPS * (nx + 1)

    def clip(v, low, high):
        return jnp.minimum(jnp.maximum(v, low), high)

    def sub(t):
        held = jnp.where(t < STEPS, t, jnp.where(t < 2 * STEPS, 0, t % STEPS))
        return jnp.where(t < image_step, held, STEPS - 1)

    def turn(t):
        return jnp.where(t < STEPS, nx - 1, clip(t // STEPS - 2, 0, nx - 2))

    return pl.pallas_call(
        functools.partial(finish_kernel, sizes),
        name="finish",
        grid=(image_step + CIN,),
        in_specs=[
            whole(tg.shape),
            pl.BlockSpec((1, 1, tokens, FEAT), lambda t: (clip(t - STEPS, 0, STEPS - 1), 0, 0, 0)),
            pl.BlockSpec((1, 1, share, FEAT), lambda t: (sub(t), 1, turn(t), 0)),
            pl.BlockSpec((CH, 1, 2 * PATCH, D), lambda t: (0, sub(t), 0, 0)),
            whole(xt.shape),
            whole(taps.shape),
            whole(sel.shape),
            pl.BlockSpec(memory_space=pl.ANY),
            whole(sums2.shape), whole(hbg.shape), whole(sums1.shape), whole(qvs.shape),
        ],
        out_specs=(
            whole((D // rows, PF // items)),
            whole((D // items, D // rows)),
            whole((D // items, D // rows)),
            whole((D // items, D // rows)),
            pl.BlockSpec((count, 1, height, IMG), lambda t: (0, clip(t - image_step, 0, CIN - 1), 0, 0)),
            whole((EARLY, 128)),
            whole((32, 128)),
        ),
        out_shape=(
            jax.ShapeDtypeStruct((D // rows, PF // items), F32),
            jax.ShapeDtypeStruct((D // items, D // rows), F32),
            jax.ShapeDtypeStruct((D // items, D // rows), F32),
            jax.ShapeDtypeStruct((D // items, D // rows), F32),
            jax.ShapeDtypeStruct((count, CIN, height, IMG), F32),
            jax.ShapeDtypeStruct((EARLY, 128), F32),
            jax.ShapeDtypeStruct((32, 128), F32),
        ),
        scratch_shapes=[
            pltpu.VMEM((tokens, D), BF),
            pltpu.VMEM((D, tokens), BF),
            pltpu.VMEM((SLABS, tokens, 128), F32),
            pltpu.VMEM((share, FEAT), BF),
            pltpu.VMEM((4 * HALF, FEAT), F32),
            pltpu.VMEM((WIN * group, NP * HALF), BF),
            pltpu.VMEM((2, group * PATCH, 128), F32),
            pltpu.VMEM((2,) + sizes + folded_shape(D // rows, feats), BF),
            pltpu.VMEM((4, CIN, group, IMG), BF),
            pltpu.SemaphoreType.DMA((2,)),
            pltpu.SemaphoreType.DMA((2,)),
            pltpu.VMEM((rows, SEQ_ITEMS, tokens // rows // SEQ_ITEMS, D), BF),
            pltpu.SemaphoreType.DMA((rows - 1,)),
            pltpu.SemaphoreType.DMA((rows,)),
            pltpu.VMEM((D // 128, share, 128), F32),
        ]
        + piece_scratch(sizes, FINISH_ORDERS[0:STEPS], folded_shape(D // rows, feats))
        + piece_scratch(sizes, FINISH_ORDERS[STEPS : STEPS + 3], square) + own_scratch(sizes, 3, square)
        + small_scratch(sizes, EARLY)
        + small_scratch(sizes, 32),
        compiler_params=params(collective_id=2, has_side_effects=True),
    )(tg, saved, saved, weight, xt, taps, sel, squares, sums2, hbg, sums1, qvs)


def feature_parts(rows):
    feat = lax.broadcasted_iota(jnp.int32, (rows, FEAT), 1)
    return feat // (2 * PATCH), feat // PATCH % 2, feat % PATCH


def tap_rows(wide, ch, r, b, half):
    parts = []
    for r2 in range(2):
        a = r - r2
        parts.append(wide[9 * ch + 3 * a + b : 9 * ch + 3 * a + b + 1, :] if 0 <= a < 3 else jnp.zeros((1, FEAT), F32))
    return jnp.where(half == 0, parts[0], parts[1])


def tap_matrix(cw_ref, cb_ref, t_ref):
    chan, _, _ = feature_parts(32)
    expand = jnp.where(chan == lax.broadcasted_iota(jnp.int32, (32, FEAT), 0), 1.0, 0.0).astype(BF)
    wide = lax.dot_general(cw_ref[...], expand, (((0,), (0,)), ((), ())), preferred_element_type=F32)
    bias = mm(jnp.broadcast_to(as_row(cb_ref), (8, CH)).astype(BF), expand)
    _, half, spot = feature_parts(1)
    line = lax.broadcasted_iota(jnp.int32, (HALF, FEAT), 0)
    for r in range(4):
        block = jnp.zeros((HALF, FEAT), F32)
        if r == 0:
            block = jnp.where(line == ONE_LANE, bias[0:1, :], block)
        for ch in range(CIN):
            for b in range(3):
                block = jnp.where(line == WIN * ch + b + spot, tap_rows(wide, ch, r, b, half), block)
        t_ref[r * HALF : (r + 1) * HALF, :] = block.astype(BF)


def tap_grad_rows(full):
    chan, half, spot = feature_parts(1)
    line = lax.broadcasted_iota(jnp.int32, (HALF, FEAT), 0)
    sums = [[None] * 3 for _ in range(9)]
    for r in range(4):
        block = full[r * HALF : (r + 1) * HALF]
        for ch in range(CIN):
            for b in range(3):
                line_sum = jnp.sum(jnp.where(line == WIN * ch + b + spot, block, 0.0), axis=0, keepdims=True)
                for a in range(3):
                    if 0 <= r - a < 2:
                        part = jnp.where(half == r - a, line_sum, 0.0)
                        old = sums[3 * ch + b][a]
                        sums[3 * ch + b][a] = part if old is None else old + part
    lines = [sums[3 * ch + b][a] for ch in range(CIN) for a in range(3) for b in range(3)]
    lines.append(full[ONE_LANE : ONE_LANE + 1])
    lines.append(jnp.zeros((4, FEAT), F32))
    table = jnp.concatenate(lines, axis=0)
    chan, _, _ = feature_parts(128)
    expand = jnp.where(chan == lax.broadcasted_iota(jnp.int32, (128, FEAT), 0), 1.0, 0.0).astype(BF)
    hi, mid, lo = three_terms(table)
    return mm_t(hi, expand) + (mm_t(mid, expand) + mm_t(lo, expand))


def on_device(
    images, item_segment, conv_weight, conv_bias, patch_weight, patch_bias, norm1_gain, norm1_bias,
    query_weight, query_bias, key_weight, value_weight, value_bias, output_weight, output_bias,
    norm2_gain, norm2_bias, hidden_weight, hidden_bias, result_weight, result_bias, cotangent,
):
    items, rows = lax.axis_size("items"), lax.axis_size("rows")
    sizes = grid_sizes(items, rows)
    count, _, height, _ = images.shape
    nrow = height // PATCH

    cw = conv_weight.reshape(CH, 27)
    weight4 = patch_weight.reshape(CH, STEPS, 2 * PATCH, D)
    tokens, saved, xt, sel, taps = stem_forward(images, cw, conv_bias, weight4, patch_bias, sizes)
    tokens = tokens.reshape(TOK, D)
    q, k, v, attended, attended32, lx, kx = attend(
        tokens, (norm1_gain, norm1_bias, query_bias, value_bias), item_segment, query_weight, key_weight, value_weight)
    block_out, middle_grad, attended_grad, wo_grad, wh_grad, wr_grad, sums2, hb_grad = mixer(
        tokens, attended, cotangent, output_weight,
        (output_bias, norm2_gain, norm2_bias, result_bias, hidden_bias), hidden_weight, result_weight, sizes,
    )
    token_grad, squares, sums1, qvs, wh_grad, wr_grad, wo_grad = attend_back(
        tokens, norm1_gain, norm1_bias, kx, middle_grad, q, k, v, attended32, attended_grad, lx,
        query_weight, key_weight, value_weight, wh_grad, wr_grad, wo_grad, sizes,
    )
    token_grad = token_grad.reshape(SEQ_ITEMS, rows, nrow * NP, D)
    pw_grad, wq_grad, wk_grad, wv_grad, image_grad, sums, tap_grads = finish(
        token_grad, saved, weight4, xt, taps, sel, squares, sums2, hb_grad, sums1, qvs, count, height, sizes
    )
    wide = D // 128

    def row_of(at):
        return sums[at * wide : (at + 1) * wide].reshape(D)

    return (
        block_out,
        image_grad,
        tap_grads[0:27, 0:CH].T.reshape(conv_weight.shape),
        tap_grads[27, 0:CH],
        pw_grad.T,
        row_of(12),
        row_of(8),
        row_of(9),
        wq_grad,
        row_of(10),
        wk_grad,
        wv_grad,
        row_of(11),
        wo_grad,
        row_of(2),
        row_of(0),
        row_of(1),
        wh_grad,
        sums[4 * wide : 8 * wide].reshape(FF),
        wr_grad.T,
        row_of(3),
    )


def solution(mesh):
    split = P("items", "rows")
    flat = P(("items", "rows"), None)
    image = P("items", None, "rows", None)
    return jax.shard_map(
        on_device,
        mesh=mesh,
        in_specs=(image, P("items")) + (P(),) * 19 + (flat,),
        out_specs=(
            flat, image, P(), P(), split, P(), P(), P(), split, P(), split, split,
            P(), split, P(), P(), P(), split, P(), split, P(),
        ),
        check_vma=False,
    )
```

```python
import functools

import jax
import jax.numpy as jnp
from jax import lax
from jax.experimental import pallas as pl
from jax.experimental.pallas import tpu as pltpu
from jax.sharding import PartitionSpec as P

BF = jnp.bfloat16
F32 = jnp.float32
D = 768
HEADS = 12
HD = 64
FF = 3072
IMG = 256
PATCH = 16
CH = 32
CIN = 3
SEQ_ITEMS = 4
NPATCH = 256
TOK = 1024
NP = IMG // PATCH
PF = CH * PATCH * PATCH
HALF = 64
WIN = PATCH + 2
ONE_LANE = CIN * WIN
SLABS = (PATCH + 2) // 2
STEPS = PATCH // 2
FEAT = PF // STEPS
GELU_A = 0.7978845608028654
GELU_B = GELU_A * 0.044715
VMEM_CAP = 60 * 1024 * 1024


def mm(left, right):
    return jnp.dot(left, right, preferred_element_type=F32)


def mm_t(left, right):
    return lax.dot_general(left, right, (((1,), (1,)), ((), ())), preferred_element_type=F32)


def params(**extra):
    return pltpu.CompilerParams(vmem_limit_bytes=VMEM_CAP, **extra)


def whole(shape):
    zeros = (0,) * len(shape)
    return pl.BlockSpec(shape, lambda *_: zeros, pipeline_mode=pl.Buffered(1))


def gelu_pair_low(v):
    bend = jnp.tanh((v * (GELU_A + GELU_B * (v * v))).astype(BF))
    low = v.astype(BF)
    gate = bend * BF(0.5) + BF(0.5)
    act = low * gate
    slope = gate + act * (BF(1.0) - gate) * (BF(2.0 * GELU_A) + BF(6.0 * GELU_B) * (low * low))
    return act, slope


def as_row(ref, at=None):
    line = ref[...] if at is None else ref[at]
    return line.astype(F32).reshape(1, line.shape[0])


def gelu_pair(v):
    square = v * v
    gate = 0.5 + 0.5 * jnp.tanh(v * (GELU_A + GELU_B * square))
    act = v * gate
    slope = gate + act * (1.0 - gate) * (2.0 * GELU_A + (6.0 * GELU_B) * square)
    return act, slope


MESH = pl.DeviceIdType.MESH


def grid_sizes(items, rows):
    nx = rows // 2
    ny = nx if items % nx == 0 else 1
    return (2, nx, ny, items // ny)


def place(sizes):
    item, row = lax.axis_index("items"), lax.axis_index("rows")
    return (row % 2, row // 2, item % sizes[2], item // sizes[2])


def peer(sizes, pos, axis, k):
    moved = list(pos)
    moved[axis] = lax.rem(pos[axis] + k, sizes[axis])
    return (moved[3] * sizes[2] + moved[2], moved[1] * 2 + moved[0]), moved[axis]


def greet(sizes, pos, near, far):
    barrier = pltpu.get_barrier_semaphore()
    item, row, rows = lax.axis_index("items"), lax.axis_index("rows"), 2 * sizes[1]
    peers = [(item, lax.rem(row + k, rows)) for k in range(1, rows)] if near else []
    for axis in (2, 3) if far else ():
        peers += [peer(sizes, pos, axis, k)[0] for k in range(1, sizes[axis])]
    for device in peers:
        pl.semaphore_signal(barrier, inc=1, device_id=device, device_id_type=MESH)
    pl.semaphore_wait(barrier, len(peers))


def turn_of(sizes, pos, x):
    return lax.rem(x + 2 * sizes[1] - 1 - pos[1], sizes[1])


def add_up(first, rest):
    total = first.astype(F32)
    for term in rest:
        total = total + term.astype(F32)
    return total


class Piece:
    def __init__(self, sizes, pos, order, source, own, bufs, send, recv):
        self.sizes, self.pos = sizes, pos
        self.source, self.own, self.bufs = source, own, bufs
        self.send, self.recv = send, recv
        self.axes = (0,) + order

    def at(self, stage, where):
        left = sorted(self.axes[stage:])
        return (slice(None),) * left.index(self.axes[stage]) + (where,)

    def copies(self, stage):
        out = []
        for k in range(1, self.sizes[self.axes[stage]]):
            device, there = peer(self.sizes, self.pos, self.axes[stage], k)
            if stage == 0:
                src, dst = self.source.at[there], self.bufs[0]
            else:
                held = self.at(stage, there)
                src = self.bufs[0].at[held] if stage == 1 else self.bufs[stage - 1].at[(0,) + held]
                dst = self.bufs[stage].at[k - 1]
            out.append(
                pltpu.make_async_remote_copy(
                    src_ref=src, dst_ref=dst, send_sem=self.send.at[stage, k - 1], recv_sem=self.recv.at[stage, k - 1],
                    device_id=device, device_id_type=MESH,
                )
            )
        return out

    def start(self, stage):
        for copy in self.copies(stage):
            copy.start()

    def gather(self, stage):
        for copy in self.copies(stage):
            copy.wait_recv()
        bufs = self.bufs
        if stage == 0:
            bufs[0][...] = bufs[0][...] + self.own[...]
            return None
        held = self.at(stage, self.pos[self.axes[stage]])
        base = bufs[0][held] if stage == 1 else bufs[stage - 1][(0,) + held]
        terms = self.sizes[self.axes[stage]] - 1
        if stage < 3 and terms == 1:
            bufs[stage][0] = base + bufs[stage][0]
            return None
        total = add_up(base, [bufs[stage][k] for k in range(terms)])
        if stage == 3:
            return total
        bufs[stage][0] = total.astype(BF)

    def advance(self, stage):
        self.gather(stage - 1)
        self.start(stage)

    def drain(self, stages=(0, 1, 2, 3)):
        for stage in stages:
            for copy in self.copies(stage):
                copy.wait_send()


def piece_scratch(sizes, orders, shape):
    out = []
    for order in orders:
        out.append(pltpu.VMEM(sizes[1:] + shape, BF))
        for stage in range(3):
            left = tuple(sizes[axis] for axis in sorted(order[stage + 1 :]))
            out.append(pltpu.VMEM((sizes[order[stage]] - 1,) + left + shape, BF))
    sems = pltpu.SemaphoreType.DMA((len(orders), 4, max(sizes) - 1))
    return out + [sems, sems]


def own_scratch(sizes, count, shape):
    return [pltpu.VMEM((count,) + sizes[1:] + shape, BF), pltpu.SemaphoreType.DMA((count,))]


def make_pieces(sizes, pos, orders, sources, owns, refs):
    count = len(orders)
    return [
        Piece(sizes, pos, orders[n], sources[n], owns[n], refs[4 * n : 4 * n + 4], refs[4 * count].at[n], refs[4 * count + 1].at[n])
        for n in range(count)
    ]


class SmallSum:
    def __init__(self, sizes, pos, bufs, send, recv):
        self.sizes, self.pos, self.bufs, self.send, self.recv = sizes, pos, bufs, send, recv

    def copies(self, axis, receive):
        buf, here = self.bufs[axis], self.pos[axis]
        out = []
        for k in range(1, self.sizes[axis]):
            device, _ = peer(self.sizes, self.pos, axis, k)
            slot = lax.rem(here + self.sizes[axis] - k, self.sizes[axis]) if receive else here
            out.append(
                pltpu.make_async_remote_copy(
                    src_ref=buf.at[here], dst_ref=buf.at[slot], send_sem=self.send.at[axis, k - 1],
                    recv_sem=self.recv.at[axis, k - 1], device_id=device, device_id_type=MESH,
                )
            )
        return out

    def start(self, axis, value):
        self.bufs[axis][self.pos[axis]] = value
        for copy in self.copies(axis, False):
            copy.start()

    def gather(self, axis):
        for copy in self.copies(axis, True):
            copy.wait_recv()
        total = self.bufs[axis][0]
        for k in range(1, self.sizes[axis]):
            total = total + self.bufs[axis][k]
        return total

    def advance(self, axis):
        self.start(axis, self.gather(axis - 1))

    def drain(self):
        for axis in range(4):
            for copy in self.copies(axis, False):
                copy.wait_send()


def small_scratch(sizes, height):
    return [pltpu.VMEM((size, height, 128), F32) for size in sizes] + [
        pltpu.SemaphoreType.DMA((4, max(sizes) - 1)),
        pltpu.SemaphoreType.DMA((4, max(sizes) - 1)),
    ]


def folds(width):
    return width % 128 == HALF and width > 128


def narrow(width):
    return 128 // width if width < 128 and 128 % width == 0 else 1


def folded_shape(height, width):
    if folds(width) or narrow(width) > 1:
        return (height * width // 128, 128)
    return (height, width)


def fold_block(block):
    height, width = block.shape
    if narrow(width) > 1:
        part = height // narrow(width)
        return jnp.concatenate([block[k * part : (k + 1) * part] for k in range(narrow(width))], axis=1)
    return block


def unfold_block(block, height, width, odd=False):
    if narrow(width) > 1:
        return jnp.concatenate([block[:, k * width : (k + 1) * width] for k in range(narrow(width))], axis=0)
    if not folds(width):
        return block
    main, side = block[:height], block[height:]
    side = jnp.concatenate([side[:, :HALF], side[:, HALF:]], axis=0)
    return jnp.where(odd, jnp.concatenate([side, main], axis=1), jnp.concatenate([main, side], axis=1))


def run_events(step, table, slots):
    for (when, slot), todo in table.items():
        if slot in slots:
            @pl.when(step == when)
            def _(todo=todo):
                for call in todo:
                    call()


def make_windows(sizes, pos, img_ref, edge, edge_copies, meanwhile, x, xt_ref, sel_ref, pix, lines):
    items, _, height, width = img_ref.shape
    nrow = height // PATCH
    group = items * nrow
    row, final_row = lax.axis_index("rows"), lax.axis_size("rows") - 1
    for ch in range(CIN):
        for item in range(items):
            full = img_ref[item, ch].astype(F32)
            for k in range(width // 128):
                pix[ch, k, item * height : (item + 1) * height, :] = full[:, k * 128 : (k + 1) * 128]

    def line(ch, r):
        return jnp.concatenate([pix[ch, k, pl.ds(r, group, stride=PATCH), :] for k in range(width // 128)], axis=1)

    for ch in range(CIN):
        first, final = line(ch, 0), line(ch, PATCH - 1)
        edge[0, ch] = pltpu.roll(first, nrow - 1, 0).astype(BF)
        edge[1, ch] = pltpu.roll(final, group - nrow + 1, 0).astype(BF)

    @pl.when(row > 0)
    def _():
        edge_copies[0].start()

    @pl.when(row < final_row)
    def _():
        edge_copies[1].start()

    meanwhile()

    for ch in range(CIN):
        cols = slice(ch * width, (ch + 1) * width)
        for r in range(PATCH):
            lines[(r + 1) * group : (r + 2) * group, cols] = line(ch, r).astype(BF)
    lane = lax.broadcasted_iota(jnp.int32, (1, NP * HALF), 1)
    col, spot = lane // HALF, lane % HALF
    for ch in range(CIN):
        inside = (spot >= WIN * ch) & (spot < WIN * (ch + 1))
        want = jnp.where(inside, PATCH * col + spot - WIN * ch - 1, -5)
        here = lax.broadcasted_iota(jnp.int32, (width, NP * HALF), 0)
        sel_ref[ch * width : (ch + 1) * width, :] = jnp.where(here == want, 1.0, 0.0).astype(BF)

    @pl.when(row < final_row)
    def _():
        edge_copies[0].wait_recv()

    @pl.when(row > 0)
    def _():
        edge_copies[1].wait_recv()

    patch_row = lax.broadcasted_iota(jnp.int32, (group, width), 0) % nrow
    for ch in range(CIN):
        cols = slice(ch * width, (ch + 1) * width)
        up = jnp.where(patch_row == 0, edge[3, ch].astype(F32), pltpu.roll(line(ch, PATCH - 1), 1, 0))
        lines[0:group, cols] = up.astype(BF)
        down = jnp.where(patch_row == nrow - 1, edge[2, ch].astype(F32), pltpu.roll(line(ch, 0), group - 1, 0))
        lines[(PATCH + 1) * group : (PATCH + 2) * group, cols] = down.astype(BF)
    lane = lax.broadcasted_iota(jnp.int32, (group, 2 * HALF), 1)
    low = lane < HALF
    ones = (lane % HALF) == ONE_LANE
    nx = sizes[1]
    share, per = items * nrow * NP // nx, group // nx
    turns = [turn_of(sizes, pos, xg) * share for xg in range(nx)]

    def put(j, c, block):
        low_bits = block.astype(BF)
        for xg in range(nx):
            x[j, pl.ds(pl.multiple_of(turns[xg] + c * per, per), per), :] = low_bits[xg * per : (xg + 1) * per]

    for quarter in range(NP * HALF // 256):
        res = mm(lines[...], sel_ref[:, quarter * 256 : (quarter + 1) * 256])
        for j in range(SLABS):
            first = res[2 * j * group : (2 * j + 1) * group]
            second = res[(2 * j + 1) * group : (2 * j + 2) * group]
            for pair in range(2):
                a = first[:, pair * 128 : (pair + 1) * 128]
                b = second[:, pair * 128 : (pair + 1) * 128]
                put(j, quarter * 4 + pair * 2, jnp.where(ones, 1.0, jnp.where(low, a, pltpu.roll(b, HALF, 1))))
                put(j, quarter * 4 + pair * 2 + 1, jnp.where(ones, 1.0, jnp.where(low, pltpu.roll(a, HALF, 1), b)))
    for j in range(SLABS):
        xt_ref[j] = x[j].T


def stem_kernel(sizes, img_ref, cw_ref, cb_ref, w_ref, pb_ref, tok_ref, saved_ref, xt_ref, sel_ref, t_ref,
                x, pix, lines, edge, edge_send, edge_recv, acc, nat, parcel, got, send, recv):
    t = pl.program_id(0)
    p = t % STEPS
    nx = sizes[1]
    rows = 2 * nx
    pos = place(sizes)
    item, row, final_row = lax.axis_index("items"), lax.axis_index("rows"), lax.axis_size("rows") - 1
    share = acc.shape[0]
    per = share // NP

    def edge_copy(n):
        return pltpu.make_async_remote_copy(
            src_ref=edge.at[n], dst_ref=edge.at[2 + n], send_sem=edge_send.at[n], recv_sem=edge_recv.at[n],
            device_id=(item, row + (2 * n - 1)), device_id_type=MESH,
        )

    @pl.when(t == 0)
    def _():
        @pl.when(row == final_row)
        def _():
            edge[2] = jnp.zeros(edge.shape[1:], BF)

        @pl.when(row == 0)
        def _():
            edge[3] = jnp.zeros(edge.shape[1:], BF)

        greet(sizes, pos, True, False)
        taps = functools.partial(tap_matrix, cw_ref, cb_ref, t_ref)
        make_windows(sizes, pos, img_ref, edge, [edge_copy(0), edge_copy(1)], taps, x, xt_ref, sel_ref, pix, lines)

    @pl.when(p == 0)
    def _():
        acc[...] = jnp.broadcast_to(as_row(pb_ref), acc.shape)

    weight = w_ref[...].reshape(FEAT, D)
    for s in range(share // 256):
        rs = slice(s * 256, (s + 1) * 256)
        here = pl.ds(pl.multiple_of(t // STEPS * share + s * 256, 256), 256)
        xs = jnp.concatenate([x[p, here, :], x[p + 1, here, :]], axis=1)
        for n in range(FEAT // 256):
            cs = slice(n * 256, (n + 1) * 256)
            act, slope = gelu_pair_low(mm(xs, t_ref[:, cs]))
            saved_ref[0, 0, rs, cs] = act
            saved_ref[0, 1, rs, cs] = slope
        acc[rs, :] += mm(saved_ref[0, 0, rs, :], weight)

    @pl.when(p == STEPS - 1)
    def _():
        for c in range(NP):
            for k in range(D // 128):
                nat[k, pl.ds(c, per, stride=NP), :] = acc[c * per : (c + 1) * per, k * 128 : (k + 1) * 128]

    def parcel_copy(turn, core, slot):
        to = lax.rem(pos[1] + 1 + turn, nx) * 2 + core
        return pltpu.make_async_remote_copy(
            src_ref=parcel.at[turn, core], dst_ref=got.at[:, row], send_sem=send.at[turn, slot], recv_sem=recv.at[row],
            device_id=(item, to), device_id_type=MESH,
        )

    for turn in range(nx):
        @pl.when(t == turn * STEPS + STEPS - 1)
        def _(turn=turn):
            for k in range(D // 128):
                cut = nat[k].astype(BF).reshape(parcel.shape[1:4] + (128,))
                parcel[turn, :, :, :, k * 128 : (k + 1) * 128] = cut
            if turn < nx - 1:
                for core in range(2):
                    parcel_copy(turn, core, core).start()
            else:
                parcel_copy(turn, 1 - pos[0], 0).start()
                got[:, row] = parcel[turn, pos[0]]

    @pl.when(t == nx * STEPS - 1)
    def _():
        for k in range(1, rows):
            source = lax.rem(row + k, rows)
            pltpu.make_async_remote_copy(
                src_ref=parcel.at[0, 0], dst_ref=got.at[:, source], send_sem=send.at[0, 0], recv_sem=recv.at[source],
                device_id=(item, source), device_id_type=MESH,
            ).wait_recv()
        tok_ref[...] = got[...]
        for turn in range(nx - 1):
            for core in range(2):
                parcel_copy(turn, core, core).wait_send()
        parcel_copy(nx - 1, 1 - pos[0], 0).wait_send()

        @pl.when(row > 0)
        def _():
            edge_copy(0).wait_send()

        @pl.when(row < final_row)
        def _():
            edge_copy(1).wait_send()


def stem_forward(images, cw, cb, weight, bias, sizes):
    count, _, height, width = images.shape
    nx = sizes[1]
    nrow = height // PATCH
    group = count * nrow
    tokens = group * NP
    share = tokens // nx
    arrived = (SEQ_ITEMS, 2 * nx, nrow * NP, D)
    return pl.pallas_call(
        functools.partial(stem_kernel, sizes),
        name="stem_forward",
        grid=(nx * STEPS,),
        in_specs=[
            whole(images.shape),
            whole(cw.shape),
            whole(cb.shape),
            pl.BlockSpec((CH, 1, 2 * PATCH, D), lambda t: (0, t % STEPS, 0, 0)),
            whole(bias.shape),
        ],
        out_specs=(
            whole(arrived),
            pl.BlockSpec((1, 2, share, FEAT), lambda t: (t % STEPS, 0, t // STEPS, 0)),
            whole((SLABS, 128, tokens)),
            whole((CIN * width, NP * HALF)),
            whole((4 * HALF, FEAT)),
        ),
        out_shape=(
            jax.ShapeDtypeStruct(arrived, BF),
            jax.ShapeDtypeStruct((STEPS, 2, tokens, FEAT), BF),
            jax.ShapeDtypeStruct((SLABS, 128, tokens), BF),
            jax.ShapeDtypeStruct((CIN * width, NP * HALF), BF),
            jax.ShapeDtypeStruct((4 * HALF, FEAT), BF),
        ),
        scratch_shapes=[
            pltpu.VMEM((SLABS, tokens, 128), BF),
            pltpu.VMEM((CIN, width // 128, count * height, 128), F32),
            pltpu.VMEM((WIN * group, CIN * width), BF),
            pltpu.VMEM((4, CIN, group, width), BF),
            pltpu.SemaphoreType.DMA((2,)),
            pltpu.SemaphoreType.DMA((2,)),
            pltpu.VMEM((share, D), F32),
            pltpu.VMEM((D // 128, share, 128), F32),
            pltpu.VMEM((nx, 2, SEQ_ITEMS, nrow * NP, D), BF),
            pltpu.VMEM(arrived, BF),
            pltpu.SemaphoreType.DMA((nx, 2)),
            pltpu.SemaphoreType.DMA((2 * nx,)),
        ],
        compiler_params=params(collective_id=0, has_side_effects=True),
    )(images, cw, cb, weight, bias)


def norm_stats(v):
    centred = v - jnp.mean(v, axis=-1, keepdims=True)
    inv = lax.rsqrt(jnp.mean(centred * centred, axis=-1, keepdims=True) + 1e-06)
    return centred * inv, inv


def three_terms(v):
    hi = v.astype(BF)
    rest = v - hi.astype(F32)
    mid = rest.astype(BF)
    lo = (rest - mid.astype(F32)).astype(BF)
    return hi, mid, lo


def minus_terms(v, lane, base):
    rest = -v - (-v).astype(BF).astype(F32)
    final = rest - rest.astype(BF).astype(F32)
    out = jnp.where(lane == 4, -v, jnp.where(lane == 5, rest, base))
    return jnp.where(lane == 6, final, out).astype(BF)


def attend_kernel(tok_ref, g_ref, b_ref, qb_ref, vb_ref, seg_ref, wq_ref, wk_ref, wv_ref,
                  q_ref, k_ref, v_ref, o_ref, o32_ref, lx_ref, kx_ref, n1, kaug, vaug):
    step = pl.program_id(0)
    line = lax.broadcasted_iota(jnp.int32, (1, 128), 1)
    first_item = lax.axis_index("rows") * SEQ_ITEMS
    same = [line == seg_ref[first_item + i] for i in range(SEQ_ITEMS)]
    terms = jnp.where((line >= 4) & (line < 7), 1.0, 0.0)
    keys_in = [jnp.where((line < 4) & ~one, -1e30, terms) for one in same]

    @pl.when(step == 0)
    def _():
        kx_ref[...] = jnp.concatenate(keys_in + [jnp.zeros((8 - SEQ_ITEMS, 128), F32)], axis=0)
        for s in range(TOK // 128):
            rs = slice(s * 128, (s + 1) * 128)
            hat, _ = norm_stats(tok_ref[rs, :].astype(F32))
            n1[rs, :] = (hat * as_row(g_ref) + as_row(b_ref)).astype(BF)

    own = pl.ds(pl.multiple_of(step * 256, 256), 256)
    q_ref[...] = ((mm(n1[...], wq_ref[...]) + as_row(qb_ref, own)).astype(BF) * 0.125).astype(BF)
    k_ref[...] = mm(n1[...], wk_ref[...]).astype(BF)
    v_ref[...] = (mm(n1[...], wv_ref[...]) + as_row(vb_ref, own)).astype(BF)
    lane = lax.broadcasted_iota(jnp.int32, (NPATCH, 128), 1)
    low = lane < HD
    for i in range(SEQ_ITEMS):
        rs = slice(i * NPATCH, (i + 1) * NPATCH)
        kaug[rs, 128:256] = jnp.broadcast_to(keys_in[i], (NPATCH, 128)).astype(BF)
        vaug[rs, 128:256] = jnp.ones((NPATCH, 128), BF)
    for pair in range(2):
        cs = slice(pair * 128, (pair + 1) * 128)
        kaug[:, 0:128] = k_ref[:, cs]
        vaug[:, 0:128] = v_ref[:, cs]
        for i in range(SEQ_ITEMS):
            rs = slice(i * NPATCH, (i + 1) * NPATCH)
            span = slice(0, (i + 1) * NPATCH)
            qp = q_ref[rs, cs]
            qx = jnp.broadcast_to(jnp.where(same[i], 1.0, 0.0), (NPATCH, 128))
            halves = []
            for h in range(2):
                mine = low if h == 0 else ~low
                qaug = jnp.concatenate([jnp.where(mine, qp, jnp.zeros_like(qp)), qx.astype(BF)], axis=1)
                scores = mm_t(qaug, kaug[span, :])
                top = jnp.max(scores, axis=1, keepdims=True)
                raised = jnp.exp(scores - top).astype(BF)
                out = mm(raised, vaug[span, :])
                total = out[:, 128:256]
                halves.append(out[:, 0:128] / total)
                lx_ref[pair * 2 + h, rs, :] = minus_terms(top + jnp.log(total), lane, qx)
            out = jnp.where(low, halves[0], halves[1])
            o32_ref[rs, cs] = out
            o_ref[rs, cs] = out.astype(BF)


def attend(tokens, vecs, segments, wq, wk, wv):
    lines = [whole(vec.shape) for vec in vecs]
    col = pl.BlockSpec((D, 256), lambda g: (0, g))
    out = pl.BlockSpec((TOK, 256), lambda g: (0, g))
    return pl.pallas_call(
        attend_kernel,
        name="attend",
        grid=(D // 256,),
        in_specs=[whole((TOK, D))] + lines + [pl.BlockSpec(memory_space=pltpu.SMEM), col, col, col],
        out_specs=(out, out, out, out, out, pl.BlockSpec((4, TOK, 128), lambda g: (g, 0, 0)), whole((8, 128))),
        out_shape=(jax.ShapeDtypeStruct((TOK, D), BF),) * 4
        + (
            jax.ShapeDtypeStruct((TOK, D), F32),
            jax.ShapeDtypeStruct((HEADS, TOK, 128), BF),
            jax.ShapeDtypeStruct((8, 128), F32),
        ),
        scratch_shapes=[pltpu.VMEM((TOK, D), BF), pltpu.VMEM((TOK, 256), BF), pltpu.VMEM((TOK, 256), BF)],
        compiler_params=params(),
    )(tokens, *vecs, segments, wq, wk, wv)


def norm_back(e, hat, inv, gain):
    f = e * gain
    return inv * (f - jnp.mean(f, axis=-1, keepdims=True) - hat * jnp.mean(f * hat, axis=-1, keepdims=True))


def col_sum(v):
    return jnp.sum(v, axis=0, keepdims=True)


def store_square(ref, n, grad):
    _, _, nx, ny, nz, _, _ = ref.shape
    height, width = D // (ny * nz), D // (2 * nx)
    if not folds(width):
        for r in range(2 * nx):
            part = grad[:, r * width : (r + 1) * width]
            for i in range(ny * nz):
                ref[n, r % 2, r // 2, i % ny, i // ny] = part[i * height : (i + 1) * height]
        return
    half = height // 2
    low = lax.broadcasted_iota(jnp.int32, (half, 128), 1) < HALF
    for x in range(nx):
        base = 2 * x * width
        shared = grad[:, base + 128 : base + 256]
        turned = jnp.concatenate([shared[:, HALF:], shared[:, :HALF]], axis=1)
        for i in range(ny * nz):
            top, end = i * height, (i + 1) * height
            mid = top + half
            ref[n, 0, x, i % ny, i // ny, 0:height] = grad[top:end, base : base + 128]
            ref[n, 0, x, i % ny, i // ny, height:] = jnp.where(low, shared[top:mid], turned[mid:end])
            ref[n, 1, x, i % ny, i // ny, 0:height] = grad[top:end, base + 256 : base + 384]
            ref[n, 1, x, i % ny, i // ny, height:] = jnp.where(low, turned[top:mid], shared[mid:end])


def mixer_kernel(tok_ref, att_ref, cot_ref, wo_ref, ob_ref, g_ref, b_ref, rb_ref, hb_ref, wh_ref, wr_ref,
                 out_ref, mid_ref, ag_ref, wog_ref, whg_ref, wrg_ref, sums_ref, hbg_ref,
                 middle, n2, n2t, cott, acc, back, act, hg, hidden_row):
    step = pl.program_id(0)
    last = pl.num_programs(0) - 1
    chunk = wh_ref.shape[1]
    tile = 2 if chunk % 256 == 0 else 3
    blocks = [slice(s * 256, (s + 1) * 256) for s in range(TOK // 256)]

    @pl.when(step == 0)
    def _():
        hidden_row[...] = as_row(hb_ref)
        for rs in blocks:
            row = tok_ref[rs, :].astype(F32) + mm(att_ref[rs, :], wo_ref[...]) + as_row(ob_ref)
            middle[rs, :] = row
            acc[rs, :] = row + as_row(rb_ref)
            back[rs, :] = jnp.zeros((256, D), F32)
            hat, _ = norm_stats(row)
            low = (hat * as_row(g_ref) + as_row(b_ref)).astype(BF)
            n2[rs, :] = low
            n2t[:, rs] = low.T
            cott[:, rs] = cot_ref[rs, :].T

    hidden_bias = hidden_row[0:1, pl.ds(pl.multiple_of(step * chunk, 128), chunk)]
    hsum = jnp.zeros((1, chunk), F32)
    for rs in blocks:
        for n in range(chunk // 128 // tile):
            cs = slice(n * 128 * tile, (n + 1) * 128 * tile)
            pre = mm(n2[rs, :], wh_ref[:, cs]) + hidden_bias[:, cs]
            up = mm_t(cot_ref[rs, :], wr_ref[cs, :])
            a, slope = gelu_pair(pre)
            act[rs, cs] = a.astype(BF)
            hg[rs, cs] = (slope * up).astype(BF)
        acc[rs, :] += mm(act[rs, :], wr_ref[...])
        back[rs, :] += mm_t(hg[rs, :], wh_ref[...])
        hsum = hsum + col_sum(hg[rs, :].astype(F32))
    hbg_ref[...] = hsum
    _, _, nx, ny, nz, height, _ = whg_ref.shape
    for n in range(3):
        width = chunk // 3
        grad = mm(n2t[...], hg[:, n * width : (n + 1) * width]).astype(BF)
        for i in range(ny * nz):
            whg_ref[n, 0, 0, i % ny, i // ny] = grad[i * height : (i + 1) * height]
    _, _, nx, ny, _, _, _ = wrg_ref.shape
    height, width = D // (2 * nx), chunk // ny // 3
    for y in range(ny):
        grad = mm(cott[...], act[:, y * 3 * width : (y + 1) * 3 * width]).astype(BF)
        for n in range(3):
            for r in range(2 * nx):
                part = grad[r * height : (r + 1) * height, n * width : (n + 1) * width]
                wrg_ref[n, r % 2, r // 2, y, 0] = fold_block(part)

    @pl.when(step == last)
    def _():
        gsum = jnp.zeros((1, D), F32)
        bsum = jnp.zeros((1, D), F32)
        osum = jnp.zeros((1, D), F32)
        rsum = jnp.zeros((1, D), F32)
        for rs in blocks:
            out_ref[rs, :] = acc[rs, :].astype(BF)
            hat, inv = norm_stats(middle[rs, :])
            e = back[rs, :]
            gsum = gsum + col_sum(e * hat)
            bsum = bsum + col_sum(e)
            cot = cot_ref[rs, :].astype(F32)
            rsum = rsum + col_sum(cot)
            mid = cot + norm_back(e, hat, inv, as_row(g_ref))
            mid_ref[rs, :] = mid
            low = mid.astype(BF)
            osum = osum + col_sum(low.astype(F32))
            n2[rs, :] = low
            n2t[:, rs] = att_ref[rs, :].T
            ag_ref[rs, :] = mm_t(low, wo_ref[...]).astype(BF)
        store_square(wog_ref, 0, mm(n2t[...], n2[...]).astype(BF))
        sums_ref[0:1, :] = gsum
        sums_ref[1:2, :] = bsum
        sums_ref[2:3, :] = osum
        sums_ref[3:4, :] = rsum


def mixer(tokens, attended, cotangent, wo, vecs, wh, wr, sizes):
    nc, nx, ny, nz = sizes
    rows, items = nc * nx, ny * nz
    chunk = FF // rows
    square = (1,) + sizes + folded_shape(D // items, D // rows)
    return pl.pallas_call(
        mixer_kernel,
        name="mixer",
        grid=(rows,),
        in_specs=[
            whole((TOK, D)), whole((TOK, D)), whole((TOK, D)), whole((D, D)),
            whole((D,)), whole((D,)), whole((D,)), whole((D,)), whole((FF,)),
            pl.BlockSpec((D, chunk), lambda r: (0, r)),
            pl.BlockSpec((chunk, D), lambda r: (r, 0)),
        ],
        out_specs=(
            whole((TOK, D)), whole((TOK, D)), whole((TOK, D)), whole(square),
            pl.BlockSpec((3, 1, 1, ny, nz, D // items, chunk // 3), lambda r: (0, r % 2, r // 2, 0, 0, 0, 0)),
            pl.BlockSpec((3, nc, nx, ny, 1) + folded_shape(D // rows, FF // items // 3), lambda r: (0, 0, 0, 0, r, 0, 0)),
            whole((8, D)),
            pl.BlockSpec((1, chunk), lambda r: (0, r)),
        ),
        out_shape=(
            jax.ShapeDtypeStruct((TOK, D), BF),
            jax.ShapeDtypeStruct((TOK, D), F32),
            jax.ShapeDtypeStruct((TOK, D), BF),
            jax.ShapeDtypeStruct(square, BF),
            jax.ShapeDtypeStruct((3,) + sizes + (D // items, chunk // 3), BF),
            jax.ShapeDtypeStruct((3,) + sizes + folded_shape(D // rows, FF // items // 3), BF),
            jax.ShapeDtypeStruct((8, D), F32),
            jax.ShapeDtypeStruct((1, FF), F32),
        ),
        scratch_shapes=[
            pltpu.VMEM((TOK, D), F32), pltpu.VMEM((TOK, D), BF), pltpu.VMEM((D, TOK), BF),
            pltpu.VMEM((D, TOK), BF), pltpu.VMEM((TOK, D), F32), pltpu.VMEM((TOK, D), F32),
            pltpu.VMEM((TOK, chunk), BF), pltpu.VMEM((TOK, chunk), BF), pltpu.VMEM((1, FF), F32),
        ],
        compiler_params=params(),
    )(tokens, attended, cotangent, wo, *vecs, wh, wr)


def attend_back_kernel(sizes, tok_ref, g_ref, b_ref, kx_ref, mid_ref, q_ref, k_ref, v_ref, o_ref, ag_ref, lx_ref,
                       wq_ref, wk_ref, wv_ref, whg_ref, wrg_ref, wog_ref,
                       tg_ref, sq_ref, sums_ref, qvs_ref, who_ref, wro_ref, woo_ref,
                       n1t, back, kaug, vaug, qaug, oaug, dqt, dq, dk, dv, square, *comm):
    step = pl.program_id(0)
    blocks = [slice(s * 256, (s + 1) * 256) for s in range(TOK // 256)]
    pos = place(sizes)
    groups = ((whg_ref, who_ref), (wrg_ref, wro_ref), (wog_ref, woo_ref))
    pieces, loads, base, at = [], [], 0, 0
    for source, _ in groups:
        count = source.shape[0]
        refs, keep = comm[at : at + 4 * count + 2], comm[at + 4 * count + 2 : at + 4 * count + 4]
        at += 4 * count + 4
        pieces += make_pieces(
            sizes, pos, BACK_ORDERS[base : base + count], [source.at[n] for n in range(count)],
            [keep[0].at[n] for n in range(count)], refs,
        )
        loads += [pltpu.make_async_copy(source.at[n, pos[0]], keep[0].at[n], keep[1].at[n]) for n in range(count)]
        base += count

    def event(index, stage):
        if stage == 0:
            pieces[index].start(0)
            loads[index].start()
        elif stage < 4:
            if stage == 1:
                loads[index].wait()
            pieces[index].advance(stage)
        else:
            total = pieces[index].gather(3)
            if index < 3:
                width = total.shape[1]
                who_ref[:, index * width : (index + 1) * width] = total
            elif index < 6:
                height, width = D // (2 * sizes[1]), FF // (sizes[2] * sizes[3]) // 3
                wro_ref[:, (index - 3) * width : (index - 2) * width] = unfold_block(total, height, width)
            else:
                woo_ref[...] = unfold_block(total, *woo_ref.shape, odd=pos[0] == 1)

    def finish():
        for part in pieces:
            part.drain()

    table = {(0, 0): [functools.partial(greet, sizes, pos, True, True)]}
    for when, index, stage in BACK_PLAN:
        if when < 2:
            key = (0, when)
        elif when < 26:
            key = ((when - 2) // 8, 2 + (when - 2) % 8)
        else:
            key = (2, 10)
        table.setdefault(key, []).append(functools.partial(event, index, stage))
    table.setdefault((2, 10), []).append(finish)
    run_events(step, table, (0,))

    @pl.when(step == 0)
    def _():
        for rs in blocks:
            hat, _ = norm_stats(tok_ref[rs, :].astype(F32))
            n1t[:, rs] = (hat * as_row(g_ref) + as_row(b_ref)).astype(BF).T
            back[rs, :] = jnp.zeros((256, D), F32)

    run_events(step, table, (1,))
    lane = lax.broadcasted_iota(jnp.int32, (NPATCH, 128), 1)
    low = lane < HD
    ones = jnp.where((lane >= 4) & (lane < 7), 1.0, 0.0).astype(BF)
    for i, rs in enumerate(blocks):
        kaug[rs, 128:256] = jnp.broadcast_to(kx_ref[i : i + 1, :], (NPATCH, 128)).astype(BF)
        vaug[rs, 128:256] = ones
    pick_row = lax.broadcasted_iota(jnp.int32, (256, 256), 0) % 128 // HD
    pick_col = lax.broadcasted_iota(jnp.int32, (256, 256), 1) // 128
    pick = jnp.where(pick_row == pick_col, 1.0, 0.0).astype(BF)
    for pair in range(2):
        cs = slice(pair * 128, (pair + 1) * 128)
        kaug[:, 0:128] = k_ref[:, cs]
        vaug[:, 0:128] = v_ref[:, cs]
        kt = k_ref[:, cs].T
        for rs in blocks:
            qp = q_ref[rs, cs]
            gp = ag_ref[rs, cs]
            prod = gp.astype(F32) * o_ref[rs, cs]
            hi = prod.astype(BF)
            both = jnp.concatenate([hi, (prod - hi.astype(F32)).astype(BF)], axis=1)
            dots = mm(both, pick)
            for h in range(2):
                mine = low if h == 0 else ~low
                qaug[h, rs, 0:128] = jnp.where(mine, qp, jnp.zeros_like(qp))
                qaug[h, rs, 128:256] = lx_ref[pair * 2 + h, rs, :]
                oaug[h, rs, 0:128] = jnp.where(mine, gp, jnp.zeros_like(gp))
                oaug[h, rs, 128:256] = minus_terms(dots[:, h * 128 : (h + 1) * 128], lane, jnp.zeros((NPATCH, 128), F32))
        for j, rs in enumerate(blocks):
            span = slice(j * NPATCH, TOK)
            parts_k, parts_v = [], []
            for h in range(2):
                probs = jnp.exp(mm_t(kaug[rs, :], qaug[h, span, :]))
                rise = mm_t(vaug[rs, :], oaug[h, span, :])
                grad = (probs * rise).astype(BF)
                probs_low = probs.astype(BF)
                parts_v.append(mm(probs_low, ag_ref[span, cs]))
                parts_k.append(mm(grad, q_ref[span, cs]))
                hs = slice(h * HD, (h + 1) * HD)
                part = mm(kt[hs, rs], grad)
                if j == 0:
                    dqt[hs, :] = part
                else:
                    dqt[hs, span] += part
            dk[rs, cs] = jnp.where(low, parts_k[0], parts_k[1]).astype(BF)
            dv[rs, cs] = jnp.where(low, parts_v[0], parts_v[1]).astype(BF)
            run_events(step, table, (2 + pair * 4 + j,))
        dq[:, cs] = (dqt[...].T * 0.125).astype(BF)
    qvs_ref[0:1, :] = col_sum(dq[...].astype(F32))
    qvs_ref[1:2, :] = col_sum(dv[...].astype(F32))
    for n, part in enumerate((dq, dk, dv)):
        square[n, step] = mm(n1t[...], part[...]).astype(BF)
    for rs in blocks:
        back[rs, :] += (
            mm_t(dq[rs, :], wq_ref[...]) + mm_t(dk[rs, :], wk_ref[...]) + mm_t(dv[rs, :], wv_ref[...])
        )

    @pl.when(step == pl.num_programs(0) - 1)
    def _():
        gsum = jnp.zeros((1, D), F32)
        bsum = jnp.zeros((1, D), F32)
        for rs in blocks:
            hat, inv = norm_stats(tok_ref[rs, :].astype(F32))
            e = back[rs, :]
            gsum = gsum + col_sum(e * hat)
            bsum = bsum + col_sum(e)
            tg_ref[rs, :] = (mid_ref[rs, :] + norm_back(e, hat, inv, as_row(g_ref))).astype(BF)
        sums_ref[0:1, :] = gsum
        sums_ref[1:2, :] = bsum
        for n in range(3):
            store_square(sq_ref, n, jnp.concatenate([square[n, g] for g in range(D // 256)], axis=1))

    run_events(step, table, (10,))


BACK_ORDERS = (
    (3, 2, 1), (2, 3, 1), (1, 2, 3), (1, 2, 3), (1, 2, 3), (1, 2, 3),
    (2, 1, 3),
)
BACK_PLAN = (
    (0, 3, 0), (0, 0, 0), (0, 1, 0), (0, 5, 0), (0, 4, 0), (0, 2, 0), (0, 6, 0), (1, 3, 1), (1, 0, 1),
    (1, 1, 1), (4, 5, 1), (6, 6, 1), (6, 2, 1), (7, 1, 2), (9, 3, 2), (9, 4, 1), (10, 5, 2), (15, 3, 3),
    (16, 2, 2), (16, 0, 2), (16, 5, 3), (17, 6, 2), (18, 3, 4), (18, 2, 3), (19, 4, 2), (19, 0, 3), (20, 1, 3),
    (21, 6, 3), (23, 4, 3), (26, 6, 4), (26, 1, 4), (26, 5, 4), (27, 0, 4), (28, 2, 4), (29, 4, 4),
)


def attend_back(tokens, gain, shift, kx, mid, q, k, v, o, ag, lx, wq, wk, wv, whg, wrg, wog, sizes):
    squares = (3,) + sizes + wog.shape[5:]
    col = pl.BlockSpec((D, 256), lambda g: (0, g))
    part = pl.BlockSpec((TOK, 256), lambda g: (0, g))
    far = pl.BlockSpec(memory_space=pl.ANY)
    items, rows = sizes[2] * sizes[3], 2 * sizes[1]
    outs = [(D // items, FF // rows), (D // rows, FF // items), (D // items, D // rows)]
    return pl.pallas_call(
        functools.partial(attend_back_kernel, sizes),
        name="attend_back",
        grid=(D // 256,),
        in_specs=[whole((TOK, D)), whole((D,)), whole((D,)), whole(kx.shape), whole((TOK, D)),
                  part, part, part, part, part, pl.BlockSpec((4, TOK, 128), lambda g: (g, 0, 0)),
                  col, col, col, far, far, far],
        out_specs=(whole((TOK, D)), whole(squares), whole((8, D)), pl.BlockSpec((8, 256), lambda g: (0, g)))
        + tuple(whole(shape) for shape in outs),
        out_shape=(
            jax.ShapeDtypeStruct((TOK, D), BF),
            jax.ShapeDtypeStruct(squares, BF),
            jax.ShapeDtypeStruct((8, D), F32),
            jax.ShapeDtypeStruct((8, D), F32),
        ) + tuple(jax.ShapeDtypeStruct(shape, F32) for shape in outs),
        scratch_shapes=[
            pltpu.VMEM((D, TOK), BF), pltpu.VMEM((TOK, D), F32),
            pltpu.VMEM((TOK, 256), BF), pltpu.VMEM((TOK, 256), BF),
            pltpu.VMEM((2, TOK, 256), BF), pltpu.VMEM((2, TOK, 256), BF),
            pltpu.VMEM((128, TOK), F32),
            pltpu.VMEM((TOK, 256), BF), pltpu.VMEM((TOK, 256), BF), pltpu.VMEM((TOK, 256), BF),
            pltpu.VMEM((3, D // 256, D, 256), BF),
        ]
        + piece_scratch(sizes, BACK_ORDERS[0:3], whg.shape[5:]) + own_scratch(sizes, 3, whg.shape[5:])
        + piece_scratch(sizes, BACK_ORDERS[3:6], wrg.shape[5:]) + own_scratch(sizes, 3, wrg.shape[5:])
        + piece_scratch(sizes, BACK_ORDERS[6:7], wog.shape[5:]) + own_scratch(sizes, 1, wog.shape[5:]),
        compiler_params=params(collective_id=1, has_side_effects=True),
    )(tokens, gain, shift, kx, mid, q, k, v, o, ag, lx, wq, wk, wv, whg, wrg, wog)


EARLY = 80
FINISH_ORDERS = (
    (1, 2, 3), (2, 1, 3), (3, 2, 1), (1, 2, 3), (2, 3, 1), (1, 2, 3),
    (2, 1, 3), (1, 2, 3), (2, 3, 1), (3, 1, 2), (2, 3, 1),
)
FINISH_PLAN = (
    (0, 8, 0), (0, 10, 0), (0, 9, 0), (1, 10, 1), (2, 9, 1), (3, 8, 1), (7, 10, 2), (9, 0, 0), (9, 8, 2),
    (10, 11, 0), (10, 1, 0), (10, 0, 1), (11, 2, 0), (11, 1, 1), (12, 3, 0), (12, 2, 1), (12, 3, 1), (13, 4, 0),
    (13, 0, 2), (14, 4, 1), (14, 5, 0), (14, 1, 2), (14, 11, 1), (15, 6, 0), (15, 5, 1), (16, 7, 0), (16, 0, 3),
    (16, 6, 1), (16, 3, 2), (17, 7, 1), (18, 4, 2), (18, 1, 3), (19, 10, 3), (19, 11, 2), (20, 5, 2), (20, 2, 2),
    (21, 8, 3), (22, 6, 2), (22, 3, 3), (22, 0, 4), (23, 4, 3), (23, 11, 3), (24, 12, 0), (24, 5, 3), (25, 7, 2),
    (25, 12, 1), (25, 6, 3), (25, 9, 2), (26, 12, 2), (26, 2, 3), (26, 10, 4), (28, 12, 3), (28, 5, 4), (29, 7, 3),
    (29, 1, 4), (30, 8, 4), (30, 2, 4), (31, 9, 3), (32, 11, 4), (32, 4, 4), (33, 3, 4), (33, 9, 4), (33, 6, 4),
    (33, 12, 4), (33, 7, 4),
)


def finish_kernel(sizes, tg_ref, act_ref, slope_ref, w_ref, xt_ref, t_ref, sel_ref, sq_ref, sums2_ref, hbg_ref, sums1_ref, qvs_ref,
                  pw_ref, sq0_ref, sq1_ref, sq2_ref, ig_ref, earlyo_ref, tapso_ref,
                  tgc, tgt, dxa, pg, cw, lines, flat, grads, edge, edge_send, edge_recv, got, send, recv, nat, *comm):
    t = pl.program_id(0)
    nc, nx, ny, nz = sizes
    items, rows = ny * nz, nc * nx
    tokens = tgc.shape[0]
    group = tokens // NP
    count, _, height, width = ig_ref.shape
    nrow = height // PATCH
    pos = place(sizes)
    item, row = lax.axis_index("items"), lax.axis_index("rows")
    final_row = lax.axis_size("rows") - 1
    far_steps = STEPS * (nx - 1)
    image_step = 2 * STEPS + far_steps
    final_step = image_step + CIN - 1
    at = 4 * STEPS + 2
    patch = make_pieces(
        sizes, pos, FINISH_ORDERS[0:STEPS], [grads.at[q % 2] for q in range(STEPS)],
        [grads.at[q % 2, pos[0]] for q in range(STEPS)], comm[0:at],
    )
    keep = comm[at + 14 : at + 16]
    square = make_pieces(
        sizes, pos, FINISH_ORDERS[STEPS : STEPS + 3], [sq_ref.at[n] for n in range(3)],
        [keep[0].at[n] for n in range(3)], comm[at : at + 14],
    )
    loads = [pltpu.make_async_copy(sq_ref.at[n, pos[0]], keep[0].at[n], keep[1].at[n]) for n in range(3)]
    at += 16
    early = SmallSum(sizes, pos, comm[at : at + 4], comm[at + 4], comm[at + 5])
    late = SmallSum(sizes, pos, comm[at + 6 : at + 10], comm[at + 10], comm[at + 11])

    def edge_copy(n):
        step = -1 if n == 0 else 1
        return pltpu.make_async_remote_copy(
            src_ref=edge.at[n], dst_ref=edge.at[2 + n], send_sem=edge_send.at[n], recv_sem=edge_recv.at[n],
            device_id=(item, row + step), device_id_type=MESH,
        )

    share, per = tokens // nx, group // nx
    turns = [turn_of(sizes, pos, xg) * share for xg in range(nx)]

    def spread(j, c):
        return jnp.concatenate(
            [dxa[j, pl.ds(pl.multiple_of(turns[xg] + c * per, per), per), :] for xg in range(nx)], axis=0
        )

    def parcel(k):
        to = lax.rem(row + k, rows)
        return pltpu.make_async_remote_copy(
            src_ref=tg_ref.at[:, to], dst_ref=got.at[row], send_sem=send.at[k - 1], recv_sem=recv.at[row],
            device_id=(item, to), device_id_type=MESH,
        )

    def arrived(source):
        pltpu.make_async_remote_copy(
            src_ref=tg_ref.at[:, source], dst_ref=got.at[source], send_sem=send.at[0], recv_sem=recv.at[source],
            device_id=(item, source), device_id_type=MESH,
        ).wait_recv()

    def unpack(xg, turn):
        for k in range(D // 128):
            cut = got[pl.ds(2 * xg, 2), :, :, k * 128 : (k + 1) * 128]
            nat[k] = cut.reshape(share, 128).astype(F32)
        for c in range(NP):
            part = jnp.concatenate([nat[k, pl.ds(c, per, stride=NP), :] for k in range(D // 128)], axis=1)
            tgc[turn * share + c * per : turn * share + (c + 1) * per, :] = part.astype(BF)

    def turn_over(turn):
        for s in range(share // 256):
            rs = slice(turn * share + s * 256, turn * share + (s + 1) * 256)
            tgt[:, rs] = tgc[rs, :].T

    def put_lines(j):
        low = lax.broadcasted_iota(jnp.int32, (group, 2 * HALF), 1) < HALF
        for pair in range(NP // 2):
            a, b = spread(j, 2 * pair), spread(j, 2 * pair + 1)
            cs = slice(pair * 128, (pair + 1) * 128)
            lines[2 * j * group : (2 * j + 1) * group, cs] = jnp.where(low, a, pltpu.roll(b, HALF, 1)).astype(BF)
            lines[(2 * j + 1) * group : (2 * j + 2) * group, cs] = jnp.where(low, pltpu.roll(a, HALF, 1), b).astype(BF)

    def event(index, stage):
        if index < STEPS:
            if stage == 0:
                patch[index].start(0)
            elif stage < 4:
                patch[index].advance(stage)
            else:
                total = unfold_block(patch[index].gather(3), D // rows, FEAT // items)
                for c in range(CH // items):
                    at = c * PATCH * PATCH + index * 2 * PATCH
                    pw_ref[:, at : at + 2 * PATCH] = total[:, c * 2 * PATCH : (c + 1) * 2 * PATCH]
        elif index < STEPS + 3:
            n = index - STEPS
            if stage == 0:
                loads[n].start()
                square[n].start(0)
                return
            if stage == 1:
                loads[n].wait()
            if stage < 4:
                square[n].advance(stage)
            else:
                out = (sq0_ref, sq1_ref, sq2_ref)[n]
                out[...] = unfold_block(square[n].gather(3), *out.shape, odd=pos[0] == 1)
        else:
            part, out = ((early, earlyo_ref), (late, tapso_ref))[index - STEPS - 3]
            if stage < 4:
                part.advance(stage)
            else:
                out[...] = part.gather(3)

    opening, table = [], {}
    for when, index, stage in FINISH_PLAN:
        if stage > 0 or index < STEPS + 3:
            call = functools.partial(event, index, stage)
            if when == 0:
                opening.append(call)
            else:
                later = when - 1 + (far_steps - STEPS if when > 3 * STEPS else 0)
                table.setdefault((min(later, final_step), 0), []).append(call)

    @pl.when(t == 0)
    def _():
        @pl.when(row == final_row)
        def _():
            edge[2] = jnp.zeros(edge.shape[1:], BF)

        @pl.when(row == 0)
        def _():
            edge[3] = jnp.zeros(edge.shape[1:], BF)

        greet(sizes, pos, True, True)
        for k in range(1, rows):
            parcel(k).start()
        for call in opening:
            call()
        got[row] = tg_ref[:, row]
        arrived(2 * pos[1] + 1 - pos[0])
        unpack(pos[1], nx - 1)
        turn_over(nx - 1)
        cw[...] = jnp.zeros_like(cw)

    @pl.when(t == STEPS)
    def _():
        for turn in range(nx - 1):
            xg = lax.rem(pos[1] + 1 + turn, nx)
            arrived(2 * xg)
            arrived(2 * xg + 1)
            unpack(xg, turn)
            turn_over(turn)

    @pl.when(t == STEPS + 1)
    def _():
        total = jnp.zeros((1, D), F32)
        for s in range(tokens // 256):
            total = total + col_sum(tgc[s * 256 : (s + 1) * 256, :].astype(F32))
        lines_in = [sums2_ref[0:1], sums2_ref[1:2], sums2_ref[2:3], sums2_ref[3:4]]
        lines_in += [hbg_ref[:, n * D : (n + 1) * D] for n in range(FF // D)]
        lines_in += [sums1_ref[0:1], sums1_ref[1:2], qvs_ref[0:1], qvs_ref[1:2], total]
        cells = [one[:, k * 128 : (k + 1) * 128] for one in lines_in for k in range(D // 128)]
        early.start(0, jnp.concatenate(cells + [jnp.zeros((EARLY - len(cells), 128), F32)], axis=0))

    @pl.when((t >= STEPS) & (t < 2 * STEPS))
    def _():
        for q in range(2, STEPS):
            @pl.when(t == STEPS + q)
            def _(q=q):
                patch[q - 2].drain((0,))

        feats = FEAT // items
        slot = t % 2
        for n in range(FEAT // 256):
            grad = mm(tgt[...], act_ref[0, 0, :, n * 256 : (n + 1) * 256]).astype(BF)
            for c in range(256 // feats):
                i = n * (256 // feats) + c
                for r in range(rows):
                    block = grad[r * (D // rows) : (r + 1) * (D // rows), c * feats : (c + 1) * feats]
                    grads[slot, r % 2, r // 2, i % ny, i // ny] = fold_block(block)

    def stem_part(p, turn):
        weight = w_ref[...].reshape(FEAT, D)

        def at(s, size):
            return pl.ds(pl.multiple_of(turn * share + s * 256, 256), size)

        @pl.when(p == 0)
        def _():
            dxa[0, at(0, share), :] = jnp.zeros((share, 128), F32)

        for s in range(share // 256):
            rs = slice(s * 256, (s + 1) * 256)
            for n in range(FEAT // 256):
                cs = slice(n * 256, (n + 1) * 256)
                da = mm_t(tgc[at(s, 256), :], weight[cs, :])
                pg[rs, cs] = (slope_ref[0, 0, rs, cs].astype(F32) * da).astype(BF)
            back = mm_t(pg[rs, :], t_ref[...])
            dxa[p, at(s, 256), :] += back[:, 0:128]
            dxa[p + 1, at(s, 256), :] = back[:, 128:256]
        xt = jnp.concatenate([xt_ref[p, :, at(0, share)], xt_ref[p + 1, :, at(0, share)]], axis=0)
        cw[...] += mm(xt, pg[...])

    near, far = t < STEPS, (t >= 2 * STEPS) & (t < image_step)

    @pl.when(near | far)
    def _():
        stem_part(t % STEPS, jnp.where(near, nx - 1, t // STEPS - 2))

    @pl.when((t >= image_step - STEPS) & (t < image_step))
    def _():
        p = t % STEPS

        @pl.when(p == 0)
        def _():
            put_lines(0)
            for ch in range(CIN):
                head = mm_t(lines[0:group], sel_ref[ch * width : (ch + 1) * width, :])
                edge[0, ch] = (pltpu.roll(head, nrow - 1, 0) if nrow > 1 else head).astype(BF)

            @pl.when(row > 0)
            def _():
                edge_copy(0).start()

        @pl.when(p == STEPS - 1)
        def _():
            put_lines(SLABS - 1)
            for ch in range(CIN):
                tail = mm_t(lines[(WIN - 1) * group : WIN * group], sel_ref[ch * width : (ch + 1) * width, :])
                edge[1, ch] = (pltpu.roll(tail, group - nrow + 1, 0) if nrow > 1 else tail).astype(BF)

            @pl.when(row < final_row)
            def _():
                edge_copy(1).start()

            late.start(0, tap_grad_rows(cw[...]))

    @pl.when(t >= image_step)
    def _():
        ch = t - image_step

        @pl.when(t == image_step)
        def _():
            for j in range(1, SLABS - 1):
                put_lines(j)

            @pl.when(row < final_row)
            def _():
                edge_copy(0).wait_recv()

            @pl.when(row > 0)
            def _():
                edge_copy(1).wait_recv()

        patch_row = lax.broadcasted_iota(jnp.int32, (group, width), 0) % nrow
        res = mm_t(lines[...], sel_ref[pl.ds(pl.multiple_of(ch * width, width), width), :])
        head = res[0:group]
        tail = res[(PATCH + 1) * group : (PATCH + 2) * group]
        for r in range(PATCH):
            v = res[(r + 1) * group : (r + 2) * group]
            if r == 0:
                v = v + jnp.where(patch_row == 0, edge[3, ch].astype(F32), pltpu.roll(tail, 1, 0))
            if r == PATCH - 1:
                v = v + jnp.where(patch_row == nrow - 1, edge[2, ch].astype(F32), pltpu.roll(head, group - 1, 0))
            flat[0, pl.ds(r, group, stride=PATCH), :] = v[:, 0:128]
            flat[1, pl.ds(r, group, stride=PATCH), :] = v[:, 128:256]
        for n in range(count):
            at = slice(n * height, (n + 1) * height)
            ig_ref[n, 0, :, 0:128] = flat[0, at, :]
            ig_ref[n, 0, :, 128:256] = flat[1, at, :]

    def close():
        for part in square:
            part.drain()
        for q, part in enumerate(patch):
            part.drain((1, 2, 3) if q < STEPS - 2 else (0, 1, 2, 3))
        early.drain()
        late.drain()
        for k in range(1, rows):
            parcel(k).wait_send()

        @pl.when(row > 0)
        def _():
            edge_copy(0).wait_send()

        @pl.when(row < final_row)
        def _():
            edge_copy(1).wait_send()

    table.setdefault((final_step, 0), []).append(close)
    run_events(t, table, (0,))


def finish(tg, saved, weight, xt, taps, sel, squares, sums2, hbg, sums1, qvs, count, height, sizes):
    nc, nx, ny, nz = sizes
    items, rows = ny * nz, nc * nx
    group = count * height // PATCH
    tokens = group * NP
    feats = FEAT // items
    square = squares.shape[5:]
    share = tokens // nx
    image_step = STEPS * (nx + 1)

    def clip(v, low, high):
        return jnp.minimum(jnp.maximum(v, low), high)

    def sub(t):
        held = jnp.where(t < STEPS, t, jnp.where(t < 2 * STEPS, 0, t % STEPS))
        return jnp.where(t < image_step, held, STEPS - 1)

    def turn(t):
        return jnp.where(t < STEPS, nx - 1, clip(t // STEPS - 2, 0, nx - 2))

    return pl.pallas_call(
        functools.partial(finish_kernel, sizes),
        name="finish",
        grid=(image_step + CIN,),
        in_specs=[
            whole(tg.shape),
            pl.BlockSpec((1, 1, tokens, FEAT), lambda t: (clip(t - STEPS, 0, STEPS - 1), 0, 0, 0)),
            pl.BlockSpec((1, 1, share, FEAT), lambda t: (sub(t), 1, turn(t), 0)),
            pl.BlockSpec((CH, 1, 2 * PATCH, D), lambda t: (0, sub(t), 0, 0)),
            whole(xt.shape),
            whole(taps.shape),
            whole(sel.shape),
            pl.BlockSpec(memory_space=pl.ANY),
            whole(sums2.shape), whole(hbg.shape), whole(sums1.shape), whole(qvs.shape),
        ],
        out_specs=(
            whole((D // rows, PF // items)),
            whole((D // items, D // rows)),
            whole((D // items, D // rows)),
            whole((D // items, D // rows)),
            pl.BlockSpec((count, 1, height, IMG), lambda t: (0, clip(t - image_step, 0, CIN - 1), 0, 0)),
            whole((EARLY, 128)),
            whole((32, 128)),
        ),
        out_shape=(
            jax.ShapeDtypeStruct((D // rows, PF // items), F32),
            jax.ShapeDtypeStruct((D // items, D // rows), F32),
            jax.ShapeDtypeStruct((D // items, D // rows), F32),
            jax.ShapeDtypeStruct((D // items, D // rows), F32),
            jax.ShapeDtypeStruct((count, CIN, height, IMG), F32),
            jax.ShapeDtypeStruct((EARLY, 128), F32),
            jax.ShapeDtypeStruct((32, 128), F32),
        ),
        scratch_shapes=[
            pltpu.VMEM((tokens, D), BF),
            pltpu.VMEM((D, tokens), BF),
            pltpu.VMEM((SLABS, tokens, 128), F32),
            pltpu.VMEM((share, FEAT), BF),
            pltpu.VMEM((4 * HALF, FEAT), F32),
            pltpu.VMEM((WIN * group, NP * HALF), BF),
            pltpu.VMEM((2, group * PATCH, 128), F32),
            pltpu.VMEM((2,) + sizes + folded_shape(D // rows, feats), BF),
            pltpu.VMEM((4, CIN, group, IMG), BF),
            pltpu.SemaphoreType.DMA((2,)),
            pltpu.SemaphoreType.DMA((2,)),
            pltpu.VMEM((rows, SEQ_ITEMS, tokens // rows // SEQ_ITEMS, D), BF),
            pltpu.SemaphoreType.DMA((rows - 1,)),
            pltpu.SemaphoreType.DMA((rows,)),
            pltpu.VMEM((D // 128, share, 128), F32),
        ]
        + piece_scratch(sizes, FINISH_ORDERS[0:STEPS], folded_shape(D // rows, feats))
        + piece_scratch(sizes, FINISH_ORDERS[STEPS : STEPS + 3], square) + own_scratch(sizes, 3, square)
        + small_scratch(sizes, EARLY)
        + small_scratch(sizes, 32),
        compiler_params=params(collective_id=2, has_side_effects=True),
    )(tg, saved, saved, weight, xt, taps, sel, squares, sums2, hbg, sums1, qvs)


def feature_parts(rows):
    feat = lax.broadcasted_iota(jnp.int32, (rows, FEAT), 1)
    return feat // (2 * PATCH), feat // PATCH % 2, feat % PATCH


def tap_rows(wide, ch, r, b, half):
    parts = []
    for r2 in range(2):
        a = r - r2
        parts.append(wide[9 * ch + 3 * a + b : 9 * ch + 3 * a + b + 1, :] if 0 <= a < 3 else jnp.zeros((1, FEAT), F32))
    return jnp.where(half == 0, parts[0], parts[1])


def tap_matrix(cw_ref, cb_ref, t_ref):
    chan, _, _ = feature_parts(32)
    expand = jnp.where(chan == lax.broadcasted_iota(jnp.int32, (32, FEAT), 0), 1.0, 0.0).astype(BF)
    wide = lax.dot_general(cw_ref[...], expand, (((0,), (0,)), ((), ())), preferred_element_type=F32)
    bias = mm(jnp.broadcast_to(as_row(cb_ref), (8, CH)).astype(BF), expand)
    _, half, spot = feature_parts(1)
    line = lax.broadcasted_iota(jnp.int32, (HALF, FEAT), 0)
    for r in range(4):
        block = jnp.zeros((HALF, FEAT), F32)
        if r == 0:
            block = jnp.where(line == ONE_LANE, bias[0:1, :], block)
        for ch in range(CIN):
            for b in range(3):
                block = jnp.where(line == WIN * ch + b + spot, tap_rows(wide, ch, r, b, half), block)
        t_ref[r * HALF : (r + 1) * HALF, :] = block.astype(BF)


def tap_grad_rows(full):
    chan, half, spot = feature_parts(1)
    line = lax.broadcasted_iota(jnp.int32, (HALF, FEAT), 0)
    sums = [[None] * 3 for _ in range(9)]
    for r in range(4):
        block = full[r * HALF : (r + 1) * HALF]
        for ch in range(CIN):
            for b in range(3):
                line_sum = jnp.sum(jnp.where(line == WIN * ch + b + spot, block, 0.0), axis=0, keepdims=True)
                for a in range(3):
                    if 0 <= r - a < 2:
                        part = jnp.where(half == r - a, line_sum, 0.0)
                        old = sums[3 * ch + b][a]
                        sums[3 * ch + b][a] = part if old is None else old + part
    lines = [sums[3 * ch + b][a] for ch in range(CIN) for a in range(3) for b in range(3)]
    lines.append(full[ONE_LANE : ONE_LANE + 1])
    lines.append(jnp.zeros((4, FEAT), F32))
    table = jnp.concatenate(lines, axis=0)
    chan, _, _ = feature_parts(128)
    expand = jnp.where(chan == lax.broadcasted_iota(jnp.int32, (128, FEAT), 0), 1.0, 0.0).astype(BF)
    hi, mid, lo = three_terms(table)
    return mm_t(hi, expand) + (mm_t(mid, expand) + mm_t(lo, expand))


def on_device(
    images, item_segment, conv_weight, conv_bias, patch_weight, patch_bias, norm1_gain, norm1_bias,
    query_weight, query_bias, key_weight, value_weight, value_bias, output_weight, output_bias,
    norm2_gain, norm2_bias, hidden_weight, hidden_bias, result_weight, result_bias, cotangent,
):
    items, rows = lax.axis_size("items"), lax.axis_size("rows")
    sizes = grid_sizes(items, rows)
    count, _, height, _ = images.shape
    nrow = height // PATCH

    cw = conv_weight.reshape(CH, 27)
    weight4 = patch_weight.reshape(CH, STEPS, 2 * PATCH, D)
    tokens, saved, xt, sel, taps = stem_forward(images, cw, conv_bias, weight4, patch_bias, sizes)
    tokens = tokens.reshape(TOK, D)
    q, k, v, attended, attended32, lx, kx = attend(
        tokens, (norm1_gain, norm1_bias, query_bias, value_bias), item_segment, query_weight, key_weight, value_weight)
    block_out, middle_grad, attended_grad, wo_grad, wh_grad, wr_grad, sums2, hb_grad = mixer(
        tokens, attended, cotangent, output_weight,
        (output_bias, norm2_gain, norm2_bias, result_bias, hidden_bias), hidden_weight, result_weight, sizes,
    )
    token_grad, squares, sums1, qvs, wh_grad, wr_grad, wo_grad = attend_back(
        tokens, norm1_gain, norm1_bias, kx, middle_grad, q, k, v, attended32, attended_grad, lx,
        query_weight, key_weight, value_weight, wh_grad, wr_grad, wo_grad, sizes,
    )
    token_grad = token_grad.reshape(SEQ_ITEMS, rows, nrow * NP, D)
    pw_grad, wq_grad, wk_grad, wv_grad, image_grad, sums, tap_grads = finish(
        token_grad, saved, weight4, xt, taps, sel, squares, sums2, hb_grad, sums1, qvs, count, height, sizes
    )
    wide = D // 128

    def row_of(at):
        return sums[at * wide : (at + 1) * wide].reshape(D)

    return (
        block_out,
        image_grad,
        tap_grads[0:27, 0:CH].T.reshape(conv_weight.shape),
        tap_grads[27, 0:CH],
        pw_grad.T,
        row_of(12),
        row_of(8),
        row_of(9),
        wq_grad,
        row_of(10),
        wk_grad,
        wv_grad,
        row_of(11),
        wo_grad,
        row_of(2),
        row_of(0),
        row_of(1),
        wh_grad,
        sums[4 * wide : 8 * wide].reshape(FF),
        wr_grad.T,
        row_of(3),
    )


def solution(mesh):
    split = P("items", "rows")
    flat = P(("items", "rows"), None)
    image = P("items", None, "rows", None)
    return jax.shard_map(
        on_device,
        mesh=mesh,
        in_specs=(image, P("items")) + (P(),) * 19 + (flat,),
        out_specs=(
            flat, image, P(), P(), split, P(), P(), P(), split, P(), split, split,
            P(), split, P(), P(), P(), split, P(), split, P(),
        ),
        check_vma=False,
    )
```
